32 devices in a mesh: dp: 8 (over y, x, core), fsdp: 4 (over z).
Axes of the slice: x: 2, y: 2, z: 4, core: 2. Of those that a mesh axis runs over, the one named last changes fastest.
Arguments:
- tokens: bfloat16 [32, 512, 1024], P(('dp', 'fsdp')), may hold values from -6 to 6
- crop_ids: int32 [32, 512], P(('dp', 'fsdp')), may hold values from 0 to 2, never falling along the last dimension, each value on 1 to 384 neighbouring positions
- kv_mask: int32 [32, 512], P(('dp', 'fsdp')), may hold values 0 or 1
- norm1_gain: bfloat16 [1024], P(('dp', 'fsdp')), may hold values from 0.099609375 to 1.8984375
- norm1_bias: bfloat16 [1024], P(('dp', 'fsdp')), may hold values from -4 to 4
- w_query: bfloat16 [1024, 1024], P(('dp', 'fsdp')), may hold values from -0.1875 to 0.1875
- w_key: bfloat16 [1024, 1024], P(('dp', 'fsdp')), may hold values from -0.1875 to 0.1875
- w_value: bfloat16 [1024, 1024], P(('dp', 'fsdp')), may hold values from -0.1875 to 0.1875
- w_out: bfloat16 [1024, 1024], P(('dp', 'fsdp')), may hold values from -2 to 2
- norm2_gain: bfloat16 [1024], P(('dp', 'fsdp')), may hold values from 0.099609375 to 1.8984375
- norm2_bias: bfloat16 [1024], P(('dp', 'fsdp')), may hold values from -4 to 4
- w_up: bfloat16 [1024, 4096], P(('dp', 'fsdp')), may hold values from -0.1875 to 0.1875
- up_bias: bfloat16 [4096], P(('dp', 'fsdp')), may hold values from -6 to 6
- w_down: bfloat16 [4096, 1024], P(('dp', 'fsdp')), may hold values from -0.09375 to 0.09375
- down_bias: bfloat16 [1024], P(('dp', 'fsdp')), may hold values from -4 to 4
- cotangent: bfloat16 [32, 512, 1024], P(('dp', 'fsdp')), may hold values from -6 to 6
Outputs:
- output: bfloat16 [32, 512, 1024], P(('dp', 'fsdp'))
- input_grad: bfloat16 [32, 512, 1024], P(('dp', 'fsdp'))
- grad_norm1_gain: float32 [1024], P(('dp', 'fsdp'))
- grad_norm1_bias: float32 [1024], P(('dp', 'fsdp'))
- grad_w_query: float32 [1024, 1024], P(('dp', 'fsdp'))
- grad_w_key: float32 [1024, 1024], P(('dp', 'fsdp'))
- grad_w_value: float32 [1024, 1024], P(('dp', 'fsdp'))
- grad_w_out: float32 [1024, 1024], P(('dp', 'fsdp'))
- grad_norm2_gain: float32 [1024], P(('dp', 'fsdp'))
- grad_norm2_bias: float32 [1024], P(('dp', 'fsdp'))
- grad_w_up: float32 [1024, 4096], P(('dp', 'fsdp'))
- grad_up_bias: float32 [4096], P(('dp', 'fsdp'))
- grad_w_down: float32 [4096, 1024], P(('dp', 'fsdp'))
- grad_down_bias: float32 [1024], P(('dp', 'fsdp'))
The draws below stay inside these ranges and needn't reach their ends.
Inputs may be any that keep to these rules, and one draw needn't show every extreme that they name: `crop_ids`: in every slot the crop ids never fall, each of the 3 crops has 1 to 384 pixels, and one crop has exactly 384.
All inputs are finite; a program needn't handle non-finite values. No bound on the sum of `kv_mask` on one device may be relied on, other than what follows from the above.
Results may differ from the reference program's by a relative error of at most 0.0093.
Values may be sent and summed in bfloat16 or wider, within the bound.
A program may use at most 192 MiB of HBM per device.

```python
import math
import jax
import jax.numpy as jnp
import numpy as np
from jax import lax

D = 1024
HEADS = 16
HEAD_DIM = 64
FF = 4096
SLOT_LEN = 512
CROP_MAX = 384
CROPS = 3
BLOCK = 512
SLOTS = 32


def set_ends(drawn, rng, low, top_value):
    place = [jax.random.randint(jax.random.fold_in(rng, axis), (), 0, length) for axis, length in enumerate(drawn.shape)]
    widest = drawn.shape.index(max(drawn.shape))
    next_to = place[:widest] + [(place[widest] + 1) % drawn.shape[widest]] + place[widest + 1:]
    return drawn.at[tuple(place)].set(low).at[tuple(next_to)].set(top_value)


def level_of(stream_key, extent, shards, least, high):
    gain, own = 1.0, jax.random.fold_in(stream_key, 6)
    for position, shards_of in shards:
        draws = jnp.exp(jax.random.uniform(jax.random.fold_in(own, position), (shards_of,), jnp.float32, least / len(shards), high / len(shards)))
        gain = gain * jnp.repeat(draws, extent[position] // shards_of).reshape([-1 if axis == position else 1 for axis in range(len(extent))])
    return gain


def profile(count, total, bound, lean):
    portions = [(1 << 20) // math.isqrt(standing ** lean) + 1 for standing in range(2, count + 1)]
    spare, given = total - bound - (count - 1), [1] * (count - 1)
    while spare > 0:
        candidates = [i for i in range(count - 1) if given[i] < bound]
        whole, left = sum([portions[i] for i in candidates]), spare
        for i in candidates:
            addition = min(bound - given[i], max(1, left * portions[i] // whole), spare)
            given[i] = given[i] + addition
            spare = spare - addition
    return np.array([bound] + given)


def uneven_parts(stream_key, count, total, reach, skew):
    if count == 2:
        one = jax.random.randint(stream_key, (), max(1, total - reach), min(reach, total - 1) + 1)
        return jnp.stack([one, total - one])
    sizes = jnp.asarray(profile(count, total, reach, skew), jnp.int32)
    twos = (count - 1) // 2
    source_of, receiver = sizes[1:1 + 2 * twos:2], sizes[2:2 + 2 * twos:2]
    margin = jnp.minimum(source_of - 1, reach - receiver)
    shifted = jax.random.randint(jax.random.fold_in(stream_key, 1), (twos,), 0, 1 << 20) % (margin + 1)
    sizes = sizes.at[1:1 + 2 * twos:2].set(source_of - shifted).at[2:2 + 2 * twos:2].set(receiver + shifted)
    return sizes[jax.random.permutation(jax.random.fold_in(stream_key, 2), count)]


def bell_draw(own_key, shape, deviation, limit, cuts=(), kind=jnp.bfloat16):
    values = jax.random.normal(own_key, shape, jnp.float32) * deviation
    if len(cuts) > 0:
        values = level_of(own_key, shape, cuts, -0.22, 0.18) * values
    return jnp.clip(values, min=-limit, max=limit).astype(kind)


def setup_inputs(seed: int = 0) -> dict:
    key_list = jax.random.split(jax.random.key(seed), 17)
    return {
        "tokens": bell_draw(key_list[0], (SLOTS, SLOT_LEN, D), 1.0, 6.0, ((0, 32),)),
        "crop_ids": jax.vmap(lambda own: jnp.searchsorted(jnp.cumsum(uneven_parts(own, CROPS, SLOT_LEN, CROP_MAX, 2)), jnp.arange(SLOT_LEN), side="right"))(jax.random.split(key_list[1], SLOTS)).reshape((SLOTS, SLOT_LEN)).astype(jnp.int32),
        "kv_mask": set_ends((jax.random.randint(key_list[2], (SLOTS, SLOT_LEN), 0, 8) < 7).astype(jnp.int32), jax.random.fold_in(key_list[2], 1), 0, 1),
        "norm1_gain": jnp.clip(1.0 + 0.18 * jax.random.normal(key_list[3], (D,), jnp.float32), 0.099609375, 1.8984375).astype(jnp.bfloat16),
        "norm1_bias": bell_draw(key_list[4], (D,), 0.3, 4.0, ((0, 32),)),
        "w_query": bell_draw(key_list[5], (D, D), D ** -0.5, 0.1875, ((0, 32),)),
        "w_key": bell_draw(key_list[6], (D, D), D ** -0.5, 0.1875, ((0, 32),)),
        "w_value": bell_draw(key_list[7], (D, D), D ** -0.5, 0.1875, ((0, 32),)),
        "w_out": bell_draw(key_list[8], (D, D), (D * 4 // CROP_MAX) ** -0.5, 2.0, ((0, 32),)),
        "norm2_gain": jnp.clip(1.0 + 0.18 * jax.random.normal(key_list[9], (D,), jnp.float32), 0.099609375, 1.8984375).astype(jnp.bfloat16),
        "norm2_bias": bell_draw(key_list[10], (D,), 0.3, 4.0, ((0, 32),)),
        "w_up": bell_draw(key_list[11], (D, FF), D ** -0.5, 0.1875, ((0, 32),)),
        "up_bias": bell_draw(key_list[12], (FF,), 0.5, 6.0, ((0, 32),)),
        "w_down": bell_draw(key_list[13], (FF, D), FF ** -0.5, 0.09375, ((0, 32),)),
        "down_bias": bell_draw(key_list[14], (D,), 0.3, 4.0, ((0, 32),)),
        "cotangent": bell_draw(key_list[15], (SLOTS, SLOT_LEN, D), 1.0, 6.0, ((0, 32),)),
    }


@jax.custom_vjp
def low(v):
    return lax.optimization_barrier(v.astype(jnp.bfloat16)).astype(jnp.float32)

@jax.custom_vjp
def low_back(v):
    return v

def low_keep(v):
    return (low(v), None)

def low_pass(kept, grad):
    return (grad,)

def back_keep(v):
    return (v, None)

def back_low(kept, grad):
    return (low(grad),)
low.defvjp(low_keep, low_pass)
low_back.defvjp(back_keep, back_low)
HIGH = lax.Precision.HIGHEST
norm_eps = 1e-05

def normalize(values):
    mean = lax.optimization_barrier(jnp.mean(values, axis=-1, keepdims=True))
    centred = values - mean
    spread = lax.optimization_barrier(jnp.mean(centred * centred, axis=-1, keepdims=True))
    return centred * lax.rsqrt(spread + norm_eps)

def matmul(left, right):
    return jnp.dot(left, right, precision=HIGH)

def feature(values):
    return jax.nn.elu(values) + 1.0

def allowed_weight(crop, keymask):
    places = jnp.arange(crop.shape[0])
    earlier = places[None, :] <= places[:, None]
    same = crop[:, None] == crop[None, :]
    visible = (keymask[None, :] > 0) | (places[None, :] == places[:, None])
    return (earlier & same & visible).astype(jnp.float32)

def attend_block(carry, pieces):
    state, norm_state, prev_crop = carry
    query_feat, key_feat, values, crop, keymask = pieces
    size = crop.shape[0]
    weight = allowed_weight(crop, keymask)
    scores = jnp.einsum('ihe,jhe->hij', query_feat, key_feat, precision=HIGH) * weight[None]
    numer = jnp.einsum('hij,jhe->ihe', scores, values, precision=HIGH)
    denom = lax.optimization_barrier(jnp.sum(scores, axis=2)).T
    follows = (crop == prev_crop).astype(query_feat.dtype)
    numer = numer + follows[:, None, None] * jnp.einsum('ihe,hef->ihf', query_feat, state, precision=HIGH)
    denom = denom + follows[:, None] * jnp.einsum('ihe,he->ih', query_feat, norm_state, precision=HIGH)
    last_crop = crop[size - 1]
    carried = (prev_crop == last_crop).astype(query_feat.dtype)
    select = ((crop == last_crop) & (keymask > 0)).astype(query_feat.dtype)
    chosen = key_feat * select[:, None, None]
    state = carried * state + jnp.einsum('jhe,jhf->hef', chosen, values, precision=HIGH)
    norm_state = carried * norm_state + lax.optimization_barrier(jnp.sum(chosen, axis=0))
    return ((state, norm_state, last_crop), numer / denom[:, :, None])

def layer(params, inputs, crop, keymask):
    gain_one, bias_one, w_query, w_key, w_value, w_out, gain_two, bias_two, w_up, up_bias, w_down, down_bias = params
    length = inputs.shape[0]
    normed = low(normalize(inputs) * gain_one + bias_one)
    query = low_back(matmul(normed, w_query))
    keys = low_back(matmul(normed, w_key))
    values = low(low_back(matmul(normed, w_value)))
    query_feat = low(feature(query)).reshape(length, HEADS, HEAD_DIM)
    key_feat = low(feature(keys)).reshape(length, HEADS, HEAD_DIM)
    values = values.reshape(length, HEADS, HEAD_DIM)
    blocks = length // BLOCK

    def split(array):
        return array.reshape((blocks, BLOCK) + array.shape[1:])
    start = (jnp.zeros((HEADS, HEAD_DIM, HEAD_DIM), jnp.float32), jnp.zeros((HEADS, HEAD_DIM), jnp.float32), jnp.int32(-1))
    finish, mixed = lax.scan(jax.checkpoint(attend_block), start, (split(query_feat), split(key_feat), split(values), split(crop), split(keymask)))
    mixed = low(mixed.reshape(length, HEADS * HEAD_DIM))
    attended = low_back(matmul(mixed, w_out))
    middle = inputs + attended
    normed_two = low(normalize(middle) * gain_two + bias_two)
    upper = low_back(matmul(normed_two, w_up) + up_bias)
    hidden = low(jax.nn.gelu(upper, approximate=False))
    return middle + matmul(hidden, w_down) + down_bias

def reference(tokens, crop_ids, kv_mask, norm1_gain, norm1_bias, w_query, w_key, w_value, w_out, norm2_gain, norm2_bias, w_up, up_bias, w_down, down_bias, cotangent):
    params = tuple((item.astype(jnp.float32) for item in (norm1_gain, norm1_bias, w_query, w_key, w_value, w_out, norm2_gain, norm2_bias, w_up, up_bias, w_down, down_bias)))

    def one_slot(summed, pieces):
        slot_tokens, crop, keymask, slot_cot = pieces

        def forward(weights, inputs):
            return layer(weights, inputs, crop, keymask)
        result, pull = jax.vjp(forward, params, slot_tokens.astype(jnp.float32))
        weight_grads, token_grad = pull(slot_cot.astype(jnp.float32))
        summed = tuple((before + gradient for before, gradient in zip(summed, weight_grads)))
        return (summed, (result.astype(jnp.bfloat16), token_grad.astype(jnp.bfloat16)))
    zeros = tuple((jnp.zeros(item.shape, jnp.float32) for item in params))
    summed, (output, input_grad) = lax.scan(one_slot, zeros, (tokens, crop_ids, kv_mask, cotangent))
    return (output, input_grad, summed[0], summed[1], summed[2], summed[3], summed[4], summed[5], summed[6], summed[7], summed[8], summed[9], summed[10], summed[11])
```

```python
import functools

import jax
import jax.numpy as jnp
from jax import lax
from jax.experimental import pallas as pl
from jax.experimental.pallas import tpu as pltpu
from jax.sharding import PartitionSpec as P

HEADS = 16
BLOCK = 512
MESH = pl.DeviceIdType.MESH
WIDE = 512
OUTER = 2


class Place:
    def __init__(self, dims):
        self.size = {"a": dims[0], "b": dims[1], "c": 2, "z": dims[2]}
        dp = lax.axis_index("dp")
        self.at = {
            "a": dp // (2 * dims[1]),
            "b": (dp // 2) % dims[1],
            "c": dp % 2,
            "z": lax.axis_index("fsdp"),
        }

    def moved(self, axis, step):
        spot = dict(self.at)
        spot[axis] = (spot[axis] + step) % self.size[axis]
        return spot

    def device(self, axis, step):
        spot = self.moved(axis, step)
        return ((spot["a"] * self.size["b"] + spot["b"]) * 2 + spot["c"], spot["z"])

    def partners(self, axis):
        return range(1, self.size[axis])

    def greet(self):
        barrier = pltpu.get_barrier_semaphore()
        count = 0
        for axis in "abcz":
            for step in self.partners(axis):
                pl.semaphore_signal(
                    barrier, 1, device_id=self.device(axis, step), device_id_type=MESH
                )
                count += 1
        pl.semaphore_wait(barrier, count)


def pieces_of(rows, columns, unit):
    wide = min(WIDE, columns)
    return [
        (row, unit, column, wide)
        for row in range(0, rows, unit)
        for column in range(0, columns, wide)
    ]


def gather_kernel(dims, orders, lag, ahead, pieces, *refs):
    count = len(pieces)
    shards, wholes = refs[:count], refs[count : 2 * count]
    local_sem, send_sem, recv_sem = refs[2 * count :]
    place = Place(dims)
    place.greet()
    chunks = [
        (shard.at[pl.ds(ro, rn), pl.ds(co, cn)], whole, pl.ds(ro, rn), pl.ds(co, cn))
        for shard, whole, items in zip(shards, wholes, pieces)
        for ro, rn, co, cn in items
    ]
    total = len(chunks)
    sent, kept = [], []

    def region(index, done, spot):
        _, whole, rows, columns = chunks[index]
        lead = tuple(slice(None) if axis in done else spot[axis] for axis in "abcz")
        return whole.at[lead + (rows, columns)]

    def copy(index, stage, step, axis, source, target):
        return pltpu.make_async_remote_copy(
            source,
            target,
            send_sem.at[index, stage, step - 1],
            recv_sem.at[index, stage, step - 1],
            device_id=place.device(axis, step),
            device_id_type=MESH,
        )

    def send(index, stage):
        order = orders[index % len(orders)]
        axis, done = order[stage], order[:stage]
        target = region(index, done, place.at)
        for step in place.partners(axis):
            item = copy(index, stage, step, axis, target if done else chunks[index][0], target)
            item.start()
            sent.append(item)

    def receive(index, stage):
        order = orders[index % len(orders)]
        axis, done = order[stage], order[:stage]
        for step in place.partners(axis):
            target = region(index, done, place.moved(axis, place.size[axis] - step))
            copy(index, stage, step, axis, target, target).wait_recv()

    def begin(index):
        if index < total:
            item = pltpu.make_async_copy(
                chunks[index][0], region(index, "", place.at), local_sem.at[index]
            )
            item.start()
            kept.append(item)
            send(index, 0)

    for index in range(ahead):
        begin(index)
    for tick in range(total + 3 * lag):
        begin(tick + ahead)
        for stage in range(4):
            index = tick - stage * lag
            if 0 <= index < total:
                receive(index, stage)
                if stage == 0:
                    kept[index].wait()
                if stage < 3:
                    send(index, stage + 1)
    for item in sent:
        item.wait_send()


def gather(dims, shards, unit, lag=3, ahead=6):
    pieces = [pieces_of(*shard.shape, min(unit, shard.shape[0])) for shard in shards]
    total = sum(len(items) for items in pieces)
    most = max(dims) - 1
    anywhere = pl.BlockSpec(memory_space=pl.ANY)
    orders = ("zbac", "zabc", "zbac", "zabc", "bzac", "azbc")
    wholes = pl.pallas_call(
        functools.partial(gather_kernel, dims, orders, lag, ahead, pieces),
        out_shape=[
            jax.ShapeDtypeStruct(dims[:2] + (2, dims[2]) + shard.shape, shard.dtype)
            for shard in shards
        ],
        in_specs=[anywhere] * len(shards),
        out_specs=[anywhere] * len(shards),
        scratch_shapes=[
            pltpu.SemaphoreType.DMA((total,)),
            pltpu.SemaphoreType.DMA((total, 4, most)),
            pltpu.SemaphoreType.DMA((total, 4, most)),
        ],
        compiler_params=pltpu.CompilerParams(collective_id=0, has_side_effects=True),
        name="gather",
    )(*shards)
    return [whole.reshape((-1, whole.shape[-1])) for whole in wholes]


def scatter_kernel(dims, lag, ahead, pieces, *refs):
    count = len(pieces)
    terms, owned = refs[:count], refs[count : 2 * count]
    main = refs[2 * count : 2 * count + 7]
    side = refs[2 * count + 7 : 2 * count + 12]
    local_sem, send_sem, recv_sem = refs[2 * count + 12 :]
    place = Place(dims)
    place.greet()
    spot = place.at
    chunks = []
    for array, items in enumerate(pieces):
        for ro, rn, co, cn in items:
            index = len(chunks)
            if array == 0:
                rooms = side
                order = "ab"
            else:
                half = (index - 1) // 2
                order = "ab" if index % 2 else "ba"
                first, second = (main[2], main[4]) if index % 2 else (main[3], main[5])
                rooms = (
                    main[0].at[index - 1],
                    main[1].at[index - 1],
                    first.at[half],
                    second.at[half],
                    main[6].at[index - 1],
                )
            chunks.append((terms[array], owned[array], pl.ds(ro, rn), pl.ds(co, cn), order, rooms))
    total = len(chunks)
    sent, kept = [], []

    def copy(index, stage, step, axis, source, target):
        return pltpu.make_async_remote_copy(
            source,
            target,
            send_sem.at[index, stage, step - 1],
            recv_sem.at[index, stage, step - 1],
            device_id=place.device(axis, step),
            device_id_type=MESH,
        )

    def send(index, stage, step, axis, source, target):
        item = copy(index, stage, step, axis, source, target)
        item.start()
        sent.append(item)

    def begin(index):
        if index < total:
            term, _, rows, columns, _, rooms = chunks[index]
            send(index, 0, 1, "c", term.at[:, :, 1 - spot["c"], :, rows, columns], rooms[1])
            item = pltpu.make_async_copy(
                term.at[:, :, spot["c"], :, rows, columns], rooms[0], local_sem.at[index]
            )
            item.start()
            kept.append(item)

    def await_all(index, stage, axis, room):
        for step in place.partners(axis):
            copy(index, stage, step, axis, room.at[step - 1], room.at[step - 1]).wait_recv()

    def pick(order, first, second):
        return (first, second) if order == "ab" else (second, first)

    def after_core(index):
        order, (own, other, came, _, _) = chunks[index][4:]
        kept[index].wait()
        copy(index, 0, 1, "c", other, other).wait_recv()
        axis, rest = order

        def add(where):
            for item in range(place.size[rest]):
                at = pick(order, where, item)
                own[at] = own[at] + other[at]

        for step in place.partners(axis):
            where = place.moved(axis, step)[axis]
            add(where)
            source = own.at[where] if order == "ab" else own.at[:, where]
            send(index, 1, step, axis, source, came.at[step - 1])
        add(spot[axis])

    def after_first(index):
        order, (own, _, came, later, _) = chunks[index][4:]
        axis, rest = order
        await_all(index, 1, axis, came)

        def add(where):
            at = pick(order, spot[axis], where)
            value = own[at].astype(jnp.float32)
            for step in place.partners(axis):
                value = value + came[step - 1, where].astype(jnp.float32)
            own[at] = value.astype(own.dtype)

        for step in place.partners(rest):
            where = place.moved(rest, step)[rest]
            add(where)
            at = pick(order, spot[axis], where)
            send(index, 2, step, rest, own.at[at], later.at[step - 1])
        add(spot[rest])

    def after_second(index):
        _, result, rows, columns, order, (own, _, _, later, last) = chunks[index]
        rest = order[1]
        await_all(index, 2, rest, later)

        def add(where):
            value = own[spot["a"], spot["b"], where].astype(jnp.float32)
            for step in place.partners(rest):
                value = value + later[step - 1, where].astype(jnp.float32)
            return value

        for step in place.partners("z"):
            where = place.moved("z", step)["z"]
            own[spot["a"], spot["b"], where] = add(where).astype(own.dtype)
            send(index, 3, step, "z", own.at[spot["a"], spot["b"], where], last.at[step - 1])
        result[rows, columns] = add(spot["z"])

    def after_last(index):
        _, result, rows, columns, _, (_, _, _, _, last) = chunks[index]
        await_all(index, 3, "z", last)
        value = result[rows, columns]
        for step in place.partners("z"):
            value = value + last[step - 1].astype(jnp.float32)
        result[rows, columns] = value

    for index in range(ahead):
        begin(index)
    for tick in range(total + 3 * lag):
        begin(tick + ahead)
        for stage, work in enumerate((after_core, after_first, after_second, after_last)):
            index = tick - stage * lag
            if 0 <= index < total:
                work(index)
    for item in sent:
        item.wait_send()


def rooms_of(dims, many, unit, wide, dtype):
    outer, inner, depth = dims
    ones, twos = (many + 1) // 2, many // 2
    tail = (unit, wide)
    return [
        pltpu.VMEM((many, outer, inner, depth) + tail, dtype),
        pltpu.VMEM((many, outer, inner, depth) + tail, dtype),
        pltpu.VMEM((ones, outer - 1, inner, depth) + tail, dtype),
        pltpu.VMEM((twos, inner - 1, outer, depth) + tail, dtype),
        pltpu.VMEM((ones, inner - 1, depth) + tail, dtype),
        pltpu.VMEM((twos, outer - 1, depth) + tail, dtype),
        pltpu.VMEM((many, depth - 1) + tail, dtype),
    ]


def scatter(dims, small, terms, unit, lag=2, ahead=4):
    outer, inner, depth = dims
    devices = 2 * outer * inner * depth
    lead = (outer, inner, 2, depth)
    arrays = [small.reshape(lead + small.shape[1:])] + [
        term.reshape(lead + (term.shape[0] // devices, term.shape[1])) for term in terms
    ]
    pieces = [pieces_of(*arrays[0].shape[4:], arrays[0].shape[4])]
    pieces += [pieces_of(*array.shape[4:], unit) for array in arrays[1:]]
    total = sum(len(items) for items in pieces)
    most = max(dims) - 1
    tail = small.shape[1:]
    side = [
        pltpu.VMEM((outer, inner, depth) + tail, jnp.float32),
        pltpu.VMEM((outer, inner, depth) + tail, jnp.float32),
        pltpu.VMEM((outer - 1, inner, depth) + tail, jnp.float32),
        pltpu.VMEM((inner - 1, depth) + tail, jnp.float32),
        pltpu.VMEM((depth - 1,) + tail, jnp.float32),
    ]
    return pl.pallas_call(
        functools.partial(scatter_kernel, dims, lag, ahead, pieces),
        out_shape=[jax.ShapeDtypeStruct(array.shape[4:], jnp.float32) for array in arrays],
        in_specs=[pl.BlockSpec(memory_space=pl.ANY)] * len(arrays),
        out_specs=[pl.BlockSpec(memory_space=pltpu.VMEM)] * len(arrays),
        scratch_shapes=rooms_of(dims, total - 1, unit, WIDE, jnp.bfloat16)
        + side
        + [
            pltpu.SemaphoreType.DMA((total,)),
            pltpu.SemaphoreType.DMA((total, 4, most)),
            pltpu.SemaphoreType.DMA((total, 4, most)),
        ],
        compiler_params=pltpu.CompilerParams(
            collective_id=1, has_side_effects=True, vmem_limit_bytes=60 << 20
        ),
        name="scatter",
    )(*arrays)


HIGH = lax.Precision.HIGHEST
norm_eps = 1e-05


def norm_affine(values, gain, shift):
    mean = jnp.mean(values, axis=-1, keepdims=True)
    centred = values - mean
    spread = jnp.mean(centred * centred, axis=-1, keepdims=True)
    return centred * lax.rsqrt(spread + norm_eps) * gain + shift


def feature(values):
    return jax.nn.elu(values) + 1.0


def gelu_exact(values):
    return jax.nn.gelu(values, approximate=False)


def allowed_weight(crop, keymask):
    places = jnp.arange(crop.shape[0])
    earlier = places[None, :] <= places[:, None]
    same = crop[:, None] == crop[None, :]
    visible = (keymask[None, :] > 0) | (places[None, :] == places[:, None])
    return (earlier & same & visible).astype(jnp.float32)


def attend_forward(carry, pieces):
    state, norm_state, prev_crop = carry
    query_feat, key_feat, values, crop, keymask = pieces
    weight = allowed_weight(crop, keymask)
    scores = (
        jnp.einsum("ihe,jhe->hij", query_feat, key_feat, preferred_element_type=jnp.float32)
        * weight[None]
    )
    value_wide = values.astype(jnp.float32)
    query_wide = query_feat.astype(jnp.float32)
    key_wide = key_feat.astype(jnp.float32)
    numer = jnp.einsum("hij,jhe->ihe", scores, value_wide, precision=HIGH)
    denom = jnp.sum(scores, axis=2).T
    follows = (crop == prev_crop).astype(jnp.float32)
    numer = numer + follows[:, None, None] * jnp.einsum(
        "ihe,hef->ihf", query_wide, state, precision=HIGH
    )
    denom = denom + follows[:, None] * jnp.einsum(
        "ihe,he->ih", query_wide, norm_state, precision=HIGH
    )
    last_crop = crop[crop.shape[0] - 1]
    carried = (prev_crop == last_crop).astype(jnp.float32)
    select = ((crop == last_crop) & (keymask > 0)).astype(jnp.float32)
    chosen = key_wide * select[:, None, None]
    new_state = carried * state + jnp.einsum("jhe,jhf->hef", chosen, value_wide, precision=HIGH)
    new_norm = carried * norm_state + jnp.sum(chosen, axis=0)
    return ((new_state, new_norm, last_crop), (numer / denom[:, :, None], denom, state, norm_state))


def attend_backward(carry, pieces):
    grad_state, grad_norm = carry
    (
        query_feat,
        key_feat,
        values,
        crop,
        keymask,
        prev_crop,
        state,
        norm_state,
        grad_numer,
        grad_denom,
    ) = pieces
    weight = allowed_weight(crop, keymask)
    scores = (
        jnp.einsum("ihe,jhe->hij", query_feat, key_feat, preferred_element_type=jnp.float32)
        * weight[None]
    )
    value_wide = values.astype(jnp.float32)
    query_wide = query_feat.astype(jnp.float32)
    key_wide = key_feat.astype(jnp.float32)
    grad_scores = (
        jnp.einsum("ihe,jhe->hij", grad_numer, value_wide, precision=HIGH)
        + grad_denom.T[:, :, None]
    ) * weight[None]
    follows = (crop == prev_crop).astype(jnp.float32)
    last_crop = crop[crop.shape[0] - 1]
    carried = (prev_crop == last_crop).astype(jnp.float32)
    select = ((crop == last_crop) & (keymask > 0)).astype(jnp.float32)
    grad_query = jnp.einsum("hij,jhe->ihe", grad_scores, key_wide, precision=HIGH)
    grad_query = grad_query + follows[:, None, None] * (
        jnp.einsum("ihf,hef->ihe", grad_numer, state, precision=HIGH)
        + grad_denom[:, :, None] * norm_state[None]
    )
    grad_key = jnp.einsum("hij,ihe->jhe", grad_scores, query_wide, precision=HIGH)
    grad_key = grad_key + select[:, None, None] * (
        jnp.einsum("jhf,hef->jhe", value_wide, grad_state, precision=HIGH) + grad_norm[None]
    )
    grad_value = jnp.einsum("hij,ihe->jhe", scores, grad_numer, precision=HIGH)
    grad_value = grad_value + select[:, None, None] * jnp.einsum(
        "jhe,hef->jhf", key_wide, grad_state, precision=HIGH
    )
    query_kept = query_wide * follows[:, None, None]
    earlier_state = carried * grad_state + jnp.einsum(
        "ihe,ihf->hef", query_kept, grad_numer, precision=HIGH
    )
    earlier_norm = carried * grad_norm + jnp.einsum(
        "ihe,ih->he", query_kept, grad_denom, precision=HIGH
    )
    return ((earlier_state, earlier_norm), (grad_query, grad_key, grad_value))


def split_blocks(array):
    blocks = array.shape[0] // BLOCK
    return array.reshape((blocks, BLOCK) + array.shape[1:])


def attend_slot(pieces):
    query_feat, key_feat, values, crop, keymask = pieces
    length, heads, head_width = query_feat.shape
    start = (
        jnp.zeros((heads, head_width, head_width), jnp.float32),
        jnp.zeros((heads, head_width), jnp.float32),
        jnp.int32(-1),
    )
    finish, (mixed, denom, states, norms) = lax.scan(
        attend_forward,
        start,
        (
            split_blocks(query_feat),
            split_blocks(key_feat),
            split_blocks(values),
            split_blocks(crop),
            split_blocks(keymask),
        ),
    )
    return (mixed.reshape(length, heads, head_width), denom.reshape(length, heads), states, norms)


def attend_slot_back(pieces):
    query_feat, key_feat, values, crop, keymask, states, norms, grad_numer, grad_denom = pieces
    length, heads, head_width = query_feat.shape
    crop_blocks = split_blocks(crop)
    prev_crops = jnp.concatenate([jnp.full((1,), -1, jnp.int32), crop_blocks[:-1, -1]])
    start = (
        jnp.zeros((heads, head_width, head_width), jnp.float32),
        jnp.zeros((heads, head_width), jnp.float32),
    )
    finish, (grad_query, grad_key, grad_value) = lax.scan(
        attend_backward,
        start,
        (
            split_blocks(query_feat),
            split_blocks(key_feat),
            split_blocks(values),
            crop_blocks,
            split_blocks(keymask),
            prev_crops,
            states,
            norms,
            split_blocks(grad_numer),
            split_blocks(grad_denom),
        ),
        reverse=True,
    )
    shape = (length, heads, head_width)
    return (grad_query.reshape(shape), grad_key.reshape(shape), grad_value.reshape(shape))


def body(
    tokens,
    crop_ids,
    kv_mask,
    norm1_gain,
    norm1_bias,
    w_query,
    w_key,
    w_value,
    w_out,
    norm2_gain,
    norm2_bias,
    w_up,
    up_bias,
    w_down,
    down_bias,
    cotangent,
):
    slots, length, width = tokens.shape
    heads = HEADS
    head_width = width // heads
    count = slots * length
    devices = lax.axis_size("dp") * lax.axis_size("fsdp")
    dims = (OUTER, lax.axis_size("dp") // (2 * OUTER), lax.axis_size("fsdp"))
    unit = width // devices
    packed = jnp.concatenate([norm1_gain, norm1_bias, norm2_gain, norm2_bias, down_bias, up_bias])
    packed = jnp.pad(packed, (0, 16 * 128 - packed.shape[0])).reshape(16, 128)
    vectors, full_query, full_key, full_value, full_out, full_up, full_down = gather(
        dims, [packed, w_query, w_key, w_value, w_out, w_up, w_down], unit
    )
    vectors = vectors.reshape(devices, 16 * 128)
    gain_one, bias_one, gain_two, bias_two, full_down_bias = (
        vectors[:, index * unit : (index + 1) * unit].reshape(-1) for index in range(5)
    )
    full_up_bias = vectors[:, 5 * unit : 5 * unit + up_bias.shape[0]].reshape(-1)
    inputs = tokens.reshape(count, width).astype(jnp.float32)
    normed_wide, pull_one = jax.vjp(
        norm_affine, inputs, gain_one.astype(jnp.float32), bias_one.astype(jnp.float32)
    )
    normed = normed_wide.astype(jnp.bfloat16)
    query = jnp.dot(normed, full_query, preferred_element_type=jnp.float32)
    keys = jnp.dot(normed, full_key, preferred_element_type=jnp.float32)
    values = jnp.dot(normed, full_value, preferred_element_type=jnp.float32).astype(jnp.bfloat16)
    query_wide, pull_query = jax.vjp(feature, query)
    key_wide, pull_key = jax.vjp(feature, keys)
    query_feat = query_wide.astype(jnp.bfloat16).reshape(slots, length, heads, head_width)
    key_feat = key_wide.astype(jnp.bfloat16).reshape(slots, length, heads, head_width)
    value_heads = values.reshape(slots, length, heads, head_width)
    mixed_wide, denom, states, norms = lax.map(
        attend_slot, (query_feat, key_feat, value_heads, crop_ids, kv_mask)
    )
    mixed = mixed_wide.reshape(count, width).astype(jnp.bfloat16)
    middle = inputs + jnp.dot(mixed, full_out, preferred_element_type=jnp.float32)
    normed_two_wide, pull_two = jax.vjp(
        norm_affine, middle, gain_two.astype(jnp.float32), bias_two.astype(jnp.float32)
    )
    normed_two = normed_two_wide.astype(jnp.bfloat16)
    upper = jnp.dot(normed_two, full_up, preferred_element_type=jnp.float32) + full_up_bias.astype(
        jnp.float32
    )
    hidden_wide, pull_gelu = jax.vjp(gelu_exact, upper)
    hidden = hidden_wide.astype(jnp.bfloat16)
    result = (
        middle
        + jnp.dot(hidden, full_down, preferred_element_type=jnp.float32)
        + full_down_bias.astype(jnp.float32)
    )
    output = result.astype(jnp.bfloat16).reshape(slots, length, width)
    back_up, back_down = full_up, full_down
    back_query, back_key, back_value, back_out = full_query, full_key, full_value, full_out
    grad_out = cotangent.reshape(count, width)
    grad_down_bias = jnp.sum(grad_out.astype(jnp.float32), axis=0)
    grad_w_down = jnp.dot(hidden.T, grad_out, preferred_element_type=jnp.float32).astype(jnp.bfloat16)
    grad_hidden = jnp.dot(grad_out, back_down.T, preferred_element_type=jnp.float32)
    grad_upper = pull_gelu(grad_hidden)[0].astype(jnp.bfloat16)
    grad_up_bias = jnp.sum(grad_upper.astype(jnp.float32), axis=0)
    grad_w_up = jnp.dot(normed_two.T, grad_upper, preferred_element_type=jnp.float32).astype(jnp.bfloat16)
    grad_normed_two = jnp.dot(grad_upper, back_up.T, preferred_element_type=jnp.float32)
    grad_middle_part, grad_gain_two, grad_bias_two = pull_two(grad_normed_two)
    grad_middle = grad_out.astype(jnp.float32) + grad_middle_part
    grad_attended = grad_middle.astype(jnp.bfloat16)
    grad_w_out = jnp.dot(mixed.T, grad_attended, preferred_element_type=jnp.float32).astype(jnp.bfloat16)
    grad_mixed = jnp.dot(grad_attended, back_out.T, preferred_element_type=jnp.float32).reshape(
        slots, length, heads, head_width
    )
    grad_numer = grad_mixed / denom[..., None]
    grad_denom = -jnp.sum(grad_mixed * mixed_wide, axis=-1) / denom
    grad_query_feat, grad_key_feat, grad_values = lax.map(
        attend_slot_back,
        (
            query_feat,
            key_feat,
            value_heads,
            crop_ids,
            kv_mask,
            states,
            norms,
            grad_numer,
            grad_denom,
        ),
    )
    grad_query = pull_query(grad_query_feat.reshape(count, width))[0].astype(jnp.bfloat16)
    grad_keys = pull_key(grad_key_feat.reshape(count, width))[0].astype(jnp.bfloat16)
    grad_values = grad_values.reshape(count, width).astype(jnp.bfloat16)
    grad_w_query = jnp.dot(normed.T, grad_query, preferred_element_type=jnp.float32).astype(jnp.bfloat16)
    grad_w_key = jnp.dot(normed.T, grad_keys, preferred_element_type=jnp.float32).astype(jnp.bfloat16)
    grad_w_value = jnp.dot(normed.T, grad_values, preferred_element_type=jnp.float32).astype(jnp.bfloat16)
    grad_normed = jnp.dot(grad_query, back_query.T, preferred_element_type=jnp.float32)
    grad_normed = grad_normed + jnp.dot(grad_keys, back_key.T, preferred_element_type=jnp.float32)
    grad_normed = grad_normed + jnp.dot(
        grad_values, back_value.T, preferred_element_type=jnp.float32
    )
    grad_input_part, grad_gain_one, grad_bias_one = pull_one(grad_normed)
    small = jnp.concatenate(
        [
            vector.reshape(devices, -1)
            for vector in (
                grad_gain_one,
                grad_bias_one,
                grad_gain_two,
                grad_bias_two,
                grad_down_bias,
                grad_up_bias,
            )
        ],
        axis=1,
    )
    small = jnp.pad(small, ((0, 0), (0, 8 * 128 - small.shape[1]))).reshape(devices, 8, 128)
    small, own_up, own_down, own_query, own_key, own_value, own_out = scatter(
        dims,
        small,
        [grad_w_up, grad_w_down, grad_w_query, grad_w_key, grad_w_value, grad_w_out],
        unit,
    )
    small = small.reshape(8 * 128)
    own_gain_one, own_bias_one, own_gain_two, own_bias_two, own_down_bias = (
        small[index * unit : (index + 1) * unit] for index in range(5)
    )
    own_up_bias = small[5 * unit : 5 * unit + up_bias.shape[0]]
    input_grad = (grad_middle + grad_input_part).astype(jnp.bfloat16).reshape(slots, length, width)
    return (
        output,
        input_grad,
        own_gain_one,
        own_bias_one,
        own_query,
        own_key,
        own_value,
        own_out,
        own_gain_two,
        own_bias_two,
        own_up,
        own_up_bias,
        own_down,
        own_down_bias,
    )


def solution(mesh):
    return jax.shard_map(
        body,
        mesh=mesh,
        in_specs=(
            P(("dp", "fsdp"), None, None),
            P(("dp", "fsdp"), None),
            P(("dp", "fsdp"), None),
            P(("dp", "fsdp")),
            P(("dp", "fsdp")),
            P(("dp", "fsdp"), None),
            P(("dp", "fsdp"), None),
            P(("dp", "fsdp"), None),
            P(("dp", "fsdp"), None),
            P(("dp", "fsdp")),
            P(("dp", "fsdp")),
            P(("dp", "fsdp"), None),
            P(("dp", "fsdp")),
            P(("dp", "fsdp"), None),
            P(("dp", "fsdp")),
            P(("dp", "fsdp"), None, None),
        ),
        out_specs=(
            P(("dp", "fsdp"), None, None),
            P(("dp", "fsdp"), None, None),
            P(("dp", "fsdp")),
            P(("dp", "fsdp")),
            P(("dp", "fsdp"), None),
            P(("dp", "fsdp"), None),
            P(("dp", "fsdp"), None),
            P(("dp", "fsdp"), None),
            P(("dp", "fsdp")),
            P(("dp", "fsdp")),
            P(("dp", "fsdp"), None),
            P(("dp", "fsdp")),
            P(("dp", "fsdp"), None),
            P(("dp", "fsdp")),
        ),
        check_vma=False,
    )
```

```python
import functools

import jax
import jax.numpy as jnp
from jax import lax
from jax.experimental import pallas as pl
from jax.experimental.pallas import tpu as pltpu
from jax.sharding import PartitionSpec as P

HEADS = 16
BLOCK = 512
MESH = pl.DeviceIdType.MESH
WIDE = 512
OUTER = 2


class Place:
    def __init__(self, dims):
        self.size = {"a": dims[0], "b": dims[1], "c": 2, "z": dims[2]}
        dp = lax.axis_index("dp")
        self.at = {
            "a": dp // (2 * dims[1]),
            "b": (dp // 2) % dims[1],
            "c": dp % 2,
            "z": lax.axis_index("fsdp"),
        }

    def moved(self, axis, step):
        spot = dict(self.at)
        spot[axis] = (spot[axis] + step) % self.size[axis]
        return spot

    def device(self, axis, step):
        spot = self.moved(axis, step)
        return ((spot["a"] * self.size["b"] + spot["b"]) * 2 + spot["c"], spot["z"])

    def partners(self, axis):
        return range(1, self.size[axis])

    def greet(self):
        barrier = pltpu.get_barrier_semaphore()
        count = 0
        for axis in "abcz":
            for step in self.partners(axis):
                pl.semaphore_signal(
                    barrier, 1, device_id=self.device(axis, step), device_id_type=MESH
                )
                count += 1
        pl.semaphore_wait(barrier, count)


def pieces_of(rows, columns, unit):
    wide = min(WIDE, columns)
    return [
        (row, unit, column, wide)
        for row in range(0, rows, unit)
        for column in range(0, columns, wide)
    ]


def gather_kernel(dims, orders, lag, ahead, pieces, *refs):
    count = len(pieces)
    shards, wholes = refs[:count], refs[count : 2 * count]
    local_sem, send_sem, recv_sem = refs[2 * count :]
    place = Place(dims)
    place.greet()
    chunks = [
        (shard.at[pl.ds(ro, rn), pl.ds(co, cn)], whole, pl.ds(ro, rn), pl.ds(co, cn))
        for shard, whole, items in zip(shards, wholes, pieces)
        for ro, rn, co, cn in items
    ]
    total = len(chunks)
    sent, kept = [], []

    def region(index, done, spot):
        _, whole, rows, columns = chunks[index]
        lead = tuple(slice(None) if axis in done else spot[axis] for axis in "abcz")
        return whole.at[lead + (rows, columns)]

    def copy(index, stage, step, axis, source, target):
        return pltpu.make_async_remote_copy(
            source,
            target,
            send_sem.at[index, stage, step - 1],
            recv_sem.at[index, stage, step - 1],
            device_id=place.device(axis, step),
            device_id_type=MESH,
        )

    def send(index, stage):
        order = orders[index % len(orders)]
        axis, done = order[stage], order[:stage]
        target = region(index, done, place.at)
        for step in place.partners(axis):
            item = copy(index, stage, step, axis, target if done else chunks[index][0], target)
            item.start()
            sent.append(item)

    def receive(index, stage):
        order = orders[index % len(orders)]
        axis, done = order[stage], order[:stage]
        for step in place.partners(axis):
            target = region(index, done, place.moved(axis, place.size[axis] - step))
            copy(index, stage, step, axis, target, target).wait_recv()

    def begin(index):
        if index < total:
            item = pltpu.make_async_copy(
                chunks[index][0], region(index, "", place.at), local_sem.at[index]
            )
            item.start()
            kept.append(item)
            send(index, 0)

    for index in range(ahead):
        begin(index)
    for tick in range(total + 3 * lag):
        begin(tick + ahead)
        for stage in range(4):
            index = tick - stage * lag
            if 0 <= index < total:
                receive(index, stage)
                if stage == 0:
                    kept[index].wait()
                if stage < 3:
                    send(index, stage + 1)
    for item in sent:
        item.wait_send()


def gather(dims, shards, unit, lag=3, ahead=6):
    pieces = [pieces_of(*shard.shape, min(unit, shard.shape[0])) for shard in shards]
    total = sum(len(items) for items in pieces)
    most = max(dims) - 1
    anywhere = pl.BlockSpec(memory_space=pl.ANY)
    orders = ("zbac", "zabc", "zbac", "zabc", "bzac", "azbc")
    wholes = pl.pallas_call(
        functools.partial(gather_kernel, dims, orders, lag, ahead, pieces),
        out_shape=[
            jax.ShapeDtypeStruct(dims[:2] + (2, dims[2]) + shard.shape, shard.dtype)
            for shard in shards
        ],
        in_specs=[anywhere] * len(shards),
        out_specs=[anywhere] * len(shards),
        scratch_shapes=[
            pltpu.SemaphoreType.DMA((total,)),
            pltpu.SemaphoreType.DMA((total, 4, most)),
            pltpu.SemaphoreType.DMA((total, 4, most)),
        ],
        compiler_params=pltpu.CompilerParams(collective_id=0, has_side_effects=True),
        name="gather",
    )(*shards)
    return [whole.reshape((-1, whole.shape[-1])) for whole in wholes]


def scatter_kernel(dims, lag, ahead, pieces, *refs):
    count = len(pieces)
    terms, owned = refs[:count], refs[count : 2 * count]
    main = refs[2 * count : 2 * count + 7]
    side = refs[2 * count + 7 : 2 * count + 12]
    local_sem, send_sem, recv_sem = refs[2 * count + 12 :]
    place = Place(dims)
    place.greet()
    spot = place.at
    chunks = []
    for array, items in enumerate(pieces):
        for ro, rn, co, cn in items:
            index = len(chunks)
            if array == 0:
                rooms = side
                order = "ab"
            else:
                half = (index - 1) // 2
                order = "ab" if index % 2 else "ba"
                first, second = (main[2], main[4]) if index % 2 else (main[3], main[5])
                rooms = (
                    main[0].at[index - 1],
                    main[1].at[index - 1],
                    first.at[half],
                    second.at[half],
                    main[6].at[index - 1],
                )
            chunks.append((terms[array], owned[array], pl.ds(ro, rn), pl.ds(co, cn), order, rooms))
    total = len(chunks)
    sent, kept = [], []

    def copy(index, stage, step, axis, source, target):
        return pltpu.make_async_remote_copy(
            source,
            target,
            send_sem.at[index, stage, step - 1],
            recv_sem.at[index, stage, step - 1],
            device_id=place.device(axis, step),
            device_id_type=MESH,
        )

    def send(index, stage, step, axis, source, target):
        item = copy(index, stage, step, axis, source, target)
        item.start()
        sent.append(item)

    def begin(index):
        if index < total:
            term, _, rows, columns, _, rooms = chunks[index]
            send(index, 0, 1, "c", term.at[:, :, 1 - spot["c"], :, rows, columns], rooms[1])
            item = pltpu.make_async_copy(
                term.at[:, :, spot["c"], :, rows, columns], rooms[0], local_sem.at[index]
            )
            item.start()
            kept.append(item)

    def await_all(index, stage, axis, room):
        for step in place.partners(axis):
            copy(index, stage, step, axis, room.at[step - 1], room.at[step - 1]).wait_recv()

    def pick(order, first, second):
        return (first, second) if order == "ab" else (second, first)

    def after_core(index):
        order, (own, other, came, _, _) = chunks[index][4:]
        kept[index].wait()
        copy(index, 0, 1, "c", other, other).wait_recv()
        axis, rest = order

        def add(where):
            for item in range(place.size[rest]):
                at = pick(order, where, item)
                own[at] = own[at] + other[at]

        for step in place.partners(axis):
            where = place.moved(axis, step)[axis]
            add(where)
            source = own.at[where] if order == "ab" else own.at[:, where]
            send(index, 1, step, axis, source, came.at[step - 1])
        add(spot[axis])

    def after_first(index):
        order, (own, _, came, later, _) = chunks[index][4:]
        axis, rest = order
        await_all(index, 1, axis, came)

        def add(where):
            at = pick(order, spot[axis], where)
            value = own[at].astype(jnp.float32)
            for step in place.partners(axis):
                value = value + came[step - 1, where].astype(jnp.float32)
            own[at] = value.astype(own.dtype)

        for step in place.partners(rest):
            where = place.moved(rest, step)[rest]
            add(where)
            at = pick(order, spot[axis], where)
            send(index, 2, step, rest, own.at[at], later.at[step - 1])
        add(spot[rest])

    def after_second(index):
        _, result, rows, columns, order, (own, _, _, later, last) = chunks[index]
        rest = order[1]
        await_all(index, 2, rest, later)

        def add(where):
            value = own[spot["a"], spot["b"], where].astype(jnp.float32)
            for step in place.partners(rest):
                value = value + later[step - 1, where].astype(jnp.float32)
            return value

        for step in place.partners("z"):
            where = place.moved("z", step)["z"]
            own[spot["a"], spot["b"], where] = add(where).astype(own.dtype)
            send(index, 3, step, "z", own.at[spot["a"], spot["b"], where], last.at[step - 1])
        result[rows, columns] = add(spot["z"])

    def after_last(index):
        _, result, rows, columns, _, (_, _, _, _, last) = chunks[index]
        await_all(index, 3, "z", last)
        value = result[rows, columns]
        for step in place.partners("z"):
            value = value + last[step - 1].astype(jnp.float32)
        result[rows, columns] = value

    for index in range(ahead):
        begin(index)
    for tick in range(total + 3 * lag):
        begin(tick + ahead)
        for stage, work in enumerate((after_core, after_first, after_second, after_last)):
            index = tick - stage * lag
            if 0 <= index < total:
                work(index)
    for item in sent:
        item.wait_send()


def rooms_of(dims, many, unit, wide, dtype):
    outer, inner, depth = dims
    ones, twos = (many + 1) // 2, many // 2
    tail = (unit, wide)
    return [
        pltpu.VMEM((many, outer, inner, depth) + tail, dtype),
        pltpu.VMEM((many, outer, inner, depth) + tail, dtype),
        pltpu.VMEM((ones, outer - 1, inner, depth) + tail, dtype),
        pltpu.VMEM((twos, inner - 1, outer, depth) + tail, dtype),
        pltpu.VMEM((ones, inner - 1, depth) + tail, dtype),
        pltpu.VMEM((twos, outer - 1, depth) + tail, dtype),
        pltpu.VMEM((many, depth - 1) + tail, dtype),
    ]


def scatter(dims, small, terms, unit, lag=2, ahead=4):
    outer, inner, depth = dims
    devices = 2 * outer * inner * depth
    lead = (outer, inner, 2, depth)
    arrays = [small.reshape(lead + small.shape[1:])] + [
        term.reshape(lead + (term.shape[0] // devices, term.shape[1])) for term in terms
    ]
    pieces = [pieces_of(*arrays[0].shape[4:], arrays[0].shape[4])]
    pieces += [pieces_of(*array.shape[4:], unit) for array in arrays[1:]]
    total = sum(len(items) for items in pieces)
    most = max(dims) - 1
    tail = small.shape[1:]
    side = [
        pltpu.VMEM((outer, inner, depth) + tail, jnp.float32),
        pltpu.VMEM((outer, inner, depth) + tail, jnp.float32),
        pltpu.VMEM((outer - 1, inner, depth) + tail, jnp.float32),
        pltpu.VMEM((inner - 1, depth) + tail, jnp.float32),
        pltpu.VMEM((depth - 1,) + tail, jnp.float32),
    ]
    return pl.pallas_call(
        functools.partial(scatter_kernel, dims, lag, ahead, pieces),
        out_shape=[jax.ShapeDtypeStruct(array.shape[4:], jnp.float32) for array in arrays],
        in_specs=[pl.BlockSpec(memory_space=pl.ANY)] * len(arrays),
        out_specs=[pl.BlockSpec(memory_space=pltpu.VMEM)] * len(arrays),
        scratch_shapes=rooms_of(dims, total - 1, unit, WIDE, jnp.bfloat16)
        + side
        + [
            pltpu.SemaphoreType.DMA((total,)),
            pltpu.SemaphoreType.DMA((total, 4, most)),
            pltpu.SemaphoreType.DMA((total, 4, most)),
        ],
        compiler_params=pltpu.CompilerParams(
            collective_id=1, has_side_effects=True, vmem_limit_bytes=60 << 20
        ),
        name="scatter",
    )(*arrays)


HIGH = lax.Precision.HIGHEST
norm_eps = 1e-05


def norm_affine(values, gain, shift):
    mean = jnp.mean(values, axis=-1, keepdims=True)
    centred = values - mean
    spread = jnp.mean(centred * centred, axis=-1, keepdims=True)
    return centred * lax.rsqrt(spread + norm_eps) * gain + shift


def feature(values):
    return jax.nn.elu(values) + 1.0


def gelu_exact(values):
    return jax.nn.gelu(values, approximate=False)


def allowed_weight(crop, keymask):
    places = jnp.arange(crop.shape[0])
    earlier = places[None, :] <= places[:, None]
    same = crop[:, None] == crop[None, :]
    visible = (keymask[None, :] > 0) | (places[None, :] == places[:, None])
    return (earlier & same & visible).astype(jnp.float32)


def attend_forward(carry, pieces):
    state, norm_state, prev_crop = carry
    query_feat, key_feat, values, crop, keymask = pieces
    weight = allowed_weight(crop, keymask)
    scores = (
        jnp.einsum("ihe,jhe->hij", query_feat, key_feat, preferred_element_type=jnp.float32)
        * weight[None]
    )
    value_wide = values.astype(jnp.float32)
    query_wide = query_feat.astype(jnp.float32)
    key_wide = key_feat.astype(jnp.float32)
    numer = jnp.einsum("hij,jhe->ihe", scores, value_wide, precision=HIGH)
    denom = jnp.sum(scores, axis=2).T
    follows = (crop == prev_crop).astype(jnp.float32)
    numer = numer + follows[:, None, None] * jnp.einsum(
        "ihe,hef->ihf", query_wide, state, precision=HIGH
    )
    denom = denom + follows[:, None] * jnp.einsum(
        "ihe,he->ih", query_wide, norm_state, precision=HIGH
    )
    last_crop = crop[crop.shape[0] - 1]
    carried = (prev_crop == last_crop).astype(jnp.float32)
    select = ((crop == last_crop) & (keymask > 0)).astype(jnp.float32)
    chosen = key_wide * select[:, None, None]
    new_state = carried * state + jnp.einsum("jhe,jhf->hef", chosen, value_wide, precision=HIGH)
    new_norm = carried * norm_state + jnp.sum(chosen, axis=0)
    return ((new_state, new_norm, last_crop), (numer / denom[:, :, None], denom, state, norm_state))


def attend_backward(carry, pieces):
    grad_state, grad_norm = carry
    (
        query_feat,
        key_feat,
        values,
        crop,
        keymask,
        prev_crop,
        state,
        norm_state,
        grad_numer,
        grad_denom,
    ) = pieces
    weight = allowed_weight(crop, keymask)
    scores = (
        jnp.einsum("ihe,jhe->hij", query_feat, key_feat, preferred_element_type=jnp.float32)
        * weight[None]
    )
    value_wide = values.astype(jnp.float32)
    query_wide = query_feat.astype(jnp.float32)
    key_wide = key_feat.astype(jnp.float32)
    grad_scores = (
        jnp.einsum("ihe,jhe->hij", grad_numer, value_wide, precision=HIGH)
        + grad_denom.T[:, :, None]
    ) * weight[None]
    follows = (crop == prev_crop).astype(jnp.float32)
    last_crop = crop[crop.shape[0] - 1]
    carried = (prev_crop == last_crop).astype(jnp.float32)
    select = ((crop == last_crop) & (keymask > 0)).astype(jnp.float32)
    grad_query = jnp.einsum("hij,jhe->ihe", grad_scores, key_wide, precision=HIGH)
    grad_query = grad_query + follows[:, None, None] * (
        jnp.einsum("ihf,hef->ihe", grad_numer, state, precision=HIGH)
        + grad_denom[:, :, None] * norm_state[None]
    )
    grad_key = jnp.einsum("hij,ihe->jhe", grad_scores, query_wide, precision=HIGH)
    grad_key = grad_key + select[:, None, None] * (
        jnp.einsum("jhf,hef->jhe", value_wide, grad_state, precision=HIGH) + grad_norm[None]
    )
    grad_value = jnp.einsum("hij,ihe->jhe", scores, grad_numer, precision=HIGH)
    grad_value = grad_value + select[:, None, None] * jnp.einsum(
        "jhe,hef->jhf", key_wide, grad_state, precision=HIGH
    )
    query_kept = query_wide * follows[:, None, None]
    earlier_state = carried * grad_state + jnp.einsum(
        "ihe,ihf->hef", query_kept, grad_numer, precision=HIGH
    )
    earlier_norm = carried * grad_norm + jnp.einsum(
        "ihe,ih->he", query_kept, grad_denom, precision=HIGH
    )
    return ((earlier_state, earlier_norm), (grad_query, grad_key, grad_value))


def split_blocks(array):
    blocks = array.shape[0] // BLOCK
    return array.reshape((blocks, BLOCK) + array.shape[1:])


def attend_slot(pieces):
    query_feat, key_feat, values, crop, keymask = pieces
    length, heads, head_width = query_feat.shape
    start = (
        jnp.zeros((heads, head_width, head_width), jnp.float32),
        jnp.zeros((heads, head_width), jnp.float32),
        jnp.int32(-1),
    )
    finish, (mixed, denom, states, norms) = lax.scan(
        attend_forward,
        start,
        (
            split_blocks(query_feat),
            split_blocks(key_feat),
            split_blocks(values),
            split_blocks(crop),
            split_blocks(keymask),
        ),
    )
    return (mixed.reshape(length, heads, head_width), denom.reshape(length, heads), states, norms)


def attend_slot_back(pieces):
    query_feat, key_feat, values, crop, keymask, states, norms, grad_numer, grad_denom = pieces
    length, heads, head_width = query_feat.shape
    crop_blocks = split_blocks(crop)
    prev_crops = jnp.concatenate([jnp.full((1,), -1, jnp.int32), crop_blocks[:-1, -1]])
    start = (
        jnp.zeros((heads, head_width, head_width), jnp.float32),
        jnp.zeros((heads, head_width), jnp.float32),
    )
    finish, (grad_query, grad_key, grad_value) = lax.scan(
        attend_backward,
        start,
        (
            split_blocks(query_feat),
            split_blocks(key_feat),
            split_blocks(values),
            crop_blocks,
            split_blocks(keymask),
            prev_crops,
            states,
            norms,
            split_blocks(grad_numer),
            split_blocks(grad_denom),
        ),
        reverse=True,
    )
    shape = (length, heads, head_width)
    return (grad_query.reshape(shape), grad_key.reshape(shape), grad_value.reshape(shape))


def general_body(
    tokens,
    crop_ids,
    kv_mask,
    norm1_gain,
    norm1_bias,
    w_query,
    w_key,
    w_value,
    w_out,
    norm2_gain,
    norm2_bias,
    w_up,
    up_bias,
    w_down,
    down_bias,
    cotangent,
):
    slots, length, width = tokens.shape
    heads = HEADS
    head_width = width // heads
    count = slots * length
    devices = lax.axis_size("dp") * lax.axis_size("fsdp")
    dims = (OUTER, lax.axis_size("dp") // (2 * OUTER), lax.axis_size("fsdp"))
    unit = width // devices
    packed = jnp.concatenate([norm1_gain, norm1_bias, norm2_gain, norm2_bias, down_bias, up_bias])
    packed = jnp.pad(packed, (0, 16 * 128 - packed.shape[0])).reshape(16, 128)
    vectors, full_query, full_key, full_value, full_out, full_up, full_down = gather(
        dims, [packed, w_query, w_key, w_value, w_out, w_up, w_down], unit
    )
    vectors = vectors.reshape(devices, 16 * 128)
    gain_one, bias_one, gain_two, bias_two, full_down_bias = (
        vectors[:, index * unit : (index + 1) * unit].reshape(-1) for index in range(5)
    )
    full_up_bias = vectors[:, 5 * unit : 5 * unit + up_bias.shape[0]].reshape(-1)
    inputs = tokens.reshape(count, width).astype(jnp.float32)
    normed_wide, pull_one = jax.vjp(
        norm_affine, inputs, gain_one.astype(jnp.float32), bias_one.astype(jnp.float32)
    )
    normed = normed_wide.astype(jnp.bfloat16)
    query = jnp.dot(normed, full_query, preferred_element_type=jnp.float32)
    keys = jnp.dot(normed, full_key, preferred_element_type=jnp.float32)
    values = jnp.dot(normed, full_value, preferred_element_type=jnp.float32).astype(jnp.bfloat16)
    query_wide, pull_query = jax.vjp(feature, query)
    key_wide, pull_key = jax.vjp(feature, keys)
    query_feat = query_wide.astype(jnp.bfloat16).reshape(slots, length, heads, head_width)
    key_feat = key_wide.astype(jnp.bfloat16).reshape(slots, length, heads, head_width)
    value_heads = values.reshape(slots, length, heads, head_width)
    mixed_wide, denom, states, norms = lax.map(
        attend_slot, (query_feat, key_feat, value_heads, crop_ids, kv_mask)
    )
    mixed = mixed_wide.reshape(count, width).astype(jnp.bfloat16)
    middle = inputs + jnp.dot(mixed, full_out, preferred_element_type=jnp.float32)
    normed_two_wide, pull_two = jax.vjp(
        norm_affine, middle, gain_two.astype(jnp.float32), bias_two.astype(jnp.float32)
    )
    normed_two = normed_two_wide.astype(jnp.bfloat16)
    upper = jnp.dot(normed_two, full_up, preferred_element_type=jnp.float32) + full_up_bias.astype(
        jnp.float32
    )
    hidden_wide, pull_gelu = jax.vjp(gelu_exact, upper)
    hidden = hidden_wide.astype(jnp.bfloat16)
    result = (
        middle
        + jnp.dot(hidden, full_down, preferred_element_type=jnp.float32)
        + full_down_bias.astype(jnp.float32)
    )
    output = result.astype(jnp.bfloat16).reshape(slots, length, width)
    back_up, back_down = full_up, full_down
    back_query, back_key, back_value, back_out = full_query, full_key, full_value, full_out
    grad_out = cotangent.reshape(count, width)
    grad_down_bias = jnp.sum(grad_out.astype(jnp.float32), axis=0)
    grad_w_down = jnp.dot(hidden.T, grad_out, preferred_element_type=jnp.float32).astype(jnp.bfloat16)
    grad_hidden = jnp.dot(grad_out, back_down.T, preferred_element_type=jnp.float32)
    grad_upper = pull_gelu(grad_hidden)[0].astype(jnp.bfloat16)
    grad_up_bias = jnp.sum(grad_upper.astype(jnp.float32), axis=0)
    grad_w_up = jnp.dot(normed_two.T, grad_upper, preferred_element_type=jnp.float32).astype(jnp.bfloat16)
    grad_normed_two = jnp.dot(grad_upper, back_up.T, preferred_element_type=jnp.float32)
    grad_middle_part, grad_gain_two, grad_bias_two = pull_two(grad_normed_two)
    grad_middle = grad_out.astype(jnp.float32) + grad_middle_part
    grad_attended = grad_middle.astype(jnp.bfloat16)
    grad_w_out = jnp.dot(mixed.T, grad_attended, preferred_element_type=jnp.float32).astype(jnp.bfloat16)
    grad_mixed = jnp.dot(grad_attended, back_out.T, preferred_element_type=jnp.float32).reshape(
        slots, length, heads, head_width
    )
    grad_numer = grad_mixed / denom[..., None]
    grad_denom = -jnp.sum(grad_mixed * mixed_wide, axis=-1) / denom
    grad_query_feat, grad_key_feat, grad_values = lax.map(
        attend_slot_back,
        (
            query_feat,
            key_feat,
            value_heads,
            crop_ids,
            kv_mask,
            states,
            norms,
            grad_numer,
            grad_denom,
        ),
    )
    grad_query = pull_query(grad_query_feat.reshape(count, width))[0].astype(jnp.bfloat16)
    grad_keys = pull_key(grad_key_feat.reshape(count, width))[0].astype(jnp.bfloat16)
    grad_values = grad_values.reshape(count, width).astype(jnp.bfloat16)
    grad_w_query = jnp.dot(normed.T, grad_query, preferred_element_type=jnp.float32).astype(jnp.bfloat16)
    grad_w_key = jnp.dot(normed.T, grad_keys, preferred_element_type=jnp.float32).astype(jnp.bfloat16)
    grad_w_value = jnp.dot(normed.T, grad_values, preferred_element_type=jnp.float32).astype(jnp.bfloat16)
    grad_normed = jnp.dot(grad_query, back_query.T, preferred_element_type=jnp.float32)
    grad_normed = grad_normed + jnp.dot(grad_keys, back_key.T, preferred_element_type=jnp.float32)
    grad_normed = grad_normed + jnp.dot(
        grad_values, back_value.T, preferred_element_type=jnp.float32
    )
    grad_input_part, grad_gain_one, grad_bias_one = pull_one(grad_normed)
    small = jnp.concatenate(
        [
            vector.reshape(devices, -1)
            for vector in (
                grad_gain_one,
                grad_bias_one,
                grad_gain_two,
                grad_bias_two,
                grad_down_bias,
                grad_up_bias,
            )
        ],
        axis=1,
    )
    small = jnp.pad(small, ((0, 0), (0, 8 * 128 - small.shape[1]))).reshape(devices, 8, 128)
    small, own_up, own_down, own_query, own_key, own_value, own_out = scatter(
        dims,
        small,
        [grad_w_up, grad_w_down, grad_w_query, grad_w_key, grad_w_value, grad_w_out],
        unit,
    )
    small = small.reshape(8 * 128)
    own_gain_one, own_bias_one, own_gain_two, own_bias_two, own_down_bias = (
        small[index * unit : (index + 1) * unit] for index in range(5)
    )
    own_up_bias = small[5 * unit : 5 * unit + up_bias.shape[0]]
    input_grad = (grad_middle + grad_input_part).astype(jnp.bfloat16).reshape(slots, length, width)
    return (
        output,
        input_grad,
        own_gain_one,
        own_bias_one,
        own_query,
        own_key,
        own_value,
        own_out,
        own_gain_two,
        own_bias_two,
        own_up,
        own_up_bias,
        own_down,
        own_down_bias,
    )


LENGTH = 512
WIDTH = 1024
HIDDEN = 4096
UNIT = 32
GATHERED = 24
DOWN, UP = 8, 16
LAG = 2
AHEAD = 4
WIDE32 = jnp.float32
HALF16 = jnp.bfloat16
VMEM_LIMIT = 63 << 20


def when(condition):
    if isinstance(condition, bool):
        return (lambda work: work()) if condition else (lambda work: None)
    return pl.when(condition)


def each(count, work):
    def step(index, carry):
        work(index)
        return carry

    lax.fori_loop(0, count, step, 0)


def dot(left, right):
    return jnp.dot(left, right, preferred_element_type=jnp.float32)


def dot_nt(left, right):
    return lax.dot_general(
        left, right, (((1,), (1,)), ((), ())), preferred_element_type=jnp.float32
    )


def dot_tn(left, right):
    return lax.dot_general(
        left, right, (((0,), (0,)), ((), ())), preferred_element_type=jnp.float32
    )


class Mover:
    def __init__(self, place, send_sem, recv_sem):
        self.place, self.send_sem, self.recv_sem = place, send_sem, recv_sem

    def copy(self, lead, stage, step, axis, source, target):
        at = lead + (stage, step - 1)
        return pltpu.make_async_remote_copy(
            source,
            target,
            self.send_sem.at[at],
            self.recv_sem.at[at],
            device_id=self.place.device(axis, step),
            device_id_type=MESH,
        )


class Gather(Mover):
    def region(self, chunk, done, spot):
        lead = tuple(slice(None) if axis in done else spot[axis] for axis in "abcz")
        return chunk.at[lead]

    def send(self, chunk, lead, order, stage):
        axis, done = order[stage], order[:stage]
        source = self.region(chunk, done, self.place.at)
        for step in self.place.partners(axis):
            self.copy(lead, stage, step, axis, source, source).start()

    def receive(self, chunk, lead, order, stage):
        axis, done = order[stage], order[:stage]
        for step in self.place.partners(axis):
            spot = self.place.moved(axis, self.place.size[axis] - step)
            target = self.region(chunk, done, spot)
            self.copy(lead, stage, step, axis, target, target).wait_recv()

    def drain(self, chunk, lead, order):
        for stage in range(4):
            axis, done = order[stage], order[:stage]
            source = self.region(chunk, done, self.place.at)
            for step in self.place.partners(axis):
                self.copy(lead, stage, step, axis, source, source).wait_send()


class Weights(Gather):
    orders = ("zbac", "zabc")

    def __init__(self, place, buffer, send_sem, recv_sem):
        super().__init__(place, send_sem, recv_sem)
        self.buffer, self.total = buffer, buffer.shape[0]

    def by_order(self, index, work):
        for parity, order in enumerate(self.orders):

            @when(index % 2 == parity)
            def _(order=order):
                work(order)

    def begin(self, index):
        @when(index < self.total)
        def _():
            self.send(self.buffer.at[index], (index,), self.orders[0], 0)

    def tick(self, now):
        self.begin(now + AHEAD)
        for stage in range(4):
            index = now - stage * LAG
            live = (index >= 0) & (index < self.total)

            @when(live)
            def _(index=index, stage=stage):
                def work(order):
                    chunk = self.buffer.at[index]
                    self.receive(chunk, (index,), order, stage)
                    if stage < 3:
                        self.send(chunk, (index,), order, stage + 1)

                self.by_order(index, work)

    def finish(self):
        each(
            self.total,
            lambda index: self.by_order(
                index, lambda order: self.drain(self.buffer.at[index], (index,), order)
            ),
        )


def moments(values):
    mean = jnp.mean(values, axis=-1, keepdims=True)
    centred = values - mean
    spread = jnp.mean(centred * centred, axis=-1, keepdims=True)
    scale = lax.rsqrt(spread + norm_eps)
    return centred * scale, scale


def gelu_pair(upper):
    bell = jnp.exp(-0.5 * upper * upper) * 0.3989422804014327
    below = 0.5 * (1.0 + lax.erf(upper * 0.7071067811865476))
    return upper * below, below + upper * bell


def matrix(buffer, index):
    return buffer[index].reshape(WIDTH, WIDE)


def column_of(row):
    tall = jnp.transpose(jnp.broadcast_to(row.astype(jnp.float32), (8, row.shape[1])))
    return tall[:, 0:1]


def read_vectors(gathered, devices):
    flat = gathered[...].reshape(devices * 8, 128).astype(jnp.bfloat16)

    def line(number):
        shape = (devices, devices * 8)
        wanted = lax.broadcasted_iota(jnp.int32, shape, 0) * 8 + number
        chosen = lax.broadcasted_iota(jnp.int32, shape, 1) == wanted
        return dot(chosen.astype(jnp.bfloat16), flat).astype(jnp.bfloat16)

    def spread(lines, start, wide):
        total = wide * devices
        lane = lax.broadcasted_iota(jnp.int32, (128, total), 1)
        wanted = lax.broadcasted_iota(jnp.int32, (128, total), 0) == start + lane % wide
        found = dot(lines, wanted.astype(jnp.bfloat16))
        owner = lax.broadcasted_iota(jnp.int32, (devices, total), 1) // wide
        mine = owner == lax.broadcasted_iota(jnp.int32, (devices, total), 0)
        return jnp.sum(jnp.where(mine, found, 0.0), axis=0, keepdims=True)

    first = line(0)
    rows = [spread(first, index * UNIT, UNIT) for index in range(4)]
    rows.append(spread(line(2), 0, UNIT))
    return rows, spread(line(1), 0, 4 * UNIT)


def write_vectors(rows, devices):
    result = None
    for index, row in enumerate(rows):
        owner = lax.broadcasted_iota(jnp.int32, (devices, WIDTH), 1) // UNIT
        mine = owner == lax.broadcasted_iota(jnp.int32, (devices, WIDTH), 0)
        spread = jnp.where(mine, row, 0.0)
        lane = lax.broadcasted_iota(jnp.int32, (WIDTH, 128), 0)
        wanted = lax.broadcasted_iota(jnp.int32, (WIDTH, 128), 1) == index * UNIT + lane % UNIT
        found = jnp.dot(
            spread,
            wanted.astype(jnp.float32),
            preferred_element_type=jnp.float32,
            precision=HIGH,
        )
        result = found if result is None else result + found
    return result


def head_lanes(which, shape):
    lane = lax.broadcasted_iota(jnp.int32, shape, 1)
    return lane < 64 if which == 0 else lane >= 64


def allowed(crop_row, mask_row):
    shape = (LENGTH, LENGTH)
    row = lax.broadcasted_iota(jnp.int32, shape, 0)
    column = lax.broadcasted_iota(jnp.int32, shape, 1)
    same = column_of(crop_row) == crop_row.astype(jnp.float32)
    seen = (mask_row > 0) | (row == column)
    return jnp.where(same & (column <= row) & seen, 1.0, 0.0).astype(jnp.bfloat16)


def allowed_back(crop_row, mask_row):
    shape = (LENGTH, LENGTH)
    row = lax.broadcasted_iota(jnp.int32, shape, 0)
    column = lax.broadcasted_iota(jnp.int32, shape, 1)
    same = column_of(crop_row) == crop_row.astype(jnp.float32)
    seen = (column_of(mask_row) > 0) | (row == column)
    return jnp.where(same & (row <= column) & seen, 1.0, 0.0).astype(jnp.bfloat16)


def transpose_into(source, target):
    def work(index):
        at = pl.ds(pl.multiple_of(index * 128, 128), 128)
        target[at, :] = jnp.transpose(source[:, at])

    each(source.shape[1] // 128, work)


def by_rows(work):
    each(LENGTH // 64, lambda index: work(pl.ds(pl.multiple_of(index * 64, 64), 64)))


def forward_heads(pair, qkv, mask, mixed, inverse, attended):
    chunk = pair // 4
    lanes = pl.ds(pl.multiple_of((pair % 4) * 128, 128), 128)
    columns = pl.ds(pl.multiple_of(pair * 128, 128), 128)
    for part in (0, 1):
        keys = 256 * (part + 1)
        rows = slice(part * 256, part * 256 + 256)
        query = qkv[chunk, rows, lanes]
        key = qkv[2 + chunk, 0:keys, lanes]
        value = qkv[4 + chunk, 0:keys, lanes]
        zero, one = jnp.zeros_like(key), jnp.ones_like(key)
        total = None
        for which in (0, 1):
            mine = head_lanes(which, key.shape)
            scores = dot_nt(query, jnp.where(mine, key, zero)).astype(jnp.bfloat16)
            scores = scores * mask[rows, 0:keys]
            right = jnp.concatenate(
                [jnp.where(mine, value, zero), jnp.where(mine, one, zero)], axis=1
            )
            term = dot(scores, right)
            total = term if total is None else total + term
        inverted = 1.0 / total[:, 128:]
        result = total[:, :128] * inverted
        mixed[rows, columns] = result
        inverse[rows, columns] = inverted
        attended[rows, columns] = result.astype(jnp.bfloat16)


def down_rows(dims, buffer, block, half):
    outer, inner, depth = dims
    at = (block // (2 * inner), (block // 2) % inner, block % 2)
    return jnp.concatenate(
        [
            buffer[(DOWN + 2 * group + half,) + at + (z,)]
            for z in range(depth)
            for group in range(4)
        ],
        axis=0,
    )


def feed_block(dims, block, refs):
    normed, normed_t, grad_out, weights, up_bias, result, grad_normed, to_up, to_down, grad_bias = refs
    up = matrix(weights, UP + block)
    upper = dot(normed[...], up) + up_bias[pl.ds(block, 1), :]
    hidden, slope = gelu_pair(upper)
    hidden = hidden.astype(jnp.bfloat16)
    grad_hidden = None
    for half in (0, 1):
        columns = slice(half * WIDE, half * WIDE + WIDE)
        down = down_rows(dims, weights, block, half)
        result[:, columns] += dot(hidden, down)
        term = dot_nt(grad_out[:, columns], down)
        grad_hidden = term if grad_hidden is None else grad_hidden + term
    grad_upper = (grad_hidden * slope).astype(jnp.bfloat16)
    grad_bias[pl.ds(block, 1), :] = jnp.sum(
        grad_upper.astype(jnp.float32), axis=0, keepdims=True
    )
    grad_normed[...] += dot_nt(grad_upper, up)
    to_up[...] = dot(normed_t[...], grad_upper).astype(jnp.bfloat16).reshape(to_up.shape)
    for half in (0, 1):
        columns = slice(half * WIDE, half * WIDE + WIDE)
        term = dot_tn(hidden, grad_out[:, columns]).astype(jnp.bfloat16)
        for z in range(dims[2]):
            for group in range(4):
                start = (z * 4 + group) * UNIT
                to_down[2 * group + half, z] = term[start : start + UNIT]


def forward_kernel(dims, *refs):
    (
        tokens,
        grad_out,
        crops,
        kept,
        gain_one,
        bias_one,
        gain_two,
        bias_two,
        bias_down,
        bias_up,
    ) = refs[:10]
    shards = refs[10:16]
    (
        output,
        sums,
        grad_up_bias,
        rows,
        qkv_out,
        mixed_out,
        inverse_out,
        attended_t_out,
        normed_t_out,
        grad_middle_out,
        attention_out,
        terms,
    ) = refs[16:28]
    (
        weights,
        vectors,
        up_bias,
        mask,
        qkv,
        mixed,
        inverse,
        attended,
        attended_t,
        normed,
        normed_t,
        middle,
        normed_two,
        normed_two_t,
        result,
        grad_normed,
        grad_middle,
        to_up,
        to_down,
        send_sem,
        recv_sem,
        vector_send_sem,
        vector_recv_sem,
        load_sem,
        store_sem,
        up_sem,
        down_sem,
    ) = refs[28:]
    outer, inner, depth = dims
    devices = 2 * outer * inner * depth
    place = Place(dims)
    spot = (place.at["a"], place.at["b"], place.at["c"], place.at["z"])
    place.greet()

    loads = []
    for index in range(GATHERED):
        if index < DOWN:
            source = shards[index // 2].at[:, pl.ds((index % 2) * WIDE, WIDE)]
        elif index < UP:
            group, half = (index - DOWN) // 2, (index - DOWN) % 2
            source = shards[5].at[pl.ds(group * UNIT, UNIT), pl.ds(half * WIDE, WIDE)]
        else:
            source = shards[4].at[:, pl.ds((index - UP) * WIDE, WIDE)]
        item = pltpu.make_async_copy(source, weights.at[(index,) + spot], load_sem.at[index])
        item.start()
        loads.append(item)

    small = Gather(place, vector_send_sem, vector_recv_sem)
    order = "zbac"
    lines = [
        jnp.concatenate([item[...] for item in (gain_one, bias_one, gain_two, bias_two)], axis=1),
        bias_up[...],
        jnp.concatenate([bias_down[...], jnp.zeros((1, 128 - UNIT), jnp.bfloat16)], axis=1),
    ]
    packed = jnp.concatenate(
        [line.astype(jnp.float32) for line in lines] + [jnp.zeros((5, 128), jnp.float32)], axis=0
    )
    vectors[spot] = packed
    small.send(vectors, (), order, 0)
    for item in loads:
        item.wait()
    gather_all = Weights(place, weights, send_sem, recv_sem)
    for index in range(AHEAD):
        gather_all.begin(index)
    mask[...] = allowed(crops[...], kept[...])
    sums[...] = jnp.zeros(sums.shape, jnp.float32)
    for stage in range(4):
        small.receive(vectors, (), order, stage)
        if stage < 3:
            small.send(vectors, (), order, stage + 1)
            gather_all.tick(stage)
    width_rows, up_row = read_vectors(vectors, devices)
    for index, row in enumerate(width_rows):
        rows[index : index + 1, :] = row
    rows[5:8, :] = jnp.zeros((3, WIDTH), jnp.float32)
    for index in range(8):
        up_bias[index : index + 1, :] = up_row[:, index * WIDE : (index + 1) * WIDE]

    def first_norm(at):
        unit, _ = moments(tokens[at, :].astype(jnp.float32))
        normed[at, :] = (unit * rows[0:1, :] + rows[1:2, :]).astype(jnp.bfloat16)

    by_rows(first_norm)
    stores = []

    def store(source, target):
        item = pltpu.make_async_copy(source, target, store_sem.at[len(stores)])
        item.start()
        stores.append(item)

    transpose_into(normed, normed_t)
    store(normed_t, normed_t_out)
    for now in range(3, 6):
        gather_all.tick(now)

    def project(index):
        gather_all.tick(6 + index)
        value = dot(normed[...], matrix(weights, index))
        mapped = jnp.where(value > 0, value + 1.0, jnp.exp(jnp.minimum(value, 0.0)))
        qkv[index] = jnp.where(index < 4, mapped, value).astype(jnp.bfloat16)

    each(6, project)
    store(qkv, qkv_out)

    def heads(pair):
        gather_all.tick(12 + pair)
        forward_heads(pair, qkv, mask, mixed, inverse, attended)

    each(8, heads)
    store(mixed, mixed_out)
    store(inverse, inverse_out)
    store(weights.at[pl.ds(0, DOWN)], attention_out)
    gather_all.tick(20)
    for half in (0, 1):
        columns = slice(half * WIDE, half * WIDE + WIDE)
        middle[:, columns] = tokens[:, columns].astype(jnp.float32) + dot(
            attended[...], matrix(weights, 6 + half)
        )
    transpose_into(attended, attended_t)
    store(attended_t, attended_t_out)
    gather_all.tick(21)

    def second_norm(at):
        value = middle[at, :]
        unit, _ = moments(value)
        normed_two[at, :] = (unit * rows[2:3, :] + rows[3:4, :]).astype(jnp.bfloat16)
        result[at, :] = value + rows[4:5, :]
        grad_normed[at, :] = jnp.zeros((64, WIDTH), jnp.float32)

    by_rows(second_norm)
    transpose_into(normed_two, normed_two_t)

    def leave(block):
        slot = block % 2
        owner = (block // (2 * inner), (block // 2) % inner, block % 2)
        return (
            pltpu.make_async_copy(to_up.at[slot], terms.at[8 + block], up_sem.at[slot]),
            pltpu.make_async_copy(
                to_down.at[slot], terms.at[(pl.ds(0, 8),) + owner], down_sem.at[slot]
            ),
        )

    def feed(block):
        gather_all.tick(22 + block)

        @pl.when(block >= 2)
        def _():
            for item in leave(block - 2):
                item.wait()

        feed_block(
            dims,
            block,
            (
                normed_two,
                normed_two_t,
                grad_out,
                weights,
                up_bias,
                result,
                grad_normed,
                to_up.at[block % 2],
                to_down.at[block % 2],
                grad_up_bias,
            ),
        )
        for item in leave(block):
            item.start()

    each(8, feed)

    def close(at):
        unit, scale = moments(middle[at, :])
        grad = grad_out[at, :].astype(jnp.float32)
        value = grad_normed[at, :]
        output[at, :] = result[at, :].astype(jnp.bfloat16)
        sums[0:1, :] += jnp.sum(value * unit, axis=0, keepdims=True)
        sums[1:2, :] += jnp.sum(value, axis=0, keepdims=True)
        sums[2:3, :] += jnp.sum(grad, axis=0, keepdims=True)
        scaled = value * rows[2:3, :]
        grad_middle[at, :] = grad + scale * (
            scaled
            - jnp.mean(scaled, axis=-1, keepdims=True)
            - unit * jnp.mean(scaled * unit, axis=-1, keepdims=True)
        )

    by_rows(close)
    store(grad_middle, grad_middle_out)
    for block in (6, 7):
        for item in leave(block):
            item.wait()
    small.drain(vectors, (), order)
    gather_all.finish()
    for item in stores:
        item.wait()


def forward(dims, tokens, cotangent, crops, kept, small, shards):
    outer, inner, depth = dims
    most = max(dims) - 1
    lead = (outer, inner, 2, depth)
    tile = (UNIT, WIDE)
    whole = (LENGTH, WIDTH)
    f32, bf16 = jnp.float32, jnp.bfloat16
    shape = jax.ShapeDtypeStruct
    vmem, anywhere = pl.BlockSpec(memory_space=pltpu.VMEM), pl.BlockSpec(memory_space=pl.ANY)
    return pl.pallas_call(
        functools.partial(forward_kernel, dims),
        out_shape=[
            shape(whole, bf16),
            shape((8, WIDTH), f32),
            shape((8, WIDE), f32),
            shape((8, WIDTH), f32),
            shape((6, LENGTH, WIDE), bf16),
            shape(whole, f32),
            shape(whole, f32),
            shape((WIDTH, LENGTH), bf16),
            shape((WIDTH, LENGTH), bf16),
            shape(whole, f32),
            shape((DOWN,) + lead + tile, bf16),
            shape((16,) + lead + tile, bf16),
        ],
        in_specs=[vmem] * 10 + [anywhere] * 6,
        out_specs=[vmem] * 4 + [anywhere] * 8,
        scratch_shapes=[
            pltpu.VMEM((GATHERED,) + lead + tile, bf16),
            pltpu.VMEM(lead + (8, 128), f32),
            pltpu.VMEM((8, WIDE), f32),
            pltpu.VMEM((LENGTH, LENGTH), bf16),
            pltpu.VMEM((6, LENGTH, WIDE), bf16),
            pltpu.VMEM(whole, f32),
            pltpu.VMEM(whole, f32),
            pltpu.VMEM(whole, bf16),
            pltpu.VMEM((WIDTH, LENGTH), bf16),
            pltpu.VMEM(whole, bf16),
            pltpu.VMEM((WIDTH, LENGTH), bf16),
            pltpu.VMEM(whole, f32),
            pltpu.VMEM(whole, bf16),
            pltpu.VMEM((WIDTH, LENGTH), bf16),
            pltpu.VMEM(whole, f32),
            pltpu.VMEM(whole, f32),
            pltpu.VMEM(whole, f32),
            pltpu.VMEM((2,) + lead + tile, bf16),
            pltpu.VMEM((2, 8, depth) + tile, bf16),
            pltpu.SemaphoreType.DMA((GATHERED, 4, most)),
            pltpu.SemaphoreType.DMA((GATHERED, 4, most)),
            pltpu.SemaphoreType.DMA((4, most)),
            pltpu.SemaphoreType.DMA((4, most)),
            pltpu.SemaphoreType.DMA((GATHERED,)),
            pltpu.SemaphoreType.DMA((8,)),
            pltpu.SemaphoreType.DMA((2,)),
            pltpu.SemaphoreType.DMA((2,)),
        ],
        compiler_params=pltpu.CompilerParams(
            collective_id=0, has_side_effects=True, vmem_limit_bytes=VMEM_LIMIT
        ),
        name="forward",
    )(tokens, cotangent, crops, kept, *small, *shards)


class Sums(Mover):
    def start(self, lead, stage, step, axis, source, target):
        self.copy(lead, stage, step, axis, source, target).start()

    def await_all(self, lead, stage, axis, room):
        for step in self.place.partners(axis):
            self.copy(lead, stage, step, axis, room.at[step - 1], room.at[step - 1]).wait_recv()

    @staticmethod
    def pick(order, first, second):
        return (first, second) if order == "ab" else (second, first)

    def after_core(self, lead, order, own, other, came):
        place = self.place
        axis, rest = order

        def add(where):
            for item in range(place.size[rest]):
                at = self.pick(order, where, item)
                other[at] = own[at] + other[at]

        for step in place.partners(axis):
            where = place.moved(axis, step)[axis]
            add(where)
            source = other.at[where] if order == "ab" else other.at[:, where]
            self.start(lead, 1, step, axis, source, came.at[step - 1])
        add(place.at[axis])

    def after_first(self, lead, order, total, came, later):
        place = self.place
        axis, rest = order
        self.await_all(lead, 1, axis, came)

        def add(where):
            at = self.pick(order, place.at[axis], where)
            value = total[at].astype(jnp.float32)
            for step in place.partners(axis):
                value = value + came[step - 1, where].astype(jnp.float32)
            total[at] = value.astype(total.dtype)

        for step in place.partners(rest):
            where = place.moved(rest, step)[rest]
            add(where)
            at = self.pick(order, place.at[axis], where)
            self.start(lead, 2, step, rest, total.at[at], later.at[step - 1])
        add(place.at[rest])

    def after_second(self, lead, order, total, later, last):
        place = self.place
        rest = order[1]
        a, b = place.at["a"], place.at["b"]
        self.await_all(lead, 2, rest, later)

        def add(where):
            value = total[a, b, where].astype(jnp.float32)
            for step in place.partners(rest):
                value = value + later[step - 1, where].astype(jnp.float32)
            return value

        for step in place.partners("z"):
            where = place.moved("z", step)["z"]
            total[a, b, where] = add(where).astype(total.dtype)
            self.start(lead, 3, step, "z", total.at[a, b, where], last.at[step - 1])
        return add(place.at["z"])

    def after_last(self, lead, value, last):
        self.await_all(lead, 3, "z", last)
        for step in self.place.partners("z"):
            value = value + last[step - 1].astype(jnp.float32)
        return value

    def drain(self, lead, order, total, came, later, last):
        place = self.place
        axis, rest = order
        self.copy(lead, 0, 1, "c", total, total).wait_send()
        for step in place.partners(axis):
            self.copy(lead, 1, step, axis, came.at[step - 1], came.at[step - 1]).wait_send()
        for step in place.partners(rest):
            self.copy(lead, 2, step, rest, later.at[step - 1], later.at[step - 1]).wait_send()
        for step in place.partners("z"):
            self.copy(lead, 3, step, "z", last.at[step - 1], last.at[step - 1]).wait_send()


class Gradients(Sums):
    def __init__(self, place, terms, rooms, results, ring, ring_sem, send_sem, recv_sem):
        super().__init__(place, send_sem, recv_sem)
        self.terms, self.rooms, self.results = terms, rooms, results
        self.ring, self.ring_sem = ring, ring_sem
        self.total = results.shape[0]
        self.first = terms[0].shape[0]

    def by_order(self, index, work):
        half = index // 2
        total, ones, others, twos, fours, last = self.rooms

        @when(index % 2 == 0)
        def _():
            work("ab", total.at[index], ones.at[half], twos.at[half], last.at[index])

        @when(index % 2 == 1)
        def _():
            work("ba", total.at[index], others.at[half], fours.at[half], last.at[index])

    def begin(self, index):
        side = self.place.at["c"]
        slot = index % (AHEAD + 1)

        def go(source):
            self.start((index,), 0, 1, "c", source.at[:, :, 1 - side], self.rooms[0].at[index])
            pltpu.make_async_copy(
                source.at[:, :, side], self.ring.at[slot], self.ring_sem.at[slot]
            ).start()

        @when(index < self.first)
        def _():
            go(self.terms[0].at[index])

        @when((index >= self.first) & (index < self.total))
        def _():
            go(self.terms[1].at[index - self.first])

    def tick(self, now):
        self.begin(now + AHEAD)

        def live(index):
            return (index >= 0) & (index < self.total)

        @when(live(now))
        def _():
            slot = now % (AHEAD + 1)
            room = self.ring.at[slot]
            pltpu.make_async_copy(room, room, self.ring_sem.at[slot]).wait()
            total = self.rooms[0].at[now]
            self.copy((now,), 0, 1, "c", total, total).wait_recv()
            self.by_order(
                now,
                lambda order, total, came, later, last: self.after_core(
                    (now,), order, room, total, came
                ),
            )

        second = now - LAG

        @when(live(second))
        def _():
            self.by_order(
                second,
                lambda order, total, came, later, last: self.after_first(
                    (second,), order, total, came, later
                ),
            )

        third = now - 2 * LAG

        @when(live(third))
        def _():
            def work(order, total, came, later, last):
                self.results[third] = self.after_second((third,), order, total, later, last)

            self.by_order(third, work)

        fourth = now - 3 * LAG

        @when(live(fourth))
        def _():
            self.results[fourth] = self.after_last(
                (fourth,), self.results[fourth], self.rooms[5].at[fourth]
            )

    def finish(self):
        def work(index):
            self.by_order(
                index,
                lambda order, total, came, later, last: self.drain(
                    (index,), order, total, came, later, last
                ),
            )

        each(self.total, work)


def backward_heads(pair, qkv, mask, mask_t, mixed, inverse, grad_mixed):
    chunk = pair // 4
    lanes = pl.ds(pl.multiple_of((pair % 4) * 128, 128), 128)
    columns = pl.ds(pl.multiple_of(pair * 128, 128), 128)
    query = qkv[chunk, :, lanes]
    key = qkv[2 + chunk, :, lanes]
    value = qkv[4 + chunk, :, lanes]
    grad_numer = (grad_mixed[:, columns] * inverse[:, columns]).astype(jnp.bfloat16)
    part = grad_numer.astype(jnp.float32) * mixed[:, columns]
    high = part.astype(jnp.bfloat16)
    low = pltpu.roll(part - high.astype(jnp.float32), 64, 1).astype(jnp.bfloat16)
    zero, minus = jnp.zeros_like(query), jnp.full_like(query, -1.0)
    heads = []
    for which in (0, 1):
        mine = head_lanes(which, query.shape)
        heads.append(
            (
                jnp.concatenate([grad_numer, jnp.where(mine, high, low)], axis=1),
                jnp.concatenate([jnp.where(mine, value, zero), minus], axis=1),
                jnp.where(mine, query, zero),
                jnp.where(mine, key, zero),
                jnp.where(mine, grad_numer, zero),
            )
        )
    for part in (0, 1):
        keys = 256 * (part + 1)
        rows = slice(part * 256, part * 256 + 256)
        total = None
        for left, right, _, own_key, _ in heads:
            grad_scores = dot_nt(left[rows], right[:keys]).astype(jnp.bfloat16)
            term = dot(grad_scores * mask[rows, 0:keys], own_key[:keys])
            total = term if total is None else total + term
        slope = jnp.minimum(query[rows].astype(jnp.float32), 1.0)
        qkv[chunk, rows, lanes] = (total * slope).astype(jnp.bfloat16)
    for part in (0, 1):
        start = part * 256
        rows = slice(start, start + 256)
        grad_key = grad_value = None
        for left, right, own_query, own_key, own_grad in heads:
            seen = mask_t[rows, start:LENGTH]
            scores = dot_nt(own_key[rows], query[start:]).astype(jnp.bfloat16) * seen
            grad_scores = dot_nt(right[rows], left[start:]).astype(jnp.bfloat16) * seen
            term = dot(scores, own_grad[start:])
            grad_value = term if grad_value is None else grad_value + term
            term = dot(grad_scores, own_query[start:])
            grad_key = term if grad_key is None else grad_key + term
        slope = jnp.minimum(key[rows].astype(jnp.float32), 1.0)
        qkv[2 + chunk, rows, lanes] = (grad_key * slope).astype(jnp.bfloat16)
        qkv[4 + chunk, rows, lanes] = grad_value.astype(jnp.bfloat16)


def backward_kernel(dims, *refs):
    tokens, crops, kept, sums_in, grad_up_bias, rows = refs[:6]
    qkv_in, mixed_in, inverse_in, attended_t_in, normed_t_in, grad_middle_in = refs[6:12]
    attention_in, terms = refs[12:14]
    input_grad, owned, owned_small, attention_terms = refs[14:18]
    (
        weights,
        mask,
        mask_t,
        grad_attended,
        grad_mixed,
        qkv,
        turned,
        mixed,
        inverse,
        grad_middle,
        sums,
        staged,
        small,
        ring,
        total,
        ones,
        others,
        twos,
        fours,
        last,
        side_other,
        side_came,
        side_later,
        side_last,
        load_sem,
        stage_sem,
        ring_sem,
        send_sem,
        recv_sem,
        side_send_sem,
        side_recv_sem,
    ) = refs[18:]
    outer, inner, depth = dims
    devices = 2 * outer * inner * depth
    place = Place(dims)
    spot = place.at
    place.greet()
    adder = Gradients(
        place,
        (terms, attention_terms),
        (total, ones, others, twos, fours, last),
        owned,
        ring,
        ring_sem,
        send_sem,
        recv_sem,
    )
    for index in range(AHEAD):
        adder.begin(index)
    loads = {}

    def load(name, source, target):
        item = pltpu.make_async_copy(source, target, load_sem.at[len(loads)])
        item.start()
        loads[name] = item

    load("grad_middle", grad_middle_in, grad_middle)
    load("out", attention_in.at[pl.ds(6, 2)], weights.at[pl.ds(6, 2)])
    load("attended", attended_t_in, turned.at[0])
    load("qkv", qkv_in, qkv)
    load("mixed", mixed_in, mixed)
    load("inverse", inverse_in, inverse)
    load("normed", normed_t_in, turned.at[1])
    load("rest", attention_in.at[pl.ds(0, 6)], weights.at[pl.ds(0, 6)])
    mask[...] = allowed(crops[...], kept[...])
    mask_t[...] = allowed_back(crops[...], kept[...])
    sums[...] = sums_in[...]
    loads["grad_middle"].wait()

    def round_rows(at):
        grad_attended[at, :] = grad_middle[at, :].astype(jnp.bfloat16)

    by_rows(round_rows)
    adder.tick(0)
    loads["out"].wait()
    grad_mixed[...] = dot_nt(grad_attended[:, 0:WIDE], matrix(weights, 6)) + dot_nt(
        grad_attended[:, WIDE:WIDTH], matrix(weights, 7)
    )
    adder.tick(1)
    loads["attended"].wait()
    for half in (0, 1):
        columns = slice(half * WIDE, half * WIDE + WIDE)
        value = dot(turned[0], grad_attended[:, columns]).astype(jnp.bfloat16)
        staged[half] = value.reshape(staged.shape[1:])
        pltpu.make_async_copy(
            staged.at[half], attention_terms.at[half], stage_sem.at[half]
        ).start()
    for name in ("qkv", "mixed", "inverse"):
        loads[name].wait()

    def heads(pair):
        adder.tick(2 + pair)
        backward_heads(pair, qkv, mask, mask_t, mixed, inverse, grad_mixed)

    each(8, heads)
    loads["normed"].wait()
    loads["rest"].wait()
    grad_normed = grad_mixed
    grad_normed[...] = jnp.zeros(grad_normed.shape, jnp.float32)

    def stage_copy(index):
        slot = index % 2
        return pltpu.make_async_copy(
            staged.at[slot], attention_terms.at[2 + index], stage_sem.at[slot]
        )

    def project(index):
        pltpu.make_async_copy(
            staged.at[index % 2], staged.at[index % 2], stage_sem.at[index % 2]
        ).wait()
        adder.tick(10 + index)
        value = dot(turned[1], qkv[index]).astype(jnp.bfloat16)
        staged[index % 2] = value.reshape(staged.shape[1:])
        stage_copy(index).start()
        grad_normed[...] += dot_nt(qkv[index], matrix(weights, index))

    each(4, project)
    for index in (4, 5):
        slot = index % 2
        stage_copy(index - 2).wait()
        value = dot(turned[1], qkv[index]).astype(jnp.bfloat16)
        staged[slot] = value.reshape(staged.shape[1:])
        stage_copy(index).start()
        grad_normed[...] += dot_nt(qkv[index], matrix(weights, index))
        adder.tick(10 + index)
    for index in (4, 5):
        stage_copy(index).wait()
    adder.tick(16)

    def close(at):
        unit, scale = moments(tokens[at, :].astype(jnp.float32))
        value = grad_normed[at, :]
        sums[3:4, :] += jnp.sum(value * unit, axis=0, keepdims=True)
        sums[4:5, :] += jnp.sum(value, axis=0, keepdims=True)
        scaled = value * rows[0:1, :]
        input_grad[at, :] = (
            grad_middle[at, :]
            + scale
            * (
                scaled
                - jnp.mean(scaled, axis=-1, keepdims=True)
                - unit * jnp.mean(scaled * unit, axis=-1, keepdims=True)
            )
        ).astype(jnp.bfloat16)

    by_rows(close)
    order = [sums[index : index + 1, :] for index in (3, 4, 0, 1)]
    first = write_vectors(order, devices)
    third = write_vectors([sums[2:3, :]], devices)
    for device in range(devices):
        at = (
            device // (2 * inner * depth),
            (device // (2 * depth)) % inner,
            (device // depth) % 2,
            device % depth,
        )
        block, lane = device // 4, (device % 4) * 128
        small[at + (slice(0, 1),)] = first[device : device + 1, :]
        small[at + (slice(1, 2),)] = grad_up_bias[block : block + 1, lane : lane + 128]
        small[at + (slice(2, 3),)] = third[device : device + 1, :]
        small[at + (slice(3, 8),)] = jnp.zeros((5, 128), jnp.float32)
    side = Sums(place, side_send_sem, side_recv_sem)
    side.start((), 0, 1, "c", small.at[:, :, 1 - spot["c"]], side_other)
    adder.tick(17)
    side.copy((), 0, 1, "c", side_other, side_other).wait_recv()
    side.after_core((), "ab", small.at[:, :, spot["c"]], side_other, side_came)
    adder.tick(18)
    side.after_first((), "ab", side_other, side_came, side_later)
    adder.tick(19)
    owned_small[...] = side.after_second((), "ab", side_other, side_later, side_last)
    adder.tick(20)
    owned_small[...] = side.after_last((), owned_small[...], side_last)
    each(GATHERED + 3 * LAG - 21, lambda index: adder.tick(21 + index))
    side.drain((), "ab", side_other, side_came, side_later, side_last)
    adder.finish()


def backward(dims, tokens, crops, kept, sums, grad_up_bias, rows, kept_values, terms):
    outer, inner, depth = dims
    most = max(dims) - 1
    lead = (outer, inner, 2, depth)
    tile = (UNIT, WIDE)
    whole = (LENGTH, WIDTH)
    f32, bf16 = jnp.float32, jnp.bfloat16
    shape = jax.ShapeDtypeStruct
    vmem, anywhere = pl.BlockSpec(memory_space=pltpu.VMEM), pl.BlockSpec(memory_space=pl.ANY)
    half = GATHERED // 2
    chip = (outer, inner, depth)
    small_tile = (8, 128)
    return pl.pallas_call(
        functools.partial(backward_kernel, dims),
        out_shape=[
            shape(whole, bf16),
            shape((GATHERED,) + tile, f32),
            shape(small_tile, f32),
            shape((8,) + lead + tile, bf16),
        ],
        in_specs=[vmem] * 6 + [anywhere] * 8,
        out_specs=[vmem] * 3 + [anywhere],
        scratch_shapes=[
            pltpu.VMEM((8,) + lead + tile, bf16),
            pltpu.VMEM((LENGTH, LENGTH), bf16),
            pltpu.VMEM((LENGTH, LENGTH), bf16),
            pltpu.VMEM(whole, bf16),
            pltpu.VMEM(whole, f32),
            pltpu.VMEM((6, LENGTH, WIDE), bf16),
            pltpu.VMEM((2, WIDTH, LENGTH), bf16),
            pltpu.VMEM(whole, f32),
            pltpu.VMEM(whole, f32),
            pltpu.VMEM(whole, f32),
            pltpu.VMEM((8, WIDTH), f32),
            pltpu.VMEM((2,) + lead + tile, bf16),
            pltpu.VMEM(lead + small_tile, f32),
            pltpu.VMEM((AHEAD + 1,) + chip + tile, bf16),
            pltpu.VMEM((GATHERED,) + chip + tile, bf16),
            pltpu.VMEM((half, outer - 1, inner, depth) + tile, bf16),
            pltpu.VMEM((half, inner - 1, outer, depth) + tile, bf16),
            pltpu.VMEM((half, inner - 1, depth) + tile, bf16),
            pltpu.VMEM((half, outer - 1, depth) + tile, bf16),
            pltpu.VMEM((GATHERED, depth - 1) + tile, bf16),
            pltpu.VMEM(chip + small_tile, f32),
            pltpu.VMEM((outer - 1, inner, depth) + small_tile, f32),
            pltpu.VMEM((inner - 1, depth) + small_tile, f32),
            pltpu.VMEM((depth - 1,) + small_tile, f32),
            pltpu.SemaphoreType.DMA((8,)),
            pltpu.SemaphoreType.DMA((2,)),
            pltpu.SemaphoreType.DMA((AHEAD + 1,)),
            pltpu.SemaphoreType.DMA((GATHERED, 4, most)),
            pltpu.SemaphoreType.DMA((GATHERED, 4, most)),
            pltpu.SemaphoreType.DMA((4, most)),
            pltpu.SemaphoreType.DMA((4, most)),
        ],
        compiler_params=pltpu.CompilerParams(
            collective_id=1, has_side_effects=True, vmem_limit_bytes=VMEM_LIMIT
        ),
        name="backward",
    )(tokens, crops, kept, sums, grad_up_bias, rows, *kept_values, terms)


def body(
    tokens,
    crop_ids,
    kv_mask,
    norm1_gain,
    norm1_bias,
    w_query,
    w_key,
    w_value,
    w_out,
    norm2_gain,
    norm2_bias,
    w_up,
    up_bias,
    w_down,
    down_bias,
    cotangent,
):
    inner = lax.axis_size("dp") // (2 * OUTER)
    dims = (OUTER, inner, lax.axis_size("fsdp"))
    fits = (
        tokens.shape == (1, LENGTH, WIDTH)
        and w_up.shape == (UNIT, HIDDEN)
        and w_down.shape == (HIDDEN // WIDTH * UNIT, WIDTH)
        and dims[2] * 4 * UNIT == WIDE
    )
    if not fits:
        return general_body(
            tokens,
            crop_ids,
            kv_mask,
            norm1_gain,
            norm1_bias,
            w_query,
            w_key,
            w_value,
            w_out,
            norm2_gain,
            norm2_bias,
            w_up,
            up_bias,
            w_down,
            down_bias,
            cotangent,
        )
    small = [
        vector.reshape(1, -1)
        for vector in (norm1_gain, norm1_bias, norm2_gain, norm2_bias, down_bias, up_bias)
    ]
    pixels = tokens.reshape(LENGTH, WIDTH)
    (output, sums, grad_up, rows, qkv, mixed, inverse, attended_t, normed_t, grad_middle, attention, terms) = (
        forward(
            dims,
            pixels,
            cotangent.reshape(LENGTH, WIDTH),
            crop_ids,
            kv_mask,
            small,
            (w_query, w_key, w_value, w_out, w_up, w_down),
        )
    )
    input_grad, owned, owned_small, _ = backward(
        dims,
        pixels,
        crop_ids,
        kv_mask,
        sums,
        grad_up,
        rows,
        (qkv, mixed, inverse, attended_t, normed_t, grad_middle, attention),
        terms,
    )

    def side_by_side(start, count):
        return owned[start : start + count].transpose(1, 0, 2).reshape(UNIT, count * WIDE)

    own_down = owned[0:8].reshape(4, 2, UNIT, WIDE).transpose(0, 2, 1, 3).reshape(4 * UNIT, WIDTH)
    own_up = side_by_side(8, 8)
    own_out, own_query, own_key, own_value = (side_by_side(16 + 2 * index, 2) for index in range(4))
    gain_one, bias_one, gain_two, bias_two = (
        owned_small[0, index * UNIT : (index + 1) * UNIT] for index in range(4)
    )
    return (
        output.reshape(tokens.shape),
        input_grad.reshape(tokens.shape),
        gain_one,
        bias_one,
        own_query,
        own_key,
        own_value,
        own_out,
        gain_two,
        bias_two,
        own_up,
        owned_small[1],
        own_down,
        owned_small[2, :UNIT],
    )


def solution(mesh):
    return jax.shard_map(
        body,
        mesh=mesh,
        in_specs=(
            P(("dp", "fsdp"), None, None),
            P(("dp", "fsdp"), None),
            P(("dp", "fsdp"), None),
            P(("dp", "fsdp")),
            P(("dp", "fsdp")),
            P(("dp", "fsdp"), None),
            P(("dp", "fsdp"), None),
            P(("dp", "fsdp"), None),
            P(("dp", "fsdp"), None),
            P(("dp", "fsdp")),
            P(("dp", "fsdp")),
            P(("dp", "fsdp"), None),
            P(("dp", "fsdp")),
            P(("dp", "fsdp"), None),
            P(("dp", "fsdp")),
            P(("dp", "fsdp"), None, None),
        ),
        out_specs=(
            P(("dp", "fsdp"), None, None),
            P(("dp", "fsdp"), None, None),
            P(("dp", "fsdp")),
            P(("dp", "fsdp")),
            P(("dp", "fsdp"), None),
            P(("dp", "fsdp"), None),
            P(("dp", "fsdp"), None),
            P(("dp", "fsdp"), None),
            P(("dp", "fsdp")),
            P(("dp", "fsdp")),
            P(("dp", "fsdp"), None),
            P(("dp", "fsdp")),
            P(("dp", "fsdp"), None),
            P(("dp", "fsdp")),
        ),
        check_vma=False,
    )
```

```python
import functools
import itertools

import jax
import jax.numpy as jnp
from jax import lax
from jax.experimental import pallas as pl
from jax.experimental.pallas import tpu as pltpu
from jax.sharding import PartitionSpec as P

HEADS = 16
BLOCK = 512
MESH = pl.DeviceIdType.MESH
WIDE = 512
OUTER = 2


class Place:
    def __init__(self, dims):
        self.size = {"a": dims[0], "b": dims[1], "c": 2, "z": dims[2]}
        dp = lax.axis_index("dp")
        self.at = {
            "a": dp // (2 * dims[1]),
            "b": (dp // 2) % dims[1],
            "c": dp % 2,
            "z": lax.axis_index("fsdp"),
        }

    def moved(self, axis, step):
        spot = dict(self.at)
        spot[axis] = (spot[axis] + step) % self.size[axis]
        return spot

    def device(self, axis, step):
        spot = self.moved(axis, step)
        return ((spot["a"] * self.size["b"] + spot["b"]) * 2 + spot["c"], spot["z"])

    def partners(self, axis):
        return range(1, self.size[axis])

    def greet(self):
        barrier = pltpu.get_barrier_semaphore()
        count = 0
        for axis in "abcz":
            for step in self.partners(axis):
                pl.semaphore_signal(
                    barrier, 1, device_id=self.device(axis, step), device_id_type=MESH
                )
                count += 1
        pl.semaphore_wait(barrier, count)


def pieces_of(rows, columns, unit):
    wide = min(WIDE, columns)
    return [
        (row, unit, column, wide)
        for row in range(0, rows, unit)
        for column in range(0, columns, wide)
    ]


def gather_kernel(dims, orders, lag, ahead, pieces, *refs):
    count = len(pieces)
    shards, wholes = refs[:count], refs[count : 2 * count]
    local_sem, send_sem, recv_sem = refs[2 * count :]
    place = Place(dims)
    place.greet()
    chunks = [
        (shard.at[pl.ds(ro, rn), pl.ds(co, cn)], whole, pl.ds(ro, rn), pl.ds(co, cn))
        for shard, whole, items in zip(shards, wholes, pieces)
        for ro, rn, co, cn in items
    ]
    total = len(chunks)
    sent, kept = [], []

    def region(index, done, spot):
        _, whole, rows, columns = chunks[index]
        lead = tuple(slice(None) if axis in done else spot[axis] for axis in "abcz")
        return whole.at[lead + (rows, columns)]

    def copy(index, stage, step, axis, source, target):
        return pltpu.make_async_remote_copy(
            source,
            target,
            send_sem.at[index, stage, step - 1],
            recv_sem.at[index, stage, step - 1],
            device_id=place.device(axis, step),
            device_id_type=MESH,
        )

    def send(index, stage):
        order = orders[index % len(orders)]
        axis, done = order[stage], order[:stage]
        target = region(index, done, place.at)
        for step in place.partners(axis):
            item = copy(index, stage, step, axis, target if done else chunks[index][0], target)
            item.start()
            sent.append(item)

    def receive(index, stage):
        order = orders[index % len(orders)]
        axis, done = order[stage], order[:stage]
        for step in place.partners(axis):
            target = region(index, done, place.moved(axis, place.size[axis] - step))
            copy(index, stage, step, axis, target, target).wait_recv()

    def begin(index):
        if index < total:
            item = pltpu.make_async_copy(
                chunks[index][0], region(index, "", place.at), local_sem.at[index]
            )
            item.start()
            kept.append(item)
            send(index, 0)

    for index in range(ahead):
        begin(index)
    for tick in range(total + 3 * lag):
        begin(tick + ahead)
        for stage in range(4):
            index = tick - stage * lag
            if 0 <= index < total:
                receive(index, stage)
                if stage == 0:
                    kept[index].wait()
                if stage < 3:
                    send(index, stage + 1)
    for item in sent:
        item.wait_send()


def gather(dims, shards, unit, lag=3, ahead=6):
    pieces = [pieces_of(*shard.shape, min(unit, shard.shape[0])) for shard in shards]
    total = sum(len(items) for items in pieces)
    most = max(dims) - 1
    anywhere = pl.BlockSpec(memory_space=pl.ANY)
    orders = ("zbac", "zabc", "zbac", "zabc", "bzac", "azbc")
    wholes = pl.pallas_call(
        functools.partial(gather_kernel, dims, orders, lag, ahead, pieces),
        out_shape=[
            jax.ShapeDtypeStruct(dims[:2] + (2, dims[2]) + shard.shape, shard.dtype)
            for shard in shards
        ],
        in_specs=[anywhere] * len(shards),
        out_specs=[anywhere] * len(shards),
        scratch_shapes=[
            pltpu.SemaphoreType.DMA((total,)),
            pltpu.SemaphoreType.DMA((total, 4, most)),
            pltpu.SemaphoreType.DMA((total, 4, most)),
        ],
        compiler_params=pltpu.CompilerParams(collective_id=0, has_side_effects=True),
        name="gather",
    )(*shards)
    return [whole.reshape((-1, whole.shape[-1])) for whole in wholes]


def scatter_kernel(dims, lag, ahead, pieces, *refs):
    count = len(pieces)
    terms, owned = refs[:count], refs[count : 2 * count]
    main = refs[2 * count : 2 * count + 7]
    side = refs[2 * count + 7 : 2 * count + 12]
    local_sem, send_sem, recv_sem = refs[2 * count + 12 :]
    place = Place(dims)
    place.greet()
    spot = place.at
    chunks = []
    for array, items in enumerate(pieces):
        for ro, rn, co, cn in items:
            index = len(chunks)
            if array == 0:
                rooms = side
                order = "ab"
            else:
                half = (index - 1) // 2
                order = "ab" if index % 2 else "ba"
                first, second = (main[2], main[4]) if index % 2 else (main[3], main[5])
                rooms = (
                    main[0].at[index - 1],
                    main[1].at[index - 1],
                    first.at[half],
                    second.at[half],
                    main[6].at[index - 1],
                )
            chunks.append((terms[array], owned[array], pl.ds(ro, rn), pl.ds(co, cn), order, rooms))
    total = len(chunks)
    sent, kept = [], []

    def copy(index, stage, step, axis, source, target):
        return pltpu.make_async_remote_copy(
            source,
            target,
            send_sem.at[index, stage, step - 1],
            recv_sem.at[index, stage, step - 1],
            device_id=place.device(axis, step),
            device_id_type=MESH,
        )

    def send(index, stage, step, axis, source, target):
        item = copy(index, stage, step, axis, source, target)
        item.start()
        sent.append(item)

    def begin(index):
        if index < total:
            term, _, rows, columns, _, rooms = chunks[index]
            send(index, 0, 1, "c", term.at[:, :, 1 - spot["c"], :, rows, columns], rooms[1])
            item = pltpu.make_async_copy(
                term.at[:, :, spot["c"], :, rows, columns], rooms[0], local_sem.at[index]
            )
            item.start()
            kept.append(item)

    def await_all(index, stage, axis, room):
        for step in place.partners(axis):
            copy(index, stage, step, axis, room.at[step - 1], room.at[step - 1]).wait_recv()

    def pick(order, first, second):
        return (first, second) if order == "ab" else (second, first)

    def after_core(index):
        order, (own, other, came, _, _) = chunks[index][4:]
        kept[index].wait()
        copy(index, 0, 1, "c", other, other).wait_recv()
        axis, rest = order

        def add(where):
            for item in range(place.size[rest]):
                at = pick(order, where, item)
                own[at] = own[at] + other[at]

        for step in place.partners(axis):
            where = place.moved(axis, step)[axis]
            add(where)
            source = own.at[where] if order == "ab" else own.at[:, where]
            send(index, 1, step, axis, source, came.at[step - 1])
        add(spot[axis])

    def after_first(index):
        order, (own, _, came, later, _) = chunks[index][4:]
        axis, rest = order
        await_all(index, 1, axis, came)

        def add(where):
            at = pick(order, spot[axis], where)
            value = own[at].astype(jnp.float32)
            for step in place.partners(axis):
                value = value + came[step - 1, where].astype(jnp.float32)
            own[at] = value.astype(own.dtype)

        for step in place.partners(rest):
            where = place.moved(rest, step)[rest]
            add(where)
            at = pick(order, spot[axis], where)
            send(index, 2, step, rest, own.at[at], later.at[step - 1])
        add(spot[rest])

    def after_second(index):
        _, result, rows, columns, order, (own, _, _, later, last) = chunks[index]
        rest = order[1]
        await_all(index, 2, rest, later)

        def add(where):
            value = own[spot["a"], spot["b"], where].astype(jnp.float32)
            for step in place.partners(rest):
                value = value + later[step - 1, where].astype(jnp.float32)
            return value

        for step in place.partners("z"):
            where = place.moved("z", step)["z"]
            own[spot["a"], spot["b"], where] = add(where).astype(own.dtype)
            send(index, 3, step, "z", own.at[spot["a"], spot["b"], where], last.at[step - 1])
        result[rows, columns] = add(spot["z"])

    def after_last(index):
        _, result, rows, columns, _, (_, _, _, _, last) = chunks[index]
        await_all(index, 3, "z", last)
        value = result[rows, columns]
        for step in place.partners("z"):
            value = value + last[step - 1].astype(jnp.float32)
        result[rows, columns] = value

    for index in range(ahead):
        begin(index)
    for tick in range(total + 3 * lag):
        begin(tick + ahead)
        for stage, work in enumerate((after_core, after_first, after_second, after_last)):
            index = tick - stage * lag
            if 0 <= index < total:
                work(index)
    for item in sent:
        item.wait_send()


def rooms_of(dims, many, unit, wide, dtype):
    outer, inner, depth = dims
    ones, twos = (many + 1) // 2, many // 2
    tail = (unit, wide)
    return [
        pltpu.VMEM((many, outer, inner, depth) + tail, dtype),
        pltpu.VMEM((many, outer, inner, depth) + tail, dtype),
        pltpu.VMEM((ones, outer - 1, inner, depth) + tail, dtype),
        pltpu.VMEM((twos, inner - 1, outer, depth) + tail, dtype),
        pltpu.VMEM((ones, inner - 1, depth) + tail, dtype),
        pltpu.VMEM((twos, outer - 1, depth) + tail, dtype),
        pltpu.VMEM((many, depth - 1) + tail, dtype),
    ]


def scatter(dims, small, terms, unit, lag=2, ahead=4):
    outer, inner, depth = dims
    devices = 2 * outer * inner * depth
    lead = (outer, inner, 2, depth)
    arrays = [small.reshape(lead + small.shape[1:])] + [
        term.reshape(lead + (term.shape[0] // devices, term.shape[1])) for term in terms
    ]
    pieces = [pieces_of(*arrays[0].shape[4:], arrays[0].shape[4])]
    pieces += [pieces_of(*array.shape[4:], unit) for array in arrays[1:]]
    total = sum(len(items) for items in pieces)
    most = max(dims) - 1
    tail = small.shape[1:]
    side = [
        pltpu.VMEM((outer, inner, depth) + tail, jnp.float32),
        pltpu.VMEM((outer, inner, depth) + tail, jnp.float32),
        pltpu.VMEM((outer - 1, inner, depth) + tail, jnp.float32),
        pltpu.VMEM((inner - 1, depth) + tail, jnp.float32),
        pltpu.VMEM((depth - 1,) + tail, jnp.float32),
    ]
    return pl.pallas_call(
        functools.partial(scatter_kernel, dims, lag, ahead, pieces),
        out_shape=[jax.ShapeDtypeStruct(array.shape[4:], jnp.float32) for array in arrays],
        in_specs=[pl.BlockSpec(memory_space=pl.ANY)] * len(arrays),
        out_specs=[pl.BlockSpec(memory_space=pltpu.VMEM)] * len(arrays),
        scratch_shapes=rooms_of(dims, total - 1, unit, WIDE, jnp.bfloat16)
        + side
        + [
            pltpu.SemaphoreType.DMA((total,)),
            pltpu.SemaphoreType.DMA((total, 4, most)),
            pltpu.SemaphoreType.DMA((total, 4, most)),
        ],
        compiler_params=pltpu.CompilerParams(
            collective_id=1, has_side_effects=True, vmem_limit_bytes=60 << 20
        ),
        name="scatter",
    )(*arrays)


HIGH = lax.Precision.HIGHEST
norm_eps = 1e-05


def norm_affine(values, gain, shift):
    mean = jnp.mean(values, axis=-1, keepdims=True)
    centred = values - mean
    spread = jnp.mean(centred * centred, axis=-1, keepdims=True)
    return centred * lax.rsqrt(spread + norm_eps) * gain + shift


def feature(values):
    return jax.nn.elu(values) + 1.0


def gelu_exact(values):
    return jax.nn.gelu(values, approximate=False)


def allowed_weight(crop, keymask):
    places = jnp.arange(crop.shape[0])
    earlier = places[None, :] <= places[:, None]
    same = crop[:, None] == crop[None, :]
    visible = (keymask[None, :] > 0) | (places[None, :] == places[:, None])
    return (earlier & same & visible).astype(jnp.float32)


def attend_forward(carry, pieces):
    state, norm_state, prev_crop = carry
    query_feat, key_feat, values, crop, keymask = pieces
    weight = allowed_weight(crop, keymask)
    scores = (
        jnp.einsum("ihe,jhe->hij", query_feat, key_feat, preferred_element_type=jnp.float32)
        * weight[None]
    )
    value_wide = values.astype(jnp.float32)
    query_wide = query_feat.astype(jnp.float32)
    key_wide = key_feat.astype(jnp.float32)
    numer = jnp.einsum("hij,jhe->ihe", scores, value_wide, precision=HIGH)
    denom = jnp.sum(scores, axis=2).T
    follows = (crop == prev_crop).astype(jnp.float32)
    numer = numer + follows[:, None, None] * jnp.einsum(
        "ihe,hef->ihf", query_wide, state, precision=HIGH
    )
    denom = denom + follows[:, None] * jnp.einsum(
        "ihe,he->ih", query_wide, norm_state, precision=HIGH
    )
    last_crop = crop[crop.shape[0] - 1]
    carried = (prev_crop == last_crop).astype(jnp.float32)
    select = ((crop == last_crop) & (keymask > 0)).astype(jnp.float32)
    chosen = key_wide * select[:, None, None]
    new_state = carried * state + jnp.einsum("jhe,jhf->hef", chosen, value_wide, precision=HIGH)
    new_norm = carried * norm_state + jnp.sum(chosen, axis=0)
    return ((new_state, new_norm, last_crop), (numer / denom[:, :, None], denom, state, norm_state))


def attend_backward(carry, pieces):
    grad_state, grad_norm = carry
    (
        query_feat,
        key_feat,
        values,
        crop,
        keymask,
        prev_crop,
        state,
        norm_state,
        grad_numer,
        grad_denom,
    ) = pieces
    weight = allowed_weight(crop, keymask)
    scores = (
        jnp.einsum("ihe,jhe->hij", query_feat, key_feat, preferred_element_type=jnp.float32)
        * weight[None]
    )
    value_wide = values.astype(jnp.float32)
    query_wide = query_feat.astype(jnp.float32)
    key_wide = key_feat.astype(jnp.float32)
    grad_scores = (
        jnp.einsum("ihe,jhe->hij", grad_numer, value_wide, precision=HIGH)
        + grad_denom.T[:, :, None]
    ) * weight[None]
    follows = (crop == prev_crop).astype(jnp.float32)
    last_crop = crop[crop.shape[0] - 1]
    carried = (prev_crop == last_crop).astype(jnp.float32)
    select = ((crop == last_crop) & (keymask > 0)).astype(jnp.float32)
    grad_query = jnp.einsum("hij,jhe->ihe", grad_scores, key_wide, precision=HIGH)
    grad_query = grad_query + follows[:, None, None] * (
        jnp.einsum("ihf,hef->ihe", grad_numer, state, precision=HIGH)
        + grad_denom[:, :, None] * norm_state[None]
    )
    grad_key = jnp.einsum("hij,ihe->jhe", grad_scores, query_wide, precision=HIGH)
    grad_key = grad_key + select[:, None, None] * (
        jnp.einsum("jhf,hef->jhe", value_wide, grad_state, precision=HIGH) + grad_norm[None]
    )
    grad_value = jnp.einsum("hij,ihe->jhe", scores, grad_numer, precision=HIGH)
    grad_value = grad_value + select[:, None, None] * jnp.einsum(
        "jhe,hef->jhf", key_wide, grad_state, precision=HIGH
    )
    query_kept = query_wide * follows[:, None, None]
    earlier_state = carried * grad_state + jnp.einsum(
        "ihe,ihf->hef", query_kept, grad_numer, precision=HIGH
    )
    earlier_norm = carried * grad_norm + jnp.einsum(
        "ihe,ih->he", query_kept, grad_denom, precision=HIGH
    )
    return ((earlier_state, earlier_norm), (grad_query, grad_key, grad_value))


def split_blocks(array):
    blocks = array.shape[0] // BLOCK
    return array.reshape((blocks, BLOCK) + array.shape[1:])


def attend_slot(pieces):
    query_feat, key_feat, values, crop, keymask = pieces
    length, heads, head_width = query_feat.shape
    start = (
        jnp.zeros((heads, head_width, head_width), jnp.float32),
        jnp.zeros((heads, head_width), jnp.float32),
        jnp.int32(-1),
    )
    finish, (mixed, denom, states, norms) = lax.scan(
        attend_forward,
        start,
        (
            split_blocks(query_feat),
            split_blocks(key_feat),
            split_blocks(values),
            split_blocks(crop),
            split_blocks(keymask),
        ),
    )
    return (mixed.reshape(length, heads, head_width), denom.reshape(length, heads), states, norms)


def attend_slot_back(pieces):
    query_feat, key_feat, values, crop, keymask, states, norms, grad_numer, grad_denom = pieces
    length, heads, head_width = query_feat.shape
    crop_blocks = split_blocks(crop)
    prev_crops = jnp.concatenate([jnp.full((1,), -1, jnp.int32), crop_blocks[:-1, -1]])
    start = (
        jnp.zeros((heads, head_width, head_width), jnp.float32),
        jnp.zeros((heads, head_width), jnp.float32),
    )
    finish, (grad_query, grad_key, grad_value) = lax.scan(
        attend_backward,
        start,
        (
            split_blocks(query_feat),
            split_blocks(key_feat),
            split_blocks(values),
            crop_blocks,
            split_blocks(keymask),
            prev_crops,
            states,
            norms,
            split_blocks(grad_numer),
            split_blocks(grad_denom),
        ),
        reverse=True,
    )
    shape = (length, heads, head_width)
    return (grad_query.reshape(shape), grad_key.reshape(shape), grad_value.reshape(shape))


def general_body(
    tokens,
    crop_ids,
    kv_mask,
    norm1_gain,
    norm1_bias,
    w_query,
    w_key,
    w_value,
    w_out,
    norm2_gain,
    norm2_bias,
    w_up,
    up_bias,
    w_down,
    down_bias,
    cotangent,
):
    slots, length, width = tokens.shape
    heads = HEADS
    head_width = width // heads
    count = slots * length
    devices = lax.axis_size("dp") * lax.axis_size("fsdp")
    dims = (OUTER, lax.axis_size("dp") // (2 * OUTER), lax.axis_size("fsdp"))
    unit = width // devices
    packed = jnp.concatenate([norm1_gain, norm1_bias, norm2_gain, norm2_bias, down_bias, up_bias])
    packed = jnp.pad(packed, (0, 16 * 128 - packed.shape[0])).reshape(16, 128)
    vectors, full_query, full_key, full_value, full_out, full_up, full_down = gather(
        dims, [packed, w_query, w_key, w_value, w_out, w_up, w_down], unit
    )
    vectors = vectors.reshape(devices, 16 * 128)
    gain_one, bias_one, gain_two, bias_two, full_down_bias = (
        vectors[:, index * unit : (index + 1) * unit].reshape(-1) for index in range(5)
    )
    full_up_bias = vectors[:, 5 * unit : 5 * unit + up_bias.shape[0]].reshape(-1)
    inputs = tokens.reshape(count, width).astype(jnp.float32)
    normed_wide, pull_one = jax.vjp(
        norm_affine, inputs, gain_one.astype(jnp.float32), bias_one.astype(jnp.float32)
    )
    normed = normed_wide.astype(jnp.bfloat16)
    query = jnp.dot(normed, full_query, preferred_element_type=jnp.float32)
    keys = jnp.dot(normed, full_key, preferred_element_type=jnp.float32)
    values = jnp.dot(normed, full_value, preferred_element_type=jnp.float32).astype(jnp.bfloat16)
    query_wide, pull_query = jax.vjp(feature, query)
    key_wide, pull_key = jax.vjp(feature, keys)
    query_feat = query_wide.astype(jnp.bfloat16).reshape(slots, length, heads, head_width)
    key_feat = key_wide.astype(jnp.bfloat16).reshape(slots, length, heads, head_width)
    value_heads = values.reshape(slots, length, heads, head_width)
    mixed_wide, denom, states, norms = lax.map(
        attend_slot, (query_feat, key_feat, value_heads, crop_ids, kv_mask)
    )
    mixed = mixed_wide.reshape(count, width).astype(jnp.bfloat16)
    middle = inputs + jnp.dot(mixed, full_out, preferred_element_type=jnp.float32)
    normed_two_wide, pull_two = jax.vjp(
        norm_affine, middle, gain_two.astype(jnp.float32), bias_two.astype(jnp.float32)
    )
    normed_two = normed_two_wide.astype(jnp.bfloat16)
    upper = jnp.dot(normed_two, full_up, preferred_element_type=jnp.float32) + full_up_bias.astype(
        jnp.float32
    )
    hidden_wide, pull_gelu = jax.vjp(gelu_exact, upper)
    hidden = hidden_wide.astype(jnp.bfloat16)
    result = (
        middle
        + jnp.dot(hidden, full_down, preferred_element_type=jnp.float32)
        + full_down_bias.astype(jnp.float32)
    )
    output = result.astype(jnp.bfloat16).reshape(slots, length, width)
    back_up, back_down = full_up, full_down
    back_query, back_key, back_value, back_out = full_query, full_key, full_value, full_out
    grad_out = cotangent.reshape(count, width)
    grad_down_bias = jnp.sum(grad_out.astype(jnp.float32), axis=0)
    grad_w_down = jnp.dot(hidden.T, grad_out, preferred_element_type=jnp.float32).astype(jnp.bfloat16)
    grad_hidden = jnp.dot(grad_out, back_down.T, preferred_element_type=jnp.float32)
    grad_upper = pull_gelu(grad_hidden)[0].astype(jnp.bfloat16)
    grad_up_bias = jnp.sum(grad_upper.astype(jnp.float32), axis=0)
    grad_w_up = jnp.dot(normed_two.T, grad_upper, preferred_element_type=jnp.float32).astype(jnp.bfloat16)
    grad_normed_two = jnp.dot(grad_upper, back_up.T, preferred_element_type=jnp.float32)
    grad_middle_part, grad_gain_two, grad_bias_two = pull_two(grad_normed_two)
    grad_middle = grad_out.astype(jnp.float32) + grad_middle_part
    grad_attended = grad_middle.astype(jnp.bfloat16)
    grad_w_out = jnp.dot(mixed.T, grad_attended, preferred_element_type=jnp.float32).astype(jnp.bfloat16)
    grad_mixed = jnp.dot(grad_attended, back_out.T, preferred_element_type=jnp.float32).reshape(
        slots, length, heads, head_width
    )
    grad_numer = grad_mixed / denom[..., None]
    grad_denom = -jnp.sum(grad_mixed * mixed_wide, axis=-1) / denom
    grad_query_feat, grad_key_feat, grad_values = lax.map(
        attend_slot_back,
        (
            query_feat,
            key_feat,
            value_heads,
            crop_ids,
            kv_mask,
            states,
            norms,
            grad_numer,
            grad_denom,
        ),
    )
    grad_query = pull_query(grad_query_feat.reshape(count, width))[0].astype(jnp.bfloat16)
    grad_keys = pull_key(grad_key_feat.reshape(count, width))[0].astype(jnp.bfloat16)
    grad_values = grad_values.reshape(count, width).astype(jnp.bfloat16)
    grad_w_query = jnp.dot(normed.T, grad_query, preferred_element_type=jnp.float32).astype(jnp.bfloat16)
    grad_w_key = jnp.dot(normed.T, grad_keys, preferred_element_type=jnp.float32).astype(jnp.bfloat16)
    grad_w_value = jnp.dot(normed.T, grad_values, preferred_element_type=jnp.float32).astype(jnp.bfloat16)
    grad_normed = jnp.dot(grad_query, back_query.T, preferred_element_type=jnp.float32)
    grad_normed = grad_normed + jnp.dot(grad_keys, back_key.T, preferred_element_type=jnp.float32)
    grad_normed = grad_normed + jnp.dot(
        grad_values, back_value.T, preferred_element_type=jnp.float32
    )
    grad_input_part, grad_gain_one, grad_bias_one = pull_one(grad_normed)
    small = jnp.concatenate(
        [
            vector.reshape(devices, -1)
            for vector in (
                grad_gain_one,
                grad_bias_one,
                grad_gain_two,
                grad_bias_two,
                grad_down_bias,
                grad_up_bias,
            )
        ],
        axis=1,
    )
    small = jnp.pad(small, ((0, 0), (0, 8 * 128 - small.shape[1]))).reshape(devices, 8, 128)
    small, own_up, own_down, own_query, own_key, own_value, own_out = scatter(
        dims,
        small,
        [grad_w_up, grad_w_down, grad_w_query, grad_w_key, grad_w_value, grad_w_out],
        unit,
    )
    small = small.reshape(8 * 128)
    own_gain_one, own_bias_one, own_gain_two, own_bias_two, own_down_bias = (
        small[index * unit : (index + 1) * unit] for index in range(5)
    )
    own_up_bias = small[5 * unit : 5 * unit + up_bias.shape[0]]
    input_grad = (grad_middle + grad_input_part).astype(jnp.bfloat16).reshape(slots, length, width)
    return (
        output,
        input_grad,
        own_gain_one,
        own_bias_one,
        own_query,
        own_key,
        own_value,
        own_out,
        own_gain_two,
        own_bias_two,
        own_up,
        own_up_bias,
        own_down,
        own_down_bias,
    )


LENGTH = 512
WIDTH = 1024
HIDDEN = 4096
UNIT = 32
GATHERED = 24
DOWN, UP = 8, 16
LAG = 2
AHEAD = 4
WIDE32 = jnp.float32
HALF16 = jnp.bfloat16
VMEM_LIMIT = 63 << 20


def when(condition):
    if isinstance(condition, bool):
        return (lambda work: work()) if condition else (lambda work: None)
    return pl.when(condition)


def each(count, work):
    def step(index, carry):
        work(index)
        return carry

    lax.fori_loop(0, count, step, 0)


def dot(left, right):
    return jnp.dot(left, right, preferred_element_type=jnp.float32)


def dot_nt(left, right):
    return lax.dot_general(
        left, right, (((1,), (1,)), ((), ())), preferred_element_type=jnp.float32
    )


def dot_tn(left, right):
    return lax.dot_general(
        left, right, (((0,), (0,)), ((), ())), preferred_element_type=jnp.float32
    )


def by_order(place, orders, index, work):
    turn = (index + 3 * place.at["c"]) % len(orders)
    for order in dict.fromkeys(orders):
        turns = [number for number, item in enumerate(orders) if item == order]
        match = turn == turns[0]
        for number in turns[1:]:
            match = match | (turn == number)

        @pl.when(match)
        def _(order=order):
            work(order)


class Mover:
    def __init__(self, place, send_sem, recv_sem):
        self.place, self.send_sem, self.recv_sem = place, send_sem, recv_sem

    def copy(self, lead, stage, step, axis, source, target):
        at = lead + (stage, step - 1)
        return pltpu.make_async_remote_copy(
            source,
            target,
            self.send_sem.at[at],
            self.recv_sem.at[at],
            device_id=self.place.device(axis, step),
            device_id_type=MESH,
        )


class Gather(Mover):
    def region(self, chunk, done, spot):
        lead = tuple(slice(None) if axis in done else spot[axis] for axis in "abcz")
        return chunk.at[lead]

    def send(self, chunk, lead, order, stage):
        axis, done = order[stage], order[:stage]
        source = self.region(chunk, done, self.place.at)
        for step in self.place.partners(axis):
            self.copy(lead, stage, step, axis, source, source).start()

    def receive(self, chunk, lead, order, stage):
        axis, done = order[stage], order[:stage]
        for step in self.place.partners(axis):
            spot = self.place.moved(axis, self.place.size[axis] - step)
            target = self.region(chunk, done, spot)
            self.copy(lead, stage, step, axis, target, target).wait_recv()

    def drain(self, chunk, lead, order):
        for stage in range(4):
            axis, done = order[stage], order[:stage]
            source = self.region(chunk, done, self.place.at)
            for step in self.place.partners(axis):
                self.copy(lead, stage, step, axis, source, source).wait_send()


class Weights(Gather):
    orders = ("zbac", "zabc", "bzac", "zbac", "zabc", "azbc")

    def __init__(self, place, buffer, send_sem, recv_sem):
        super().__init__(place, send_sem, recv_sem)
        self.buffer, self.total = buffer, buffer.shape[0]

    def by_order(self, index, work):
        by_order(self.place, self.orders, index, work)

    def begin(self, index):
        @when(index < self.total)
        def _():
            self.by_order(
                index, lambda order: self.send(self.buffer.at[index], (index,), order, 0)
            )

    def tick(self, now):
        self.begin(now + AHEAD)
        for stage in range(4):
            index = now - stage * LAG
            live = (index >= 0) & (index < self.total)

            @when(live)
            def _(index=index, stage=stage):
                def work(order):
                    chunk = self.buffer.at[index]
                    self.receive(chunk, (index,), order, stage)
                    if stage < 3:
                        self.send(chunk, (index,), order, stage + 1)

                self.by_order(index, work)

    def finish(self):
        each(
            self.total,
            lambda index: self.by_order(
                index, lambda order: self.drain(self.buffer.at[index], (index,), order)
            ),
        )


def moments(values):
    mean = jnp.mean(values, axis=-1, keepdims=True)
    centred = values - mean
    spread = jnp.mean(centred * centred, axis=-1, keepdims=True)
    scale = lax.rsqrt(spread + norm_eps)
    return centred * scale, scale


def gelu_pair(upper):
    bell = jnp.exp(-0.5 * upper * upper) * 0.3989422804014327
    below = 0.5 * (1.0 + lax.erf(upper * 0.7071067811865476))
    return upper * below, below + upper * bell


def matrix(buffer, index):
    return buffer[index].reshape(WIDTH, WIDE)


def column_of(row):
    tall = jnp.transpose(jnp.broadcast_to(row.astype(jnp.float32), (8, row.shape[1])))
    return tall[:, 0:1]


def read_vectors(gathered, devices):
    flat = gathered[...].reshape(devices * 8, 128).astype(jnp.bfloat16)

    def line(number):
        shape = (devices, devices * 8)
        wanted = lax.broadcasted_iota(jnp.int32, shape, 0) * 8 + number
        chosen = lax.broadcasted_iota(jnp.int32, shape, 1) == wanted
        return dot(chosen.astype(jnp.bfloat16), flat).astype(jnp.bfloat16)

    def spread(lines, start, wide):
        total = wide * devices
        lane = lax.broadcasted_iota(jnp.int32, (128, total), 1)
        wanted = lax.broadcasted_iota(jnp.int32, (128, total), 0) == start + lane % wide
        found = dot(lines, wanted.astype(jnp.bfloat16))
        owner = lax.broadcasted_iota(jnp.int32, (devices, total), 1) // wide
        mine = owner == lax.broadcasted_iota(jnp.int32, (devices, total), 0)
        return jnp.sum(jnp.where(mine, found, 0.0), axis=0, keepdims=True)

    first = line(0)
    rows = [spread(first, index * UNIT, UNIT) for index in range(4)]
    rows.append(spread(line(2), 0, UNIT))
    return rows, spread(line(1), 0, 4 * UNIT)


def write_vectors(rows, devices):
    result = None
    for index, row in enumerate(rows):
        owner = lax.broadcasted_iota(jnp.int32, (devices, WIDTH), 1) // UNIT
        mine = owner == lax.broadcasted_iota(jnp.int32, (devices, WIDTH), 0)
        spread = jnp.where(mine, row, 0.0)
        lane = lax.broadcasted_iota(jnp.int32, (WIDTH, 128), 0)
        wanted = lax.broadcasted_iota(jnp.int32, (WIDTH, 128), 1) == index * UNIT + lane % UNIT
        found = jnp.dot(
            spread,
            wanted.astype(jnp.float32),
            preferred_element_type=jnp.float32,
            precision=HIGH,
        )
        result = found if result is None else result + found
    return result


def head_lanes(which, shape):
    lane = lax.broadcasted_iota(jnp.int32, shape, 1)
    return lane < 64 if which == 0 else lane >= 64


def allowed(crop_row, mask_row):
    shape = (LENGTH, LENGTH)
    row = lax.broadcasted_iota(jnp.int32, shape, 0)
    column = lax.broadcasted_iota(jnp.int32, shape, 1)
    same = column_of(crop_row) == crop_row.astype(jnp.float32)
    seen = (mask_row > 0) | (row == column)
    return jnp.where(same & (column <= row) & seen, 1.0, 0.0).astype(jnp.bfloat16)


def allowed_back(crop_row, mask_row):
    shape = (LENGTH, LENGTH)
    row = lax.broadcasted_iota(jnp.int32, shape, 0)
    column = lax.broadcasted_iota(jnp.int32, shape, 1)
    same = column_of(crop_row) == crop_row.astype(jnp.float32)
    seen = (column_of(mask_row) > 0) | (row == column)
    return jnp.where(same & (row <= column) & seen, 1.0, 0.0).astype(jnp.bfloat16)


def transpose_into(source, target):
    def work(index):
        at = pl.ds(pl.multiple_of(index * 128, 128), 128)
        target[at, :] = jnp.transpose(source[:, at])

    each(source.shape[1] // 128, work)


def by_rows(work):
    each(LENGTH // 64, lambda index: work(pl.ds(pl.multiple_of(index * 64, 64), 64)))


def forward_heads(pair, qkv, mask, mixed, inverse, attended):
    chunk = pair // 4
    lanes = pl.ds(pl.multiple_of((pair % 4) * 128, 128), 128)
    columns = pl.ds(pl.multiple_of(pair * 128, 128), 128)
    for part in (0, 1):
        keys = 256 * (part + 1)
        rows = slice(part * 256, part * 256 + 256)
        query = qkv[chunk, rows, lanes]
        key = qkv[2 + chunk, 0:keys, lanes]
        value = qkv[4 + chunk, 0:keys, lanes]
        zero, one = jnp.zeros_like(key), jnp.ones_like(key)
        total = None
        for which in (0, 1):
            mine = head_lanes(which, key.shape)
            scores = dot_nt(query, jnp.where(mine, key, zero)).astype(jnp.bfloat16)
            scores = scores * mask[rows, 0:keys]
            right = jnp.concatenate(
                [jnp.where(mine, value, zero), jnp.where(mine, one, zero)], axis=1
            )
            term = dot(scores, right)
            total = term if total is None else total + term
        inverted = 1.0 / total[:, 128:]
        result = total[:, :128] * inverted
        mixed[rows, columns] = result
        inverse[rows, columns] = inverted
        attended[rows, columns] = result.astype(jnp.bfloat16)


def down_rows(dims, buffer, block, half):
    outer, inner, depth = dims
    at = (block // (2 * inner), (block // 2) % inner, block % 2)
    return jnp.concatenate(
        [
            buffer[(DOWN + 2 * group + half,) + at + (z,)]
            for z in range(depth)
            for group in range(4)
        ],
        axis=0,
    )


def feed_block(dims, block, refs):
    normed, normed_t, grad_out, weights, up_bias, result, grad_normed, to_up, to_down, grad_bias = refs
    up = matrix(weights, UP + block)
    upper = dot(normed[...], up) + up_bias[pl.ds(block, 1), :]
    hidden, slope = gelu_pair(upper)
    hidden = hidden.astype(jnp.bfloat16)
    grad_hidden = None
    for half in (0, 1):
        columns = slice(half * WIDE, half * WIDE + WIDE)
        down = down_rows(dims, weights, block, half)
        result[:, columns] += dot(hidden, down)
        term = dot_nt(grad_out[:, columns], down)
        grad_hidden = term if grad_hidden is None else grad_hidden + term
    grad_upper = (grad_hidden * slope).astype(jnp.bfloat16)
    grad_bias[pl.ds(block, 1), :] = jnp.sum(
        grad_upper.astype(jnp.float32), axis=0, keepdims=True
    )
    grad_normed[...] += dot_nt(grad_upper, up)
    to_up[...] = dot(normed_t[...], grad_upper).astype(jnp.bfloat16).reshape(to_up.shape)
    for half in (0, 1):
        columns = slice(half * WIDE, half * WIDE + WIDE)
        term = dot_tn(hidden, grad_out[:, columns]).astype(jnp.bfloat16)
        for z in range(dims[2]):
            for group in range(4):
                start = (z * 4 + group) * UNIT
                to_down[2 * group + half, z] = term[start : start + UNIT]


def forward_kernel(dims, *refs):
    (
        crops,
        kept,
        gain_one,
        bias_one,
        gain_two,
        bias_two,
        bias_down,
        bias_up,
        tokens_in,
        grad_out_in,
    ) = refs[:10]
    shards = refs[10:16]
    (
        grad_up_bias,
        rows,
        qkv_out,
        mixed_out,
        inverse_out,
        attended_t_out,
        normed_t_out,
        middle_out,
        result_out,
        grad_normed_out,
        attention_out,
        terms,
    ) = refs[16:28]
    (
        tokens,
        grad_out,
        weights,
        vectors,
        up_bias,
        mask,
        qkv,
        mixed,
        inverse,
        attended,
        attended_t,
        normed,
        normed_t,
        middle,
        normed_two,
        normed_two_t,
        result,
        grad_normed,
        to_up,
        to_down,
        send_sem,
        recv_sem,
        vector_send_sem,
        vector_recv_sem,
        load_sem,
        store_sem,
        up_sem,
        down_sem,
    ) = refs[28:]
    outer, inner, depth = dims
    devices = 2 * outer * inner * depth
    place = Place(dims)
    spot = (place.at["a"], place.at["b"], place.at["c"], place.at["z"])

    loads = []
    for index in range(GATHERED):
        if index < DOWN:
            source = shards[index // 2].at[:, pl.ds((index % 2) * WIDE, WIDE)]
        elif index < UP:
            group, half = (index - DOWN) // 2, (index - DOWN) % 2
            source = shards[5].at[pl.ds(group * UNIT, UNIT), pl.ds(half * WIDE, WIDE)]
        else:
            source = shards[4].at[:, pl.ds((index - UP) * WIDE, WIDE)]
        item = pltpu.make_async_copy(source, weights.at[(index,) + spot], load_sem.at[index])
        item.start()
        loads.append(item)
    for index, (source, target) in enumerate(((tokens_in, tokens), (grad_out_in, grad_out))):
        item = pltpu.make_async_copy(source, target, load_sem.at[GATHERED + index])
        item.start()
        loads.append(item)

    small = Gather(place, vector_send_sem, vector_recv_sem)
    order = "zbac"
    lines = [
        jnp.concatenate([item[...] for item in (gain_one, bias_one, gain_two, bias_two)], axis=1),
        bias_up[...],
        jnp.concatenate([bias_down[...], jnp.zeros((1, 128 - UNIT), jnp.bfloat16)], axis=1),
    ]
    packed = jnp.concatenate(
        [line.astype(jnp.float32) for line in lines] + [jnp.zeros((5, 128), jnp.float32)], axis=0
    )
    vectors[spot] = packed
    place.greet()
    small.send(vectors, (), order, 0)
    gather_all = Weights(place, weights, send_sem, recv_sem)
    for index in range(AHEAD):
        loads[index].wait()
        gather_all.begin(index)
    for item in loads[AHEAD:]:
        item.wait()
    mask[...] = allowed(crops[...], kept[...])
    for stage in range(4):
        small.receive(vectors, (), order, stage)
        if stage < 3:
            small.send(vectors, (), order, stage + 1)
            gather_all.tick(stage)
    width_rows, up_row = read_vectors(vectors, devices)
    for index, row in enumerate(width_rows):
        rows[index : index + 1, :] = row
    rows[5:8, :] = jnp.zeros((3, WIDTH), jnp.float32)
    for index in range(8):
        up_bias[index : index + 1, :] = up_row[:, index * WIDE : (index + 1) * WIDE]

    def first_norm(at):
        unit, _ = moments(tokens[at, :].astype(jnp.float32))
        normed[at, :] = (unit * rows[0:1, :] + rows[1:2, :]).astype(jnp.bfloat16)

    by_rows(first_norm)
    stores = []

    def store(source, target):
        item = pltpu.make_async_copy(source, target, store_sem.at[len(stores)])
        item.start()
        stores.append(item)

    transpose_into(normed, normed_t)
    store(normed_t, normed_t_out)
    for now in range(3, 6):
        gather_all.tick(now)

    def project(index):
        gather_all.tick(6 + index)
        value = dot(normed[...], matrix(weights, index))
        mapped = jnp.where(value > 0, value + 1.0, jnp.exp(jnp.minimum(value, 0.0)))
        qkv[index] = jnp.where(index < 4, mapped, value).astype(jnp.bfloat16)

    each(6, project)
    store(qkv, qkv_out)

    def heads(pair):
        gather_all.tick(12 + pair)
        forward_heads(pair, qkv, mask, mixed, inverse, attended)

    each(8, heads)
    store(mixed, mixed_out)
    store(inverse, inverse_out)
    store(weights.at[pl.ds(0, DOWN)], attention_out)
    gather_all.tick(20)
    for half in (0, 1):
        columns = slice(half * WIDE, half * WIDE + WIDE)
        middle[:, columns] = tokens[:, columns].astype(jnp.float32) + dot(
            attended[...], matrix(weights, 6 + half)
        )
    transpose_into(attended, attended_t)
    store(attended_t, attended_t_out)
    gather_all.tick(21)

    def second_norm(at):
        value = middle[at, :]
        unit, _ = moments(value)
        normed_two[at, :] = (unit * rows[2:3, :] + rows[3:4, :]).astype(jnp.bfloat16)
        result[at, :] = value + rows[4:5, :]
        grad_normed[at, :] = jnp.zeros((64, WIDTH), jnp.float32)

    by_rows(second_norm)
    store(middle, middle_out)
    transpose_into(normed_two, normed_two_t)

    def leave(block):
        slot = block % 2
        owner = (block // (2 * inner), (block // 2) % inner, block % 2)
        return (
            pltpu.make_async_copy(to_up.at[slot], terms.at[8 + block], up_sem.at[slot]),
            pltpu.make_async_copy(
                to_down.at[slot], terms.at[(pl.ds(0, 8),) + owner], down_sem.at[slot]
            ),
        )

    def feed(block):
        gather_all.tick(22 + block)

        @pl.when(block >= 2)
        def _():
            for item in leave(block - 2):
                item.wait()

        feed_block(
            dims,
            block,
            (
                normed_two,
                normed_two_t,
                grad_out,
                weights,
                up_bias,
                result,
                grad_normed,
                to_up.at[block % 2],
                to_down.at[block % 2],
                grad_up_bias,
            ),
        )
        for item in leave(block):
            item.start()

    each(8, feed)

    store(result, result_out)
    store(grad_normed, grad_normed_out)
    for block in (6, 7):
        for item in leave(block):
            item.wait()
    small.drain(vectors, (), order)
    gather_all.finish()
    for item in stores:
        item.wait()


def forward(dims, tokens, cotangent, crops, kept, small, shards):
    outer, inner, depth = dims
    most = max(dims) - 1
    lead = (outer, inner, 2, depth)
    tile = (UNIT, WIDE)
    whole = (LENGTH, WIDTH)
    f32, bf16 = jnp.float32, jnp.bfloat16
    shape = jax.ShapeDtypeStruct
    vmem, anywhere = pl.BlockSpec(memory_space=pltpu.VMEM), pl.BlockSpec(memory_space=pl.ANY)
    return pl.pallas_call(
        functools.partial(forward_kernel, dims),
        out_shape=[
            shape((8, WIDE), f32),
            shape((8, WIDTH), f32),
            shape((6, LENGTH, WIDE), bf16),
            shape(whole, f32),
            shape(whole, f32),
            shape((WIDTH, LENGTH), bf16),
            shape((WIDTH, LENGTH), bf16),
            shape(whole, f32),
            shape(whole, f32),
            shape(whole, f32),
            shape((DOWN,) + lead + tile, bf16),
            shape((16,) + lead + tile, bf16),
        ],
        in_specs=[vmem] * 8 + [anywhere] * 8,
        out_specs=[vmem] * 2 + [anywhere] * 10,
        scratch_shapes=[
            pltpu.VMEM(whole, bf16),
            pltpu.VMEM(whole, bf16),
            pltpu.VMEM((GATHERED,) + lead + tile, bf16),
            pltpu.VMEM(lead + (8, 128), f32),
            pltpu.VMEM((8, WIDE), f32),
            pltpu.VMEM((LENGTH, LENGTH), bf16),
            pltpu.VMEM((6, LENGTH, WIDE), bf16),
            pltpu.VMEM(whole, f32),
            pltpu.VMEM(whole, f32),
            pltpu.VMEM(whole, bf16),
            pltpu.VMEM((WIDTH, LENGTH), bf16),
            pltpu.VMEM(whole, bf16),
            pltpu.VMEM((WIDTH, LENGTH), bf16),
            pltpu.VMEM(whole, f32),
            pltpu.VMEM(whole, bf16),
            pltpu.VMEM((WIDTH, LENGTH), bf16),
            pltpu.VMEM(whole, f32),
            pltpu.VMEM(whole, f32),
            pltpu.VMEM((2,) + lead + tile, bf16),
            pltpu.VMEM((2, 8, depth) + tile, bf16),
            pltpu.SemaphoreType.DMA((GATHERED, 4, most)),
            pltpu.SemaphoreType.DMA((GATHERED, 4, most)),
            pltpu.SemaphoreType.DMA((4, most)),
            pltpu.SemaphoreType.DMA((4, most)),
            pltpu.SemaphoreType.DMA((GATHERED + 2,)),
            pltpu.SemaphoreType.DMA((9,)),
            pltpu.SemaphoreType.DMA((2,)),
            pltpu.SemaphoreType.DMA((2,)),
        ],
        compiler_params=pltpu.CompilerParams(
            collective_id=0, has_side_effects=True, vmem_limit_bytes=VMEM_LIMIT
        ),
        name="forward",
    )(crops, kept, *small, tokens, cotangent, *shards)


class Sums(Mover):
    def start(self, lead, stage, step, axis, source, target):
        self.copy(lead, stage, step, axis, source, target).start()

    def region(self, order, stage, where):
        at = {axis: self.place.at[axis] for axis in order[:stage]}
        at[order[stage]] = where
        return tuple(at.get(axis, slice(None)) for axis in "abz")

    def blocks(self, order, stage, where):
        rest = [axis for axis in "abz" if axis in order[stage + 1 :]]
        base = self.region(order, stage, where)
        sizes = [self.place.size[axis] for axis in rest]
        for inner in itertools.product(*(range(size) for size in sizes)):
            place = dict(zip(rest, inner))
            yield (
                tuple(place.get(axis, item) for axis, item in zip("abz", base)),
                inner,
            )

    def room(self, order, stage, rooms, step):
        if stage == 0:
            return rooms[0]
        if stage == 1:
            size = self.place.size[order[2]]
            return rooms[1].at[pl.ds((step - 1) * size, size)]
        return rooms[2].at[step - 1]

    def send_stage(self, lead, order, stage, total, rooms, add):
        axis = order[stage]
        for step in self.place.partners(axis):
            where = self.place.moved(axis, step)[axis]
            for at, _ in self.blocks(order, stage, where):
                add(at)
            source = total.at[self.region(order, stage, where)]
            room = self.room(order, stage, rooms, step)
            self.start(lead, stage + 1, step, axis, source, room)
        for at, _ in self.blocks(order, stage, self.place.at[axis]):
            add(at)

    def await_stage(self, lead, order, stage, rooms):
        axis = order[stage]
        for step in self.place.partners(axis):
            room = self.room(order, stage, rooms, step)
            self.copy(lead, stage + 1, step, axis, room, room).wait_recv()

    def after_core(self, lead, order, own, total, rooms):
        def add(at):
            total[at] = own[at] + total[at]

        self.send_stage(lead, order, 0, total, rooms, add)

    def came_in(self, order, stage, total, rooms, at):
        rest = [axis for axis in "abz" if axis in order[stage + 1 :]]
        inner = tuple(item for axis, item in zip("abz", at) if axis in rest)
        value = total[at].astype(jnp.float32)
        for step in self.place.partners(order[stage]):
            room = self.room(order, stage, rooms, step)
            value = value + (room[inner] if inner else room[...]).astype(jnp.float32)
        return value

    def after_stage(self, lead, order, stage, total, rooms):
        self.await_stage(lead, order, stage - 1, rooms)

        def add(at):
            total[at] = self.came_in(order, stage - 1, total, rooms, at).astype(total.dtype)

        self.send_stage(lead, order, stage, total, rooms, add)

    def after_last(self, lead, order, total, rooms):
        self.await_stage(lead, order, 2, rooms)
        at = tuple(self.place.at[axis] for axis in "abz")
        return self.came_in(order, 2, total, rooms, at)

    def drain(self, lead, order, total, rooms):
        self.copy(lead, 0, 1, "c", total, total).wait_send()
        for stage in range(3):
            axis = order[stage]
            for step in self.place.partners(axis):
                room = self.room(order, stage, rooms, step)
                self.copy(lead, stage + 1, step, axis, room, room).wait_send()


class Gradients(Sums):
    orders = ("abz", "baz", "azb", "abz", "baz", "bza")

    def __init__(self, place, terms, total, rooms, results, ring, ring_sem, send_sem, recv_sem):
        super().__init__(place, send_sem, recv_sem)
        self.terms, self.sums, self.rooms, self.results = terms, total, rooms, results
        self.ring, self.ring_sem = ring, ring_sem
        self.total = results.shape[0]
        self.first = terms[0].shape[0]

    def by_order(self, index, work):
        rooms = [room.at[index] for room in self.rooms]
        total = self.sums.at[index]
        by_order(self.place, self.orders, index, lambda order: work(order, total, rooms))

    def begin(self, index):
        side = self.place.at["c"]
        slot = index % (AHEAD + 1)

        def go(source):
            self.start((index,), 0, 1, "c", source.at[:, :, 1 - side], self.sums.at[index])
            pltpu.make_async_copy(
                source.at[:, :, side], self.ring.at[slot], self.ring_sem.at[slot]
            ).start()

        @when(index < self.first)
        def _():
            go(self.terms[0].at[index])

        @when((index >= self.first) & (index < self.total))
        def _():
            go(self.terms[1].at[index - self.first])

    def tick(self, now):
        self.begin(now + AHEAD)

        def live(index):
            return (index >= 0) & (index < self.total)

        @when(live(now))
        def _():
            slot = now % (AHEAD + 1)
            own = self.ring.at[slot]
            pltpu.make_async_copy(own, own, self.ring_sem.at[slot]).wait()
            total = self.sums.at[now]
            self.copy((now,), 0, 1, "c", total, total).wait_recv()
            self.by_order(
                now,
                lambda order, total, rooms: self.after_core((now,), order, own, total, rooms),
            )

        for stage in (1, 2):
            index = now - stage * LAG

            @when(live(index))
            def _(index=index, stage=stage):
                self.by_order(
                    index,
                    lambda order, total, rooms: self.after_stage(
                        (index,), order, stage, total, rooms
                    ),
                )

        index = now - 3 * LAG

        @when(live(index))
        def _():
            def work(order, total, rooms):
                self.results[index] = self.after_last((index,), order, total, rooms)

            self.by_order(index, work)

    def finish(self):
        def work(index):
            self.by_order(
                index,
                lambda order, total, rooms: self.drain((index,), order, total, rooms),
            )

        each(self.total, work)


def backward_heads(pair, qkv, mask, mask_t, mixed, inverse, grad_mixed):
    chunk = pair // 4
    lanes = pl.ds(pl.multiple_of((pair % 4) * 128, 128), 128)
    columns = pl.ds(pl.multiple_of(pair * 128, 128), 128)
    query = qkv[chunk, :, lanes]
    key = qkv[2 + chunk, :, lanes]
    value = qkv[4 + chunk, :, lanes]
    grad_numer = (grad_mixed[:, columns] * inverse[:, columns]).astype(jnp.bfloat16)
    part = grad_numer.astype(jnp.float32) * mixed[:, columns]
    high = part.astype(jnp.bfloat16)
    low = pltpu.roll(part - high.astype(jnp.float32), 64, 1).astype(jnp.bfloat16)
    zero, minus = jnp.zeros_like(query), jnp.full_like(query, -1.0)
    heads = []
    for which in (0, 1):
        mine = head_lanes(which, query.shape)
        heads.append(
            (
                jnp.concatenate([grad_numer, jnp.where(mine, high, low)], axis=1),
                jnp.concatenate([jnp.where(mine, value, zero), minus], axis=1),
                jnp.where(mine, query, zero),
                jnp.where(mine, key, zero),
                jnp.where(mine, grad_numer, zero),
            )
        )
    for part in (0, 1):
        keys = 256 * (part + 1)
        rows = slice(part * 256, part * 256 + 256)
        total = None
        for left, right, _, own_key, _ in heads:
            grad_scores = dot_nt(left[rows], right[:keys]).astype(jnp.bfloat16)
            term = dot(grad_scores * mask[rows, 0:keys], own_key[:keys])
            total = term if total is None else total + term
        slope = jnp.minimum(query[rows].astype(jnp.float32), 1.0)
        qkv[chunk, rows, lanes] = (total * slope).astype(jnp.bfloat16)
    for part in (0, 1):
        start = part * 256
        rows = slice(start, start + 256)
        grad_key = grad_value = None
        for left, right, own_query, own_key, own_grad in heads:
            seen = mask_t[rows, start:LENGTH]
            scores = dot_nt(own_key[rows], query[start:]).astype(jnp.bfloat16) * seen
            grad_scores = dot_nt(right[rows], left[start:]).astype(jnp.bfloat16) * seen
            term = dot(scores, own_grad[start:])
            grad_value = term if grad_value is None else grad_value + term
            term = dot(grad_scores, own_query[start:])
            grad_key = term if grad_key is None else grad_key + term
        slope = jnp.minimum(key[rows].astype(jnp.float32), 1.0)
        qkv[2 + chunk, rows, lanes] = (grad_key * slope).astype(jnp.bfloat16)
        qkv[4 + chunk, rows, lanes] = grad_value.astype(jnp.bfloat16)


def backward_kernel(dims, *refs):
    crops, kept, grad_up_bias, rows = refs[:4]
    tokens_in, grad_out_in, qkv_in, mixed_in, inverse_in, attended_t_in, normed_t_in = refs[4:11]
    middle_in, result_in, grad_normed_in, attention_in, terms = refs[11:16]
    output, input_grad, owned, owned_small, attention_terms = refs[16:21]
    (
        tokens,
        weights,
        mask,
        mask_t,
        grad_attended,
        grad_mixed,
        qkv,
        turned,
        mixed,
        inverse,
        grad_middle,
        sums,
        staged,
        small,
        ring,
        total,
        rooms_one,
        rooms_two,
        rooms_three,
        side_total,
        side_one,
        side_two,
        side_three,
        load_sem,
        stage_sem,
        ring_sem,
        send_sem,
        recv_sem,
        side_send_sem,
        side_recv_sem,
    ) = refs[21:]
    outer, inner, depth = dims
    devices = 2 * outer * inner * depth
    place = Place(dims)
    spot = place.at
    loads = {}

    def load(name, source, target):
        item = pltpu.make_async_copy(source, target, load_sem.at[len(loads)])
        item.start()
        loads[name] = item

    load("grad_normed", grad_normed_in, inverse)
    load("middle", middle_in, mixed)
    load("grad_out", grad_out_in, grad_attended)
    load("result", result_in, grad_mixed)
    adder = Gradients(
        place,
        (terms, attention_terms),
        total,
        (rooms_one, rooms_two, rooms_three),
        owned,
        ring,
        ring_sem,
        send_sem,
        recv_sem,
    )
    place.greet()
    for index in range(AHEAD):
        adder.begin(index)
    load("out", attention_in.at[pl.ds(6, 2)], weights.at[pl.ds(6, 2)])
    load("attended", attended_t_in, turned.at[0])
    load("qkv", qkv_in, qkv)
    load("normed", normed_t_in, turned.at[1])
    load("rest", attention_in.at[pl.ds(0, 6)], weights.at[pl.ds(0, 6)])
    load("tokens", tokens_in, tokens)
    adder.tick(0)
    mask[...] = allowed(crops[...], kept[...])
    mask_t[...] = allowed_back(crops[...], kept[...])
    sums[...] = jnp.zeros(sums.shape, jnp.float32)
    for name in ("grad_normed", "middle", "grad_out", "result"):
        loads[name].wait()

    def close_branch(at):
        unit, scale = moments(mixed[at, :])
        grad = grad_attended[at, :].astype(jnp.float32)
        value = inverse[at, :]
        input_grad[at, :] = grad_mixed[at, :].astype(jnp.bfloat16)
        sums[0:1, :] += jnp.sum(value * unit, axis=0, keepdims=True)
        sums[1:2, :] += jnp.sum(value, axis=0, keepdims=True)
        sums[2:3, :] += jnp.sum(grad, axis=0, keepdims=True)
        scaled = value * rows[2:3, :]
        summed = grad + scale * (
            scaled
            - jnp.mean(scaled, axis=-1, keepdims=True)
            - unit * jnp.mean(scaled * unit, axis=-1, keepdims=True)
        )
        grad_middle[at, :] = summed
        grad_attended[at, :] = summed.astype(jnp.bfloat16)

    adder.tick(1)
    by_rows(close_branch)
    load("mixed", mixed_in, mixed)
    load("inverse", inverse_in, inverse)
    load("output", input_grad, output)
    adder.tick(2)
    loads["out"].wait()
    grad_mixed[...] = dot_nt(grad_attended[:, 0:WIDE], matrix(weights, 6)) + dot_nt(
        grad_attended[:, WIDE:WIDTH], matrix(weights, 7)
    )
    adder.tick(3)
    loads["attended"].wait()
    for half in (0, 1):
        columns = slice(half * WIDE, half * WIDE + WIDE)
        value = dot(turned[0], grad_attended[:, columns]).astype(jnp.bfloat16)
        staged[half] = value.reshape(staged.shape[1:])
        pltpu.make_async_copy(
            staged.at[half], attention_terms.at[half], stage_sem.at[half]
        ).start()
    for name in ("qkv", "mixed", "inverse"):
        loads[name].wait()

    loads["output"].wait()

    def heads(pair):
        adder.tick(4 + pair)
        backward_heads(pair, qkv, mask, mask_t, mixed, inverse, grad_mixed)

    each(8, heads)
    loads["normed"].wait()
    loads["rest"].wait()
    grad_normed = grad_mixed
    grad_normed[...] = jnp.zeros(grad_normed.shape, jnp.float32)

    def stage_copy(index):
        slot = index % 2
        return pltpu.make_async_copy(
            staged.at[slot], attention_terms.at[2 + index], stage_sem.at[slot]
        )

    for half in (0, 1):
        pltpu.make_async_copy(
            staged.at[half], attention_terms.at[half], stage_sem.at[half]
        ).wait()

    def project(index):
        @pl.when(index >= 2)
        def _():
            stage_copy(index - 2).wait()

        value = dot(turned[1], qkv[index]).astype(jnp.bfloat16)
        staged[index % 2] = value.reshape(staged.shape[1:])
        stage_copy(index).start()
        grad_normed[...] += dot_nt(qkv[index], matrix(weights, index))

        @pl.when(index < 4)
        def _():
            adder.tick(12 + index)

    each(6, project)
    for index in (4, 5):
        stage_copy(index).wait()
    adder.tick(16)
    loads["tokens"].wait()

    def close(at):
        unit, scale = moments(tokens[at, :].astype(jnp.float32))
        value = grad_normed[at, :]
        sums[3:4, :] += jnp.sum(value * unit, axis=0, keepdims=True)
        sums[4:5, :] += jnp.sum(value, axis=0, keepdims=True)
        scaled = value * rows[0:1, :]
        input_grad[at, :] = (
            grad_middle[at, :]
            + scale
            * (
                scaled
                - jnp.mean(scaled, axis=-1, keepdims=True)
                - unit * jnp.mean(scaled * unit, axis=-1, keepdims=True)
            )
        ).astype(jnp.bfloat16)

    by_rows(close)
    order = [sums[index : index + 1, :] for index in (3, 4, 0, 1)]
    first = write_vectors(order, devices)
    third = write_vectors([sums[2:3, :]], devices)
    for device in range(devices):
        at = (
            device // (2 * inner * depth),
            (device // (2 * depth)) % inner,
            (device // depth) % 2,
            device % depth,
        )
        block, lane = device // 4, (device % 4) * 128
        small[at + (slice(0, 1),)] = first[device : device + 1, :]
        small[at + (slice(1, 2),)] = grad_up_bias[block : block + 1, lane : lane + 128]
        small[at + (slice(2, 3),)] = third[device : device + 1, :]
        small[at + (slice(3, 8),)] = jnp.zeros((5, 128), jnp.float32)
    side = Sums(place, side_send_sem, side_recv_sem)
    rooms = (side_one, side_two, side_three)
    side.start((), 0, 1, "c", small.at[:, :, 1 - spot["c"]], side_total)

    def last_ticks(step):
        adder.tick(17 + step)

        @pl.when(step == 0)
        def _():
            side.copy((), 0, 1, "c", side_total, side_total).wait_recv()
            side.after_core((), "abz", small.at[:, :, spot["c"]], side_total, rooms)

        for stage in (1, 2):

            @pl.when(step == stage)
            def _(stage=stage):
                side.after_stage((), "abz", stage, side_total, rooms)

        @pl.when(step == 3)
        def _():
            owned_small[...] = side.after_last((), "abz", side_total, rooms)

    each(GATHERED + 3 * LAG - 17, last_ticks)
    side.drain((), "abz", side_total, rooms)
    adder.finish()


def backward(dims, crops, kept, grad_up_bias, rows, arrays):
    outer, inner, depth = dims
    most = max(dims) - 1
    lead = (outer, inner, 2, depth)
    tile = (UNIT, WIDE)
    whole = (LENGTH, WIDTH)
    f32, bf16 = jnp.float32, jnp.bfloat16
    shape = jax.ShapeDtypeStruct
    vmem, anywhere = pl.BlockSpec(memory_space=pltpu.VMEM), pl.BlockSpec(memory_space=pl.ANY)
    chip = (outer, inner, depth)
    small_tile = (8, 128)
    return pl.pallas_call(
        functools.partial(backward_kernel, dims),
        out_shape=[
            shape(whole, bf16),
            shape(whole, bf16),
            shape((GATHERED,) + tile, f32),
            shape(small_tile, f32),
            shape((8,) + lead + tile, bf16),
        ],
        in_specs=[vmem] * 4 + [anywhere] * 12,
        out_specs=[anywhere] + [vmem] * 3 + [anywhere],
        scratch_shapes=[
            pltpu.VMEM(whole, bf16),
            pltpu.VMEM((8,) + lead + tile, bf16),
            pltpu.VMEM((LENGTH, LENGTH), bf16),
            pltpu.VMEM((LENGTH, LENGTH), bf16),
            pltpu.VMEM(whole, bf16),
            pltpu.VMEM(whole, f32),
            pltpu.VMEM((6, LENGTH, WIDE), bf16),
            pltpu.VMEM((2, WIDTH, LENGTH), bf16),
            pltpu.VMEM(whole, f32),
            pltpu.VMEM(whole, f32),
            pltpu.VMEM(whole, f32),
            pltpu.VMEM((8, WIDTH), f32),
            pltpu.VMEM((2,) + lead + tile, bf16),
            pltpu.VMEM(lead + small_tile, f32),
            pltpu.VMEM((AHEAD + 1,) + chip + tile, bf16),
            pltpu.VMEM((GATHERED,) + chip + tile, bf16),
            pltpu.VMEM((GATHERED, 2, 4) + tile, bf16),
            pltpu.VMEM((GATHERED, 6) + tile, bf16),
            pltpu.VMEM((GATHERED, 3) + tile, bf16),
            pltpu.VMEM(chip + small_tile, f32),
            pltpu.VMEM((2, 4) + small_tile, f32),
            pltpu.VMEM((6,) + small_tile, f32),
            pltpu.VMEM((3,) + small_tile, f32),
            pltpu.SemaphoreType.DMA((13,)),
            pltpu.SemaphoreType.DMA((2,)),
            pltpu.SemaphoreType.DMA((AHEAD + 1,)),
            pltpu.SemaphoreType.DMA((GATHERED, 4, most)),
            pltpu.SemaphoreType.DMA((GATHERED, 4, most)),
            pltpu.SemaphoreType.DMA((4, most)),
            pltpu.SemaphoreType.DMA((4, most)),
        ],
        compiler_params=pltpu.CompilerParams(
            collective_id=1, has_side_effects=True, vmem_limit_bytes=VMEM_LIMIT
        ),
        name="backward",
    )(crops, kept, grad_up_bias, rows, *arrays)


def place_kernel(*refs):
    result, input_grad, owned, small = refs[:4]
    result_out, input_grad_out, query, key, value, out, up, down = refs[4:12]
    vectors, bias_up = refs[12:17], refs[17]
    sems = refs[18]
    copies = [(result, result_out.at[0]), (input_grad, input_grad_out.at[0])]
    for index in range(GATHERED):
        if index < 8:
            group, half = index // 2, index % 2
            target = down.at[pl.ds(group * UNIT, UNIT), pl.ds(half * WIDE, WIDE)]
        elif index < 16:
            target = up.at[:, pl.ds((index - 8) * WIDE, WIDE)]
        else:
            matrix_out = (out, query, key, value)[(index - 16) // 2]
            target = matrix_out.at[:, pl.ds((index % 2) * WIDE, WIDE)]
        copies.append((owned.at[index], target))
    items = [
        pltpu.make_async_copy(source, target, sems.at[index])
        for index, (source, target) in enumerate(copies)
    ]
    for item in items:
        item.start()
    for index in range(4):
        vectors[index][...] = small[0, index * UNIT : (index + 1) * UNIT]
    vectors[4][...] = small[2, 0:UNIT]
    bias_up[...] = small[1, :]
    for item in items:
        item.wait()


def place_results(result, input_grad, owned, small):
    f32, bf16 = jnp.float32, jnp.bfloat16
    shape = jax.ShapeDtypeStruct
    vmem, anywhere = pl.BlockSpec(memory_space=pltpu.VMEM), pl.BlockSpec(memory_space=pl.ANY)
    return pl.pallas_call(
        place_kernel,
        out_shape=[shape((1, LENGTH, WIDTH), bf16)] * 2
        + [shape((UNIT, WIDTH), f32)] * 4
        + [shape((UNIT, HIDDEN), f32), shape((4 * UNIT, WIDTH), f32)]
        + [shape((UNIT,), f32)] * 5
        + [shape((4 * UNIT,), f32)],
        in_specs=[anywhere] * 3 + [vmem],
        out_specs=[vmem] * 14,
        scratch_shapes=[pltpu.SemaphoreType.DMA((GATHERED + 2,))],
        name="results",
    )(result, input_grad, owned, small)


def body(
    tokens,
    crop_ids,
    kv_mask,
    norm1_gain,
    norm1_bias,
    w_query,
    w_key,
    w_value,
    w_out,
    norm2_gain,
    norm2_bias,
    w_up,
    up_bias,
    w_down,
    down_bias,
    cotangent,
):
    inner = lax.axis_size("dp") // (2 * OUTER)
    dims = (OUTER, inner, lax.axis_size("fsdp"))
    fits = (
        tokens.shape == (1, LENGTH, WIDTH)
        and w_up.shape == (UNIT, HIDDEN)
        and w_down.shape == (HIDDEN // WIDTH * UNIT, WIDTH)
        and dims == (2, 2, 4)
    )
    if not fits:
        return general_body(
            tokens,
            crop_ids,
            kv_mask,
            norm1_gain,
            norm1_bias,
            w_query,
            w_key,
            w_value,
            w_out,
            norm2_gain,
            norm2_bias,
            w_up,
            up_bias,
            w_down,
            down_bias,
            cotangent,
        )
    small = [
        vector.reshape(1, -1)
        for vector in (norm1_gain, norm1_bias, norm2_gain, norm2_bias, down_bias, up_bias)
    ]
    pixels, grads = tokens.reshape(LENGTH, WIDTH), cotangent.reshape(LENGTH, WIDTH)
    shards = (w_query, w_key, w_value, w_out, w_up, w_down)
    grad_up, rows, *arrays = forward(dims, pixels, grads, crop_ids, kv_mask, small, shards)
    result, input_grad, owned, owned_small, _ = backward(
        dims, crop_ids, kv_mask, grad_up, rows, (pixels, grads, *arrays)
    )
    (
        output,
        grad_tokens,
        grad_query,
        grad_key,
        grad_value,
        grad_out,
        grad_up,
        grad_down,
        grad_gain_one,
        grad_bias_one,
        grad_gain_two,
        grad_bias_two,
        grad_bias_down,
        grad_bias_up,
    ) = place_results(result, input_grad, owned, owned_small)
    return (
        output,
        grad_tokens,
        grad_gain_one,
        grad_bias_one,
        grad_query,
        grad_key,
        grad_value,
        grad_out,
        grad_gain_two,
        grad_bias_two,
        grad_up,
        grad_bias_up,
        grad_down,
        grad_bias_down,
    )


def solution(mesh):
    return jax.shard_map(
        body,
        mesh=mesh,
        in_specs=(
            P(("dp", "fsdp"), None, None),
            P(("dp", "fsdp"), None),
            P(("dp", "fsdp"), None),
            P(("dp", "fsdp")),
            P(("dp", "fsdp")),
            P(("dp", "fsdp"), None),
            P(("dp", "fsdp"), None),
            P(("dp", "fsdp"), None),
            P(("dp", "fsdp"), None),
            P(("dp", "fsdp")),
            P(("dp", "fsdp")),
            P(("dp", "fsdp"), None),
            P(("dp", "fsdp")),
            P(("dp", "fsdp"), None),
            P(("dp", "fsdp")),
            P(("dp", "fsdp"), None, None),
        ),
        out_specs=(
            P(("dp", "fsdp"), None, None),
            P(("dp", "fsdp"), None, None),
            P(("dp", "fsdp")),
            P(("dp", "fsdp")),
            P(("dp", "fsdp"), None),
            P(("dp", "fsdp"), None),
            P(("dp", "fsdp"), None),
            P(("dp", "fsdp"), None),
            P(("dp", "fsdp")),
            P(("dp", "fsdp")),
            P(("dp", "fsdp"), None),
            P(("dp", "fsdp")),
            P(("dp", "fsdp"), None),
            P(("dp", "fsdp")),
        ),
        check_vma=False,
    )
```

```python
import functools
import itertools

import jax
import jax.numpy as jnp
from jax import lax
from jax.experimental import pallas as pl
from jax.experimental.pallas import tpu as pltpu
from jax.sharding import PartitionSpec as P

HEADS = 16
BLOCK = 512
MESH = pl.DeviceIdType.MESH
WIDE = 512
OUTER = 2


class Place:
    def __init__(self, dims):
        self.size = {"a": dims[0], "b": dims[1], "c": 2, "z": dims[2]}
        dp = lax.axis_index("dp")
        self.at = {
            "a": dp // (2 * dims[1]),
            "b": (dp // 2) % dims[1],
            "c": dp % 2,
            "z": lax.axis_index("fsdp"),
        }

    def moved(self, axis, step):
        spot = dict(self.at)
        spot[axis] = (spot[axis] + step) % self.size[axis]
        return spot

    def device(self, axis, step):
        spot = self.moved(axis, step)
        return ((spot["a"] * self.size["b"] + spot["b"]) * 2 + spot["c"], spot["z"])

    def partners(self, axis):
        return range(1, self.size[axis])

    def greet(self):
        barrier = pltpu.get_barrier_semaphore()
        count = 0
        for axis in "abcz":
            for step in self.partners(axis):
                pl.semaphore_signal(
                    barrier, 1, device_id=self.device(axis, step), device_id_type=MESH
                )
                count += 1
        pl.semaphore_wait(barrier, count)


def pieces_of(rows, columns, unit):
    wide = min(WIDE, columns)
    return [
        (row, unit, column, wide)
        for row in range(0, rows, unit)
        for column in range(0, columns, wide)
    ]


def gather_kernel(dims, orders, lag, ahead, pieces, *refs):
    count = len(pieces)
    shards, wholes = refs[:count], refs[count : 2 * count]
    local_sem, send_sem, recv_sem = refs[2 * count :]
    place = Place(dims)
    place.greet()
    chunks = [
        (shard.at[pl.ds(ro, rn), pl.ds(co, cn)], whole, pl.ds(ro, rn), pl.ds(co, cn))
        for shard, whole, items in zip(shards, wholes, pieces)
        for ro, rn, co, cn in items
    ]
    total = len(chunks)
    sent, kept = [], []

    def region(index, done, spot):
        _, whole, rows, columns = chunks[index]
        lead = tuple(slice(None) if axis in done else spot[axis] for axis in "abcz")
        return whole.at[lead + (rows, columns)]

    def copy(index, stage, step, axis, source, target):
        return pltpu.make_async_remote_copy(
            source,
            target,
            send_sem.at[index, stage, step - 1],
            recv_sem.at[index, stage, step - 1],
            device_id=place.device(axis, step),
            device_id_type=MESH,
        )

    def send(index, stage):
        order = orders[index % len(orders)]
        axis, done = order[stage], order[:stage]
        target = region(index, done, place.at)
        for step in place.partners(axis):
            item = copy(index, stage, step, axis, target if done else chunks[index][0], target)
            item.start()
            sent.append(item)

    def receive(index, stage):
        order = orders[index % len(orders)]
        axis, done = order[stage], order[:stage]
        for step in place.partners(axis):
            target = region(index, done, place.moved(axis, place.size[axis] - step))
            copy(index, stage, step, axis, target, target).wait_recv()

    def begin(index):
        if index < total:
            item = pltpu.make_async_copy(
                chunks[index][0], region(index, "", place.at), local_sem.at[index]
            )
            item.start()
            kept.append(item)
            send(index, 0)

    for index in range(ahead):
        begin(index)
    for tick in range(total + 3 * lag):
        begin(tick + ahead)
        for stage in range(4):
            index = tick - stage * lag
            if 0 <= index < total:
                receive(index, stage)
                if stage == 0:
                    kept[index].wait()
                if stage < 3:
                    send(index, stage + 1)
    for item in sent:
        item.wait_send()


def gather(dims, shards, unit, lag=3, ahead=6):
    pieces = [pieces_of(*shard.shape, min(unit, shard.shape[0])) for shard in shards]
    total = sum(len(items) for items in pieces)
    most = max(dims) - 1
    anywhere = pl.BlockSpec(memory_space=pl.ANY)
    orders = ("zbac", "zabc", "zbac", "zabc", "bzac", "azbc")
    wholes = pl.pallas_call(
        functools.partial(gather_kernel, dims, orders, lag, ahead, pieces),
        out_shape=[
            jax.ShapeDtypeStruct(dims[:2] + (2, dims[2]) + shard.shape, shard.dtype)
            for shard in shards
        ],
        in_specs=[anywhere] * len(shards),
        out_specs=[anywhere] * len(shards),
        scratch_shapes=[
            pltpu.SemaphoreType.DMA((total,)),
            pltpu.SemaphoreType.DMA((total, 4, most)),
            pltpu.SemaphoreType.DMA((total, 4, most)),
        ],
        compiler_params=pltpu.CompilerParams(collective_id=0, has_side_effects=True),
        name="gather",
    )(*shards)
    return [whole.reshape((-1, whole.shape[-1])) for whole in wholes]


def scatter_kernel(dims, lag, ahead, pieces, *refs):
    count = len(pieces)
    terms, owned = refs[:count], refs[count : 2 * count]
    main = refs[2 * count : 2 * count + 7]
    side = refs[2 * count + 7 : 2 * count + 12]
    local_sem, send_sem, recv_sem = refs[2 * count + 12 :]
    place = Place(dims)
    place.greet()
    spot = place.at
    chunks = []
    for array, items in enumerate(pieces):
        for ro, rn, co, cn in items:
            index = len(chunks)
            if array == 0:
                rooms = side
                order = "ab"
            else:
                half = (index - 1) // 2
                order = "ab" if index % 2 else "ba"
                first, second = (main[2], main[4]) if index % 2 else (main[3], main[5])
                rooms = (
                    main[0].at[index - 1],
                    main[1].at[index - 1],
                    first.at[half],
                    second.at[half],
                    main[6].at[index - 1],
                )
            chunks.append((terms[array], owned[array], pl.ds(ro, rn), pl.ds(co, cn), order, rooms))
    total = len(chunks)
    sent, kept = [], []

    def copy(index, stage, step, axis, source, target):
        return pltpu.make_async_remote_copy(
            source,
            target,
            send_sem.at[index, stage, step - 1],
            recv_sem.at[index, stage, step - 1],
            device_id=place.device(axis, step),
            device_id_type=MESH,
        )

    def send(index, stage, step, axis, source, target):
        item = copy(index, stage, step, axis, source, target)
        item.start()
        sent.append(item)

    def begin(index):
        if index < total:
            term, _, rows, columns, _, rooms = chunks[index]
            send(index, 0, 1, "c", term.at[:, :, 1 - spot["c"], :, rows, columns], rooms[1])
            item = pltpu.make_async_copy(
                term.at[:, :, spot["c"], :, rows, columns], rooms[0], local_sem.at[index]
            )
            item.start()
            kept.append(item)

    def await_all(index, stage, axis, room):
        for step in place.partners(axis):
            copy(index, stage, step, axis, room.at[step - 1], room.at[step - 1]).wait_recv()

    def pick(order, first, second):
        return (first, second) if order == "ab" else (second, first)

    def after_core(index):
        order, (own, other, came, _, _) = chunks[index][4:]
        kept[index].wait()
        copy(index, 0, 1, "c", other, other).wait_recv()
        axis, rest = order

        def add(where):
            for item in range(place.size[rest]):
                at = pick(order, where, item)
                own[at] = own[at] + other[at]

        for step in place.partners(axis):
            where = place.moved(axis, step)[axis]
            add(where)
            source = own.at[where] if order == "ab" else own.at[:, where]
            send(index, 1, step, axis, source, came.at[step - 1])
        add(spot[axis])

    def after_first(index):
        order, (own, _, came, later, _) = chunks[index][4:]
        axis, rest = order
        await_all(index, 1, axis, came)

        def add(where):
            at = pick(order, spot[axis], where)
            value = own[at].astype(jnp.float32)
            for step in place.partners(axis):
                value = value + came[step - 1, where].astype(jnp.float32)
            own[at] = value.astype(own.dtype)

        for step in place.partners(rest):
            where = place.moved(rest, step)[rest]
            add(where)
            at = pick(order, spot[axis], where)
            send(index, 2, step, rest, own.at[at], later.at[step - 1])
        add(spot[rest])

    def after_second(index):
        _, result, rows, columns, order, (own, _, _, later, last) = chunks[index]
        rest = order[1]
        await_all(index, 2, rest, later)

        def add(where):
            value = own[spot["a"], spot["b"], where].astype(jnp.float32)
            for step in place.partners(rest):
                value = value + later[step - 1, where].astype(jnp.float32)
            return value

        for step in place.partners("z"):
            where = place.moved("z", step)["z"]
            own[spot["a"], spot["b"], where] = add(where).astype(own.dtype)
            send(index, 3, step, "z", own.at[spot["a"], spot["b"], where], last.at[step - 1])
        result[rows, columns] = add(spot["z"])

    def after_last(index):
        _, result, rows, columns, _, (_, _, _, _, last) = chunks[index]
        await_all(index, 3, "z", last)
        value = result[rows, columns]
        for step in place.partners("z"):
            value = value + last[step - 1].astype(jnp.float32)
        result[rows, columns] = value

    for index in range(ahead):
        begin(index)
    for tick in range(total + 3 * lag):
        begin(tick + ahead)
        for stage, work in enumerate((after_core, after_first, after_second, after_last)):
            index = tick - stage * lag
            if 0 <= index < total:
                work(index)
    for item in sent:
        item.wait_send()


def rooms_of(dims, many, unit, wide, dtype):
    outer, inner, depth = dims
    ones, twos = (many + 1) // 2, many // 2
    tail = (unit, wide)
    return [
        pltpu.VMEM((many, outer, inner, depth) + tail, dtype),
        pltpu.VMEM((many, outer, inner, depth) + tail, dtype),
        pltpu.VMEM((ones, outer - 1, inner, depth) + tail, dtype),
        pltpu.VMEM((twos, inner - 1, outer, depth) + tail, dtype),
        pltpu.VMEM((ones, inner - 1, depth) + tail, dtype),
        pltpu.VMEM((twos, outer - 1, depth) + tail, dtype),
        pltpu.VMEM((many, depth - 1) + tail, dtype),
    ]


def scatter(dims, small, terms, unit, lag=2, ahead=4):
    outer, inner, depth = dims
    devices = 2 * outer * inner * depth
    lead = (outer, inner, 2, depth)
    arrays = [small.reshape(lead + small.shape[1:])] + [
        term.reshape(lead + (term.shape[0] // devices, term.shape[1])) for term in terms
    ]
    pieces = [pieces_of(*arrays[0].shape[4:], arrays[0].shape[4])]
    pieces += [pieces_of(*array.shape[4:], unit) for array in arrays[1:]]
    total = sum(len(items) for items in pieces)
    most = max(dims) - 1
    tail = small.shape[1:]
    side = [
        pltpu.VMEM((outer, inner, depth) + tail, jnp.float32),
        pltpu.VMEM((outer, inner, depth) + tail, jnp.float32),
        pltpu.VMEM((outer - 1, inner, depth) + tail, jnp.float32),
        pltpu.VMEM((inner - 1, depth) + tail, jnp.float32),
        pltpu.VMEM((depth - 1,) + tail, jnp.float32),
    ]
    return pl.pallas_call(
        functools.partial(scatter_kernel, dims, lag, ahead, pieces),
        out_shape=[jax.ShapeDtypeStruct(array.shape[4:], jnp.float32) for array in arrays],
        in_specs=[pl.BlockSpec(memory_space=pl.ANY)] * len(arrays),
        out_specs=[pl.BlockSpec(memory_space=pltpu.VMEM)] * len(arrays),
        scratch_shapes=rooms_of(dims, total - 1, unit, WIDE, jnp.bfloat16)
        + side
        + [
            pltpu.SemaphoreType.DMA((total,)),
            pltpu.SemaphoreType.DMA((total, 4, most)),
            pltpu.SemaphoreType.DMA((total, 4, most)),
        ],
        compiler_params=pltpu.CompilerParams(
            collective_id=1, has_side_effects=True, vmem_limit_bytes=60 << 20
        ),
        name="scatter",
    )(*arrays)


HIGH = lax.Precision.HIGHEST
norm_eps = 1e-05


def norm_affine(values, gain, shift):
    mean = jnp.mean(values, axis=-1, keepdims=True)
    centred = values - mean
    spread = jnp.mean(centred * centred, axis=-1, keepdims=True)
    return centred * lax.rsqrt(spread + norm_eps) * gain + shift


def feature(values):
    return jax.nn.elu(values) + 1.0


def gelu_exact(values):
    return jax.nn.gelu(values, approximate=False)


def allowed_weight(crop, keymask):
    places = jnp.arange(crop.shape[0])
    earlier = places[None, :] <= places[:, None]
    same = crop[:, None] == crop[None, :]
    visible = (keymask[None, :] > 0) | (places[None, :] == places[:, None])
    return (earlier & same & visible).astype(jnp.float32)


def attend_forward(carry, pieces):
    state, norm_state, prev_crop = carry
    query_feat, key_feat, values, crop, keymask = pieces
    weight = allowed_weight(crop, keymask)
    scores = (
        jnp.einsum("ihe,jhe->hij", query_feat, key_feat, preferred_element_type=jnp.float32)
        * weight[None]
    )
    value_wide = values.astype(jnp.float32)
    query_wide = query_feat.astype(jnp.float32)
    key_wide = key_feat.astype(jnp.float32)
    numer = jnp.einsum("hij,jhe->ihe", scores, value_wide, precision=HIGH)
    denom = jnp.sum(scores, axis=2).T
    follows = (crop == prev_crop).astype(jnp.float32)
    numer = numer + follows[:, None, None] * jnp.einsum(
        "ihe,hef->ihf", query_wide, state, precision=HIGH
    )
    denom = denom + follows[:, None] * jnp.einsum(
        "ihe,he->ih", query_wide, norm_state, precision=HIGH
    )
    last_crop = crop[crop.shape[0] - 1]
    carried = (prev_crop == last_crop).astype(jnp.float32)
    select = ((crop == last_crop) & (keymask > 0)).astype(jnp.float32)
    chosen = key_wide * select[:, None, None]
    new_state = carried * state + jnp.einsum("jhe,jhf->hef", chosen, value_wide, precision=HIGH)
    new_norm = carried * norm_state + jnp.sum(chosen, axis=0)
    return ((new_state, new_norm, last_crop), (numer / denom[:, :, None], denom, state, norm_state))


def attend_backward(carry, pieces):
    grad_state, grad_norm = carry
    (
        query_feat,
        key_feat,
        values,
        crop,
        keymask,
        prev_crop,
        state,
        norm_state,
        grad_numer,
        grad_denom,
    ) = pieces
    weight = allowed_weight(crop, keymask)
    scores = (
        jnp.einsum("ihe,jhe->hij", query_feat, key_feat, preferred_element_type=jnp.float32)
        * weight[None]
    )
    value_wide = values.astype(jnp.float32)
    query_wide = query_feat.astype(jnp.float32)
    key_wide = key_feat.astype(jnp.float32)
    grad_scores = (
        jnp.einsum("ihe,jhe->hij", grad_numer, value_wide, precision=HIGH)
        + grad_denom.T[:, :, None]
    ) * weight[None]
    follows = (crop == prev_crop).astype(jnp.float32)
    last_crop = crop[crop.shape[0] - 1]
    carried = (prev_crop == last_crop).astype(jnp.float32)
    select = ((crop == last_crop) & (keymask > 0)).astype(jnp.float32)
    grad_query = jnp.einsum("hij,jhe->ihe", grad_scores, key_wide, precision=HIGH)
    grad_query = grad_query + follows[:, None, None] * (
        jnp.einsum("ihf,hef->ihe", grad_numer, state, precision=HIGH)
        + grad_denom[:, :, None] * norm_state[None]
    )
    grad_key = jnp.einsum("hij,ihe->jhe", grad_scores, query_wide, precision=HIGH)
    grad_key = grad_key + select[:, None, None] * (
        jnp.einsum("jhf,hef->jhe", value_wide, grad_state, precision=HIGH) + grad_norm[None]
    )
    grad_value = jnp.einsum("hij,ihe->jhe", scores, grad_numer, precision=HIGH)
    grad_value = grad_value + select[:, None, None] * jnp.einsum(
        "jhe,hef->jhf", key_wide, grad_state, precision=HIGH
    )
    query_kept = query_wide * follows[:, None, None]
    earlier_state = carried * grad_state + jnp.einsum(
        "ihe,ihf->hef", query_kept, grad_numer, precision=HIGH
    )
    earlier_norm = carried * grad_norm + jnp.einsum(
        "ihe,ih->he", query_kept, grad_denom, precision=HIGH
    )
    return ((earlier_state, earlier_norm), (grad_query, grad_key, grad_value))


def split_blocks(array):
    blocks = array.shape[0] // BLOCK
    return array.reshape((blocks, BLOCK) + array.shape[1:])


def attend_slot(pieces):
    query_feat, key_feat, values, crop, keymask = pieces
    length, heads, head_width = query_feat.shape
    start = (
        jnp.zeros((heads, head_width, head_width), jnp.float32),
        jnp.zeros((heads, head_width), jnp.float32),
        jnp.int32(-1),
    )
    finish, (mixed, denom, states, norms) = lax.scan(
        attend_forward,
        start,
        (
            split_blocks(query_feat),
            split_blocks(key_feat),
            split_blocks(values),
            split_blocks(crop),
            split_blocks(keymask),
        ),
    )
    return (mixed.reshape(length, heads, head_width), denom.reshape(length, heads), states, norms)


def attend_slot_back(pieces):
    query_feat, key_feat, values, crop, keymask, states, norms, grad_numer, grad_denom = pieces
    length, heads, head_width = query_feat.shape
    crop_blocks = split_blocks(crop)
    prev_crops = jnp.concatenate([jnp.full((1,), -1, jnp.int32), crop_blocks[:-1, -1]])
    start = (
        jnp.zeros((heads, head_width, head_width), jnp.float32),
        jnp.zeros((heads, head_width), jnp.float32),
    )
    finish, (grad_query, grad_key, grad_value) = lax.scan(
        attend_backward,
        start,
        (
            split_blocks(query_feat),
            split_blocks(key_feat),
            split_blocks(values),
            crop_blocks,
            split_blocks(keymask),
            prev_crops,
            states,
            norms,
            split_blocks(grad_numer),
            split_blocks(grad_denom),
        ),
        reverse=True,
    )
    shape = (length, heads, head_width)
    return (grad_query.reshape(shape), grad_key.reshape(shape), grad_value.reshape(shape))


def general_body(
    tokens,
    crop_ids,
    kv_mask,
    norm1_gain,
    norm1_bias,
    w_query,
    w_key,
    w_value,
    w_out,
    norm2_gain,
    norm2_bias,
    w_up,
    up_bias,
    w_down,
    down_bias,
    cotangent,
):
    slots, length, width = tokens.shape
    heads = HEADS
    head_width = width // heads
    count = slots * length
    devices = lax.axis_size("dp") * lax.axis_size("fsdp")
    dims = (OUTER, lax.axis_size("dp") // (2 * OUTER), lax.axis_size("fsdp"))
    unit = width // devices
    packed = jnp.concatenate([norm1_gain, norm1_bias, norm2_gain, norm2_bias, down_bias, up_bias])
    packed = jnp.pad(packed, (0, 16 * 128 - packed.shape[0])).reshape(16, 128)
    vectors, full_query, full_key, full_value, full_out, full_up, full_down = gather(
        dims, [packed, w_query, w_key, w_value, w_out, w_up, w_down], unit
    )
    vectors = vectors.reshape(devices, 16 * 128)
    gain_one, bias_one, gain_two, bias_two, full_down_bias = (
        vectors[:, index * unit : (index + 1) * unit].reshape(-1) for index in range(5)
    )
    full_up_bias = vectors[:, 5 * unit : 5 * unit + up_bias.shape[0]].reshape(-1)
    inputs = tokens.reshape(count, width).astype(jnp.float32)
    normed_wide, pull_one = jax.vjp(
        norm_affine, inputs, gain_one.astype(jnp.float32), bias_one.astype(jnp.float32)
    )
    normed = normed_wide.astype(jnp.bfloat16)
    query = jnp.dot(normed, full_query, preferred_element_type=jnp.float32)
    keys = jnp.dot(normed, full_key, preferred_element_type=jnp.float32)
    values = jnp.dot(normed, full_value, preferred_element_type=jnp.float32).astype(jnp.bfloat16)
    query_wide, pull_query = jax.vjp(feature, query)
    key_wide, pull_key = jax.vjp(feature, keys)
    query_feat = query_wide.astype(jnp.bfloat16).reshape(slots, length, heads, head_width)
    key_feat = key_wide.astype(jnp.bfloat16).reshape(slots, length, heads, head_width)
    value_heads = values.reshape(slots, length, heads, head_width)
    mixed_wide, denom, states, norms = lax.map(
        attend_slot, (query_feat, key_feat, value_heads, crop_ids, kv_mask)
    )
    mixed = mixed_wide.reshape(count, width).astype(jnp.bfloat16)
    middle = inputs + jnp.dot(mixed, full_out, preferred_element_type=jnp.float32)
    normed_two_wide, pull_two = jax.vjp(
        norm_affine, middle, gain_two.astype(jnp.float32), bias_two.astype(jnp.float32)
    )
    normed_two = normed_two_wide.astype(jnp.bfloat16)
    upper = jnp.dot(normed_two, full_up, preferred_element_type=jnp.float32) + full_up_bias.astype(
        jnp.float32
    )
    hidden_wide, pull_gelu = jax.vjp(gelu_exact, upper)
    hidden = hidden_wide.astype(jnp.bfloat16)
    result = (
        middle
        + jnp.dot(hidden, full_down, preferred_element_type=jnp.float32)
        + full_down_bias.astype(jnp.float32)
    )
    output = result.astype(jnp.bfloat16).reshape(slots, length, width)
    back_up, back_down = full_up, full_down
    back_query, back_key, back_value, back_out = full_query, full_key, full_value, full_out
    grad_out = cotangent.reshape(count, width)
    grad_down_bias = jnp.sum(grad_out.astype(jnp.float32), axis=0)
    grad_w_down = jnp.dot(hidden.T, grad_out, preferred_element_type=jnp.float32).astype(jnp.bfloat16)
    grad_hidden = jnp.dot(grad_out, back_down.T, preferred_element_type=jnp.float32)
    grad_upper = pull_gelu(grad_hidden)[0].astype(jnp.bfloat16)
    grad_up_bias = jnp.sum(grad_upper.astype(jnp.float32), axis=0)
    grad_w_up = jnp.dot(normed_two.T, grad_upper, preferred_element_type=jnp.float32).astype(jnp.bfloat16)
    grad_normed_two = jnp.dot(grad_upper, back_up.T, preferred_element_type=jnp.float32)
    grad_middle_part, grad_gain_two, grad_bias_two = pull_two(grad_normed_two)
    grad_middle = grad_out.astype(jnp.float32) + grad_middle_part
    grad_attended = grad_middle.astype(jnp.bfloat16)
    grad_w_out = jnp.dot(mixed.T, grad_attended, preferred_element_type=jnp.float32).astype(jnp.bfloat16)
    grad_mixed = jnp.dot(grad_attended, back_out.T, preferred_element_type=jnp.float32).reshape(
        slots, length, heads, head_width
    )
    grad_numer = grad_mixed / denom[..., None]
    grad_denom = -jnp.sum(grad_mixed * mixed_wide, axis=-1) / denom
    grad_query_feat, grad_key_feat, grad_values = lax.map(
        attend_slot_back,
        (
            query_feat,
            key_feat,
            value_heads,
            crop_ids,
            kv_mask,
            states,
            norms,
            grad_numer,
            grad_denom,
        ),
    )
    grad_query = pull_query(grad_query_feat.reshape(count, width))[0].astype(jnp.bfloat16)
    grad_keys = pull_key(grad_key_feat.reshape(count, width))[0].astype(jnp.bfloat16)
    grad_values = grad_values.reshape(count, width).astype(jnp.bfloat16)
    grad_w_query = jnp.dot(normed.T, grad_query, preferred_element_type=jnp.float32).astype(jnp.bfloat16)
    grad_w_key = jnp.dot(normed.T, grad_keys, preferred_element_type=jnp.float32).astype(jnp.bfloat16)
    grad_w_value = jnp.dot(normed.T, grad_values, preferred_element_type=jnp.float32).astype(jnp.bfloat16)
    grad_normed = jnp.dot(grad_query, back_query.T, preferred_element_type=jnp.float32)
    grad_normed = grad_normed + jnp.dot(grad_keys, back_key.T, preferred_element_type=jnp.float32)
    grad_normed = grad_normed + jnp.dot(
        grad_values, back_value.T, preferred_element_type=jnp.float32
    )
    grad_input_part, grad_gain_one, grad_bias_one = pull_one(grad_normed)
    small = jnp.concatenate(
        [
            vector.reshape(devices, -1)
            for vector in (
                grad_gain_one,
                grad_bias_one,
                grad_gain_two,
                grad_bias_two,
                grad_down_bias,
                grad_up_bias,
            )
        ],
        axis=1,
    )
    small = jnp.pad(small, ((0, 0), (0, 8 * 128 - small.shape[1]))).reshape(devices, 8, 128)
    small, own_up, own_down, own_query, own_key, own_value, own_out = scatter(
        dims,
        small,
        [grad_w_up, grad_w_down, grad_w_query, grad_w_key, grad_w_value, grad_w_out],
        unit,
    )
    small = small.reshape(8 * 128)
    own_gain_one, own_bias_one, own_gain_two, own_bias_two, own_down_bias = (
        small[index * unit : (index + 1) * unit] for index in range(5)
    )
    own_up_bias = small[5 * unit : 5 * unit + up_bias.shape[0]]
    input_grad = (grad_middle + grad_input_part).astype(jnp.bfloat16).reshape(slots, length, width)
    return (
        output,
        input_grad,
        own_gain_one,
        own_bias_one,
        own_query,
        own_key,
        own_value,
        own_out,
        own_gain_two,
        own_bias_two,
        own_up,
        own_up_bias,
        own_down,
        own_down_bias,
    )


LENGTH = 512
WIDTH = 1024
HIDDEN = 4096
UNIT = 32
CHUNKS = 24
FEED = 8
ROOMS = 12
LAG = 2
AHEAD = 4
TERMS_AHEAD = 3
TERMS_START = 23
VMEM_LIMIT = 63 << 20


def when(condition):
    if isinstance(condition, bool):
        return (lambda work: work()) if condition else (lambda work: None)
    return pl.when(condition)


def each(count, work):
    def step(index, carry):
        work(index)
        return carry

    lax.fori_loop(0, count, step, 0)


def dot(left, right):
    return jnp.dot(left, right, preferred_element_type=jnp.float32)


def dot_nt(left, right):
    return lax.dot_general(
        left, right, (((1,), (1,)), ((), ())), preferred_element_type=jnp.float32
    )


def dot_tn(left, right):
    return lax.dot_general(
        left, right, (((0,), (0,)), ((), ())), preferred_element_type=jnp.float32
    )


def by_order(place, orders, index, work):
    turn = (index + 3 * place.at["c"]) % len(orders)
    for order in dict.fromkeys(orders):
        turns = [number for number, item in enumerate(orders) if item == order]
        match = turn == turns[0]
        for number in turns[1:]:
            match = match | (turn == number)

        @pl.when(match)
        def _(order=order):
            work(order)


class Mover:
    def __init__(self, place, send_sem, recv_sem):
        self.place, self.send_sem, self.recv_sem = place, send_sem, recv_sem

    def copy(self, lead, stage, step, axis, source, target):
        at = lead + (stage, step - 1)
        return pltpu.make_async_remote_copy(
            source,
            target,
            self.send_sem.at[at],
            self.recv_sem.at[at],
            device_id=self.place.device(axis, step),
            device_id_type=MESH,
        )


class Gather(Mover):
    def region(self, chunk, done, spot):
        lead = tuple(slice(None) if axis in done else spot[axis] for axis in "abcz")
        return chunk.at[lead]

    def send(self, chunk, lead, order, stage):
        axis, done = order[stage], order[:stage]
        source = self.region(chunk, done, self.place.at)
        for step in self.place.partners(axis):
            self.copy(lead, stage, step, axis, source, source).start()

    def receive(self, chunk, lead, order, stage):
        axis, done = order[stage], order[:stage]
        for step in self.place.partners(axis):
            spot = self.place.moved(axis, self.place.size[axis] - step)
            target = self.region(chunk, done, spot)
            self.copy(lead, stage, step, axis, target, target).wait_recv()

    def drain(self, chunk, lead, order):
        for stage in range(4):
            axis, done = order[stage], order[:stage]
            source = self.region(chunk, done, self.place.at)
            for step in self.place.partners(axis):
                self.copy(lead, stage, step, axis, source, source).wait_send()


class Weights(Gather):
    orders = ("zbac", "zabc", "bzac", "zbac", "zabc", "azbc")

    def __init__(self, place, buffer, send_sem, recv_sem):
        super().__init__(place, send_sem, recv_sem)
        self.buffer, self.total = buffer, buffer.shape[0]

    def by_order(self, index, work):
        by_order(self.place, self.orders, index, work)

    def begin(self, index):
        @when(index < self.total)
        def _():
            self.by_order(
                index, lambda order: self.send(self.buffer.at[index], (index,), order, 0)
            )

    def tick(self, now):
        self.begin(now + AHEAD)
        for stage in range(4):
            index = now - stage * LAG
            live = (index >= 0) & (index < self.total)

            @when(live)
            def _(index=index, stage=stage):
                def work(order):
                    chunk = self.buffer.at[index]
                    self.receive(chunk, (index,), order, stage)
                    if stage < 3:
                        self.send(chunk, (index,), order, stage + 1)

                self.by_order(index, work)

    def finish(self, first, count):
        def work(step):
            index = first + step
            self.by_order(
                index, lambda order: self.drain(self.buffer.at[index], (index,), order)
            )

        each(count, work)


def moments(values):
    mean = jnp.mean(values, axis=-1, keepdims=True)
    centred = values - mean
    spread = jnp.mean(centred * centred, axis=-1, keepdims=True)
    scale = lax.rsqrt(spread + norm_eps)
    return centred * scale, scale


def gelu_pair(upper):
    bell = jnp.exp(-0.5 * upper * upper) * 0.3989422804014327
    below = 0.5 * (1.0 + lax.erf(upper * 0.7071067811865476))
    return upper * below, below + upper * bell


def matrix(buffer, index):
    return buffer[index].reshape(WIDTH, WIDE)


def column_of(row):
    tall = jnp.transpose(jnp.broadcast_to(row.astype(jnp.float32), (8, row.shape[1])))
    return tall[:, 0:1]


def read_vectors(gathered, devices):
    flat = gathered[...].reshape(devices * 8, 128).astype(jnp.bfloat16)

    def line(number):
        shape = (devices, devices * 8)
        wanted = lax.broadcasted_iota(jnp.int32, shape, 0) * 8 + number
        chosen = lax.broadcasted_iota(jnp.int32, shape, 1) == wanted
        return dot(chosen.astype(jnp.bfloat16), flat).astype(jnp.bfloat16)

    def spread(lines, start, wide):
        total = wide * devices
        lane = lax.broadcasted_iota(jnp.int32, (128, total), 1)
        wanted = lax.broadcasted_iota(jnp.int32, (128, total), 0) == start + lane % wide
        found = dot(lines, wanted.astype(jnp.bfloat16))
        owner = lax.broadcasted_iota(jnp.int32, (devices, total), 1) // wide
        mine = owner == lax.broadcasted_iota(jnp.int32, (devices, total), 0)
        return jnp.sum(jnp.where(mine, found, 0.0), axis=0, keepdims=True)

    first, second = line(0), line(1)
    rows = [spread(first, index * UNIT, UNIT) for index in range(4)]
    rows.append(spread(line(2), 0, UNIT))
    return rows, [spread(second, index * UNIT, UNIT) for index in range(4)]


def write_vectors(rows, devices):
    result = None
    for index, row in enumerate(rows):
        owner = lax.broadcasted_iota(jnp.int32, (devices, WIDTH), 1) // UNIT
        mine = owner == lax.broadcasted_iota(jnp.int32, (devices, WIDTH), 0)
        spread = jnp.where(mine, row, 0.0)
        lane = lax.broadcasted_iota(jnp.int32, (WIDTH, 128), 0)
        wanted = lax.broadcasted_iota(jnp.int32, (WIDTH, 128), 1) == index * UNIT + lane % UNIT
        found = jnp.dot(
            spread,
            wanted.astype(jnp.float32),
            preferred_element_type=jnp.float32,
            precision=HIGH,
        )
        result = found if result is None else result + found
    return result


def head_lanes(which, shape):
    lane = lax.broadcasted_iota(jnp.int32, shape, 1)
    return lane < 64 if which == 0 else lane >= 64


def allowed(crop_row, mask_row):
    shape = (LENGTH, LENGTH)
    row = lax.broadcasted_iota(jnp.int32, shape, 0)
    column = lax.broadcasted_iota(jnp.int32, shape, 1)
    same = column_of(crop_row) == crop_row.astype(jnp.float32)
    seen = (mask_row > 0) | (row == column)
    return jnp.where(same & (column <= row) & seen, 1.0, 0.0).astype(jnp.bfloat16)


def allowed_back(crop_row, mask_row):
    shape = (LENGTH, LENGTH)
    row = lax.broadcasted_iota(jnp.int32, shape, 0)
    column = lax.broadcasted_iota(jnp.int32, shape, 1)
    same = column_of(crop_row) == crop_row.astype(jnp.float32)
    seen = (column_of(mask_row) > 0) | (row == column)
    return jnp.where(same & (row <= column) & seen, 1.0, 0.0).astype(jnp.bfloat16)


def transpose_into(source, target):
    def work(index):
        at = pl.ds(pl.multiple_of(index * 128, 128), 128)
        target[at, :] = jnp.transpose(source[:, at])

    each(source.shape[1] // 128, work)


def by_rows(work):
    each(LENGTH // 64, lambda index: work(pl.ds(pl.multiple_of(index * 64, 64), 64)))


def forward_heads(pair, qkv, mask, mixed, inverse, attended):
    chunk = pair // 4
    lanes = pl.ds(pl.multiple_of((pair % 4) * 128, 128), 128)
    columns = pl.ds(pl.multiple_of(pair * 128, 128), 128)
    for part in (0, 1):
        keys = 256 * (part + 1)
        rows = slice(part * 256, part * 256 + 256)
        query = qkv[chunk, rows, lanes]
        key = qkv[2 + chunk, 0:keys, lanes]
        value = qkv[4 + chunk, 0:keys, lanes]
        zero, one = jnp.zeros_like(key), jnp.ones_like(key)
        total = None
        for which in (0, 1):
            mine = head_lanes(which, key.shape)
            scores = dot_nt(query, jnp.where(mine, key, zero)).astype(jnp.bfloat16)
            scores = scores * mask[rows, 0:keys]
            right = jnp.concatenate(
                [jnp.where(mine, value, zero), jnp.where(mine, one, zero)], axis=1
            )
            term = dot(scores, right)
            total = term if total is None else total + term
        inverted = 1.0 / total[:, 128:]
        result = total[:, :128] * inverted
        mixed[rows, columns] = result
        inverse[rows, columns] = inverted
        attended[rows, columns] = result.astype(jnp.bfloat16)


def hidden_order(flip):
    shape = (4 * 128, 4 * 128)
    rows, columns = (lax.broadcasted_iota(jnp.int32, shape, axis) for axis in (0, 1))
    if flip:
        rows, columns = columns, rows
    wanted = (rows // UNIT) % 4 * 128 + rows // 128 * UNIT + rows % UNIT
    return columns == wanted


def feed_block(block, refs):
    normed, normed_t, grad_out, weights, up_bias, result, grad_normed, staged, grad_bias = refs
    group, half = block // 2, block % 2
    first = FEED + 4 * group
    up = matrix(weights, first + 2 + half)
    upper = dot(normed[...], up) + up_bias[pl.ds(block, 1), :]
    hidden, slope = gelu_pair(upper)
    hidden = hidden.astype(jnp.bfloat16)
    grad_hidden = None
    for side in (0, 1):
        columns = slice(side * WIDE, side * WIDE + WIDE)
        down = weights[first + side, half].reshape(WIDE, WIDE)
        result[:, columns] += dot(hidden, down)
        term = dot_nt(grad_out[:, columns], down)
        grad_hidden = term if grad_hidden is None else grad_hidden + term
    grad_upper = (grad_hidden * slope).astype(jnp.bfloat16)
    grad_bias[pl.ds(block, 1), :] = jnp.sum(
        grad_upper.astype(jnp.float32), axis=0, keepdims=True
    )
    grad_normed[...] += dot_nt(grad_upper, up)
    value = dot(normed_t[...], grad_upper).astype(jnp.bfloat16)
    staged[0] = value.reshape(staged.shape[1:])
    for side in (0, 1):
        columns = slice(side * WIDE, side * WIDE + WIDE)
        value = dot_tn(hidden, grad_out[:, columns]).astype(jnp.bfloat16)
        staged[1, side] = value.reshape(staged.shape[2:])


class Sums(Mover):
    def start(self, lead, stage, step, axis, source, target):
        self.copy(lead, stage, step, axis, source, target).start()

    def region(self, order, stage, where):
        at = {axis: self.place.at[axis] for axis in order[:stage]}
        at[order[stage]] = where
        return tuple(at.get(axis, slice(None)) for axis in "abz")

    def blocks(self, order, stage, where):
        rest = [axis for axis in "abz" if axis in order[stage + 1 :]]
        base = self.region(order, stage, where)
        sizes = [self.place.size[axis] for axis in rest]
        for inner in itertools.product(*(range(size) for size in sizes)):
            place = dict(zip(rest, inner))
            yield (
                tuple(place.get(axis, item) for axis, item in zip("abz", base)),
                inner,
            )

    def room(self, order, stage, rooms, step):
        if stage == 0:
            return rooms[0]
        if stage == 1:
            size = self.place.size[order[2]]
            return rooms[1].at[pl.ds((step - 1) * size, size)]
        return rooms[2].at[step - 1]

    def send_stage(self, lead, order, stage, total, rooms, add):
        axis = order[stage]
        for step in self.place.partners(axis):
            where = self.place.moved(axis, step)[axis]
            for at, _ in self.blocks(order, stage, where):
                add(at)
            source = total.at[self.region(order, stage, where)]
            room = self.room(order, stage, rooms, step)
            self.start(lead, stage + 1, step, axis, source, room)
        for at, _ in self.blocks(order, stage, self.place.at[axis]):
            add(at)

    def await_stage(self, lead, order, stage, rooms):
        axis = order[stage]
        for step in self.place.partners(axis):
            room = self.room(order, stage, rooms, step)
            self.copy(lead, stage + 1, step, axis, room, room).wait_recv()

    def after_core(self, lead, order, own, total, rooms):
        def add(at):
            total[at] = own[at] + total[at]

        self.send_stage(lead, order, 0, total, rooms, add)

    def came_in(self, order, stage, total, rooms, at):
        rest = [axis for axis in "abz" if axis in order[stage + 1 :]]
        inner = tuple(item for axis, item in zip("abz", at) if axis in rest)
        steps = self.place.partners(order[stage])
        wide = total.dtype if len(steps) == 1 and stage < 2 else jnp.float32
        value = total[at].astype(wide)
        for step in steps:
            room = self.room(order, stage, rooms, step)
            value = value + (room[inner] if inner else room[...]).astype(wide)
        return value

    def after_stage(self, lead, order, stage, total, rooms):
        self.await_stage(lead, order, stage - 1, rooms)

        def add(at):
            total[at] = self.came_in(order, stage - 1, total, rooms, at).astype(total.dtype)

        self.send_stage(lead, order, stage, total, rooms, add)

    def after_last(self, lead, order, total, rooms):
        self.await_stage(lead, order, 2, rooms)
        at = tuple(self.place.at[axis] for axis in "abz")
        return self.came_in(order, 2, total, rooms, at)

    def drain(self, lead, order, total, rooms):
        self.copy(lead, 0, 1, "c", total, total).wait_send()
        for stage in range(3):
            axis = order[stage]
            for step in self.place.partners(axis):
                room = self.room(order, stage, rooms, step)
                self.copy(lead, stage + 1, step, axis, room, room).wait_send()


class Gradients(Sums):
    orders = ("abz", "baz", "azb", "abz", "baz", "bza")

    def __init__(self, place, terms, sums, rooms, results, ring, ring_sem, send_sem, recv_sem):
        super().__init__(place, send_sem, recv_sem)
        self.terms, self.sums, self.rooms, self.results = terms, sums, rooms, results
        self.ring, self.ring_sem = ring, ring_sem
        self.total = results.shape[0]

    def sum_at(self, index):
        return self.sums.at[index // 2, :, :, index % 2]

    def by_order(self, index, work):
        rooms = [room.at[index % ROOMS] for room in self.rooms]
        total = self.sum_at(index)
        by_order(self.place, self.orders, index, lambda order: work(order, total, rooms))

    def begin(self, index):
        @when(index < self.total)
        def _():
            side = self.place.at["c"]
            slot = index % (TERMS_AHEAD + 1)
            source = self.terms.at[index]
            self.start((index,), 0, 1, "c", source.at[:, :, 1 - side], self.sum_at(index))
            pltpu.make_async_copy(
                source.at[:, :, side], self.ring.at[slot], self.ring_sem.at[slot]
            ).start()

    def tick(self, now):
        self.begin(now + TERMS_AHEAD)

        def live(index):
            return (index >= 0) & (index < self.total)

        @when(live(now))
        def _():
            slot = now % (TERMS_AHEAD + 1)
            own = self.ring.at[slot]
            pltpu.make_async_copy(own, own, self.ring_sem.at[slot]).wait()
            total = self.sum_at(now)
            self.copy((now,), 0, 1, "c", total, total).wait_recv()
            self.by_order(
                now,
                lambda order, total, rooms: self.after_core((now,), order, own, total, rooms),
            )

        for stage in (1, 2):
            index = now - stage * LAG

            @when(live(index))
            def _(index=index, stage=stage):
                self.by_order(
                    index,
                    lambda order, total, rooms: self.after_stage(
                        (index,), order, stage, total, rooms
                    ),
                )

        index = now - 3 * LAG

        @when(live(index))
        def _():
            def work(order, total, rooms):
                self.results[index] = self.after_last((index,), order, total, rooms)

            self.by_order(index, work)

    def finish(self):
        def work(index):
            self.by_order(
                index,
                lambda order, total, rooms: self.drain((index,), order, total, rooms),
            )

        each(self.total, work)


def backward_heads(pair, qkv, mask, mask_t, mixed, inverse, grad_mixed):
    chunk = pair // 4
    lanes = pl.ds(pl.multiple_of((pair % 4) * 128, 128), 128)
    columns = pl.ds(pl.multiple_of(pair * 128, 128), 128)
    query = qkv[chunk, :, lanes]
    key = qkv[2 + chunk, :, lanes]
    value = qkv[4 + chunk, :, lanes]
    grad_numer = (grad_mixed[:, columns] * inverse[:, columns]).astype(jnp.bfloat16)
    part = grad_numer.astype(jnp.float32) * mixed[:, columns]
    high = part.astype(jnp.bfloat16)
    low = pltpu.roll(part - high.astype(jnp.float32), 64, 1).astype(jnp.bfloat16)
    zero, minus = jnp.zeros_like(query), jnp.full_like(query, -1.0)
    heads = []
    for which in (0, 1):
        mine = head_lanes(which, query.shape)
        heads.append(
            (
                jnp.concatenate([grad_numer, jnp.where(mine, high, low)], axis=1),
                jnp.concatenate([jnp.where(mine, value, zero), minus], axis=1),
                jnp.where(mine, query, zero),
                jnp.where(mine, key, zero),
                jnp.where(mine, grad_numer, zero),
            )
        )
    for part in (0, 1):
        keys = 256 * (part + 1)
        rows = slice(part * 256, part * 256 + 256)
        total = None
        for left, right, _, own_key, _ in heads:
            grad_scores = dot_nt(left[rows], right[:keys]).astype(jnp.bfloat16)
            term = dot(grad_scores * mask[rows, 0:keys], own_key[:keys])
            total = term if total is None else total + term
        slope = jnp.minimum(query[rows].astype(jnp.float32), 1.0)
        qkv[chunk, rows, lanes] = (total * slope).astype(jnp.bfloat16)
    for part in (0, 1):
        start = part * 256
        rows = slice(start, start + 256)
        grad_key = grad_value = None
        for left, right, own_query, own_key, own_grad in heads:
            seen = mask_t[rows, start:LENGTH]
            scores = dot_nt(own_key[rows], query[start:]).astype(jnp.bfloat16) * seen
            grad_scores = dot_nt(right[rows], left[start:]).astype(jnp.bfloat16) * seen
            term = dot(scores, own_grad[start:])
            grad_value = term if grad_value is None else grad_value + term
            term = dot(grad_scores, own_query[start:])
            grad_key = term if grad_key is None else grad_key + term
        slope = jnp.minimum(key[rows].astype(jnp.float32), 1.0)
        qkv[2 + chunk, rows, lanes] = (grad_key * slope).astype(jnp.bfloat16)
        qkv[4 + chunk, rows, lanes] = grad_value.astype(jnp.bfloat16)


def layer_kernel(dims, *refs):
    crops, kept, gain_one, bias_one, gain_two, bias_two, bias_down, bias_up = refs[:8]
    tokens_in, grad_out_in = refs[8:10]
    shards = refs[10:16]
    output, input_grad, mixed_kept, inverse_kept, normed_t_kept, attention_kept, terms = refs[16:23]
    owned, owned_up, owned_small = refs[23:26]
    (
        pixels,
        grad_out,
        weights,
        up_shard,
        vectors,
        rows,
        up_bias,
        mask,
        mask_t,
        qkv,
        normed,
        turned_one,
        turned_two,
        middle,
        wide_one,
        wide_two,
        wide_three,
        staged,
        grad_up_bias,
        sums,
        small,
        ring,
        rooms_one,
        rooms_two,
        rooms_three,
        side_total,
        side_one,
        side_two,
        side_three,
        send_sem,
        recv_sem,
        vector_send_sem,
        vector_recv_sem,
        load_sem,
        store_sem,
        stage_sem,
        ring_sem,
        terms_send_sem,
        terms_recv_sem,
        side_send_sem,
        side_recv_sem,
        sibling_sem,
    ) = refs[26:]
    outer, inner, depth = dims
    devices = 2 * outer * inner * depth
    place = Place(dims)
    spot = (place.at["a"], place.at["b"], place.at["c"], place.at["z"])
    copies = {}

    def move(name, source, target):
        item = pltpu.make_async_copy(source, target, load_sem.at[len(copies)])
        item.start()
        copies[name] = item

    for index in range(FEED):
        source = shards[index // 2].at[:, pl.ds((index % 2) * WIDE, WIDE)]
        move(index, source, weights.at[(index,) + spot])
    move("tokens", tokens_in, pixels)
    move("up", shards[4], up_shard)
    for group in range(4):
        for half in (0, 1):
            source = shards[5].at[pl.ds(group * UNIT, UNIT), pl.ds(half * WIDE, WIDE)]
            index = FEED + 4 * group + half
            move(index, source, weights.at[(index,) + spot])
    move("grad_out", grad_out_in, grad_out)

    vector_gather = Gather(place, vector_send_sem, vector_recv_sem)
    vector_order = "zbac"
    lines = [
        jnp.concatenate([item[...] for item in (gain_one, bias_one, gain_two, bias_two)], axis=1),
        bias_up[...],
        jnp.concatenate([bias_down[...], jnp.zeros((1, 128 - UNIT), jnp.bfloat16)], axis=1),
    ]
    vectors[spot] = jnp.concatenate(
        [line.astype(jnp.float32) for line in lines] + [jnp.zeros((5, 128), jnp.float32)], axis=0
    )
    place.greet()
    vector_gather.send(vectors, (), vector_order, 0)
    gather_all = Weights(place, weights, send_sem, recv_sem)
    for index in range(AHEAD):
        copies[index].wait()
        gather_all.begin(index)
    copies["up"].wait()
    stacked = jnp.concatenate(
        [up_shard[:, index * WIDE : (index + 1) * WIDE] for index in range(8)], axis=0
    )
    stacked = dot(stacked, hidden_order(False).astype(jnp.bfloat16)).astype(jnp.bfloat16)
    for part in range(8):
        for group in range(4):
            at = (FEED + 4 * group + 2 + part // 4,) + spot
            lanes = slice((part % 4) * 128, (part % 4) * 128 + 128)
            weights[at + (slice(None), lanes)] = stacked[
                part * UNIT : (part + 1) * UNIT, group * 128 : (group + 1) * 128
            ]
    for name, item in copies.items():
        if name not in (0, 1, 2, 3, "up"):
            item.wait()
    for stage in range(4):
        vector_gather.receive(vectors, (), vector_order, stage)
        if stage < 3:
            vector_gather.send(vectors, (), vector_order, stage + 1)
            gather_all.tick(stage)
    width_rows, up_rows = read_vectors(vectors, devices)
    for index, row in enumerate(width_rows):
        rows[index : index + 1, :] = row
    for group, row in enumerate(up_rows):
        for half in (0, 1):
            up_bias[2 * group + half : 2 * group + half + 1, :] = row[
                :, half * WIDE : half * WIDE + WIDE
            ]
    mask[...] = allowed(crops[...], kept[...])
    mask_t[...] = allowed_back(crops[...], kept[...])
    sums[...] = jnp.zeros(sums.shape, jnp.float32)

    def first_norm(at):
        value = pixels[at, :].astype(jnp.float32)
        unit, _ = moments(value)
        normed[at, :] = (unit * rows[0:1, :] + rows[1:2, :]).astype(jnp.bfloat16)
        middle[at, :] = value

    by_rows(first_norm)
    stores = {}

    def store(name, source, target):
        item = pltpu.make_async_copy(source, target, store_sem.at[len(stores)])
        item.start()
        stores[name] = item

    transpose_into(normed, turned_one)
    store("normed", turned_one, normed_t_kept)
    each(3, lambda index: gather_all.tick(3 + index))

    def project(index):
        gather_all.tick(6 + index)
        value = dot(normed[...], matrix(weights, index))
        mapped = jnp.where(value > 0, value + 1.0, jnp.exp(jnp.minimum(value, 0.0)))
        qkv[index] = jnp.where(index < 4, mapped, value).astype(jnp.bfloat16)

    each(6, project)
    attended, mixed, inverse = pixels, wide_one, wide_two

    def heads(pair):
        @pl.when(pair % 2 == 0)
        def _():
            gather_all.tick(12 + pair // 2)

        forward_heads(pair, qkv, mask, mixed, inverse, attended)

    each(8, heads)
    store("mixed", mixed, mixed_kept)
    store("inverse", inverse, inverse_kept)
    store("attention", weights.at[pl.ds(0, FEED)], attention_kept)
    for half in (0, 1):
        columns = slice(half * WIDE, half * WIDE + WIDE)
        middle[:, columns] += dot(attended[...], matrix(weights, 6 + half))
    stores["normed"].wait()
    transpose_into(attended, turned_one)
    result, grad_normed, normed_two = wide_one, wide_two, normed
    stores["mixed"].wait()
    stores["inverse"].wait()

    def second_norm(at):
        value = middle[at, :]
        unit, _ = moments(value)
        normed_two[at, :] = (unit * rows[2:3, :] + rows[3:4, :]).astype(jnp.bfloat16)
        result[at, :] = value + rows[4:5, :]
        grad_normed[at, :] = jnp.zeros((64, WIDTH), jnp.float32)

    by_rows(second_norm)
    transpose_into(normed_two, turned_two)

    adder = Gradients(
        place,
        terms,
        weights,
        (rooms_one, rooms_two, rooms_three),
        owned,
        ring,
        ring_sem,
        terms_send_sem,
        terms_recv_sem,
    )

    def leave(block):
        first, half = 4 * (block // 2), block % 2
        return (
            pltpu.make_async_copy(staged.at[0], terms.at[first + 2 + half], stage_sem.at[0]),
            pltpu.make_async_copy(
                staged.at[1], terms.at[pl.ds(first, 2), half], stage_sem.at[1]
            ),
        )

    def last_tick(block):
        return 16 + 4 * (block // 2) + block % 2

    def feed(block):
        begin = last_tick(block - 1) + 1

        def both(step, carry):
            @pl.when(step >= 16)
            def _():
                gather_all.tick(step)

            @pl.when((step == begin) & (block > 0))
            def _():
                for item in leave(block - 1):
                    item.wait()

            @pl.when(step == TERMS_START)
            def _():
                pl.semaphore_wait(sibling_sem, 1)
                for index in range(TERMS_AHEAD):
                    adder.begin(index)

            @pl.when(step >= TERMS_START)
            def _():
                adder.tick(step - TERMS_START)

            return carry

        lax.fori_loop(begin, last_tick(block) + 1, both, 0)
        feed_block(
            block,
            (
                normed_two,
                turned_two,
                grad_out,
                weights,
                up_bias,
                result,
                grad_normed,
                staged,
                grad_up_bias,
            ),
        )
        for item in leave(block):
            item.start()

        @pl.when(block == 1)
        def _():
            gather_all.finish(0, ROOMS)
            stores["attention"].wait()
            pl.semaphore_signal(
                sibling_sem, 1, device_id=place.device("c", 1), device_id_type=MESH
            )

    each(8, feed)
    done = last_tick(7) + 1 - TERMS_START
    adder.tick(done)
    for item in leave(7):
        item.wait()
    gather_all.finish(ROOMS, CHUNKS - ROOMS)
    loads = {}

    def load(name, source, target):
        item = pltpu.make_async_copy(source, target, store_sem.at[4 + len(loads)])
        item.start()
        loads[name] = item

    load("out", attention_kept.at[pl.ds(6, 2)], weights.at[pl.ds(ROOMS + 6, 2)])
    load("normed", normed_t_kept, turned_two)
    load("rest", attention_kept.at[pl.ds(0, 6)], weights.at[pl.ds(ROOMS, 6)])
    grad_attended, shown, grad_middle = pixels, normed, middle

    def close_branch(at):
        unit, scale = moments(middle[at, :])
        grad = grad_out[at, :].astype(jnp.float32)
        value = grad_normed[at, :]
        shown[at, :] = result[at, :].astype(jnp.bfloat16)
        sums[0:1, :] += jnp.sum(value * unit, axis=0, keepdims=True)
        sums[1:2, :] += jnp.sum(value, axis=0, keepdims=True)
        sums[2:3, :] += jnp.sum(grad, axis=0, keepdims=True)
        scaled = value * rows[2:3, :]
        summed = grad + scale * (
            scaled
            - jnp.mean(scaled, axis=-1, keepdims=True)
            - unit * jnp.mean(scaled * unit, axis=-1, keepdims=True)
        )
        grad_middle[at, :] = summed
        grad_attended[at, :] = summed.astype(jnp.bfloat16)

    by_rows(close_branch)
    load("mixed", mixed_kept, mixed)
    load("inverse", inverse_kept, inverse)
    load("output", shown, output)
    adder.tick(done + 1)
    loads["out"].wait()
    grad_mixed = wide_three
    grad_mixed[...] = dot_nt(grad_attended[:, 0:WIDE], matrix(weights, ROOMS + 6)) + dot_nt(
        grad_attended[:, WIDE:WIDTH], matrix(weights, ROOMS + 7)
    )
    adder.tick(done + 2)

    def stage_out(slot, index):
        return pltpu.make_async_copy(staged.at[slot], terms.at[index], stage_sem.at[slot])

    for half in (0, 1):
        columns = slice(half * WIDE, half * WIDE + WIDE)
        value = dot(turned_one[...], grad_attended[:, columns]).astype(jnp.bfloat16)
        staged[half] = value.reshape(staged.shape[1:])
        stage_out(half, 16 + half).start()
    load("tokens", tokens_in, pixels)
    adder.tick(done + 3)
    for name in ("mixed", "inverse", "normed", "rest"):
        loads[name].wait()
    for half in (0, 1):
        stage_out(half, 16 + half).wait()
    spread = 14 - (done + 4)

    def back_heads(pair):
        @pl.when((pair + 1) * spread // 8 > pair * spread // 8)
        def _():
            adder.tick(done + 4 + pair * spread // 8)

        backward_heads(pair, qkv, mask, mask_t, mixed, inverse, grad_mixed)

    each(8, back_heads)
    grad_first = grad_mixed
    grad_first[...] = jnp.zeros(grad_first.shape, jnp.float32)

    def back_project(index):
        value = dot(turned_two[...], qkv[index]).astype(jnp.bfloat16)
        staged[index % 2] = value.reshape(staged.shape[1:])
        stage_out(index % 2, 18 + index).start()
        grad_first[...] += dot_nt(qkv[index], matrix(weights, ROOMS + index))

        @pl.when(index > 0)
        def _():
            stage_out((index - 1) % 2, 17 + index).wait()

        adder.tick(14 + index)

    each(6, back_project)
    stage_out(1, 23).wait()
    adder.tick(20)
    loads["tokens"].wait()
    loads["output"].wait()

    def close(at):
        unit, scale = moments(pixels[at, :].astype(jnp.float32))
        value = grad_first[at, :]
        sums[3:4, :] += jnp.sum(value * unit, axis=0, keepdims=True)
        sums[4:5, :] += jnp.sum(value, axis=0, keepdims=True)
        scaled = value * rows[0:1, :]
        shown[at, :] = (
            grad_middle[at, :]
            + scale
            * (
                scaled
                - jnp.mean(scaled, axis=-1, keepdims=True)
                - unit * jnp.mean(scaled * unit, axis=-1, keepdims=True)
            )
        ).astype(jnp.bfloat16)

    by_rows(close)
    load("input_grad", shown, input_grad)
    adder.tick(21)
    groups = [
        jnp.concatenate(
            [grad_up_bias[2 * group + half : 2 * group + half + 1, :] for half in (0, 1)], axis=1
        )
        for group in range(4)
    ]
    lines = [
        write_vectors([sums[index : index + 1, :] for index in (3, 4, 0, 1)], devices),
        write_vectors(groups, devices),
        write_vectors([sums[2:3, :]], devices),
    ]
    for device in range(devices):
        at = (
            device // (2 * inner * depth),
            (device // (2 * depth)) % inner,
            (device // depth) % 2,
            device % depth,
        )
        for row, line in enumerate(lines):
            small[at + (slice(row, row + 1),)] = line[device : device + 1, :]
        small[at + (slice(3, 8),)] = jnp.zeros((5, 128), jnp.float32)
    side = Sums(place, side_send_sem, side_recv_sem)
    rooms = (side_one, side_two, side_three)
    core = place.at["c"]
    side.start((), 0, 1, "c", small.at[:, :, 1 - core], side_total)

    def last_ticks(step):
        adder.tick(22 + step)

        @pl.when(step == 0)
        def _():
            side.copy((), 0, 1, "c", side_total, side_total).wait_recv()
            side.after_core((), "abz", small.at[:, :, core], side_total, rooms)

        for stage in (1, 2):

            @pl.when(step == stage)
            def _(stage=stage):
                side.after_stage((), "abz", stage, side_total, rooms)

        @pl.when(step == 3)
        def _():
            owned_small[...] = side.after_last((), "abz", side_total, rooms)

        @pl.when(step == 4)
        def _():
            back = hidden_order(True).astype(jnp.float32)
            for part in range(8):
                lanes = slice((part % 4) * 128, (part % 4) * 128 + 128)
                value = jnp.concatenate(
                    [owned[4 * group + 2 + part // 4, :, lanes] for group in range(4)], axis=1
                )
                owned_up[:, part * WIDE : (part + 1) * WIDE] = jnp.dot(
                    value, back, preferred_element_type=jnp.float32, precision=HIGH
                )

    each(CHUNKS + 3 * LAG - 22, last_ticks)
    vector_gather.drain(vectors, (), vector_order)
    side.drain((), "abz", side_total, rooms)
    adder.finish()
    loads["input_grad"].wait()


def layer(dims, tokens, cotangent, crops, kept, small, shards):
    outer, inner, depth = dims
    most = max(dims) - 1
    lead = (outer, inner, 2, depth)
    chip = (outer, inner, depth)
    tile, small_tile = (UNIT, WIDE), (8, 128)
    whole, turned = (LENGTH, WIDTH), (WIDTH, LENGTH)
    f32, bf16 = jnp.float32, jnp.bfloat16
    shape = jax.ShapeDtypeStruct
    room, dma = pltpu.VMEM, pltpu.SemaphoreType.DMA
    vmem, anywhere = pl.BlockSpec(memory_space=pltpu.VMEM), pl.BlockSpec(memory_space=pl.ANY)
    return pl.pallas_call(
        functools.partial(layer_kernel, dims),
        out_shape=[
            shape(whole, bf16),
            shape(whole, bf16),
            shape(whole, f32),
            shape(whole, f32),
            shape(turned, bf16),
            shape((FEED,) + lead + tile, bf16),
            shape((CHUNKS,) + lead + tile, bf16),
            shape((CHUNKS,) + tile, f32),
            shape((UNIT, HIDDEN), f32),
            shape(small_tile, f32),
        ],
        in_specs=[vmem] * 8 + [anywhere] * 8,
        out_specs=[anywhere] * 7 + [vmem] * 3,
        scratch_shapes=[
            room(whole, bf16),
            room(whole, bf16),
            room((CHUNKS,) + lead + tile, bf16),
            room((UNIT, HIDDEN), bf16),
            room(lead + small_tile, f32),
            room((8, WIDTH), f32),
            room((8, WIDE), f32),
            room((LENGTH, LENGTH), bf16),
            room((LENGTH, LENGTH), bf16),
            room((6, LENGTH, WIDE), bf16),
            room(whole, bf16),
            room(turned, bf16),
            room(turned, bf16),
            room(whole, f32),
            room(whole, f32),
            room(whole, f32),
            room(whole, f32),
            room((2,) + lead + tile, bf16),
            room((8, WIDE), f32),
            room((8, WIDTH), f32),
            room(lead + small_tile, f32),
            room((TERMS_AHEAD + 1,) + chip + tile, bf16),
            room((ROOMS, 2, 4) + tile, bf16),
            room((ROOMS, 6) + tile, bf16),
            room((ROOMS, 3) + tile, bf16),
            room(chip + small_tile, f32),
            room((2, 4) + small_tile, f32),
            room((6,) + small_tile, f32),
            room((3,) + small_tile, f32),
            dma((CHUNKS, 4, most)),
            dma((CHUNKS, 4, most)),
            dma((4, most)),
            dma((4, most)),
            dma((19,)),
            dma((12,)),
            dma((2,)),
            dma((TERMS_AHEAD + 1,)),
            dma((CHUNKS, 4, most)),
            dma((CHUNKS, 4, most)),
            dma((4, most)),
            dma((4, most)),
            pltpu.SemaphoreType.REGULAR,
        ],
        compiler_params=pltpu.CompilerParams(
            collective_id=0, has_side_effects=True, vmem_limit_bytes=VMEM_LIMIT
        ),
        name="layer",
    )(crops, kept, *small, tokens, cotangent, *shards)


def place_kernel(*refs):
    result, input_grad, owned, owned_up, small = refs[:5]
    result_out, input_grad_out, query, key, value, out, up, down = refs[5:13]
    vectors, bias_up = refs[13:18], refs[18]
    sems = refs[19]
    copies = [(result, result_out.at[0]), (input_grad, input_grad_out.at[0]), (owned_up, up)]
    for index in range(CHUNKS):
        if index < 16:
            group, half = index // 4, index % 4
            if half >= 2:
                continue
            target = down.at[pl.ds(group * UNIT, UNIT), pl.ds(half * WIDE, WIDE)]
        else:
            matrix_out = (out, query, key, value)[(index - 16) // 2]
            target = matrix_out.at[:, pl.ds((index % 2) * WIDE, WIDE)]
        copies.append((owned.at[index], target))
    items = [
        pltpu.make_async_copy(source, target, sems.at[index])
        for index, (source, target) in enumerate(copies)
    ]
    for item in items:
        item.start()
    for index in range(4):
        vectors[index][...] = small[0, index * UNIT : (index + 1) * UNIT]
    vectors[4][...] = small[2, 0:UNIT]
    bias_up[...] = small[1, :]
    for item in items:
        item.wait()


def place_results(result, input_grad, owned, owned_up, small):
    f32, bf16 = jnp.float32, jnp.bfloat16
    shape = jax.ShapeDtypeStruct
    vmem, anywhere = pl.BlockSpec(memory_space=pltpu.VMEM), pl.BlockSpec(memory_space=pl.ANY)
    return pl.pallas_call(
        place_kernel,
        out_shape=[shape((1, LENGTH, WIDTH), bf16)] * 2
        + [shape((UNIT, WIDTH), f32)] * 4
        + [shape((UNIT, HIDDEN), f32), shape((4 * UNIT, WIDTH), f32)]
        + [shape((UNIT,), f32)] * 5
        + [shape((4 * UNIT,), f32)],
        in_specs=[anywhere] * 4 + [vmem],
        out_specs=[vmem] * 14,
        scratch_shapes=[pltpu.SemaphoreType.DMA((19,))],
        name="results",
    )(result, input_grad, owned, owned_up, small)


def body(
    tokens,
    crop_ids,
    kv_mask,
    norm1_gain,
    norm1_bias,
    w_query,
    w_key,
    w_value,
    w_out,
    norm2_gain,
    norm2_bias,
    w_up,
    up_bias,
    w_down,
    down_bias,
    cotangent,
):
    inner = lax.axis_size("dp") // (2 * OUTER)
    dims = (OUTER, inner, lax.axis_size("fsdp"))
    fits = (
        tokens.shape == (1, LENGTH, WIDTH)
        and w_up.shape == (UNIT, HIDDEN)
        and w_down.shape == (HIDDEN // WIDTH * UNIT, WIDTH)
        and dims == (2, 2, 4)
    )
    if not fits:
        return general_body(
            tokens,
            crop_ids,
            kv_mask,
            norm1_gain,
            norm1_bias,
            w_query,
            w_key,
            w_value,
            w_out,
            norm2_gain,
            norm2_bias,
            w_up,
            up_bias,
            w_down,
            down_bias,
            cotangent,
        )
    small = [
        vector.reshape(1, -1)
        for vector in (norm1_gain, norm1_bias, norm2_gain, norm2_bias, down_bias, up_bias)
    ]
    pixels, grads = tokens.reshape(LENGTH, WIDTH), cotangent.reshape(LENGTH, WIDTH)
    shards = (w_query, w_key, w_value, w_out, w_up, w_down)
    result, input_grad, *_, owned, owned_up, owned_small = layer(
        dims, pixels, grads, crop_ids, kv_mask, small, shards
    )
    (
        output,
        grad_tokens,
        grad_query,
        grad_key,
        grad_value,
        grad_out,
        grad_up,
        grad_down,
        grad_gain_one,
        grad_bias_one,
        grad_gain_two,
        grad_bias_two,
        grad_bias_down,
        grad_bias_up,
    ) = place_results(result, input_grad, owned, owned_up, owned_small)
    return (
        output,
        grad_tokens,
        grad_gain_one,
        grad_bias_one,
        grad_query,
        grad_key,
        grad_value,
        grad_out,
        grad_gain_two,
        grad_bias_two,
        grad_up,
        grad_bias_up,
        grad_down,
        grad_bias_down,
    )


def solution(mesh):
    return jax.shard_map(
        body,
        mesh=mesh,
        in_specs=(
            P(("dp", "fsdp"), None, None),
            P(("dp", "fsdp"), None),
            P(("dp", "fsdp"), None),
            P(("dp", "fsdp")),
            P(("dp", "fsdp")),
            P(("dp", "fsdp"), None),
            P(("dp", "fsdp"), None),
            P(("dp", "fsdp"), None),
            P(("dp", "fsdp"), None),
            P(("dp", "fsdp")),
            P(("dp", "fsdp")),
            P(("dp", "fsdp"), None),
            P(("dp", "fsdp")),
            P(("dp", "fsdp"), None),
            P(("dp", "fsdp")),
            P(("dp", "fsdp"), None, None),
        ),
        out_specs=(
            P(("dp", "fsdp"), None, None),
            P(("dp", "fsdp"), None, None),
            P(("dp", "fsdp")),
            P(("dp", "fsdp")),
            P(("dp", "fsdp"), None),
            P(("dp", "fsdp"), None),
            P(("dp", "fsdp"), None),
            P(("dp", "fsdp"), None),
            P(("dp", "fsdp")),
            P(("dp", "fsdp")),
            P(("dp", "fsdp"), None),
            P(("dp", "fsdp")),
            P(("dp", "fsdp"), None),
            P(("dp", "fsdp")),
        ),
        check_vma=False,
    )
```

```python
import functools
import itertools

import jax
import jax.numpy as jnp
from jax import lax
from jax.experimental import pallas as pl
from jax.experimental.pallas import tpu as pltpu
from jax.sharding import PartitionSpec as P

HEADS = 16
BLOCK = 512
MESH = pl.DeviceIdType.MESH
WIDE = 512
OUTER = 2


class Place:
    def __init__(self, dims):
        self.size = {"a": dims[0], "b": dims[1], "c": 2, "z": dims[2]}
        dp = lax.axis_index("dp")
        self.at = {
            "a": dp // (2 * dims[1]),
            "b": (dp // 2) % dims[1],
            "c": dp % 2,
            "z": lax.axis_index("fsdp"),
        }

    def moved(self, axis, step):
        spot = dict(self.at)
        spot[axis] = (spot[axis] + step) % self.size[axis]
        return spot

    def device(self, axis, step):
        spot = self.moved(axis, step)
        return ((spot["a"] * self.size["b"] + spot["b"]) * 2 + spot["c"], spot["z"])

    def partners(self, axis):
        return range(1, self.size[axis])

    def greet(self):
        barrier = pltpu.get_barrier_semaphore()
        count = 0
        for axis in "abcz":
            for step in self.partners(axis):
                pl.semaphore_signal(
                    barrier, 1, device_id=self.device(axis, step), device_id_type=MESH
                )
                count += 1
        pl.semaphore_wait(barrier, count)


def pieces_of(rows, columns, unit):
    wide = min(WIDE, columns)
    return [
        (row, unit, column, wide)
        for row in range(0, rows, unit)
        for column in range(0, columns, wide)
    ]


def gather_kernel(dims, orders, lag, ahead, pieces, *refs):
    count = len(pieces)
    shards, wholes = refs[:count], refs[count : 2 * count]
    local_sem, send_sem, recv_sem = refs[2 * count :]
    place = Place(dims)
    place.greet()
    chunks = [
        (shard.at[pl.ds(ro, rn), pl.ds(co, cn)], whole, pl.ds(ro, rn), pl.ds(co, cn))
        for shard, whole, items in zip(shards, wholes, pieces)
        for ro, rn, co, cn in items
    ]
    total = len(chunks)
    sent, kept = [], []

    def region(index, done, spot):
        _, whole, rows, columns = chunks[index]
        lead = tuple(slice(None) if axis in done else spot[axis] for axis in "abcz")
        return whole.at[lead + (rows, columns)]

    def copy(index, stage, step, axis, source, target):
        return pltpu.make_async_remote_copy(
            source,
            target,
            send_sem.at[index, stage, step - 1],
            recv_sem.at[index, stage, step - 1],
            device_id=place.device(axis, step),
            device_id_type=MESH,
        )

    def send(index, stage):
        order = orders[index % len(orders)]
        axis, done = order[stage], order[:stage]
        target = region(index, done, place.at)
        for step in place.partners(axis):
            item = copy(index, stage, step, axis, target if done else chunks[index][0], target)
            item.start()
            sent.append(item)

    def receive(index, stage):
        order = orders[index % len(orders)]
        axis, done = order[stage], order[:stage]
        for step in place.partners(axis):
            target = region(index, done, place.moved(axis, place.size[axis] - step))
            copy(index, stage, step, axis, target, target).wait_recv()

    def begin(index):
        if index < total:
            item = pltpu.make_async_copy(
                chunks[index][0], region(index, "", place.at), local_sem.at[index]
            )
            item.start()
            kept.append(item)
            send(index, 0)

    for index in range(ahead):
        begin(index)
    for tick in range(total + 3 * lag):
        begin(tick + ahead)
        for stage in range(4):
            index = tick - stage * lag
            if 0 <= index < total:
                receive(index, stage)
                if stage == 0:
                    kept[index].wait()
                if stage < 3:
                    send(index, stage + 1)
    for item in sent:
        item.wait_send()


def gather(dims, shards, unit, lag=3, ahead=6):
    pieces = [pieces_of(*shard.shape, min(unit, shard.shape[0])) for shard in shards]
    total = sum(len(items) for items in pieces)
    most = max(dims) - 1
    anywhere = pl.BlockSpec(memory_space=pl.ANY)
    orders = ("zbac", "zabc", "zbac", "zabc", "bzac", "azbc")
    wholes = pl.pallas_call(
        functools.partial(gather_kernel, dims, orders, lag, ahead, pieces),
        out_shape=[
            jax.ShapeDtypeStruct(dims[:2] + (2, dims[2]) + shard.shape, shard.dtype)
            for shard in shards
        ],
        in_specs=[anywhere] * len(shards),
        out_specs=[anywhere] * len(shards),
        scratch_shapes=[
            pltpu.SemaphoreType.DMA((total,)),
            pltpu.SemaphoreType.DMA((total, 4, most)),
            pltpu.SemaphoreType.DMA((total, 4, most)),
        ],
        compiler_params=pltpu.CompilerParams(collective_id=0, has_side_effects=True),
        name="gather",
    )(*shards)
    return [whole.reshape((-1, whole.shape[-1])) for whole in wholes]


def scatter_kernel(dims, lag, ahead, pieces, *refs):
    count = len(pieces)
    terms, owned = refs[:count], refs[count : 2 * count]
    main = refs[2 * count : 2 * count + 7]
    side = refs[2 * count + 7 : 2 * count + 12]
    local_sem, send_sem, recv_sem = refs[2 * count + 12 :]
    place = Place(dims)
    place.greet()
    spot = place.at
    chunks = []
    for array, items in enumerate(pieces):
        for ro, rn, co, cn in items:
            index = len(chunks)
            if array == 0:
                rooms = side
                order = "ab"
            else:
                half = (index - 1) // 2
                order = "ab" if index % 2 else "ba"
                first, second = (main[2], main[4]) if index % 2 else (main[3], main[5])
                rooms = (
                    main[0].at[index - 1],
                    main[1].at[index - 1],
                    first.at[half],
                    second.at[half],
                    main[6].at[index - 1],
                )
            chunks.append((terms[array], owned[array], pl.ds(ro, rn), pl.ds(co, cn), order, rooms))
    total = len(chunks)
    sent, kept = [], []

    def copy(index, stage, step, axis, source, target):
        return pltpu.make_async_remote_copy(
            source,
            target,
            send_sem.at[index, stage, step - 1],
            recv_sem.at[index, stage, step - 1],
            device_id=place.device(axis, step),
            device_id_type=MESH,
        )

    def send(index, stage, step, axis, source, target):
        item = copy(index, stage, step, axis, source, target)
        item.start()
        sent.append(item)

    def begin(index):
        if index < total:
            term, _, rows, columns, _, rooms = chunks[index]
            send(index, 0, 1, "c", term.at[:, :, 1 - spot["c"], :, rows, columns], rooms[1])
            item = pltpu.make_async_copy(
                term.at[:, :, spot["c"], :, rows, columns], rooms[0], local_sem.at[index]
            )
            item.start()
            kept.append(item)

    def await_all(index, stage, axis, room):
        for step in place.partners(axis):
            copy(index, stage, step, axis, room.at[step - 1], room.at[step - 1]).wait_recv()

    def pick(order, first, second):
        return (first, second) if order == "ab" else (second, first)

    def after_core(index):
        order, (own, other, came, _, _) = chunks[index][4:]
        kept[index].wait()
        copy(index, 0, 1, "c", other, other).wait_recv()
        axis, rest = order

        def add(where):
            for item in range(place.size[rest]):
                at = pick(order, where, item)
                own[at] = own[at] + other[at]

        for step in place.partners(axis):
            where = place.moved(axis, step)[axis]
            add(where)
            source = own.at[where] if order == "ab" else own.at[:, where]
            send(index, 1, step, axis, source, came.at[step - 1])
        add(spot[axis])

    def after_first(index):
        order, (own, _, came, later, _) = chunks[index][4:]
        axis, rest = order
        await_all(index, 1, axis, came)

        def add(where):
            at = pick(order, spot[axis], where)
            value = own[at].astype(jnp.float32)
            for step in place.partners(axis):
                value = value + came[step - 1, where].astype(jnp.float32)
            own[at] = value.astype(own.dtype)

        for step in place.partners(rest):
            where = place.moved(rest, step)[rest]
            add(where)
            at = pick(order, spot[axis], where)
            send(index, 2, step, rest, own.at[at], later.at[step - 1])
        add(spot[rest])

    def after_second(index):
        _, result, rows, columns, order, (own, _, _, later, last) = chunks[index]
        rest = order[1]
        await_all(index, 2, rest, later)

        def add(where):
            value = own[spot["a"], spot["b"], where].astype(jnp.float32)
            for step in place.partners(rest):
                value = value + later[step - 1, where].astype(jnp.float32)
            return value

        for step in place.partners("z"):
            where = place.moved("z", step)["z"]
            own[spot["a"], spot["b"], where] = add(where).astype(own.dtype)
            send(index, 3, step, "z", own.at[spot["a"], spot["b"], where], last.at[step - 1])
        result[rows, columns] = add(spot["z"])

    def after_last(index):
        _, result, rows, columns, _, (_, _, _, _, last) = chunks[index]
        await_all(index, 3, "z", last)
        value = result[rows, columns]
        for step in place.partners("z"):
            value = value + last[step - 1].astype(jnp.float32)
        result[rows, columns] = value

    for index in range(ahead):
        begin(index)
    for tick in range(total + 3 * lag):
        begin(tick + ahead)
        for stage, work in enumerate((after_core, after_first, after_second, after_last)):
            index = tick - stage * lag
            if 0 <= index < total:
                work(index)
    for item in sent:
        item.wait_send()


def rooms_of(dims, many, unit, wide, dtype):
    outer, inner, depth = dims
    ones, twos = (many + 1) // 2, many // 2
    tail = (unit, wide)
    return [
        pltpu.VMEM((many, outer, inner, depth) + tail, dtype),
        pltpu.VMEM((many, outer, inner, depth) + tail, dtype),
        pltpu.VMEM((ones, outer - 1, inner, depth) + tail, dtype),
        pltpu.VMEM((twos, inner - 1, outer, depth) + tail, dtype),
        pltpu.VMEM((ones, inner - 1, depth) + tail, dtype),
        pltpu.VMEM((twos, outer - 1, depth) + tail, dtype),
        pltpu.VMEM((many, depth - 1) + tail, dtype),
    ]


def scatter(dims, small, terms, unit, lag=2, ahead=4):
    outer, inner, depth = dims
    devices = 2 * outer * inner * depth
    lead = (outer, inner, 2, depth)
    arrays = [small.reshape(lead + small.shape[1:])] + [
        term.reshape(lead + (term.shape[0] // devices, term.shape[1])) for term in terms
    ]
    pieces = [pieces_of(*arrays[0].shape[4:], arrays[0].shape[4])]
    pieces += [pieces_of(*array.shape[4:], unit) for array in arrays[1:]]
    total = sum(len(items) for items in pieces)
    most = max(dims) - 1
    tail = small.shape[1:]
    side = [
        pltpu.VMEM((outer, inner, depth) + tail, jnp.float32),
        pltpu.VMEM((outer, inner, depth) + tail, jnp.float32),
        pltpu.VMEM((outer - 1, inner, depth) + tail, jnp.float32),
        pltpu.VMEM((inner - 1, depth) + tail, jnp.float32),
        pltpu.VMEM((depth - 1,) + tail, jnp.float32),
    ]
    return pl.pallas_call(
        functools.partial(scatter_kernel, dims, lag, ahead, pieces),
        out_shape=[jax.ShapeDtypeStruct(array.shape[4:], jnp.float32) for array in arrays],
        in_specs=[pl.BlockSpec(memory_space=pl.ANY)] * len(arrays),
        out_specs=[pl.BlockSpec(memory_space=pltpu.VMEM)] * len(arrays),
        scratch_shapes=rooms_of(dims, total - 1, unit, WIDE, jnp.bfloat16)
        + side
        + [
            pltpu.SemaphoreType.DMA((total,)),
            pltpu.SemaphoreType.DMA((total, 4, most)),
            pltpu.SemaphoreType.DMA((total, 4, most)),
        ],
        compiler_params=pltpu.CompilerParams(
            collective_id=1, has_side_effects=True, vmem_limit_bytes=60 << 20
        ),
        name="scatter",
    )(*arrays)


HIGH = lax.Precision.HIGHEST
norm_eps = 1e-05


def norm_affine(values, gain, shift):
    mean = jnp.mean(values, axis=-1, keepdims=True)
    centred = values - mean
    spread = jnp.mean(centred * centred, axis=-1, keepdims=True)
    return centred * lax.rsqrt(spread + norm_eps) * gain + shift


def feature(values):
    return jax.nn.elu(values) + 1.0


def gelu_exact(values):
    return jax.nn.gelu(values, approximate=False)


def allowed_weight(crop, keymask):
    places = jnp.arange(crop.shape[0])
    earlier = places[None, :] <= places[:, None]
    same = crop[:, None] == crop[None, :]
    visible = (keymask[None, :] > 0) | (places[None, :] == places[:, None])
    return (earlier & same & visible).astype(jnp.float32)


def attend_forward(carry, pieces):
    state, norm_state, prev_crop = carry
    query_feat, key_feat, values, crop, keymask = pieces
    weight = allowed_weight(crop, keymask)
    scores = (
        jnp.einsum("ihe,jhe->hij", query_feat, key_feat, preferred_element_type=jnp.float32)
        * weight[None]
    )
    value_wide = values.astype(jnp.float32)
    query_wide = query_feat.astype(jnp.float32)
    key_wide = key_feat.astype(jnp.float32)
    numer = jnp.einsum("hij,jhe->ihe", scores, value_wide, precision=HIGH)
    denom = jnp.sum(scores, axis=2).T
    follows = (crop == prev_crop).astype(jnp.float32)
    numer = numer + follows[:, None, None] * jnp.einsum(
        "ihe,hef->ihf", query_wide, state, precision=HIGH
    )
    denom = denom + follows[:, None] * jnp.einsum(
        "ihe,he->ih", query_wide, norm_state, precision=HIGH
    )
    last_crop = crop[crop.shape[0] - 1]
    carried = (prev_crop == last_crop).astype(jnp.float32)
    select = ((crop == last_crop) & (keymask > 0)).astype(jnp.float32)
    chosen = key_wide * select[:, None, None]
    new_state = carried * state + jnp.einsum("jhe,jhf->hef", chosen, value_wide, precision=HIGH)
    new_norm = carried * norm_state + jnp.sum(chosen, axis=0)
    return ((new_state, new_norm, last_crop), (numer / denom[:, :, None], denom, state, norm_state))


def attend_backward(carry, pieces):
    grad_state, grad_norm = carry
    (
        query_feat,
        key_feat,
        values,
        crop,
        keymask,
        prev_crop,
        state,
        norm_state,
        grad_numer,
        grad_denom,
    ) = pieces
    weight = allowed_weight(crop, keymask)
    scores = (
        jnp.einsum("ihe,jhe->hij", query_feat, key_feat, preferred_element_type=jnp.float32)
        * weight[None]
    )
    value_wide = values.astype(jnp.float32)
    query_wide = query_feat.astype(jnp.float32)
    key_wide = key_feat.astype(jnp.float32)
    grad_scores = (
        jnp.einsum("ihe,jhe->hij", grad_numer, value_wide, precision=HIGH)
        + grad_denom.T[:, :, None]
    ) * weight[None]
    follows = (crop == prev_crop).astype(jnp.float32)
    last_crop = crop[crop.shape[0] - 1]
    carried = (prev_crop == last_crop).astype(jnp.float32)
    select = ((crop == last_crop) & (keymask > 0)).astype(jnp.float32)
    grad_query = jnp.einsum("hij,jhe->ihe", grad_scores, key_wide, precision=HIGH)
    grad_query = grad_query + follows[:, None, None] * (
        jnp.einsum("ihf,hef->ihe", grad_numer, state, precision=HIGH)
        + grad_denom[:, :, None] * norm_state[None]
    )
    grad_key = jnp.einsum("hij,ihe->jhe", grad_scores, query_wide, precision=HIGH)
    grad_key = grad_key + select[:, None, None] * (
        jnp.einsum("jhf,hef->jhe", value_wide, grad_state, precision=HIGH) + grad_norm[None]
    )
    grad_value = jnp.einsum("hij,ihe->jhe", scores, grad_numer, precision=HIGH)
    grad_value = grad_value + select[:, None, None] * jnp.einsum(
        "jhe,hef->jhf", key_wide, grad_state, precision=HIGH
    )
    query_kept = query_wide * follows[:, None, None]
    earlier_state = carried * grad_state + jnp.einsum(
        "ihe,ihf->hef", query_kept, grad_numer, precision=HIGH
    )
    earlier_norm = carried * grad_norm + jnp.einsum(
        "ihe,ih->he", query_kept, grad_denom, precision=HIGH
    )
    return ((earlier_state, earlier_norm), (grad_query, grad_key, grad_value))


def split_blocks(array):
    blocks = array.shape[0] // BLOCK
    return array.reshape((blocks, BLOCK) + array.shape[1:])


def attend_slot(pieces):
    query_feat, key_feat, values, crop, keymask = pieces
    length, heads, head_width = query_feat.shape
    start = (
        jnp.zeros((heads, head_width, head_width), jnp.float32),
        jnp.zeros((heads, head_width), jnp.float32),
        jnp.int32(-1),
    )
    finish, (mixed, denom, states, norms) = lax.scan(
        attend_forward,
        start,
        (
            split_blocks(query_feat),
            split_blocks(key_feat),
            split_blocks(values),
            split_blocks(crop),
            split_blocks(keymask),
        ),
    )
    return (mixed.reshape(length, heads, head_width), denom.reshape(length, heads), states, norms)


def attend_slot_back(pieces):
    query_feat, key_feat, values, crop, keymask, states, norms, grad_numer, grad_denom = pieces
    length, heads, head_width = query_feat.shape
    crop_blocks = split_blocks(crop)
    prev_crops = jnp.concatenate([jnp.full((1,), -1, jnp.int32), crop_blocks[:-1, -1]])
    start = (
        jnp.zeros((heads, head_width, head_width), jnp.float32),
        jnp.zeros((heads, head_width), jnp.float32),
    )
    finish, (grad_query, grad_key, grad_value) = lax.scan(
        attend_backward,
        start,
        (
            split_blocks(query_feat),
            split_blocks(key_feat),
            split_blocks(values),
            crop_blocks,
            split_blocks(keymask),
            prev_crops,
            states,
            norms,
            split_blocks(grad_numer),
            split_blocks(grad_denom),
        ),
        reverse=True,
    )
    shape = (length, heads, head_width)
    return (grad_query.reshape(shape), grad_key.reshape(shape), grad_value.reshape(shape))


def general_body(
    tokens,
    crop_ids,
    kv_mask,
    norm1_gain,
    norm1_bias,
    w_query,
    w_key,
    w_value,
    w_out,
    norm2_gain,
    norm2_bias,
    w_up,
    up_bias,
    w_down,
    down_bias,
    cotangent,
):
    slots, length, width = tokens.shape
    heads = HEADS
    head_width = width // heads
    count = slots * length
    devices = lax.axis_size("dp") * lax.axis_size("fsdp")
    dims = (OUTER, lax.axis_size("dp") // (2 * OUTER), lax.axis_size("fsdp"))
    unit = width // devices
    packed = jnp.concatenate([norm1_gain, norm1_bias, norm2_gain, norm2_bias, down_bias, up_bias])
    packed = jnp.pad(packed, (0, 16 * 128 - packed.shape[0])).reshape(16, 128)
    vectors, full_query, full_key, full_value, full_out, full_up, full_down = gather(
        dims, [packed, w_query, w_key, w_value, w_out, w_up, w_down], unit
    )
    vectors = vectors.reshape(devices, 16 * 128)
    gain_one, bias_one, gain_two, bias_two, full_down_bias = (
        vectors[:, index * unit : (index + 1) * unit].reshape(-1) for index in range(5)
    )
    full_up_bias = vectors[:, 5 * unit : 5 * unit + up_bias.shape[0]].reshape(-1)
    inputs = tokens.reshape(count, width).astype(jnp.float32)
    normed_wide, pull_one = jax.vjp(
        norm_affine, inputs, gain_one.astype(jnp.float32), bias_one.astype(jnp.float32)
    )
    normed = normed_wide.astype(jnp.bfloat16)
    query = jnp.dot(normed, full_query, preferred_element_type=jnp.float32)
    keys = jnp.dot(normed, full_key, preferred_element_type=jnp.float32)
    values = jnp.dot(normed, full_value, preferred_element_type=jnp.float32).astype(jnp.bfloat16)
    query_wide, pull_query = jax.vjp(feature, query)
    key_wide, pull_key = jax.vjp(feature, keys)
    query_feat = query_wide.astype(jnp.bfloat16).reshape(slots, length, heads, head_width)
    key_feat = key_wide.astype(jnp.bfloat16).reshape(slots, length, heads, head_width)
    value_heads = values.reshape(slots, length, heads, head_width)
    mixed_wide, denom, states, norms = lax.map(
        attend_slot, (query_feat, key_feat, value_heads, crop_ids, kv_mask)
    )
    mixed = mixed_wide.reshape(count, width).astype(jnp.bfloat16)
    middle = inputs + jnp.dot(mixed, full_out, preferred_element_type=jnp.float32)
    normed_two_wide, pull_two = jax.vjp(
        norm_affine, middle, gain_two.astype(jnp.float32), bias_two.astype(jnp.float32)
    )
    normed_two = normed_two_wide.astype(jnp.bfloat16)
    upper = jnp.dot(normed_two, full_up, preferred_element_type=jnp.float32) + full_up_bias.astype(
        jnp.float32
    )
    hidden_wide, pull_gelu = jax.vjp(gelu_exact, upper)
    hidden = hidden_wide.astype(jnp.bfloat16)
    result = (
        middle
        + jnp.dot(hidden, full_down, preferred_element_type=jnp.float32)
        + full_down_bias.astype(jnp.float32)
    )
    output = result.astype(jnp.bfloat16).reshape(slots, length, width)
    back_up, back_down = full_up, full_down
    back_query, back_key, back_value, back_out = full_query, full_key, full_value, full_out
    grad_out = cotangent.reshape(count, width)
    grad_down_bias = jnp.sum(grad_out.astype(jnp.float32), axis=0)
    grad_w_down = jnp.dot(hidden.T, grad_out, preferred_element_type=jnp.float32).astype(jnp.bfloat16)
    grad_hidden = jnp.dot(grad_out, back_down.T, preferred_element_type=jnp.float32)
    grad_upper = pull_gelu(grad_hidden)[0].astype(jnp.bfloat16)
    grad_up_bias = jnp.sum(grad_upper.astype(jnp.float32), axis=0)
    grad_w_up = jnp.dot(normed_two.T, grad_upper, preferred_element_type=jnp.float32).astype(jnp.bfloat16)
    grad_normed_two = jnp.dot(grad_upper, back_up.T, preferred_element_type=jnp.float32)
    grad_middle_part, grad_gain_two, grad_bias_two = pull_two(grad_normed_two)
    grad_middle = grad_out.astype(jnp.float32) + grad_middle_part
    grad_attended = grad_middle.astype(jnp.bfloat16)
    grad_w_out = jnp.dot(mixed.T, grad_attended, preferred_element_type=jnp.float32).astype(jnp.bfloat16)
    grad_mixed = jnp.dot(grad_attended, back_out.T, preferred_element_type=jnp.float32).reshape(
        slots, length, heads, head_width
    )
    grad_numer = grad_mixed / denom[..., None]
    grad_denom = -jnp.sum(grad_mixed * mixed_wide, axis=-1) / denom
    grad_query_feat, grad_key_feat, grad_values = lax.map(
        attend_slot_back,
        (
            query_feat,
            key_feat,
            value_heads,
            crop_ids,
            kv_mask,
            states,
            norms,
            grad_numer,
            grad_denom,
        ),
    )
    grad_query = pull_query(grad_query_feat.reshape(count, width))[0].astype(jnp.bfloat16)
    grad_keys = pull_key(grad_key_feat.reshape(count, width))[0].astype(jnp.bfloat16)
    grad_values = grad_values.reshape(count, width).astype(jnp.bfloat16)
    grad_w_query = jnp.dot(normed.T, grad_query, preferred_element_type=jnp.float32).astype(jnp.bfloat16)
    grad_w_key = jnp.dot(normed.T, grad_keys, preferred_element_type=jnp.float32).astype(jnp.bfloat16)
    grad_w_value = jnp.dot(normed.T, grad_values, preferred_element_type=jnp.float32).astype(jnp.bfloat16)
    grad_normed = jnp.dot(grad_query, back_query.T, preferred_element_type=jnp.float32)
    grad_normed = grad_normed + jnp.dot(grad_keys, back_key.T, preferred_element_type=jnp.float32)
    grad_normed = grad_normed + jnp.dot(
        grad_values, back_value.T, preferred_element_type=jnp.float32
    )
    grad_input_part, grad_gain_one, grad_bias_one = pull_one(grad_normed)
    small = jnp.concatenate(
        [
            vector.reshape(devices, -1)
            for vector in (
                grad_gain_one,
                grad_bias_one,
                grad_gain_two,
                grad_bias_two,
                grad_down_bias,
                grad_up_bias,
            )
        ],
        axis=1,
    )
    small = jnp.pad(small, ((0, 0), (0, 8 * 128 - small.shape[1]))).reshape(devices, 8, 128)
    small, own_up, own_down, own_query, own_key, own_value, own_out = scatter(
        dims,
        small,
        [grad_w_up, grad_w_down, grad_w_query, grad_w_key, grad_w_value, grad_w_out],
        unit,
    )
    small = small.reshape(8 * 128)
    own_gain_one, own_bias_one, own_gain_two, own_bias_two, own_down_bias = (
        small[index * unit : (index + 1) * unit] for index in range(5)
    )
    own_up_bias = small[5 * unit : 5 * unit + up_bias.shape[0]]
    input_grad = (grad_middle + grad_input_part).astype(jnp.bfloat16).reshape(slots, length, width)
    return (
        output,
        input_grad,
        own_gain_one,
        own_bias_one,
        own_query,
        own_key,
        own_value,
        own_out,
        own_gain_two,
        own_bias_two,
        own_up,
        own_up_bias,
        own_down,
        own_down_bias,
    )


LENGTH = 512
WIDTH = 1024
HIDDEN = 4096
UNIT = 32
CHUNKS = 24
FEED = 8
ROOMS = 12
LAG = 3
LATE = 3 * LAG
AHEAD = 4
PASS_AHEAD = 2
TERMS_AHEAD = 3
TERMS_START = 26
PASS_AFTER = 2
TERMS_PASS_AFTER = 2
VMEM_LIMIT = 63 << 20


def when(condition):
    if isinstance(condition, bool):
        return (lambda work: work()) if condition else (lambda work: None)
    return pl.when(condition)


def each(count, work):
    def step(index, carry):
        work(index)
        return carry

    lax.fori_loop(0, count, step, 0)


def dot(left, right):
    return jnp.dot(left, right, preferred_element_type=jnp.float32)


def dot_nt(left, right):
    return lax.dot_general(
        left, right, (((1,), (1,)), ((), ())), preferred_element_type=jnp.float32
    )


def dot_tn(left, right):
    return lax.dot_general(
        left, right, (((0,), (0,)), ((), ())), preferred_element_type=jnp.float32
    )


def by_order(place, orders, index, work):
    turn = (index + 3 * place.at["c"]) % len(orders)
    for order in dict.fromkeys(orders):
        turns = [number for number, item in enumerate(orders) if item == order]
        match = turn == turns[0]
        for number in turns[1:]:
            match = match | (turn == number)

        @pl.when(match)
        def _(order=order):
            work(order)


class Mover:
    def __init__(self, place, send_sem, recv_sem):
        self.place, self.send_sem, self.recv_sem = place, send_sem, recv_sem

    def copy(self, lead, stage, step, axis, source, target):
        at = lead + (stage, step - 1)
        return pltpu.make_async_remote_copy(
            source,
            target,
            self.send_sem.at[at],
            self.recv_sem.at[at],
            device_id=self.place.device(axis, step),
            device_id_type=MESH,
        )


class Gather(Mover):
    def region(self, chunk, done, spot):
        lead = tuple(slice(None) if axis in done else spot[axis] for axis in "abcz")
        return chunk.at[lead]

    def unless_passed(self, axis, step, work):
        z = self.place.at["z"]
        if axis == "z" and step == 3:
            pl.when(z != 0)(work)
        elif axis == "z" and step == 1:
            pl.when(z != 3)(work)
        else:
            work()

    def send(self, chunk, lead, order, stage):
        axis, done = order[stage], order[:stage]
        source = self.region(chunk, done, self.place.at)
        for step in self.place.partners(axis):
            self.unless_passed(
                axis, step, self.copy(lead, stage, step, axis, source, source).start
            )

    def passing(self, chunk, lead, order):
        stage = order.index("z")
        spot = dict(self.place.at)
        z = spot["z"]
        spot["z"] = 3 * (2 - z)
        source = self.region(chunk, order[:stage], spot)
        came = self.copy(lead, stage, 2, "z", source, source)
        onward = pltpu.make_async_remote_copy(
            source,
            source,
            self.send_sem.at[lead + (stage, 3)],
            self.recv_sem.at[lead + (stage, 2 * (z - 1))],
            device_id={"fsdp": 3 * (z - 1)},
            device_id_type=MESH,
        )
        return came, onward

    def pass_on(self, chunk, lead, order):
        z = self.place.at["z"]

        @pl.when((z == 1) | (z == 2))
        def _():
            came, onward = self.passing(chunk, lead, order)
            came.wait_recv()
            onward.start()

    def receive(self, chunk, lead, order, stage):
        axis, done = order[stage], order[:stage]
        z = self.place.at["z"]
        for step in self.place.partners(axis):
            spot = self.place.moved(axis, self.place.size[axis] - step)
            target = self.region(chunk, done, spot)
            item = self.copy(lead, stage, step, axis, target, target)
            if axis == "z" and step == 2:
                pl.when((z == 0) | (z == 3))(item.wait_recv)
            else:
                item.wait_recv()

    def drain(self, chunk, lead, order):
        z = self.place.at["z"]
        for stage in range(4):
            axis, done = order[stage], order[:stage]
            source = self.region(chunk, done, self.place.at)
            for step in self.place.partners(axis):
                self.unless_passed(
                    axis, step, self.copy(lead, stage, step, axis, source, source).wait_send
                )
            if axis == "z":

                @pl.when((z == 1) | (z == 2))
                def _():
                    self.passing(chunk, lead, order)[1].wait_send()


class Weights(Gather):
    orders = ("bzac", "azbc", "zbac", "azbc", "bzac", "zabc")

    def __init__(self, place, buffer, send_sem, recv_sem):
        super().__init__(place, send_sem, recv_sem)
        self.buffer, self.total = buffer, buffer.shape[0]

    def by_order(self, index, work):
        by_order(self.place, self.orders, index, work)

    def begin(self, index):
        @when(index < self.total)
        def _():
            self.by_order(
                index, lambda order: self.send(self.buffer.at[index], (index,), order, 0)
            )

    def pass_on_at(self, index, stage):
        @when((index >= 0) & (index < self.total))
        def _():
            def work(order):
                if order.index("z") == stage:
                    self.pass_on(self.buffer.at[index], (index,), order)

            self.by_order(index, work)

    def tick(self, now):
        self.begin(now + AHEAD)
        self.pass_on_at(now + PASS_AHEAD, 0)
        self.pass_on_at(now - PASS_AFTER, 1)
        for stage in range(4):
            index = now - stage * LAG
            live = (index >= 0) & (index < self.total)

            @when(live)
            def _(index=index, stage=stage):
                def work(order):
                    chunk = self.buffer.at[index]
                    self.receive(chunk, (index,), order, stage)
                    if stage < 3:
                        self.send(chunk, (index,), order, stage + 1)

                self.by_order(index, work)

    def finish(self, first, count):
        def work(step):
            index = first + step
            self.by_order(
                index, lambda order: self.drain(self.buffer.at[index], (index,), order)
            )

        each(count, work)


def moments(values):
    mean = jnp.mean(values, axis=-1, keepdims=True)
    centred = values - mean
    spread = jnp.mean(centred * centred, axis=-1, keepdims=True)
    scale = lax.rsqrt(spread + norm_eps)
    return centred * scale, scale


def gelu_pair(upper):
    bell = jnp.exp(-0.5 * upper * upper) * 0.3989422804014327
    below = 0.5 * (1.0 + lax.erf(upper * 0.7071067811865476))
    return upper * below, below + upper * bell


def matrix(buffer, index):
    return buffer[index].reshape(WIDTH, WIDE)


def column_of(row):
    tall = jnp.transpose(jnp.broadcast_to(row.astype(jnp.float32), (8, row.shape[1])))
    return tall[:, 0:1]


def read_vectors(gathered, devices):
    flat = gathered[...].reshape(devices * 8, 128).astype(jnp.bfloat16)

    def line(number):
        shape = (devices, devices * 8)
        wanted = lax.broadcasted_iota(jnp.int32, shape, 0) * 8 + number
        chosen = lax.broadcasted_iota(jnp.int32, shape, 1) == wanted
        return dot(chosen.astype(jnp.bfloat16), flat).astype(jnp.bfloat16)

    def spread(lines, start, wide):
        total = wide * devices
        lane = lax.broadcasted_iota(jnp.int32, (128, total), 1)
        wanted = lax.broadcasted_iota(jnp.int32, (128, total), 0) == start + lane % wide
        found = dot(lines, wanted.astype(jnp.bfloat16))
        owner = lax.broadcasted_iota(jnp.int32, (devices, total), 1) // wide
        mine = owner == lax.broadcasted_iota(jnp.int32, (devices, total), 0)
        return jnp.sum(jnp.where(mine, found, 0.0), axis=0, keepdims=True)

    first, second = line(0), line(1)
    rows = [spread(first, index * UNIT, UNIT) for index in range(4)]
    rows.append(spread(line(2), 0, UNIT))
    return rows, [spread(second, index * UNIT, UNIT) for index in range(4)]


def write_vectors(rows, devices):
    result = None
    for index, row in enumerate(rows):
        owner = lax.broadcasted_iota(jnp.int32, (devices, WIDTH), 1) // UNIT
        mine = owner == lax.broadcasted_iota(jnp.int32, (devices, WIDTH), 0)
        spread = jnp.where(mine, row, 0.0)
        lane = lax.broadcasted_iota(jnp.int32, (WIDTH, 128), 0)
        wanted = lax.broadcasted_iota(jnp.int32, (WIDTH, 128), 1) == index * UNIT + lane % UNIT
        found = jnp.dot(
            spread,
            wanted.astype(jnp.float32),
            preferred_element_type=jnp.float32,
            precision=HIGH,
        )
        result = found if result is None else result + found
    return result


def head_lanes(which, shape):
    lane = lax.broadcasted_iota(jnp.int32, shape, 1)
    return lane < 64 if which == 0 else lane >= 64


def allowed(crop_row, mask_row):
    shape = (LENGTH, LENGTH)
    row = lax.broadcasted_iota(jnp.int32, shape, 0)
    column = lax.broadcasted_iota(jnp.int32, shape, 1)
    same = column_of(crop_row) == crop_row.astype(jnp.float32)
    seen = (mask_row > 0) | (row == column)
    return jnp.where(same & (column <= row) & seen, 1.0, 0.0).astype(jnp.bfloat16)


def allowed_back(crop_row, mask_row):
    shape = (LENGTH, LENGTH)
    row = lax.broadcasted_iota(jnp.int32, shape, 0)
    column = lax.broadcasted_iota(jnp.int32, shape, 1)
    same = column_of(crop_row) == crop_row.astype(jnp.float32)
    seen = (column_of(mask_row) > 0) | (row == column)
    return jnp.where(same & (row <= column) & seen, 1.0, 0.0).astype(jnp.bfloat16)


def transpose_into(source, target):
    def work(index):
        at = pl.ds(pl.multiple_of(index * 128, 128), 128)
        target[at, :] = jnp.transpose(source[:, at])

    each(source.shape[1] // 128, work)


def by_rows(work):
    each(LENGTH // 64, lambda index: work(pl.ds(pl.multiple_of(index * 64, 64), 64)))


def forward_heads(pair, qkv, mask, mixed, inverse, attended):
    chunk = pair // 4
    lanes = pl.ds(pl.multiple_of((pair % 4) * 128, 128), 128)
    columns = pl.ds(pl.multiple_of(pair * 128, 128), 128)
    for part in (0, 1):
        keys = 256 * (part + 1)
        rows = slice(part * 256, part * 256 + 256)
        query = qkv[chunk, rows, lanes]
        key = qkv[2 + chunk, 0:keys, lanes]
        value = qkv[4 + chunk, 0:keys, lanes]
        zero, one = jnp.zeros_like(key), jnp.ones_like(key)
        total = None
        for which in (0, 1):
            mine = head_lanes(which, key.shape)
            scores = dot_nt(query, jnp.where(mine, key, zero)).astype(jnp.bfloat16)
            scores = scores * mask[rows, 0:keys]
            right = jnp.concatenate(
                [jnp.where(mine, value, zero), jnp.where(mine, one, zero)], axis=1
            )
            term = dot(scores, right)
            total = term if total is None else total + term
        inverted = 1.0 / total[:, 128:]
        result = total[:, :128] * inverted
        mixed[rows, columns] = result
        inverse[rows, columns] = inverted
        attended[rows, columns] = result.astype(jnp.bfloat16)


def hidden_order(flip):
    shape = (4 * 128, 4 * 128)
    rows, columns = (lax.broadcasted_iota(jnp.int32, shape, axis) for axis in (0, 1))
    if flip:
        rows, columns = columns, rows
    wanted = (rows // UNIT) % 4 * 128 + rows // 128 * UNIT + rows % UNIT
    return columns == wanted


def feed_block(block, refs):
    normed, normed_t, grad_out, weights, up_bias, result, grad_normed, staged, grad_bias = refs
    group, half = block // 2, block % 2
    first = FEED + 4 * group
    up = matrix(weights, first + 2 + half)
    upper = dot(normed[...], up) + up_bias[pl.ds(block, 1), :]
    hidden, slope = gelu_pair(upper)
    hidden = hidden.astype(jnp.bfloat16)
    grad_hidden = None
    for side in (0, 1):
        columns = slice(side * WIDE, side * WIDE + WIDE)
        down = weights[first + side, half].reshape(WIDE, WIDE)
        result[:, columns] += dot(hidden, down)
        term = dot_nt(grad_out[:, columns], down)
        grad_hidden = term if grad_hidden is None else grad_hidden + term
    grad_upper = (grad_hidden * slope).astype(jnp.bfloat16)
    grad_bias[pl.ds(block, 1), :] = jnp.sum(
        grad_upper.astype(jnp.float32), axis=0, keepdims=True
    )
    grad_normed[...] += dot_nt(grad_upper, up)
    value = dot(normed_t[...], grad_upper).astype(jnp.bfloat16)
    staged[0] = value.reshape(staged.shape[1:])
    for side in (0, 1):
        columns = slice(side * WIDE, side * WIDE + WIDE)
        value = dot_tn(hidden, grad_out[:, columns]).astype(jnp.bfloat16)
        staged[1, side] = value.reshape(staged.shape[2:])


class Sums(Mover):
    def start(self, lead, stage, step, axis, source, target):
        self.copy(lead, stage, step, axis, source, target).start()

    def region(self, order, stage, where):
        at = {axis: self.place.at[axis] for axis in order[:stage]}
        at[order[stage]] = where
        return tuple(at.get(axis, slice(None)) for axis in "abz")

    def blocks(self, order, stage, where):
        rest = [axis for axis in "abz" if axis in order[stage + 1 :]]
        base = self.region(order, stage, where)
        sizes = [self.place.size[axis] for axis in rest]
        for inner in itertools.product(*(range(size) for size in sizes)):
            place = dict(zip(rest, inner))
            yield (
                tuple(place.get(axis, item) for axis, item in zip("abz", base)),
                inner,
            )

    def room(self, order, stage, rooms, step):
        if stage == 0:
            return rooms[0]
        if stage == 1:
            size = self.place.size[order[2]]
            return rooms[1].at[pl.ds((step - 1) * size, size)]
        return rooms[2].at[step - 1]

    def send_stage(self, lead, order, stage, total, rooms, add):
        axis = order[stage]
        z = self.place.at["z"]
        for step in self.place.partners(axis):
            where = self.place.moved(axis, step)[axis]
            for at, _ in self.blocks(order, stage, where):
                add(at)
            source = total.at[self.region(order, stage, where)]
            room = self.room(order, stage, rooms, step)
            item = self.copy(lead, stage + 1, step, axis, source, room)
            if axis != "z":
                item.start()
            elif step == 2:
                pl.when((z == 0) | (z == 3))(item.start)
            else:
                far = 3 if step == 1 else 0
                pl.when(z != far)(item.start)

                @pl.when(z == far)
                def _(step=step, source=source, far=far):
                    pltpu.make_async_remote_copy(
                        source,
                        self.room(order, stage, rooms, 4),
                        self.send_sem.at[lead + (stage + 1, step - 1)],
                        self.recv_sem.at[lead + (stage + 1, 3)],
                        device_id={"fsdp": 2 if far == 3 else 1},
                        device_id_type=MESH,
                    ).start()

        for at, _ in self.blocks(order, stage, self.place.at[axis]):
            add(at)

    def pass_on(self, lead, order, total, rooms):
        z = self.place.at["z"]
        stage = order.index("z")

        @pl.when((z == 1) | (z == 2))
        def _():
            came = self.room(order, stage, rooms, 4)
            self.copy(lead, stage + 1, 4, "z", came, came).wait_recv()
            where = 3 * (2 - z)
            for at, inner in self.blocks(order, stage, where):
                total[at] = total[at] + (came[inner] if inner else came[...])
            source = total.at[self.region(order, stage, where)]
            self.start(lead, stage + 1, 2, "z", source, self.room(order, stage, rooms, 2))

    def await_stage(self, lead, order, stage, rooms):
        axis = order[stage]
        for step in self.place.partners(axis):
            room = self.room(order, stage, rooms, step)
            item = self.copy(lead, stage + 1, step, axis, room, room)
            if axis == "z" and step != 2:
                pl.when(self.place.at["z"] != (0 if step == 1 else 3))(item.wait_recv)
            else:
                item.wait_recv()

    def after_core(self, lead, order, own, total, rooms):
        def add(at):
            total[at] = own[at] + total[at]

        self.send_stage(lead, order, 0, total, rooms, add)

    def came_in(self, order, stage, total, rooms, at):
        rest = [axis for axis in "abz" if axis in order[stage + 1 :]]
        inner = tuple(item for axis, item in zip("abz", at) if axis in rest)
        steps = self.place.partners(order[stage])
        wide = total.dtype if len(steps) == 1 and stage < 2 else jnp.float32
        value = total[at].astype(wide)
        for step in steps:
            room = self.room(order, stage, rooms, step)
            term = (room[inner] if inner else room[...]).astype(wide)
            if order[stage] == "z" and step != 2:
                near = self.place.at["z"] != (0 if step == 1 else 3)
                term = jnp.where(near, term, jnp.zeros_like(term))
            value = value + term
        return value

    def after_stage(self, lead, order, stage, total, rooms):
        self.await_stage(lead, order, stage - 1, rooms)

        def add(at):
            total[at] = self.came_in(order, stage - 1, total, rooms, at).astype(total.dtype)

        self.send_stage(lead, order, stage, total, rooms, add)

    def after_last(self, lead, order, total, rooms):
        self.await_stage(lead, order, 2, rooms)
        at = tuple(self.place.at[axis] for axis in "abz")
        return self.came_in(order, 2, total, rooms, at)

    def drain(self, lead, order, total, rooms):
        self.copy(lead, 0, 1, "c", total, total).wait_send()
        for stage in range(3):
            axis = order[stage]
            for step in self.place.partners(axis):
                room = self.room(order, stage, rooms, step)
                self.copy(lead, stage + 1, step, axis, room, room).wait_send()


class Gradients(Sums):
    orders = ("azb", "bza", "abz", "bza", "azb", "baz")

    def __init__(self, place, terms, sums, rooms, results, ring, ring_sem, send_sem, recv_sem):
        super().__init__(place, send_sem, recv_sem)
        self.terms, self.sums, self.rooms, self.results = terms, sums, rooms, results
        self.ring, self.ring_sem = ring, ring_sem
        self.total = results.shape[0]

    def sum_at(self, index):
        return self.sums.at[index // 2, :, :, index % 2]

    def by_order(self, index, work):
        rooms = [room.at[index % ROOMS] for room in self.rooms]
        total = self.sum_at(index)
        by_order(self.place, self.orders, index, lambda order: work(order, total, rooms))

    def begin(self, index):
        @when(index < self.total)
        def _():
            side = self.place.at["c"]
            slot = index % (TERMS_AHEAD + 1)
            source = self.terms.at[index]
            self.start((index,), 0, 1, "c", source.at[:, :, 1 - side], self.sum_at(index))
            pltpu.make_async_copy(
                source.at[:, :, side], self.ring.at[slot], self.ring_sem.at[slot]
            ).start()

    def tick(self, now):
        self.begin(now + TERMS_AHEAD)

        def live(index):
            return (index >= 0) & (index < self.total)

        @when(live(now))
        def _():
            slot = now % (TERMS_AHEAD + 1)
            own = self.ring.at[slot]
            pltpu.make_async_copy(own, own, self.ring_sem.at[slot]).wait()
            total = self.sum_at(now)
            self.copy((now,), 0, 1, "c", total, total).wait_recv()
            self.by_order(
                now,
                lambda order, total, rooms: self.after_core((now,), order, own, total, rooms),
            )

        for stage in (1, 2):
            index = now - stage * LAG

            @when(live(index))
            def _(index=index, stage=stage):
                self.by_order(
                    index,
                    lambda order, total, rooms: self.after_stage(
                        (index,), order, stage, total, rooms
                    ),
                )

        for stage in (1, 2):
            index = now - stage * LAG - TERMS_PASS_AFTER

            @when(live(index))
            def _(index=index, stage=stage):
                def work(order, total, rooms):
                    if order.index("z") == stage:
                        self.pass_on((index,), order, total, rooms)

                self.by_order(index, work)

        index = now - 3 * LAG

        @when(live(index))
        def _():
            def work(order, total, rooms):
                self.results[index] = self.after_last((index,), order, total, rooms)

            self.by_order(index, work)

    def finish(self):
        def work(index):
            self.by_order(
                index,
                lambda order, total, rooms: self.drain((index,), order, total, rooms),
            )

        each(self.total, work)


def backward_heads(pair, qkv, mask, mask_t, mixed, inverse, grad_mixed):
    chunk = pair // 4
    lanes = pl.ds(pl.multiple_of((pair % 4) * 128, 128), 128)
    columns = pl.ds(pl.multiple_of(pair * 128, 128), 128)
    query = qkv[chunk, :, lanes]
    key = qkv[2 + chunk, :, lanes]
    value = qkv[4 + chunk, :, lanes]
    grad_numer = (grad_mixed[:, columns] * inverse[:, columns]).astype(jnp.bfloat16)
    part = grad_numer.astype(jnp.float32) * mixed[:, columns]
    high = part.astype(jnp.bfloat16)
    low = pltpu.roll(part - high.astype(jnp.float32), 64, 1).astype(jnp.bfloat16)
    zero, minus = jnp.zeros_like(query), jnp.full_like(query, -1.0)
    heads = []
    for which in (0, 1):
        mine = head_lanes(which, query.shape)
        heads.append(
            (
                jnp.concatenate([grad_numer, jnp.where(mine, high, low)], axis=1),
                jnp.concatenate([jnp.where(mine, value, zero), minus], axis=1),
                jnp.where(mine, query, zero),
                jnp.where(mine, key, zero),
                jnp.where(mine, grad_numer, zero),
            )
        )
    for part in (0, 1):
        keys = 256 * (part + 1)
        rows = slice(part * 256, part * 256 + 256)
        total = None
        for left, right, _, own_key, _ in heads:
            grad_scores = dot_nt(left[rows], right[:keys]).astype(jnp.bfloat16)
            term = dot(grad_scores * mask[rows, 0:keys], own_key[:keys])
            total = term if total is None else total + term
        slope = jnp.minimum(query[rows].astype(jnp.float32), 1.0)
        qkv[chunk, rows, lanes] = (total * slope).astype(jnp.bfloat16)
    for part in (0, 1):
        start = part * 256
        rows = slice(start, start + 256)
        grad_key = grad_value = None
        for left, right, own_query, own_key, own_grad in heads:
            seen = mask_t[rows, start:LENGTH]
            scores = dot_nt(own_key[rows], query[start:]).astype(jnp.bfloat16) * seen
            grad_scores = dot_nt(right[rows], left[start:]).astype(jnp.bfloat16) * seen
            term = dot(scores, own_grad[start:])
            grad_value = term if grad_value is None else grad_value + term
            term = dot(grad_scores, own_query[start:])
            grad_key = term if grad_key is None else grad_key + term
        slope = jnp.minimum(key[rows].astype(jnp.float32), 1.0)
        qkv[2 + chunk, rows, lanes] = (grad_key * slope).astype(jnp.bfloat16)
        qkv[4 + chunk, rows, lanes] = grad_value.astype(jnp.bfloat16)


def layer_kernel(dims, *refs):
    crops, kept, gain_one, bias_one, gain_two, bias_two, bias_down, bias_up = refs[:8]
    tokens_in, grad_out_in = refs[8:10]
    shards = refs[10:16]
    output, input_grad, mixed_kept, inverse_kept, normed_t_kept, attention_kept, terms = refs[16:23]
    owned, owned_up, owned_small = refs[23:26]
    (
        pixels,
        grad_out,
        weights,
        up_shard,
        vectors,
        rows,
        up_bias,
        mask,
        mask_t,
        qkv,
        normed,
        turned_one,
        turned_two,
        middle,
        wide_one,
        wide_two,
        wide_three,
        staged,
        grad_up_bias,
        sums,
        small,
        ring,
        rooms_one,
        rooms_two,
        rooms_three,
        side_total,
        side_one,
        side_two,
        side_three,
        send_sem,
        recv_sem,
        vector_send_sem,
        vector_recv_sem,
        load_sem,
        store_sem,
        stage_sem,
        ring_sem,
        terms_send_sem,
        terms_recv_sem,
        side_send_sem,
        side_recv_sem,
        sibling_sem,
    ) = refs[26:]
    outer, inner, depth = dims
    devices = 2 * outer * inner * depth
    place = Place(dims)
    spot = (place.at["a"], place.at["b"], place.at["c"], place.at["z"])
    copies = {}

    def move(name, source, target):
        item = pltpu.make_async_copy(source, target, load_sem.at[len(copies)])
        item.start()
        copies[name] = item

    for index in range(FEED):
        source = shards[index // 2].at[:, pl.ds((index % 2) * WIDE, WIDE)]
        move(index, source, weights.at[(index,) + spot])
    move("tokens", tokens_in, pixels)
    move("up", shards[4], up_shard)
    for group in range(4):
        for half in (0, 1):
            source = shards[5].at[pl.ds(group * UNIT, UNIT), pl.ds(half * WIDE, WIDE)]
            index = FEED + 4 * group + half
            move(index, source, weights.at[(index,) + spot])
    move("grad_out", grad_out_in, grad_out)

    vector_gather = Gather(place, vector_send_sem, vector_recv_sem)
    vector_order = "zbac"
    lines = [
        jnp.concatenate([item[...] for item in (gain_one, bias_one, gain_two, bias_two)], axis=1),
        bias_up[...],
        jnp.concatenate([bias_down[...], jnp.zeros((1, 128 - UNIT), jnp.bfloat16)], axis=1),
    ]
    vectors[spot] = jnp.concatenate(
        [line.astype(jnp.float32) for line in lines] + [jnp.zeros((5, 128), jnp.float32)], axis=0
    )
    place.greet()
    vector_gather.send(vectors, (), vector_order, 0)
    gather_all = Weights(place, weights, send_sem, recv_sem)
    for index in range(AHEAD):
        copies[index].wait()
        gather_all.begin(index)
    for index in range(PASS_AHEAD):
        gather_all.pass_on_at(index, 0)
    copies["up"].wait()
    stacked = jnp.concatenate(
        [up_shard[:, index * WIDE : (index + 1) * WIDE] for index in range(8)], axis=0
    )
    stacked = dot(stacked, hidden_order(False).astype(jnp.bfloat16)).astype(jnp.bfloat16)
    for part in range(8):
        for group in range(4):
            at = (FEED + 4 * group + 2 + part // 4,) + spot
            lanes = slice((part % 4) * 128, (part % 4) * 128 + 128)
            weights[at + (slice(None), lanes)] = stacked[
                part * UNIT : (part + 1) * UNIT, group * 128 : (group + 1) * 128
            ]
    for name, item in copies.items():
        if name not in (0, 1, 2, 3, "up"):
            item.wait()
    vector_gather.pass_on(vectors, (), vector_order)
    for stage in range(4):
        vector_gather.receive(vectors, (), vector_order, stage)
        if stage < 3:
            vector_gather.send(vectors, (), vector_order, stage + 1)
            gather_all.tick(stage)
    width_rows, up_rows = read_vectors(vectors, devices)
    for index, row in enumerate(width_rows):
        rows[index : index + 1, :] = row
    for group, row in enumerate(up_rows):
        for half in (0, 1):
            up_bias[2 * group + half : 2 * group + half + 1, :] = row[
                :, half * WIDE : half * WIDE + WIDE
            ]
    mask[...] = allowed(crops[...], kept[...])
    mask_t[...] = allowed_back(crops[...], kept[...])
    sums[...] = jnp.zeros(sums.shape, jnp.float32)

    def first_norm(at):
        value = pixels[at, :].astype(jnp.float32)
        unit, _ = moments(value)
        normed[at, :] = (unit * rows[0:1, :] + rows[1:2, :]).astype(jnp.bfloat16)
        middle[at, :] = value

    by_rows(first_norm)
    stores = {}

    def store(name, source, target):
        item = pltpu.make_async_copy(source, target, store_sem.at[len(stores)])
        item.start()
        stores[name] = item

    transpose_into(normed, turned_one)
    store("normed", turned_one, normed_t_kept)
    each(LATE - 3, lambda index: gather_all.tick(3 + index))

    def project(index):
        gather_all.tick(LATE + index)
        value = dot(normed[...], matrix(weights, index))
        mapped = jnp.where(value > 0, value + 1.0, jnp.exp(jnp.minimum(value, 0.0)))
        qkv[index] = jnp.where(index < 4, mapped, value).astype(jnp.bfloat16)

    each(6, project)
    attended, mixed, inverse = pixels, wide_one, wide_two

    def heads(pair):
        @pl.when(pair % 2 == 0)
        def _():
            gather_all.tick(LATE + 6 + pair // 2)

        forward_heads(pair, qkv, mask, mixed, inverse, attended)

    each(8, heads)
    store("mixed", mixed, mixed_kept)
    store("inverse", inverse, inverse_kept)
    store("attention", weights.at[pl.ds(0, FEED)], attention_kept)
    for half in (0, 1):
        columns = slice(half * WIDE, half * WIDE + WIDE)
        middle[:, columns] += dot(attended[...], matrix(weights, 6 + half))
    stores["normed"].wait()
    transpose_into(attended, turned_one)
    result, grad_normed, normed_two = wide_one, wide_two, normed
    stores["mixed"].wait()
    stores["inverse"].wait()

    def second_norm(at):
        value = middle[at, :]
        unit, _ = moments(value)
        normed_two[at, :] = (unit * rows[2:3, :] + rows[3:4, :]).astype(jnp.bfloat16)
        result[at, :] = value + rows[4:5, :]
        grad_normed[at, :] = jnp.zeros((64, WIDTH), jnp.float32)

    by_rows(second_norm)
    transpose_into(normed_two, turned_two)

    adder = Gradients(
        place,
        terms,
        weights,
        (rooms_one, rooms_two, rooms_three),
        owned,
        ring,
        ring_sem,
        terms_send_sem,
        terms_recv_sem,
    )

    def leave(block):
        first, half = 4 * (block // 2), block % 2
        return (
            pltpu.make_async_copy(staged.at[0], terms.at[first + 2 + half], stage_sem.at[0]),
            pltpu.make_async_copy(
                staged.at[1], terms.at[pl.ds(first, 2), half], stage_sem.at[1]
            ),
        )

    def last_tick(block):
        return LATE + 10 + 4 * (block // 2) + block % 2

    def feed(block):
        begin = last_tick(block - 1) + 1

        def both(step, carry):
            @pl.when(step >= LATE + 10)
            def _():
                gather_all.tick(step)

            @pl.when((step == begin) & (block > 0))
            def _():
                for item in leave(block - 1):
                    item.wait()

            @pl.when(step == TERMS_START)
            def _():
                pl.semaphore_wait(sibling_sem, 1)
                for index in range(TERMS_AHEAD):
                    adder.begin(index)

            @pl.when(step >= TERMS_START)
            def _():
                adder.tick(step - TERMS_START)

            return carry

        lax.fori_loop(begin, last_tick(block) + 1, both, 0)
        feed_block(
            block,
            (
                normed_two,
                turned_two,
                grad_out,
                weights,
                up_bias,
                result,
                grad_normed,
                staged,
                grad_up_bias,
            ),
        )
        for item in leave(block):
            item.start()

        @pl.when(block == 1)
        def _():
            gather_all.finish(0, ROOMS)
            stores["attention"].wait()
            pl.semaphore_signal(
                sibling_sem, 1, device_id=place.device("c", 1), device_id_type=MESH
            )

    each(8, feed)
    done = last_tick(7) + 1 - TERMS_START
    adder.tick(done)
    for item in leave(7):
        item.wait()
    gather_all.finish(ROOMS, CHUNKS - ROOMS)
    loads = {}

    def load(name, source, target):
        item = pltpu.make_async_copy(source, target, store_sem.at[4 + len(loads)])
        item.start()
        loads[name] = item

    load("out", attention_kept.at[pl.ds(6, 2)], weights.at[pl.ds(ROOMS + 6, 2)])
    load("normed", normed_t_kept, turned_two)
    load("rest", attention_kept.at[pl.ds(0, 6)], weights.at[pl.ds(ROOMS, 6)])
    grad_attended, shown, grad_middle = pixels, normed, middle

    def close_branch(at):
        unit, scale = moments(middle[at, :])
        grad = grad_out[at, :].astype(jnp.float32)
        value = grad_normed[at, :]
        shown[at, :] = result[at, :].astype(jnp.bfloat16)
        sums[0:1, :] += jnp.sum(value * unit, axis=0, keepdims=True)
        sums[1:2, :] += jnp.sum(value, axis=0, keepdims=True)
        sums[2:3, :] += jnp.sum(grad, axis=0, keepdims=True)
        scaled = value * rows[2:3, :]
        summed = grad + scale * (
            scaled
            - jnp.mean(scaled, axis=-1, keepdims=True)
            - unit * jnp.mean(scaled * unit, axis=-1, keepdims=True)
        )
        grad_middle[at, :] = summed
        grad_attended[at, :] = summed.astype(jnp.bfloat16)

    by_rows(close_branch)
    load("mixed", mixed_kept, mixed)
    load("inverse", inverse_kept, inverse)
    load("output", shown, output)
    adder.tick(done + 1)
    loads["out"].wait()
    grad_mixed = wide_three
    grad_mixed[...] = dot_nt(grad_attended[:, 0:WIDE], matrix(weights, ROOMS + 6)) + dot_nt(
        grad_attended[:, WIDE:WIDTH], matrix(weights, ROOMS + 7)
    )
    adder.tick(done + 2)

    def stage_out(slot, index):
        return pltpu.make_async_copy(staged.at[slot], terms.at[index], stage_sem.at[slot])

    for half in (0, 1):
        columns = slice(half * WIDE, half * WIDE + WIDE)
        value = dot(turned_one[...], grad_attended[:, columns]).astype(jnp.bfloat16)
        staged[half] = value.reshape(staged.shape[1:])
        stage_out(half, 16 + half).start()
    load("tokens", tokens_in, pixels)
    adder.tick(done + 3)
    for name in ("mixed", "inverse", "normed", "rest"):
        loads[name].wait()
    for half in (0, 1):
        stage_out(half, 16 + half).wait()
    spread = 14 - (done + 4)

    def back_heads(pair):
        @pl.when((pair + 1) * spread // 8 > pair * spread // 8)
        def _():
            adder.tick(done + 4 + pair * spread // 8)

        backward_heads(pair, qkv, mask, mask_t, mixed, inverse, grad_mixed)

    each(8, back_heads)
    grad_first = grad_mixed
    grad_first[...] = jnp.zeros(grad_first.shape, jnp.float32)

    def back_project(index):
        value = dot(turned_two[...], qkv[index]).astype(jnp.bfloat16)
        staged[index % 2] = value.reshape(staged.shape[1:])
        stage_out(index % 2, 18 + index).start()
        grad_first[...] += dot_nt(qkv[index], matrix(weights, ROOMS + index))

        @pl.when(index > 0)
        def _():
            stage_out((index - 1) % 2, 17 + index).wait()

        adder.tick(14 + index)

    each(6, back_project)
    stage_out(1, 23).wait()
    adder.tick(20)
    loads["tokens"].wait()
    loads["output"].wait()

    def close(at):
        unit, scale = moments(pixels[at, :].astype(jnp.float32))
        value = grad_first[at, :]
        sums[3:4, :] += jnp.sum(value * unit, axis=0, keepdims=True)
        sums[4:5, :] += jnp.sum(value, axis=0, keepdims=True)
        scaled = value * rows[0:1, :]
        shown[at, :] = (
            grad_middle[at, :]
            + scale
            * (
                scaled
                - jnp.mean(scaled, axis=-1, keepdims=True)
                - unit * jnp.mean(scaled * unit, axis=-1, keepdims=True)
            )
        ).astype(jnp.bfloat16)

    by_rows(close)
    load("input_grad", shown, input_grad)
    adder.tick(21)
    groups = [
        jnp.concatenate(
            [grad_up_bias[2 * group + half : 2 * group + half + 1, :] for half in (0, 1)], axis=1
        )
        for group in range(4)
    ]
    lines = [
        write_vectors([sums[index : index + 1, :] for index in (3, 4, 0, 1)], devices),
        write_vectors(groups, devices),
        write_vectors([sums[2:3, :]], devices),
    ]
    for device in range(devices):
        at = (
            device // (2 * inner * depth),
            (device // (2 * depth)) % inner,
            (device // depth) % 2,
            device % depth,
        )
        for row, line in enumerate(lines):
            small[at + (slice(row, row + 1),)] = line[device : device + 1, :]
        small[at + (slice(3, 8),)] = jnp.zeros((5, 128), jnp.float32)
    side = Sums(place, side_send_sem, side_recv_sem)
    rooms = (side_one, side_two, side_three)
    core = place.at["c"]
    side.start((), 0, 1, "c", small.at[:, :, 1 - core], side_total)

    def last_ticks(step):
        adder.tick(22 + step)

        @pl.when(step == 0)
        def _():
            side.copy((), 0, 1, "c", side_total, side_total).wait_recv()
            side.after_core((), "abz", small.at[:, :, core], side_total, rooms)

        for stage in (1, 2):

            @pl.when(step == stage)
            def _(stage=stage):
                side.after_stage((), "abz", stage, side_total, rooms)

        @pl.when(step == 3)
        def _():
            side.pass_on((), "abz", side_total, rooms)

        @pl.when(step == 4)
        def _():
            owned_small[...] = side.after_last((), "abz", side_total, rooms)

        @pl.when(step == 5)
        def _():
            back = hidden_order(True).astype(jnp.float32)
            for part in range(8):
                lanes = slice((part % 4) * 128, (part % 4) * 128 + 128)
                value = jnp.concatenate(
                    [owned[4 * group + 2 + part // 4, :, lanes] for group in range(4)], axis=1
                )
                owned_up[:, part * WIDE : (part + 1) * WIDE] = jnp.dot(
                    value, back, preferred_element_type=jnp.float32, precision=HIGH
                )

    each(CHUNKS + 3 * LAG - 22, last_ticks)
    vector_gather.drain(vectors, (), vector_order)
    side.drain((), "abz", side_total, rooms)
    adder.finish()
    loads["input_grad"].wait()


def layer(dims, tokens, cotangent, crops, kept, small, shards):
    outer, inner, depth = dims
    most = max(dims)
    lead = (outer, inner, 2, depth)
    chip = (outer, inner, depth)
    tile, small_tile = (UNIT, WIDE), (8, 128)
    whole, turned = (LENGTH, WIDTH), (WIDTH, LENGTH)
    f32, bf16 = jnp.float32, jnp.bfloat16
    shape = jax.ShapeDtypeStruct
    room, dma = pltpu.VMEM, pltpu.SemaphoreType.DMA
    vmem, anywhere = pl.BlockSpec(memory_space=pltpu.VMEM), pl.BlockSpec(memory_space=pl.ANY)
    return pl.pallas_call(
        functools.partial(layer_kernel, dims),
        out_shape=[
            shape(whole, bf16),
            shape(whole, bf16),
            shape(whole, f32),
            shape(whole, f32),
            shape(turned, bf16),
            shape((FEED,) + lead + tile, bf16),
            shape((CHUNKS,) + lead + tile, bf16),
            shape((CHUNKS,) + tile, f32),
            shape((UNIT, HIDDEN), f32),
            shape(small_tile, f32),
        ],
        in_specs=[vmem] * 8 + [anywhere] * 8,
        out_specs=[anywhere] * 7 + [vmem] * 3,
        scratch_shapes=[
            room(whole, bf16),
            room(whole, bf16),
            room((CHUNKS,) + lead + tile, bf16),
            room((UNIT, HIDDEN), bf16),
            room(lead + small_tile, f32),
            room((8, WIDTH), f32),
            room((8, WIDE), f32),
            room((LENGTH, LENGTH), bf16),
            room((LENGTH, LENGTH), bf16),
            room((6, LENGTH, WIDE), bf16),
            room(whole, bf16),
            room(turned, bf16),
            room(turned, bf16),
            room(whole, f32),
            room(whole, f32),
            room(whole, f32),
            room(whole, f32),
            room((2,) + lead + tile, bf16),
            room((8, WIDE), f32),
            room((8, WIDTH), f32),
            room(lead + small_tile, f32),
            room((TERMS_AHEAD + 1,) + chip + tile, bf16),
            room((ROOMS, 2, 4) + tile, bf16),
            room((ROOMS, 8) + tile, bf16),
            room((ROOMS, 4) + tile, bf16),
            room(chip + small_tile, f32),
            room((2, 4) + small_tile, f32),
            room((8,) + small_tile, f32),
            room((4,) + small_tile, f32),
            dma((CHUNKS, 4, most)),
            dma((CHUNKS, 4, most)),
            dma((4, most)),
            dma((4, most)),
            dma((19,)),
            dma((12,)),
            dma((2,)),
            dma((TERMS_AHEAD + 1,)),
            dma((CHUNKS, 4, most)),
            dma((CHUNKS, 4, most)),
            dma((4, most)),
            dma((4, most)),
            pltpu.SemaphoreType.REGULAR,
        ],
        compiler_params=pltpu.CompilerParams(
            collective_id=0, has_side_effects=True, vmem_limit_bytes=VMEM_LIMIT
        ),
        name="layer",
    )(crops, kept, *small, tokens, cotangent, *shards)


def place_kernel(*refs):
    result, input_grad, owned, owned_up, small = refs[:5]
    result_out, input_grad_out, query, key, value, out, up, down = refs[5:13]
    vectors, bias_up = refs[13:18], refs[18]
    sems = refs[19]
    copies = [(result, result_out.at[0]), (input_grad, input_grad_out.at[0]), (owned_up, up)]
    for index in range(CHUNKS):
        if index < 16:
            group, half = index // 4, index % 4
            if half >= 2:
                continue
            target = down.at[pl.ds(group * UNIT, UNIT), pl.ds(half * WIDE, WIDE)]
        else:
            matrix_out = (out, query, key, value)[(index - 16) // 2]
            target = matrix_out.at[:, pl.ds((index % 2) * WIDE, WIDE)]
        copies.append((owned.at[index], target))
    items = [
        pltpu.make_async_copy(source, target, sems.at[index])
        for index, (source, target) in enumerate(copies)
    ]
    for item in items:
        item.start()
    for index in range(4):
        vectors[index][...] = small[0, index * UNIT : (index + 1) * UNIT]
    vectors[4][...] = small[2, 0:UNIT]
    bias_up[...] = small[1, :]
    for item in items:
        item.wait()


def place_results(result, input_grad, owned, owned_up, small):
    f32, bf16 = jnp.float32, jnp.bfloat16
    shape = jax.ShapeDtypeStruct
    vmem, anywhere = pl.BlockSpec(memory_space=pltpu.VMEM), pl.BlockSpec(memory_space=pl.ANY)
    return pl.pallas_call(
        place_kernel,
        out_shape=[shape((1, LENGTH, WIDTH), bf16)] * 2
        + [shape((UNIT, WIDTH), f32)] * 4
        + [shape((UNIT, HIDDEN), f32), shape((4 * UNIT, WIDTH), f32)]
        + [shape((UNIT,), f32)] * 5
        + [shape((4 * UNIT,), f32)],
        in_specs=[anywhere] * 4 + [vmem],
        out_specs=[vmem] * 14,
        scratch_shapes=[pltpu.SemaphoreType.DMA((19,))],
        name="results",
    )(result, input_grad, owned, owned_up, small)


def body(
    tokens,
    crop_ids,
    kv_mask,
    norm1_gain,
    norm1_bias,
    w_query,
    w_key,
    w_value,
    w_out,
    norm2_gain,
    norm2_bias,
    w_up,
    up_bias,
    w_down,
    down_bias,
    cotangent,
):
    inner = lax.axis_size("dp") // (2 * OUTER)
    dims = (OUTER, inner, lax.axis_size("fsdp"))
    fits = (
        tokens.shape == (1, LENGTH, WIDTH)
        and w_up.shape == (UNIT, HIDDEN)
        and w_down.shape == (HIDDEN // WIDTH * UNIT, WIDTH)
        and dims == (2, 2, 4)
    )
    if not fits:
        return general_body(
            tokens,
            crop_ids,
            kv_mask,
            norm1_gain,
            norm1_bias,
            w_query,
            w_key,
            w_value,
            w_out,
            norm2_gain,
            norm2_bias,
            w_up,
            up_bias,
            w_down,
            down_bias,
            cotangent,
        )
    small = [
        vector.reshape(1, -1)
        for vector in (norm1_gain, norm1_bias, norm2_gain, norm2_bias, down_bias, up_bias)
    ]
    pixels, grads = tokens.reshape(LENGTH, WIDTH), cotangent.reshape(LENGTH, WIDTH)
    shards = (w_query, w_key, w_value, w_out, w_up, w_down)
    result, input_grad, *_, owned, owned_up, owned_small = layer(
        dims, pixels, grads, crop_ids, kv_mask, small, shards
    )
    (
        output,
        grad_tokens,
        grad_query,
        grad_key,
        grad_value,
        grad_out,
        grad_up,
        grad_down,
        grad_gain_one,
        grad_bias_one,
        grad_gain_two,
        grad_bias_two,
        grad_bias_down,
        grad_bias_up,
    ) = place_results(result, input_grad, owned, owned_up, owned_small)
    return (
        output,
        grad_tokens,
        grad_gain_one,
        grad_bias_one,
        grad_query,
        grad_key,
        grad_value,
        grad_out,
        grad_gain_two,
        grad_bias_two,
        grad_up,
        grad_bias_up,
        grad_down,
        grad_bias_down,
    )


def solution(mesh):
    return jax.shard_map(
        body,
        mesh=mesh,
        in_specs=(
            P(("dp", "fsdp"), None, None),
            P(("dp", "fsdp"), None),
            P(("dp", "fsdp"), None),
            P(("dp", "fsdp")),
            P(("dp", "fsdp")),
            P(("dp", "fsdp"), None),
            P(("dp", "fsdp"), None),
            P(("dp", "fsdp"), None),
            P(("dp", "fsdp"), None),
            P(("dp", "fsdp")),
            P(("dp", "fsdp")),
            P(("dp", "fsdp"), None),
            P(("dp", "fsdp")),
            P(("dp", "fsdp"), None),
            P(("dp", "fsdp")),
            P(("dp", "fsdp"), None, None),
        ),
        out_specs=(
            P(("dp", "fsdp"), None, None),
            P(("dp", "fsdp"), None, None),
            P(("dp", "fsdp")),
            P(("dp", "fsdp")),
            P(("dp", "fsdp"), None),
            P(("dp", "fsdp"), None),
            P(("dp", "fsdp"), None),
            P(("dp", "fsdp"), None),
            P(("dp", "fsdp")),
            P(("dp", "fsdp")),
            P(("dp", "fsdp"), None),
            P(("dp", "fsdp")),
            P(("dp", "fsdp"), None),
            P(("dp", "fsdp")),
        ),
        check_vma=False,
    )
```

```python
import functools
import itertools

import jax
import jax.numpy as jnp
from jax import lax
from jax.experimental import pallas as pl
from jax.experimental.pallas import tpu as pltpu
from jax.sharding import PartitionSpec as P

HEADS = 16
BLOCK = 512
MESH = pl.DeviceIdType.MESH
WIDE = 512
OUTER = 2


class Place:
    def __init__(self, dims):
        self.size = {"a": dims[0], "b": dims[1], "c": 2, "z": dims[2]}
        dp = lax.axis_index("dp")
        self.at = {
            "a": dp // (2 * dims[1]),
            "b": (dp // 2) % dims[1],
            "c": dp % 2,
            "z": lax.axis_index("fsdp"),
        }

    def moved(self, axis, step):
        spot = dict(self.at)
        spot[axis] = (spot[axis] + step) % self.size[axis]
        return spot

    def device(self, axis, step):
        spot = self.moved(axis, step)
        return ((spot["a"] * self.size["b"] + spot["b"]) * 2 + spot["c"], spot["z"])

    def partners(self, axis):
        return range(1, self.size[axis])

    def greet(self):
        barrier = pltpu.get_barrier_semaphore()
        count = 0
        for axis in "abcz":
            for step in self.partners(axis):
                pl.semaphore_signal(
                    barrier, 1, device_id=self.device(axis, step), device_id_type=MESH
                )
                count += 1
        pl.semaphore_wait(barrier, count)


def pieces_of(rows, columns, unit):
    wide = min(WIDE, columns)
    return [
        (row, unit, column, wide)
        for row in range(0, rows, unit)
        for column in range(0, columns, wide)
    ]


def gather_kernel(dims, orders, lag, ahead, pieces, *refs):
    count = len(pieces)
    shards, wholes = refs[:count], refs[count : 2 * count]
    local_sem, send_sem, recv_sem = refs[2 * count :]
    place = Place(dims)
    place.greet()
    chunks = [
        (shard.at[pl.ds(ro, rn), pl.ds(co, cn)], whole, pl.ds(ro, rn), pl.ds(co, cn))
        for shard, whole, items in zip(shards, wholes, pieces)
        for ro, rn, co, cn in items
    ]
    total = len(chunks)
    sent, kept = [], []

    def region(index, done, spot):
        _, whole, rows, columns = chunks[index]
        lead = tuple(slice(None) if axis in done else spot[axis] for axis in "abcz")
        return whole.at[lead + (rows, columns)]

    def copy(index, stage, step, axis, source, target):
        return pltpu.make_async_remote_copy(
            source,
            target,
            send_sem.at[index, stage, step - 1],
            recv_sem.at[index, stage, step - 1],
            device_id=place.device(axis, step),
            device_id_type=MESH,
        )

    def send(index, stage):
        order = orders[index % len(orders)]
        axis, done = order[stage], order[:stage]
        target = region(index, done, place.at)
        for step in place.partners(axis):
            item = copy(index, stage, step, axis, target if done else chunks[index][0], target)
            item.start()
            sent.append(item)

    def receive(index, stage):
        order = orders[index % len(orders)]
        axis, done = order[stage], order[:stage]
        for step in place.partners(axis):
            target = region(index, done, place.moved(axis, place.size[axis] - step))
            copy(index, stage, step, axis, target, target).wait_recv()

    def begin(index):
        if index < total:
            item = pltpu.make_async_copy(
                chunks[index][0], region(index, "", place.at), local_sem.at[index]
            )
            item.start()
            kept.append(item)
            send(index, 0)

    for index in range(ahead):
        begin(index)
    for tick in range(total + 3 * lag):
        begin(tick + ahead)
        for stage in range(4):
            index = tick - stage * lag
            if 0 <= index < total:
                receive(index, stage)
                if stage == 0:
                    kept[index].wait()
                if stage < 3:
                    send(index, stage + 1)
    for item in sent:
        item.wait_send()


def gather(dims, shards, unit, lag=3, ahead=6):
    pieces = [pieces_of(*shard.shape, min(unit, shard.shape[0])) for shard in shards]
    total = sum(len(items) for items in pieces)
    most = max(dims) - 1
    anywhere = pl.BlockSpec(memory_space=pl.ANY)
    orders = ("zbac", "zabc", "zbac", "zabc", "bzac", "azbc")
    wholes = pl.pallas_call(
        functools.partial(gather_kernel, dims, orders, lag, ahead, pieces),
        out_shape=[
            jax.ShapeDtypeStruct(dims[:2] + (2, dims[2]) + shard.shape, shard.dtype)
            for shard in shards
        ],
        in_specs=[anywhere] * len(shards),
        out_specs=[anywhere] * len(shards),
        scratch_shapes=[
            pltpu.SemaphoreType.DMA((total,)),
            pltpu.SemaphoreType.DMA((total, 4, most)),
            pltpu.SemaphoreType.DMA((total, 4, most)),
        ],
        compiler_params=pltpu.CompilerParams(collective_id=0, has_side_effects=True),
        name="gather",
    )(*shards)
    return [whole.reshape((-1, whole.shape[-1])) for whole in wholes]


def scatter_kernel(dims, lag, ahead, pieces, *refs):
    count = len(pieces)
    terms, owned = refs[:count], refs[count : 2 * count]
    main = refs[2 * count : 2 * count + 7]
    side = refs[2 * count + 7 : 2 * count + 12]
    local_sem, send_sem, recv_sem = refs[2 * count + 12 :]
    place = Place(dims)
    place.greet()
    spot = place.at
    chunks = []
    for array, items in enumerate(pieces):
        for ro, rn, co, cn in items:
            index = len(chunks)
            if array == 0:
                rooms = side
                order = "ab"
            else:
                half = (index - 1) // 2
                order = "ab" if index % 2 else "ba"
                first, second = (main[2], main[4]) if index % 2 else (main[3], main[5])
                rooms = (
                    main[0].at[index - 1],
                    main[1].at[index - 1],
                    first.at[half],
                    second.at[half],
                    main[6].at[index - 1],
                )
            chunks.append((terms[array], owned[array], pl.ds(ro, rn), pl.ds(co, cn), order, rooms))
    total = len(chunks)
    sent, kept = [], []

    def copy(index, stage, step, axis, source, target):
        return pltpu.make_async_remote_copy(
            source,
            target,
            send_sem.at[index, stage, step - 1],
            recv_sem.at[index, stage, step - 1],
            device_id=place.device(axis, step),
            device_id_type=MESH,
        )

    def send(index, stage, step, axis, source, target):
        item = copy(index, stage, step, axis, source, target)
        item.start()
        sent.append(item)

    def begin(index):
        if index < total:
            term, _, rows, columns, _, rooms = chunks[index]
            send(index, 0, 1, "c", term.at[:, :, 1 - spot["c"], :, rows, columns], rooms[1])
            item = pltpu.make_async_copy(
                term.at[:, :, spot["c"], :, rows, columns], rooms[0], local_sem.at[index]
            )
            item.start()
            kept.append(item)

    def await_all(index, stage, axis, room):
        for step in place.partners(axis):
            copy(index, stage, step, axis, room.at[step - 1], room.at[step - 1]).wait_recv()

    def pick(order, first, second):
        return (first, second) if order == "ab" else (second, first)

    def after_core(index):
        order, (own, other, came, _, _) = chunks[index][4:]
        kept[index].wait()
        copy(index, 0, 1, "c", other, other).wait_recv()
        axis, rest = order

        def add(where):
            for item in range(place.size[rest]):
                at = pick(order, where, item)
                own[at] = own[at] + other[at]

        for step in place.partners(axis):
            where = place.moved(axis, step)[axis]
            add(where)
            source = own.at[where] if order == "ab" else own.at[:, where]
            send(index, 1, step, axis, source, came.at[step - 1])
        add(spot[axis])

    def after_first(index):
        order, (own, _, came, later, _) = chunks[index][4:]
        axis, rest = order
        await_all(index, 1, axis, came)

        def add(where):
            at = pick(order, spot[axis], where)
            value = own[at].astype(jnp.float32)
            for step in place.partners(axis):
                value = value + came[step - 1, where].astype(jnp.float32)
            own[at] = value.astype(own.dtype)

        for step in place.partners(rest):
            where = place.moved(rest, step)[rest]
            add(where)
            at = pick(order, spot[axis], where)
            send(index, 2, step, rest, own.at[at], later.at[step - 1])
        add(spot[rest])

    def after_second(index):
        _, result, rows, columns, order, (own, _, _, later, last) = chunks[index]
        rest = order[1]
        await_all(index, 2, rest, later)

        def add(where):
            value = own[spot["a"], spot["b"], where].astype(jnp.float32)
            for step in place.partners(rest):
                value = value + later[step - 1, where].astype(jnp.float32)
            return value

        for step in place.partners("z"):
            where = place.moved("z", step)["z"]
            own[spot["a"], spot["b"], where] = add(where).astype(own.dtype)
            send(index, 3, step, "z", own.at[spot["a"], spot["b"], where], last.at[step - 1])
        result[rows, columns] = add(spot["z"])

    def after_last(index):
        _, result, rows, columns, _, (_, _, _, _, last) = chunks[index]
        await_all(index, 3, "z", last)
        value = result[rows, columns]
        for step in place.partners("z"):
            value = value + last[step - 1].astype(jnp.float32)
        result[rows, columns] = value

    for index in range(ahead):
        begin(index)
    for tick in range(total + 3 * lag):
        begin(tick + ahead)
        for stage, work in enumerate((after_core, after_first, after_second, after_last)):
            index = tick - stage * lag
            if 0 <= index < total:
                work(index)
    for item in sent:
        item.wait_send()


def rooms_of(dims, many, unit, wide, dtype):
    outer, inner, depth = dims
    ones, twos = (many + 1) // 2, many // 2
    tail = (unit, wide)
    return [
        pltpu.VMEM((many, outer, inner, depth) + tail, dtype),
        pltpu.VMEM((many, outer, inner, depth) + tail, dtype),
        pltpu.VMEM((ones, outer - 1, inner, depth) + tail, dtype),
        pltpu.VMEM((twos, inner - 1, outer, depth) + tail, dtype),
        pltpu.VMEM((ones, inner - 1, depth) + tail, dtype),
        pltpu.VMEM((twos, outer - 1, depth) + tail, dtype),
        pltpu.VMEM((many, depth - 1) + tail, dtype),
    ]


def scatter(dims, small, terms, unit, lag=2, ahead=4):
    outer, inner, depth = dims
    devices = 2 * outer * inner * depth
    lead = (outer, inner, 2, depth)
    arrays = [small.reshape(lead + small.shape[1:])] + [
        term.reshape(lead + (term.shape[0] // devices, term.shape[1])) for term in terms
    ]
    pieces = [pieces_of(*arrays[0].shape[4:], arrays[0].shape[4])]
    pieces += [pieces_of(*array.shape[4:], unit) for array in arrays[1:]]
    total = sum(len(items) for items in pieces)
    most = max(dims) - 1
    tail = small.shape[1:]
    side = [
        pltpu.VMEM((outer, inner, depth) + tail, jnp.float32),
        pltpu.VMEM((outer, inner, depth) + tail, jnp.float32),
        pltpu.VMEM((outer - 1, inner, depth) + tail, jnp.float32),
        pltpu.VMEM((inner - 1, depth) + tail, jnp.float32),
        pltpu.VMEM((depth - 1,) + tail, jnp.float32),
    ]
    return pl.pallas_call(
        functools.partial(scatter_kernel, dims, lag, ahead, pieces),
        out_shape=[jax.ShapeDtypeStruct(array.shape[4:], jnp.float32) for array in arrays],
        in_specs=[pl.BlockSpec(memory_space=pl.ANY)] * len(arrays),
        out_specs=[pl.BlockSpec(memory_space=pltpu.VMEM)] * len(arrays),
        scratch_shapes=rooms_of(dims, total - 1, unit, WIDE, jnp.bfloat16)
        + side
        + [
            pltpu.SemaphoreType.DMA((total,)),
            pltpu.SemaphoreType.DMA((total, 4, most)),
            pltpu.SemaphoreType.DMA((total, 4, most)),
        ],
        compiler_params=pltpu.CompilerParams(
            collective_id=1, has_side_effects=True, vmem_limit_bytes=60 << 20
        ),
        name="scatter",
    )(*arrays)


HIGH = lax.Precision.HIGHEST
norm_eps = 1e-05


def norm_affine(values, gain, shift):
    mean = jnp.mean(values, axis=-1, keepdims=True)
    centred = values - mean
    spread = jnp.mean(centred * centred, axis=-1, keepdims=True)
    return centred * lax.rsqrt(spread + norm_eps) * gain + shift


def feature(values):
    return jax.nn.elu(values) + 1.0


def gelu_exact(values):
    return jax.nn.gelu(values, approximate=False)


def allowed_weight(crop, keymask):
    places = jnp.arange(crop.shape[0])
    earlier = places[None, :] <= places[:, None]
    same = crop[:, None] == crop[None, :]
    visible = (keymask[None, :] > 0) | (places[None, :] == places[:, None])
    return (earlier & same & visible).astype(jnp.float32)


def attend_forward(carry, pieces):
    state, norm_state, prev_crop = carry
    query_feat, key_feat, values, crop, keymask = pieces
    weight = allowed_weight(crop, keymask)
    scores = (
        jnp.einsum("ihe,jhe->hij", query_feat, key_feat, preferred_element_type=jnp.float32)
        * weight[None]
    )
    value_wide = values.astype(jnp.float32)
    query_wide = query_feat.astype(jnp.float32)
    key_wide = key_feat.astype(jnp.float32)
    numer = jnp.einsum("hij,jhe->ihe", scores, value_wide, precision=HIGH)
    denom = jnp.sum(scores, axis=2).T
    follows = (crop == prev_crop).astype(jnp.float32)
    numer = numer + follows[:, None, None] * jnp.einsum(
        "ihe,hef->ihf", query_wide, state, precision=HIGH
    )
    denom = denom + follows[:, None] * jnp.einsum(
        "ihe,he->ih", query_wide, norm_state, precision=HIGH
    )
    last_crop = crop[crop.shape[0] - 1]
    carried = (prev_crop == last_crop).astype(jnp.float32)
    select = ((crop == last_crop) & (keymask > 0)).astype(jnp.float32)
    chosen = key_wide * select[:, None, None]
    new_state = carried * state + jnp.einsum("jhe,jhf->hef", chosen, value_wide, precision=HIGH)
    new_norm = carried * norm_state + jnp.sum(chosen, axis=0)
    return ((new_state, new_norm, last_crop), (numer / denom[:, :, None], denom, state, norm_state))


def attend_backward(carry, pieces):
    grad_state, grad_norm = carry
    (
        query_feat,
        key_feat,
        values,
        crop,
        keymask,
        prev_crop,
        state,
        norm_state,
        grad_numer,
        grad_denom,
    ) = pieces
    weight = allowed_weight(crop, keymask)
    scores = (
        jnp.einsum("ihe,jhe->hij", query_feat, key_feat, preferred_element_type=jnp.float32)
        * weight[None]
    )
    value_wide = values.astype(jnp.float32)
    query_wide = query_feat.astype(jnp.float32)
    key_wide = key_feat.astype(jnp.float32)
    grad_scores = (
        jnp.einsum("ihe,jhe->hij", grad_numer, value_wide, precision=HIGH)
        + grad_denom.T[:, :, None]
    ) * weight[None]
    follows = (crop == prev_crop).astype(jnp.float32)
    last_crop = crop[crop.shape[0] - 1]
    carried = (prev_crop == last_crop).astype(jnp.float32)
    select = ((crop == last_crop) & (keymask > 0)).astype(jnp.float32)
    grad_query = jnp.einsum("hij,jhe->ihe", grad_scores, key_wide, precision=HIGH)
    grad_query = grad_query + follows[:, None, None] * (
        jnp.einsum("ihf,hef->ihe", grad_numer, state, precision=HIGH)
        + grad_denom[:, :, None] * norm_state[None]
    )
    grad_key = jnp.einsum("hij,ihe->jhe", grad_scores, query_wide, precision=HIGH)
    grad_key = grad_key + select[:, None, None] * (
        jnp.einsum("jhf,hef->jhe", value_wide, grad_state, precision=HIGH) + grad_norm[None]
    )
    grad_value = jnp.einsum("hij,ihe->jhe", scores, grad_numer, precision=HIGH)
    grad_value = grad_value + select[:, None, None] * jnp.einsum(
        "jhe,hef->jhf", key_wide, grad_state, precision=HIGH
    )
    query_kept = query_wide * follows[:, None, None]
    earlier_state = carried * grad_state + jnp.einsum(
        "ihe,ihf->hef", query_kept, grad_numer, precision=HIGH
    )
    earlier_norm = carried * grad_norm + jnp.einsum(
        "ihe,ih->he", query_kept, grad_denom, precision=HIGH
    )
    return ((earlier_state, earlier_norm), (grad_query, grad_key, grad_value))


def split_blocks(array):
    blocks = array.shape[0] // BLOCK
    return array.reshape((blocks, BLOCK) + array.shape[1:])


def attend_slot(pieces):
    query_feat, key_feat, values, crop, keymask = pieces
    length, heads, head_width = query_feat.shape
    start = (
        jnp.zeros((heads, head_width, head_width), jnp.float32),
        jnp.zeros((heads, head_width), jnp.float32),
        jnp.int32(-1),
    )
    finish, (mixed, denom, states, norms) = lax.scan(
        attend_forward,
        start,
        (
            split_blocks(query_feat),
            split_blocks(key_feat),
            split_blocks(values),
            split_blocks(crop),
            split_blocks(keymask),
        ),
    )
    return (mixed.reshape(length, heads, head_width), denom.reshape(length, heads), states, norms)


def attend_slot_back(pieces):
    query_feat, key_feat, values, crop, keymask, states, norms, grad_numer, grad_denom = pieces
    length, heads, head_width = query_feat.shape
    crop_blocks = split_blocks(crop)
    prev_crops = jnp.concatenate([jnp.full((1,), -1, jnp.int32), crop_blocks[:-1, -1]])
    start = (
        jnp.zeros((heads, head_width, head_width), jnp.float32),
        jnp.zeros((heads, head_width), jnp.float32),
    )
    finish, (grad_query, grad_key, grad_value) = lax.scan(
        attend_backward,
        start,
        (
            split_blocks(query_feat),
            split_blocks(key_feat),
            split_blocks(values),
            crop_blocks,
            split_blocks(keymask),
            prev_crops,
            states,
            norms,
            split_blocks(grad_numer),
            split_blocks(grad_denom),
        ),
        reverse=True,
    )
    shape = (length, heads, head_width)
    return (grad_query.reshape(shape), grad_key.reshape(shape), grad_value.reshape(shape))


def general_body(
    tokens,
    crop_ids,
    kv_mask,
    norm1_gain,
    norm1_bias,
    w_query,
    w_key,
    w_value,
    w_out,
    norm2_gain,
    norm2_bias,
    w_up,
    up_bias,
    w_down,
    down_bias,
    cotangent,
):
    slots, length, width = tokens.shape
    heads = HEADS
    head_width = width // heads
    count = slots * length
    devices = lax.axis_size("dp") * lax.axis_size("fsdp")
    dims = (OUTER, lax.axis_size("dp") // (2 * OUTER), lax.axis_size("fsdp"))
    unit = width // devices
    packed = jnp.concatenate([norm1_gain, norm1_bias, norm2_gain, norm2_bias, down_bias, up_bias])
    packed = jnp.pad(packed, (0, 16 * 128 - packed.shape[0])).reshape(16, 128)
    vectors, full_query, full_key, full_value, full_out, full_up, full_down = gather(
        dims, [packed, w_query, w_key, w_value, w_out, w_up, w_down], unit
    )
    vectors = vectors.reshape(devices, 16 * 128)
    gain_one, bias_one, gain_two, bias_two, full_down_bias = (
        vectors[:, index * unit : (index + 1) * unit].reshape(-1) for index in range(5)
    )
    full_up_bias = vectors[:, 5 * unit : 5 * unit + up_bias.shape[0]].reshape(-1)
    inputs = tokens.reshape(count, width).astype(jnp.float32)
    normed_wide, pull_one = jax.vjp(
        norm_affine, inputs, gain_one.astype(jnp.float32), bias_one.astype(jnp.float32)
    )
    normed = normed_wide.astype(jnp.bfloat16)
    query = jnp.dot(normed, full_query, preferred_element_type=jnp.float32)
    keys = jnp.dot(normed, full_key, preferred_element_type=jnp.float32)
    values = jnp.dot(normed, full_value, preferred_element_type=jnp.float32).astype(jnp.bfloat16)
    query_wide, pull_query = jax.vjp(feature, query)
    key_wide, pull_key = jax.vjp(feature, keys)
    query_feat = query_wide.astype(jnp.bfloat16).reshape(slots, length, heads, head_width)
    key_feat = key_wide.astype(jnp.bfloat16).reshape(slots, length, heads, head_width)
    value_heads = values.reshape(slots, length, heads, head_width)
    mixed_wide, denom, states, norms = lax.map(
        attend_slot, (query_feat, key_feat, value_heads, crop_ids, kv_mask)
    )
    mixed = mixed_wide.reshape(count, width).astype(jnp.bfloat16)
    middle = inputs + jnp.dot(mixed, full_out, preferred_element_type=jnp.float32)
    normed_two_wide, pull_two = jax.vjp(
        norm_affine, middle, gain_two.astype(jnp.float32), bias_two.astype(jnp.float32)
    )
    normed_two = normed_two_wide.astype(jnp.bfloat16)
    upper = jnp.dot(normed_two, full_up, preferred_element_type=jnp.float32) + full_up_bias.astype(
        jnp.float32
    )
    hidden_wide, pull_gelu = jax.vjp(gelu_exact, upper)
    hidden = hidden_wide.astype(jnp.bfloat16)
    result = (
        middle
        + jnp.dot(hidden, full_down, preferred_element_type=jnp.float32)
        + full_down_bias.astype(jnp.float32)
    )
    output = result.astype(jnp.bfloat16).reshape(slots, length, width)
    back_up, back_down = full_up, full_down
    back_query, back_key, back_value, back_out = full_query, full_key, full_value, full_out
    grad_out = cotangent.reshape(count, width)
    grad_down_bias = jnp.sum(grad_out.astype(jnp.float32), axis=0)
    grad_w_down = jnp.dot(hidden.T, grad_out, preferred_element_type=jnp.float32).astype(jnp.bfloat16)
    grad_hidden = jnp.dot(grad_out, back_down.T, preferred_element_type=jnp.float32)
    grad_upper = pull_gelu(grad_hidden)[0].astype(jnp.bfloat16)
    grad_up_bias = jnp.sum(grad_upper.astype(jnp.float32), axis=0)
    grad_w_up = jnp.dot(normed_two.T, grad_upper, preferred_element_type=jnp.float32).astype(jnp.bfloat16)
    grad_normed_two = jnp.dot(grad_upper, back_up.T, preferred_element_type=jnp.float32)
    grad_middle_part, grad_gain_two, grad_bias_two = pull_two(grad_normed_two)
    grad_middle = grad_out.astype(jnp.float32) + grad_middle_part
    grad_attended = grad_middle.astype(jnp.bfloat16)
    grad_w_out = jnp.dot(mixed.T, grad_attended, preferred_element_type=jnp.float32).astype(jnp.bfloat16)
    grad_mixed = jnp.dot(grad_attended, back_out.T, preferred_element_type=jnp.float32).reshape(
        slots, length, heads, head_width
    )
    grad_numer = grad_mixed / denom[..., None]
    grad_denom = -jnp.sum(grad_mixed * mixed_wide, axis=-1) / denom
    grad_query_feat, grad_key_feat, grad_values = lax.map(
        attend_slot_back,
        (
            query_feat,
            key_feat,
            value_heads,
            crop_ids,
            kv_mask,
            states,
            norms,
            grad_numer,
            grad_denom,
        ),
    )
    grad_query = pull_query(grad_query_feat.reshape(count, width))[0].astype(jnp.bfloat16)
    grad_keys = pull_key(grad_key_feat.reshape(count, width))[0].astype(jnp.bfloat16)
    grad_values = grad_values.reshape(count, width).astype(jnp.bfloat16)
    grad_w_query = jnp.dot(normed.T, grad_query, preferred_element_type=jnp.float32).astype(jnp.bfloat16)
    grad_w_key = jnp.dot(normed.T, grad_keys, preferred_element_type=jnp.float32).astype(jnp.bfloat16)
    grad_w_value = jnp.dot(normed.T, grad_values, preferred_element_type=jnp.float32).astype(jnp.bfloat16)
    grad_normed = jnp.dot(grad_query, back_query.T, preferred_element_type=jnp.float32)
    grad_normed = grad_normed + jnp.dot(grad_keys, back_key.T, preferred_element_type=jnp.float32)
    grad_normed = grad_normed + jnp.dot(
        grad_values, back_value.T, preferred_element_type=jnp.float32
    )
    grad_input_part, grad_gain_one, grad_bias_one = pull_one(grad_normed)
    small = jnp.concatenate(
        [
            vector.reshape(devices, -1)
            for vector in (
                grad_gain_one,
                grad_bias_one,
                grad_gain_two,
                grad_bias_two,
                grad_down_bias,
                grad_up_bias,
            )
        ],
        axis=1,
    )
    small = jnp.pad(small, ((0, 0), (0, 8 * 128 - small.shape[1]))).reshape(devices, 8, 128)
    small, own_up, own_down, own_query, own_key, own_value, own_out = scatter(
        dims,
        small,
        [grad_w_up, grad_w_down, grad_w_query, grad_w_key, grad_w_value, grad_w_out],
        unit,
    )
    small = small.reshape(8 * 128)
    own_gain_one, own_bias_one, own_gain_two, own_bias_two, own_down_bias = (
        small[index * unit : (index + 1) * unit] for index in range(5)
    )
    own_up_bias = small[5 * unit : 5 * unit + up_bias.shape[0]]
    input_grad = (grad_middle + grad_input_part).astype(jnp.bfloat16).reshape(slots, length, width)
    return (
        output,
        input_grad,
        own_gain_one,
        own_bias_one,
        own_query,
        own_key,
        own_value,
        own_out,
        own_gain_two,
        own_bias_two,
        own_up,
        own_up_bias,
        own_down,
        own_down_bias,
    )


LENGTH = 512
WIDTH = 1024
HIDDEN = 4096
UNIT = 32
CHUNKS = 24
FEED = 8
ROOMS = 12
DRAINED = 12
LAG = 3
LATE = 3 * LAG
AHEAD = 4
PASS_AHEAD = 2
TERMS_AHEAD = 3
TERMS_START = 27
PASS_AFTER = 2
TERMS_PASS_AFTER = 2
VMEM_LIMIT = 63 << 20


def when(condition):
    if isinstance(condition, bool):
        return (lambda work: work()) if condition else (lambda work: None)
    return pl.when(condition)


def each(count, work):
    def step(index, carry):
        work(index)
        return carry

    lax.fori_loop(0, count, step, 0)


def dot(left, right):
    return jnp.dot(left, right, preferred_element_type=jnp.float32)


def dot_nt(left, right):
    return lax.dot_general(
        left, right, (((1,), (1,)), ((), ())), preferred_element_type=jnp.float32
    )


def dot_tn(left, right):
    return lax.dot_general(
        left, right, (((0,), (0,)), ((), ())), preferred_element_type=jnp.float32
    )


def by_order(place, orders, index, work):
    turn = (index + 3 * place.at["c"]) % len(orders)
    for order in dict.fromkeys(orders):
        turns = [number for number, item in enumerate(orders) if item == order]
        match = turn == turns[0]
        for number in turns[1:]:
            match = match | (turn == number)

        @pl.when(match)
        def _(order=order):
            work(order)


class Mover:
    def __init__(self, place, send_sem, recv_sem):
        self.place, self.send_sem, self.recv_sem = place, send_sem, recv_sem

    def copy(self, lead, stage, step, axis, source, target):
        at = lead + (stage, step - 1)
        return pltpu.make_async_remote_copy(
            source,
            target,
            self.send_sem.at[at],
            self.recv_sem.at[at],
            device_id=self.place.device(axis, step),
            device_id_type=MESH,
        )


class Gather(Mover):
    def region(self, chunk, done, spot):
        lead = tuple(slice(None) if axis in done else spot[axis] for axis in "abcz")
        return chunk.at[lead]

    def unless_passed(self, axis, step, work):
        z = self.place.at["z"]
        if axis == "z" and step == 3:
            pl.when(z != 0)(work)
        elif axis == "z" and step == 1:
            pl.when(z != 3)(work)
        else:
            work()

    def send(self, chunk, lead, order, stage):
        axis, done = order[stage], order[:stage]
        source = self.region(chunk, done, self.place.at)
        for step in self.place.partners(axis):
            self.unless_passed(
                axis, step, self.copy(lead, stage, step, axis, source, source).start
            )

    def passing(self, chunk, lead, order):
        stage = order.index("z")
        spot = dict(self.place.at)
        z = spot["z"]
        spot["z"] = 3 * (2 - z)
        source = self.region(chunk, order[:stage], spot)
        came = self.copy(lead, stage, 2, "z", source, source)
        onward = pltpu.make_async_remote_copy(
            source,
            source,
            self.send_sem.at[lead + (stage, 3)],
            self.recv_sem.at[lead + (stage, 2 * (z - 1))],
            device_id={"fsdp": 3 * (z - 1)},
            device_id_type=MESH,
        )
        return came, onward

    def pass_on(self, chunk, lead, order):
        z = self.place.at["z"]

        @pl.when((z == 1) | (z == 2))
        def _():
            came, onward = self.passing(chunk, lead, order)
            came.wait_recv()
            onward.start()

    def receive(self, chunk, lead, order, stage):
        axis, done = order[stage], order[:stage]
        z = self.place.at["z"]
        for step in self.place.partners(axis):
            spot = self.place.moved(axis, self.place.size[axis] - step)
            target = self.region(chunk, done, spot)
            item = self.copy(lead, stage, step, axis, target, target)
            if axis == "z" and step == 2:
                pl.when((z == 0) | (z == 3))(item.wait_recv)
            else:
                item.wait_recv()

    def drain(self, chunk, lead, order):
        z = self.place.at["z"]
        for stage in range(4):
            axis, done = order[stage], order[:stage]
            source = self.region(chunk, done, self.place.at)
            for step in self.place.partners(axis):
                self.unless_passed(
                    axis, step, self.copy(lead, stage, step, axis, source, source).wait_send
                )
            if axis == "z":

                @pl.when((z == 1) | (z == 2))
                def _():
                    self.passing(chunk, lead, order)[1].wait_send()


class Weights(Gather):
    orders = ("bzac", "azbc", "zbac", "azbc", "bzac", "zabc")

    def __init__(self, place, buffer, send_sem, recv_sem):
        super().__init__(place, send_sem, recv_sem)
        self.buffer, self.total = buffer, buffer.shape[0]

    def by_order(self, index, work):
        by_order(self.place, self.orders, index, work)

    def begin(self, index):
        @when(index < self.total)
        def _():
            self.by_order(
                index, lambda order: self.send(self.buffer.at[index], (index,), order, 0)
            )

    def pass_on_at(self, index, stage):
        @when((index >= 0) & (index < self.total))
        def _():
            def work(order):
                if order.index("z") == stage:
                    self.pass_on(self.buffer.at[index], (index,), order)

            self.by_order(index, work)

    def tick(self, now):
        self.begin(now + AHEAD)
        past = now - DRAINED

        @when((past >= 0) & (past < self.total))
        def _():
            self.finish_one(past)

        self.pass_on_at(now + PASS_AHEAD, 0)
        self.pass_on_at(now - PASS_AFTER, 1)
        for stage in range(4):
            index = now - stage * LAG
            live = (index >= 0) & (index < self.total)

            @when(live)
            def _(index=index, stage=stage):
                def work(order):
                    chunk = self.buffer.at[index]
                    self.receive(chunk, (index,), order, stage)
                    if stage < 3:
                        self.send(chunk, (index,), order, stage + 1)

                self.by_order(index, work)

    def finish_one(self, index):
        self.by_order(index, lambda order: self.drain(self.buffer.at[index], (index,), order))

    def finish(self, first, end):
        each(end - first, lambda step: self.finish_one(first + step))


def moments(values):
    mean = jnp.mean(values, axis=-1, keepdims=True)
    centred = values - mean
    spread = jnp.mean(centred * centred, axis=-1, keepdims=True)
    scale = lax.rsqrt(spread + norm_eps)
    return centred * scale, scale


def gelu_pair(upper):
    bell = jnp.exp(-0.5 * upper * upper) * 0.3989422804014327
    below = 0.5 * (1.0 + lax.erf(upper * 0.7071067811865476))
    return upper * below, below + upper * bell


def matrix(buffer, index):
    return buffer[index].reshape(WIDTH, WIDE)


def column_of(row):
    tall = jnp.transpose(jnp.broadcast_to(row.astype(jnp.float32), (8, row.shape[1])))
    return tall[:, 0:1]


def read_vectors(gathered, devices):
    flat = gathered[...].reshape(devices * 8, 128).astype(jnp.bfloat16)

    def line(number):
        shape = (devices, devices * 8)
        wanted = lax.broadcasted_iota(jnp.int32, shape, 0) * 8 + number
        chosen = lax.broadcasted_iota(jnp.int32, shape, 1) == wanted
        return dot(chosen.astype(jnp.bfloat16), flat).astype(jnp.bfloat16)

    def spread(lines, start, wide):
        total = wide * devices
        lane = lax.broadcasted_iota(jnp.int32, (128, total), 1)
        wanted = lax.broadcasted_iota(jnp.int32, (128, total), 0) == start + lane % wide
        found = dot(lines, wanted.astype(jnp.bfloat16))
        owner = lax.broadcasted_iota(jnp.int32, (devices, total), 1) // wide
        mine = owner == lax.broadcasted_iota(jnp.int32, (devices, total), 0)
        return jnp.sum(jnp.where(mine, found, 0.0), axis=0, keepdims=True)

    first, second = line(0), line(1)
    rows = [spread(first, index * UNIT, UNIT) for index in range(4)]
    rows.append(spread(line(2), 0, UNIT))
    return rows, [spread(second, index * UNIT, UNIT) for index in range(4)]


def write_vectors(rows, devices):
    result = None
    for index, row in enumerate(rows):
        owner = lax.broadcasted_iota(jnp.int32, (devices, WIDTH), 1) // UNIT
        mine = owner == lax.broadcasted_iota(jnp.int32, (devices, WIDTH), 0)
        spread = jnp.where(mine, row, 0.0)
        lane = lax.broadcasted_iota(jnp.int32, (WIDTH, 128), 0)
        wanted = lax.broadcasted_iota(jnp.int32, (WIDTH, 128), 1) == index * UNIT + lane % UNIT
        found = jnp.dot(
            spread,
            wanted.astype(jnp.float32),
            preferred_element_type=jnp.float32,
            precision=HIGH,
        )
        result = found if result is None else result + found
    return result


def head_lanes(which, shape):
    lane = lax.broadcasted_iota(jnp.int32, shape, 1)
    return lane < 64 if which == 0 else lane >= 64


def allowed(crop_row, mask_row):
    shape = (LENGTH, LENGTH)
    row = lax.broadcasted_iota(jnp.int32, shape, 0)
    column = lax.broadcasted_iota(jnp.int32, shape, 1)
    same = column_of(crop_row) == crop_row.astype(jnp.float32)
    seen = (mask_row > 0) | (row == column)
    return jnp.where(same & (column <= row) & seen, 1.0, 0.0).astype(jnp.bfloat16)


def allowed_back(crop_row, mask_row):
    shape = (LENGTH, LENGTH)
    row = lax.broadcasted_iota(jnp.int32, shape, 0)
    column = lax.broadcasted_iota(jnp.int32, shape, 1)
    same = column_of(crop_row) == crop_row.astype(jnp.float32)
    seen = (column_of(mask_row) > 0) | (row == column)
    return jnp.where(same & (row <= column) & seen, 1.0, 0.0).astype(jnp.bfloat16)


def transpose_into(source, target):
    def work(index):
        at = pl.ds(pl.multiple_of(index * 128, 128), 128)
        target[at, :] = jnp.transpose(source[:, at])

    each(source.shape[1] // 128, work)


def by_rows(work):
    each(LENGTH // 64, lambda index: work(pl.ds(pl.multiple_of(index * 64, 64), 64)))


def forward_heads(pair, qkv, mask, mixed, inverse, attended):
    chunk = pair // 4
    lanes = pl.ds(pl.multiple_of((pair % 4) * 128, 128), 128)
    columns = pl.ds(pl.multiple_of(pair * 128, 128), 128)
    for part in (0, 1):
        keys = 256 * (part + 1)
        rows = slice(part * 256, part * 256 + 256)
        query = qkv[chunk, rows, lanes]
        key = qkv[2 + chunk, 0:keys, lanes]
        value = qkv[4 + chunk, 0:keys, lanes]
        zero, one = jnp.zeros_like(key), jnp.ones_like(key)
        total = None
        for which in (0, 1):
            mine = head_lanes(which, key.shape)
            scores = dot_nt(query, jnp.where(mine, key, zero)).astype(jnp.bfloat16)
            scores = scores * mask[rows, 0:keys]
            right = jnp.concatenate(
                [jnp.where(mine, value, zero), jnp.where(mine, one, zero)], axis=1
            )
            term = dot(scores, right)
            total = term if total is None else total + term
        inverted = 1.0 / total[:, 128:]
        result = total[:, :128] * inverted
        mixed[rows, columns] = result
        inverse[rows, columns] = inverted
        attended[rows, columns] = result.astype(jnp.bfloat16)


def hidden_order(flip):
    shape = (4 * 128, 4 * 128)
    rows, columns = (lax.broadcasted_iota(jnp.int32, shape, axis) for axis in (0, 1))
    if flip:
        rows, columns = columns, rows
    wanted = (rows // UNIT) % 4 * 128 + rows // 128 * UNIT + rows % UNIT
    return columns == wanted


def feed_block(block, refs):
    normed, normed_t, grad_out, weights, up_bias, result, grad_normed, staged, grad_bias = refs
    group, half = block // 2, block % 2
    first = FEED + 4 * group
    up = matrix(weights, first + 2 + half)
    upper = dot(normed[...], up) + up_bias[pl.ds(block, 1), :]
    hidden, slope = gelu_pair(upper)
    hidden = hidden.astype(jnp.bfloat16)
    grad_hidden = None
    for side in (0, 1):
        columns = slice(side * WIDE, side * WIDE + WIDE)
        down = weights[first + side, half].reshape(WIDE, WIDE)
        result[:, columns] += dot(hidden, down)
        term = dot_nt(grad_out[:, columns], down)
        grad_hidden = term if grad_hidden is None else grad_hidden + term
    grad_upper = (grad_hidden * slope).astype(jnp.bfloat16)
    grad_bias[pl.ds(block, 1), :] = jnp.sum(
        grad_upper.astype(jnp.float32), axis=0, keepdims=True
    )
    grad_normed[...] += dot_nt(grad_upper, up)
    value = dot(normed_t[...], grad_upper).astype(jnp.bfloat16)
    staged[0] = value.reshape(staged.shape[1:])
    for side in (0, 1):
        columns = slice(side * WIDE, side * WIDE + WIDE)
        value = dot_tn(hidden, grad_out[:, columns]).astype(jnp.bfloat16)
        staged[1, side] = value.reshape(staged.shape[2:])


class Sums(Mover):
    def start(self, lead, stage, step, axis, source, target):
        self.copy(lead, stage, step, axis, source, target).start()

    def region(self, order, stage, where):
        at = {axis: self.place.at[axis] for axis in order[:stage]}
        at[order[stage]] = where
        return tuple(at.get(axis, slice(None)) for axis in "abz")

    def blocks(self, order, stage, where):
        rest = [axis for axis in "abz" if axis in order[stage + 1 :]]
        base = self.region(order, stage, where)
        sizes = [self.place.size[axis] for axis in rest]
        for inner in itertools.product(*(range(size) for size in sizes)):
            place = dict(zip(rest, inner))
            yield (
                tuple(place.get(axis, item) for axis, item in zip("abz", base)),
                inner,
            )

    def room(self, order, stage, rooms, step):
        if stage == 0:
            return rooms[0]
        if stage == 1:
            size = self.place.size[order[2]]
            return rooms[1].at[pl.ds((step - 1) * size, size)]
        return rooms[2].at[step - 1]

    def send_stage(self, lead, order, stage, total, rooms, add):
        axis = order[stage]
        z = self.place.at["z"]
        for step in self.place.partners(axis):
            where = self.place.moved(axis, step)[axis]
            for at, _ in self.blocks(order, stage, where):
                add(at)
            source = total.at[self.region(order, stage, where)]
            room = self.room(order, stage, rooms, step)
            item = self.copy(lead, stage + 1, step, axis, source, room)
            if axis != "z":
                item.start()
            elif step == 2:
                pl.when((z == 0) | (z == 3))(item.start)
            else:
                far = 3 if step == 1 else 0
                pl.when(z != far)(item.start)

                @pl.when(z == far)
                def _(step=step, source=source, far=far):
                    pltpu.make_async_remote_copy(
                        source,
                        self.room(order, stage, rooms, 4),
                        self.send_sem.at[lead + (stage + 1, step - 1)],
                        self.recv_sem.at[lead + (stage + 1, 3)],
                        device_id={"fsdp": 2 if far == 3 else 1},
                        device_id_type=MESH,
                    ).start()

        for at, _ in self.blocks(order, stage, self.place.at[axis]):
            add(at)

    def pass_on(self, lead, order, total, rooms):
        z = self.place.at["z"]
        stage = order.index("z")

        @pl.when((z == 1) | (z == 2))
        def _():
            came = self.room(order, stage, rooms, 4)
            self.copy(lead, stage + 1, 4, "z", came, came).wait_recv()
            where = 3 * (2 - z)
            for at, inner in self.blocks(order, stage, where):
                total[at] = total[at] + (came[inner] if inner else came[...])
            source = total.at[self.region(order, stage, where)]
            self.start(lead, stage + 1, 2, "z", source, self.room(order, stage, rooms, 2))

    def await_stage(self, lead, order, stage, rooms):
        axis = order[stage]
        for step in self.place.partners(axis):
            room = self.room(order, stage, rooms, step)
            item = self.copy(lead, stage + 1, step, axis, room, room)
            if axis == "z" and step != 2:
                pl.when(self.place.at["z"] != (0 if step == 1 else 3))(item.wait_recv)
            else:
                item.wait_recv()

    def after_core(self, lead, order, own, total, rooms):
        def add(at):
            total[at] = own[at] + total[at]

        self.send_stage(lead, order, 0, total, rooms, add)

    def came_in(self, order, stage, total, rooms, at):
        rest = [axis for axis in "abz" if axis in order[stage + 1 :]]
        inner = tuple(item for axis, item in zip("abz", at) if axis in rest)
        steps = self.place.partners(order[stage])
        wide = total.dtype if len(steps) == 1 and stage < 2 else jnp.float32
        value = total[at].astype(wide)
        for step in steps:
            room = self.room(order, stage, rooms, step)
            term = (room[inner] if inner else room[...]).astype(wide)
            if order[stage] == "z" and step != 2:
                near = self.place.at["z"] != (0 if step == 1 else 3)
                term = jnp.where(near, term, jnp.zeros_like(term))
            value = value + term
        return value

    def after_stage(self, lead, order, stage, total, rooms):
        self.await_stage(lead, order, stage - 1, rooms)

        def add(at):
            total[at] = self.came_in(order, stage - 1, total, rooms, at).astype(total.dtype)

        self.send_stage(lead, order, stage, total, rooms, add)

    def after_last(self, lead, order, total, rooms):
        self.await_stage(lead, order, 2, rooms)
        at = tuple(self.place.at[axis] for axis in "abz")
        return self.came_in(order, 2, total, rooms, at)

    def drain(self, lead, order, total, rooms):
        self.copy(lead, 0, 1, "c", total, total).wait_send()
        for stage in range(3):
            axis = order[stage]
            for step in self.place.partners(axis):
                room = self.room(order, stage, rooms, step)
                self.copy(lead, stage + 1, step, axis, room, room).wait_send()


class Gradients(Sums):
    orders = ("azb", "bza", "abz", "bza", "azb", "baz")

    def __init__(self, place, terms, sums, rooms, results, ring, ring_sem, send_sem, recv_sem):
        super().__init__(place, send_sem, recv_sem)
        self.terms, self.sums, self.rooms, self.results = terms, sums, rooms, results
        self.ring, self.ring_sem = ring, ring_sem
        self.total = results.shape[0]

    def sum_at(self, index):
        return self.sums.at[index // 2, :, :, index % 2]

    def by_order(self, index, work):
        rooms = [room.at[index % ROOMS] for room in self.rooms]
        total = self.sum_at(index)
        by_order(self.place, self.orders, index, lambda order: work(order, total, rooms))

    def begin(self, index):
        @when(index < self.total)
        def _():
            side = self.place.at["c"]
            slot = index % (TERMS_AHEAD + 1)
            source = self.terms.at[index]
            self.start((index,), 0, 1, "c", source.at[:, :, 1 - side], self.sum_at(index))
            pltpu.make_async_copy(
                source.at[:, :, side], self.ring.at[slot], self.ring_sem.at[slot]
            ).start()

    def tick(self, now):
        self.begin(now + TERMS_AHEAD)

        def live(index):
            return (index >= 0) & (index < self.total)

        @when(live(now - DRAINED))
        def _():
            self.finish_one(now - DRAINED)

        @when(live(now))
        def _():
            slot = now % (TERMS_AHEAD + 1)
            own = self.ring.at[slot]
            pltpu.make_async_copy(own, own, self.ring_sem.at[slot]).wait()
            total = self.sum_at(now)
            self.copy((now,), 0, 1, "c", total, total).wait_recv()
            self.by_order(
                now,
                lambda order, total, rooms: self.after_core((now,), order, own, total, rooms),
            )

        for stage in (1, 2):
            index = now - stage * LAG

            @when(live(index))
            def _(index=index, stage=stage):
                self.by_order(
                    index,
                    lambda order, total, rooms: self.after_stage(
                        (index,), order, stage, total, rooms
                    ),
                )

        for stage in (1, 2):
            index = now - stage * LAG - TERMS_PASS_AFTER

            @when(live(index))
            def _(index=index, stage=stage):
                def work(order, total, rooms):
                    if order.index("z") == stage:
                        self.pass_on((index,), order, total, rooms)

                self.by_order(index, work)

        index = now - 3 * LAG

        @when(live(index))
        def _():
            def work(order, total, rooms):
                self.results[index] = self.after_last((index,), order, total, rooms)

            self.by_order(index, work)

    def finish_one(self, index):
        self.by_order(
            index, lambda order, total, rooms: self.drain((index,), order, total, rooms)
        )

    def finish(self, first):
        each(self.total - first, lambda step: self.finish_one(first + step))


def backward_heads(pair, qkv, mask, mask_t, mixed, inverse, grad_mixed):
    chunk = pair // 4
    lanes = pl.ds(pl.multiple_of((pair % 4) * 128, 128), 128)
    columns = pl.ds(pl.multiple_of(pair * 128, 128), 128)
    query = qkv[chunk, :, lanes]
    key = qkv[2 + chunk, :, lanes]
    value = qkv[4 + chunk, :, lanes]
    grad_numer = (grad_mixed[:, columns] * inverse[:, columns]).astype(jnp.bfloat16)
    part = grad_numer.astype(jnp.float32) * mixed[:, columns]
    high = part.astype(jnp.bfloat16)
    low = pltpu.roll(part - high.astype(jnp.float32), 64, 1).astype(jnp.bfloat16)
    zero, minus = jnp.zeros_like(query), jnp.full_like(query, -1.0)
    heads = []
    for which in (0, 1):
        mine = head_lanes(which, query.shape)
        heads.append(
            (
                jnp.concatenate([grad_numer, jnp.where(mine, high, low)], axis=1),
                jnp.concatenate([jnp.where(mine, value, zero), minus], axis=1),
                jnp.where(mine, query, zero),
                jnp.where(mine, key, zero),
                jnp.where(mine, grad_numer, zero),
            )
        )
    for part in (0, 1):
        keys = 256 * (part + 1)
        rows = slice(part * 256, part * 256 + 256)
        total = None
        for left, right, _, own_key, _ in heads:
            grad_scores = dot_nt(left[rows], right[:keys]).astype(jnp.bfloat16)
            term = dot(grad_scores * mask[rows, 0:keys], own_key[:keys])
            total = term if total is None else total + term
        slope = jnp.minimum(query[rows].astype(jnp.float32), 1.0)
        qkv[chunk, rows, lanes] = (total * slope).astype(jnp.bfloat16)
    for part in (0, 1):
        start = part * 256
        rows = slice(start, start + 256)
        grad_key = grad_value = None
        for left, right, own_query, own_key, own_grad in heads:
            seen = mask_t[rows, start:LENGTH]
            scores = dot_nt(own_key[rows], query[start:]).astype(jnp.bfloat16) * seen
            grad_scores = dot_nt(right[rows], left[start:]).astype(jnp.bfloat16) * seen
            term = dot(scores, own_grad[start:])
            grad_value = term if grad_value is None else grad_value + term
            term = dot(grad_scores, own_query[start:])
            grad_key = term if grad_key is None else grad_key + term
        slope = jnp.minimum(key[rows].astype(jnp.float32), 1.0)
        qkv[2 + chunk, rows, lanes] = (grad_key * slope).astype(jnp.bfloat16)
        qkv[4 + chunk, rows, lanes] = grad_value.astype(jnp.bfloat16)


def layer_kernel(dims, *refs):
    crops, kept, gain_one, bias_one, gain_two, bias_two, bias_down, bias_up = refs[:8]
    tokens_in, grad_out_in = refs[8:10]
    shards = refs[10:16]
    output, input_grad, mixed_kept, inverse_kept, normed_t_kept, attention_kept, terms = refs[16:23]
    owned_out, owned_up_out, owned_small = refs[23:26]
    (
        owned,
        owned_up,
        pixels,
        grad_out,
        weights,
        up_shard,
        vectors,
        rows,
        up_bias,
        mask,
        mask_t,
        qkv,
        normed,
        turned_one,
        turned_two,
        middle,
        wide_one,
        wide_two,
        wide_three,
        staged,
        grad_up_bias,
        sums,
        small,
        ring,
        rooms_one,
        rooms_two,
        rooms_three,
        side_total,
        side_one,
        side_two,
        side_three,
        send_sem,
        recv_sem,
        vector_send_sem,
        vector_recv_sem,
        load_sem,
        store_sem,
        stage_sem,
        ring_sem,
        terms_send_sem,
        terms_recv_sem,
        side_send_sem,
        side_recv_sem,
        sibling_sem,
    ) = refs[26:]
    outer, inner, depth = dims
    devices = 2 * outer * inner * depth
    place = Place(dims)
    spot = (place.at["a"], place.at["b"], place.at["c"], place.at["z"])
    copies = {}

    def move(name, source, target):
        item = pltpu.make_async_copy(source, target, load_sem.at[len(copies)])
        item.start()
        copies[name] = item

    for index in range(FEED):
        source = shards[index // 2].at[:, pl.ds((index % 2) * WIDE, WIDE)]
        move(index, source, weights.at[(index,) + spot])
    move("tokens", tokens_in, pixels)
    move("up", shards[4], up_shard)
    for group in range(4):
        for half in (0, 1):
            source = shards[5].at[pl.ds(group * UNIT, UNIT), pl.ds(half * WIDE, WIDE)]
            index = FEED + 4 * group + half
            move(index, source, weights.at[(index,) + spot])
    move("grad_out", grad_out_in, grad_out)

    vector_gather = Gather(place, vector_send_sem, vector_recv_sem)
    vector_order = "zbac"
    lines = [
        jnp.concatenate([item[...] for item in (gain_one, bias_one, gain_two, bias_two)], axis=1),
        bias_up[...],
        jnp.concatenate([bias_down[...], jnp.zeros((1, 128 - UNIT), jnp.bfloat16)], axis=1),
    ]
    vectors[spot] = jnp.concatenate(
        [line.astype(jnp.float32) for line in lines] + [jnp.zeros((5, 128), jnp.float32)], axis=0
    )
    place.greet()
    vector_gather.send(vectors, (), vector_order, 0)
    gather_all = Weights(place, weights, send_sem, recv_sem)
    for index in range(AHEAD):
        copies[index].wait()
        gather_all.begin(index)
    for index in range(PASS_AHEAD):
        gather_all.pass_on_at(index, 0)
    for name, item in copies.items():
        if name not in range(AHEAD) and name not in ("up", "tokens", "grad_out"):
            item.wait()
    vector_gather.pass_on(vectors, (), vector_order)
    vector_gather.receive(vectors, (), vector_order, 0)
    vector_gather.send(vectors, (), vector_order, 1)
    gather_all.tick(0)
    copies["up"].wait()
    stacked = jnp.concatenate(
        [up_shard[:, index * WIDE : (index + 1) * WIDE] for index in range(8)], axis=0
    )
    stacked = dot(stacked, hidden_order(False).astype(jnp.bfloat16)).astype(jnp.bfloat16)
    for part in range(8):
        for group in range(4):
            at = (FEED + 4 * group + 2 + part // 4,) + spot
            lanes = slice((part % 4) * 128, (part % 4) * 128 + 128)
            weights[at + (slice(None), lanes)] = stacked[
                part * UNIT : (part + 1) * UNIT, group * 128 : (group + 1) * 128
            ]
    vector_gather.receive(vectors, (), vector_order, 1)
    vector_gather.send(vectors, (), vector_order, 2)
    gather_all.tick(1)
    mask[...] = allowed(crops[...], kept[...])
    vector_gather.receive(vectors, (), vector_order, 2)
    vector_gather.send(vectors, (), vector_order, 3)
    gather_all.tick(2)
    copies["tokens"].wait()
    copies["grad_out"].wait()
    sums[...] = jnp.zeros(sums.shape, jnp.float32)
    vector_gather.receive(vectors, (), vector_order, 3)
    width_rows, up_rows = read_vectors(vectors, devices)
    for index, row in enumerate(width_rows):
        rows[index : index + 1, :] = row
    for group, row in enumerate(up_rows):
        for half in (0, 1):
            up_bias[2 * group + half : 2 * group + half + 1, :] = row[
                :, half * WIDE : half * WIDE + WIDE
            ]
    gather_all.tick(3)

    def first_norm(at):
        value = pixels[at, :].astype(jnp.float32)
        unit, _ = moments(value)
        normed[at, :] = (unit * rows[0:1, :] + rows[1:2, :]).astype(jnp.bfloat16)
        middle[at, :] = value

    by_rows(first_norm)
    gather_all.tick(4)
    stores = {}

    def store(name, source, target):
        item = pltpu.make_async_copy(source, target, store_sem.at[len(stores)])
        item.start()
        stores[name] = item

    transpose_into(normed, turned_one)
    store("normed", turned_one, normed_t_kept)
    each(LATE - 5, lambda index: gather_all.tick(5 + index))

    def project(index):
        gather_all.tick(LATE + index)
        value = dot(normed[...], matrix(weights, index))
        mapped = jnp.where(value > 0, value + 1.0, jnp.exp(jnp.minimum(value, 0.0)))
        qkv[index] = jnp.where(index < 4, mapped, value).astype(jnp.bfloat16)

    each(6, project)
    attended, mixed, inverse = pixels, wide_one, wide_two

    def heads(pair):
        @pl.when(pair % 2 == 0)
        def _():
            gather_all.tick(LATE + 6 + pair // 2)

        forward_heads(pair, qkv, mask, mixed, inverse, attended)

    each(8, heads)
    store("mixed", mixed, mixed_kept)
    store("inverse", inverse, inverse_kept)
    store("attention", weights.at[pl.ds(0, FEED)], attention_kept)
    mask_t[...] = allowed_back(crops[...], kept[...])
    for half in (0, 1):
        columns = slice(half * WIDE, half * WIDE + WIDE)
        middle[:, columns] += dot(attended[...], matrix(weights, 6 + half))
    stores["normed"].wait()
    transpose_into(attended, turned_one)
    result, grad_normed, normed_two = wide_one, wide_two, normed
    stores["mixed"].wait()
    stores["inverse"].wait()

    def second_norm(at):
        value = middle[at, :]
        unit, _ = moments(value)
        normed_two[at, :] = (unit * rows[2:3, :] + rows[3:4, :]).astype(jnp.bfloat16)
        result[at, :] = value + rows[4:5, :]
        grad_normed[at, :] = jnp.zeros((64, WIDTH), jnp.float32)

    by_rows(second_norm)
    transpose_into(normed_two, turned_two)

    adder = Gradients(
        place,
        terms,
        weights,
        (rooms_one, rooms_two, rooms_three),
        owned,
        ring,
        ring_sem,
        terms_send_sem,
        terms_recv_sem,
    )

    def leave(block):
        first, half = 4 * (block // 2), block % 2
        return (
            pltpu.make_async_copy(staged.at[0], terms.at[first + 2 + half], stage_sem.at[0]),
            pltpu.make_async_copy(
                staged.at[1], terms.at[pl.ds(first, 2), half], stage_sem.at[1]
            ),
        )

    def last_tick(block):
        return LATE + 10 + 4 * (block // 2) + block % 2

    def feed(block):
        begin = last_tick(block - 1) + 1

        def both(step, carry):
            @pl.when(step >= LATE + 10)
            def _():
                gather_all.tick(step)

            @pl.when((step == begin) & (block > 0))
            def _():
                for item in leave(block - 1):
                    item.wait()

            @pl.when(step == TERMS_START)
            def _():
                pl.semaphore_wait(sibling_sem, 1)
                for index in range(TERMS_AHEAD):
                    adder.begin(index)

            @pl.when(step >= TERMS_START)
            def _():
                adder.tick(step - TERMS_START)

            return carry

        lax.fori_loop(begin, last_tick(block) + 1, both, 0)
        feed_block(
            block,
            (
                normed_two,
                turned_two,
                grad_out,
                weights,
                up_bias,
                result,
                grad_normed,
                staged,
                grad_up_bias,
            ),
        )
        for item in leave(block):
            item.start()

        @pl.when(block == 2)
        def _():
            stores["attention"].wait()
            pl.semaphore_signal(
                sibling_sem, 1, device_id=place.device("c", 1), device_id_type=MESH
            )

    each(8, feed)
    done = last_tick(7) + 1 - TERMS_START
    adder.tick(done)
    for item in leave(7):
        item.wait()
    gather_all.finish(LATE + 24 - DRAINED, CHUNKS)
    loads = {}

    def load(name, source, target):
        item = pltpu.make_async_copy(source, target, store_sem.at[4 + len(loads)])
        item.start()
        loads[name] = item

    load("out", attention_kept.at[pl.ds(6, 2)], weights.at[pl.ds(ROOMS + 6, 2)])
    load("normed", normed_t_kept, turned_two)
    load("rest", attention_kept.at[pl.ds(0, 6)], weights.at[pl.ds(ROOMS, 6)])
    grad_attended, shown, grad_middle = pixels, normed, middle

    def close_branch(at):
        unit, scale = moments(middle[at, :])
        grad = grad_out[at, :].astype(jnp.float32)
        value = grad_normed[at, :]
        shown[at, :] = result[at, :].astype(jnp.bfloat16)
        sums[0:1, :] += jnp.sum(value * unit, axis=0, keepdims=True)
        sums[1:2, :] += jnp.sum(value, axis=0, keepdims=True)
        sums[2:3, :] += jnp.sum(grad, axis=0, keepdims=True)
        scaled = value * rows[2:3, :]
        summed = grad + scale * (
            scaled
            - jnp.mean(scaled, axis=-1, keepdims=True)
            - unit * jnp.mean(scaled * unit, axis=-1, keepdims=True)
        )
        grad_middle[at, :] = summed
        grad_attended[at, :] = summed.astype(jnp.bfloat16)

    by_rows(close_branch)
    load("mixed", mixed_kept, mixed)
    load("inverse", inverse_kept, inverse)
    load("output", shown, output)
    adder.tick(done + 1)
    loads["out"].wait()
    grad_mixed = wide_three
    grad_mixed[...] = dot_nt(grad_attended[:, 0:WIDE], matrix(weights, ROOMS + 6)) + dot_nt(
        grad_attended[:, WIDE:WIDTH], matrix(weights, ROOMS + 7)
    )
    adder.tick(done + 2)

    def stage_out(slot, index):
        return pltpu.make_async_copy(staged.at[slot], terms.at[index], stage_sem.at[slot])

    for half in (0, 1):
        columns = slice(half * WIDE, half * WIDE + WIDE)
        value = dot(turned_one[...], grad_attended[:, columns]).astype(jnp.bfloat16)
        staged[half] = value.reshape(staged.shape[1:])
        stage_out(half, 16 + half).start()
    load("tokens", tokens_in, pixels)
    adder.tick(done + 3)
    for name in ("mixed", "inverse", "normed", "rest"):
        loads[name].wait()
    for half in (0, 1):
        stage_out(half, 16 + half).wait()
    spread = 14 - (done + 4)

    def back_heads(pair):
        @pl.when((pair + 1) * spread // 8 > pair * spread // 8)
        def _():
            adder.tick(done + 4 + pair * spread // 8)

        backward_heads(pair, qkv, mask, mask_t, mixed, inverse, grad_mixed)

    each(8, back_heads)
    grad_first = grad_mixed
    grad_first[...] = jnp.zeros(grad_first.shape, jnp.float32)

    def back_project(index):
        value = dot(turned_two[...], qkv[index]).astype(jnp.bfloat16)
        staged[index % 2] = value.reshape(staged.shape[1:])
        stage_out(index % 2, 18 + index).start()
        grad_first[...] += dot_nt(qkv[index], matrix(weights, ROOMS + index))

        @pl.when(index > 0)
        def _():
            stage_out((index - 1) % 2, 17 + index).wait()

        adder.tick(14 + index)

    each(6, back_project)
    stage_out(1, 23).wait()
    adder.tick(20)
    loads["tokens"].wait()
    loads["output"].wait()

    def close(at):
        unit, scale = moments(pixels[at, :].astype(jnp.float32))
        value = grad_first[at, :]
        sums[3:4, :] += jnp.sum(value * unit, axis=0, keepdims=True)
        sums[4:5, :] += jnp.sum(value, axis=0, keepdims=True)
        scaled = value * rows[0:1, :]
        shown[at, :] = (
            grad_middle[at, :]
            + scale
            * (
                scaled
                - jnp.mean(scaled, axis=-1, keepdims=True)
                - unit * jnp.mean(scaled * unit, axis=-1, keepdims=True)
            )
        ).astype(jnp.bfloat16)

    by_rows(close)
    load("input_grad", shown, input_grad)
    adder.tick(21)
    groups = [
        jnp.concatenate(
            [grad_up_bias[2 * group + half : 2 * group + half + 1, :] for half in (0, 1)], axis=1
        )
        for group in range(4)
    ]
    lines = [
        write_vectors([sums[index : index + 1, :] for index in (3, 4, 0, 1)], devices),
        write_vectors(groups, devices),
        write_vectors([sums[2:3, :]], devices),
    ]
    for device in range(devices):
        at = (
            device // (2 * inner * depth),
            (device // (2 * depth)) % inner,
            (device // depth) % 2,
            device % depth,
        )
        for row, line in enumerate(lines):
            small[at + (slice(row, row + 1),)] = line[device : device + 1, :]
        small[at + (slice(3, 8),)] = jnp.zeros((5, 128), jnp.float32)
    side = Sums(place, side_send_sem, side_recv_sem)
    rooms = (side_one, side_two, side_three)
    core = place.at["c"]
    side.start((), 0, 1, "c", small.at[:, :, 1 - core], side_total)

    def last_ticks(step):
        adder.tick(22 + step)

        @pl.when(step == 0)
        def _():
            side.copy((), 0, 1, "c", side_total, side_total).wait_recv()
            side.after_core((), "abz", small.at[:, :, core], side_total, rooms)

        for stage in (1, 2):

            @pl.when(step == stage)
            def _(stage=stage):
                side.after_stage((), "abz", stage, side_total, rooms)

        @pl.when(step == 3)
        def _():
            side.pass_on((), "abz", side_total, rooms)

        @pl.when(step == 4)
        def _():
            owned_small[...] = side.after_last((), "abz", side_total, rooms)

        @pl.when(step == 5)
        def _():
            back = hidden_order(True).astype(jnp.float32)
            for part in range(8):
                lanes = slice((part % 4) * 128, (part % 4) * 128 + 128)
                value = jnp.concatenate(
                    [owned[4 * group + 2 + part // 4, :, lanes] for group in range(4)], axis=1
                )
                owned_up[:, part * WIDE : (part + 1) * WIDE] = jnp.dot(
                    value, back, preferred_element_type=jnp.float32, precision=HIGH
                )

    each(CHUNKS + LATE - 23, last_ticks)
    load("up", owned_up, owned_up_out)
    load("feed", owned.at[pl.ds(0, 16)], owned_out.at[pl.ds(0, 16)])
    adder.tick(CHUNKS + LATE - 1)
    load("attention", owned.at[pl.ds(16, 8)], owned_out.at[pl.ds(16, 8)])
    vector_gather.drain(vectors, (), vector_order)
    side.drain((), "abz", side_total, rooms)
    adder.finish(CHUNKS + LATE - DRAINED)
    for name in ("input_grad", "up", "feed", "attention"):
        loads[name].wait()


def layer(dims, tokens, cotangent, crops, kept, small, shards):
    outer, inner, depth = dims
    most = max(dims)
    lead = (outer, inner, 2, depth)
    chip = (outer, inner, depth)
    tile, small_tile = (UNIT, WIDE), (8, 128)
    whole, turned = (LENGTH, WIDTH), (WIDTH, LENGTH)
    f32, bf16 = jnp.float32, jnp.bfloat16
    shape = jax.ShapeDtypeStruct
    room, dma = pltpu.VMEM, pltpu.SemaphoreType.DMA
    vmem, anywhere = pl.BlockSpec(memory_space=pltpu.VMEM), pl.BlockSpec(memory_space=pl.ANY)
    return pl.pallas_call(
        functools.partial(layer_kernel, dims),
        out_shape=[
            shape(whole, bf16),
            shape(whole, bf16),
            shape(whole, f32),
            shape(whole, f32),
            shape(turned, bf16),
            shape((FEED,) + lead + tile, bf16),
            shape((CHUNKS,) + lead + tile, bf16),
            shape((CHUNKS,) + tile, f32),
            shape((UNIT, HIDDEN), f32),
            shape(small_tile, f32),
        ],
        in_specs=[vmem] * 8 + [anywhere] * 8,
        out_specs=[anywhere] * 9 + [vmem],
        scratch_shapes=[
            room((CHUNKS,) + tile, f32),
            room((UNIT, HIDDEN), f32),
            room(whole, bf16),
            room(whole, bf16),
            room((CHUNKS,) + lead + tile, bf16),
            room((UNIT, HIDDEN), bf16),
            room(lead + small_tile, f32),
            room((8, WIDTH), f32),
            room((8, WIDE), f32),
            room((LENGTH, LENGTH), bf16),
            room((LENGTH, LENGTH), bf16),
            room((6, LENGTH, WIDE), bf16),
            room(whole, bf16),
            room(turned, bf16),
            room(turned, bf16),
            room(whole, f32),
            room(whole, f32),
            room(whole, f32),
            room(whole, f32),
            room((2,) + lead + tile, bf16),
            room((8, WIDE), f32),
            room((8, WIDTH), f32),
            room(lead + small_tile, f32),
            room((TERMS_AHEAD + 1,) + chip + tile, bf16),
            room((ROOMS, 2, 4) + tile, bf16),
            room((ROOMS, 8) + tile, bf16),
            room((ROOMS, 4) + tile, bf16),
            room(chip + small_tile, f32),
            room((2, 4) + small_tile, f32),
            room((8,) + small_tile, f32),
            room((4,) + small_tile, f32),
            dma((CHUNKS, 4, most)),
            dma((CHUNKS, 4, most)),
            dma((4, most)),
            dma((4, most)),
            dma((19,)),
            dma((15,)),
            dma((2,)),
            dma((TERMS_AHEAD + 1,)),
            dma((CHUNKS, 4, most)),
            dma((CHUNKS, 4, most)),
            dma((4, most)),
            dma((4, most)),
            pltpu.SemaphoreType.REGULAR,
        ],
        compiler_params=pltpu.CompilerParams(
            collective_id=0, has_side_effects=True, vmem_limit_bytes=VMEM_LIMIT
        ),
        name="layer",
    )(crops, kept, *small, tokens, cotangent, *shards)


def place_kernel(*refs):
    result, input_grad, owned, owned_up, small = refs[:5]
    outs, vectors, bias_up = refs[5:13], refs[13:18], refs[18]
    buffers, in_sem, out_sem = refs[19:27], refs[27], refs[28]
    _, _, query, key, value, out, _, down = buffers
    parts = [[(result, buffers[0].at[0])], [(input_grad, buffers[1].at[0])]]
    for number in (1, 2, 3, 0):
        target = (out, query, key, value)[number]
        parts.append(
            [
                (owned.at[16 + 2 * number + half], target.at[:, pl.ds(half * WIDE, WIDE)])
                for half in (0, 1)
            ]
        )
    parts.append([(owned_up, buffers[6])])
    parts.append(
        [
            (
                owned.at[4 * group + half],
                down.at[pl.ds(group * UNIT, UNIT), pl.ds(half * WIDE, WIDE)],
            )
            for group in range(4)
            for half in (0, 1)
        ]
    )
    loads, count = [], 0
    for items in parts:
        group = []
        for source, target in items:
            group.append(pltpu.make_async_copy(source, target, in_sem.at[count]))
            group[-1].start()
            count += 1
        loads.append(group)
    for index in range(4):
        vectors[index][...] = small[0, index * UNIT : (index + 1) * UNIT]
    vectors[4][...] = small[2, 0:UNIT]
    bias_up[...] = small[1, :]
    stores = []
    for index, group in enumerate(loads):
        for item in group:
            item.wait()
        stores.append(pltpu.make_async_copy(buffers[index], outs[index], out_sem.at[index]))
        stores[-1].start()
    for item in stores:
        item.wait()


def place_results(result, input_grad, owned, owned_up, small):
    f32, bf16 = jnp.float32, jnp.bfloat16
    shape = jax.ShapeDtypeStruct
    vmem, anywhere = pl.BlockSpec(memory_space=pltpu.VMEM), pl.BlockSpec(memory_space=pl.ANY)
    large = (
        [shape((1, LENGTH, WIDTH), bf16)] * 2
        + [shape((UNIT, WIDTH), f32)] * 4
        + [shape((UNIT, HIDDEN), f32), shape((4 * UNIT, WIDTH), f32)]
    )
    return pl.pallas_call(
        place_kernel,
        out_shape=large + [shape((UNIT,), f32)] * 5 + [shape((4 * UNIT,), f32)],
        in_specs=[anywhere] * 4 + [vmem],
        out_specs=[anywhere] * 8 + [vmem] * 6,
        scratch_shapes=[pltpu.VMEM(item.shape, item.dtype) for item in large]
        + [pltpu.SemaphoreType.DMA((19,)), pltpu.SemaphoreType.DMA((8,))],
        name="results",
    )(result, input_grad, owned, owned_up, small)


def body(
    tokens,
    crop_ids,
    kv_mask,
    norm1_gain,
    norm1_bias,
    w_query,
    w_key,
    w_value,
    w_out,
    norm2_gain,
    norm2_bias,
    w_up,
    up_bias,
    w_down,
    down_bias,
    cotangent,
):
    inner = lax.axis_size("dp") // (2 * OUTER)
    dims = (OUTER, inner, lax.axis_size("fsdp"))
    fits = (
        tokens.shape == (1, LENGTH, WIDTH)
        and w_up.shape == (UNIT, HIDDEN)
        and w_down.shape == (HIDDEN // WIDTH * UNIT, WIDTH)
        and dims == (2, 2, 4)
    )
    if not fits:
        return general_body(
            tokens,
            crop_ids,
            kv_mask,
            norm1_gain,
            norm1_bias,
            w_query,
            w_key,
            w_value,
            w_out,
            norm2_gain,
            norm2_bias,
            w_up,
            up_bias,
            w_down,
            down_bias,
            cotangent,
        )
    small = [
        vector.reshape(1, -1)
        for vector in (norm1_gain, norm1_bias, norm2_gain, norm2_bias, down_bias, up_bias)
    ]
    pixels, grads = tokens.reshape(LENGTH, WIDTH), cotangent.reshape(LENGTH, WIDTH)
    shards = (w_query, w_key, w_value, w_out, w_up, w_down)
    result, input_grad, *_, owned, owned_up, owned_small = layer(
        dims, pixels, grads, crop_ids, kv_mask, small, shards
    )
    (
        output,
        grad_tokens,
        grad_query,
        grad_key,
        grad_value,
        grad_out,
        grad_up,
        grad_down,
        grad_gain_one,
        grad_bias_one,
        grad_gain_two,
        grad_bias_two,
        grad_bias_down,
        grad_bias_up,
    ) = place_results(result, input_grad, owned, owned_up, owned_small)
    return (
        output,
        grad_tokens,
        grad_gain_one,
        grad_bias_one,
        grad_query,
        grad_key,
        grad_value,
        grad_out,
        grad_gain_two,
        grad_bias_two,
        grad_up,
        grad_bias_up,
        grad_down,
        grad_bias_down,
    )


def solution(mesh):
    return jax.shard_map(
        body,
        mesh=mesh,
        in_specs=(
            P(("dp", "fsdp"), None, None),
            P(("dp", "fsdp"), None),
            P(("dp", "fsdp"), None),
            P(("dp", "fsdp")),
            P(("dp", "fsdp")),
            P(("dp", "fsdp"), None),
            P(("dp", "fsdp"), None),
            P(("dp", "fsdp"), None),
            P(("dp", "fsdp"), None),
            P(("dp", "fsdp")),
            P(("dp", "fsdp")),
            P(("dp", "fsdp"), None),
            P(("dp", "fsdp")),
            P(("dp", "fsdp"), None),
            P(("dp", "fsdp")),
            P(("dp", "fsdp"), None, None),
        ),
        out_specs=(
            P(("dp", "fsdp"), None, None),
            P(("dp", "fsdp"), None, None),
            P(("dp", "fsdp")),
            P(("dp", "fsdp")),
            P(("dp", "fsdp"), None),
            P(("dp", "fsdp"), None),
            P(("dp", "fsdp"), None),
            P(("dp", "fsdp"), None),
            P(("dp", "fsdp")),
            P(("dp", "fsdp")),
            P(("dp", "fsdp"), None),
            P(("dp", "fsdp")),
            P(("dp", "fsdp"), None),
            P(("dp", "fsdp")),
        ),
        check_vma=False,
    )
```

```python
import functools
import itertools

import jax
import jax.numpy as jnp
from jax import lax
from jax.experimental import pallas as pl
from jax.experimental.pallas import tpu as pltpu
from jax.sharding import PartitionSpec as P

HEADS = 16
BLOCK = 512
MESH = pl.DeviceIdType.MESH
WIDE = 512
OUTER = 2


class Place:
    def __init__(self, dims):
        self.size = {"a": dims[0], "b": dims[1], "c": 2, "z": dims[2]}
        dp = lax.axis_index("dp")
        self.at = {
            "a": dp // (2 * dims[1]),
            "b": (dp // 2) % dims[1],
            "c": dp % 2,
            "z": lax.axis_index("fsdp"),
        }

    def moved(self, axis, step):
        spot = dict(self.at)
        spot[axis] = (spot[axis] + step) % self.size[axis]
        return spot

    def device(self, axis, step):
        spot = self.moved(axis, step)
        return ((spot["a"] * self.size["b"] + spot["b"]) * 2 + spot["c"], spot["z"])

    def partners(self, axis):
        return range(1, self.size[axis])

    def greet(self):
        barrier = pltpu.get_barrier_semaphore()
        count = 0
        for axis in "abcz":
            for step in self.partners(axis):
                pl.semaphore_signal(
                    barrier, 1, device_id=self.device(axis, step), device_id_type=MESH
                )
                count += 1
        pl.semaphore_wait(barrier, count)


def pieces_of(rows, columns, unit):
    wide = min(WIDE, columns)
    return [
        (row, unit, column, wide)
        for row in range(0, rows, unit)
        for column in range(0, columns, wide)
    ]


def gather_kernel(dims, orders, lag, ahead, pieces, *refs):
    count = len(pieces)
    shards, wholes = refs[:count], refs[count : 2 * count]
    local_sem, send_sem, recv_sem = refs[2 * count :]
    place = Place(dims)
    place.greet()
    chunks = [
        (shard.at[pl.ds(ro, rn), pl.ds(co, cn)], whole, pl.ds(ro, rn), pl.ds(co, cn))
        for shard, whole, items in zip(shards, wholes, pieces)
        for ro, rn, co, cn in items
    ]
    total = len(chunks)
    sent, kept = [], []

    def region(index, done, spot):
        _, whole, rows, columns = chunks[index]
        lead = tuple(slice(None) if axis in done else spot[axis] for axis in "abcz")
        return whole.at[lead + (rows, columns)]

    def copy(index, stage, step, axis, source, target):
        return pltpu.make_async_remote_copy(
            source,
            target,
            send_sem.at[index, stage, step - 1],
            recv_sem.at[index, stage, step - 1],
            device_id=place.device(axis, step),
            device_id_type=MESH,
        )

    def send(index, stage):
        order = orders[index % len(orders)]
        axis, done = order[stage], order[:stage]
        target = region(index, done, place.at)
        for step in place.partners(axis):
            item = copy(index, stage, step, axis, target if done else chunks[index][0], target)
            item.start()
            sent.append(item)

    def receive(index, stage):
        order = orders[index % len(orders)]
        axis, done = order[stage], order[:stage]
        for step in place.partners(axis):
            target = region(index, done, place.moved(axis, place.size[axis] - step))
            copy(index, stage, step, axis, target, target).wait_recv()

    def begin(index):
        if index < total:
            item = pltpu.make_async_copy(
                chunks[index][0], region(index, "", place.at), local_sem.at[index]
            )
            item.start()
            kept.append(item)
            send(index, 0)

    for index in range(ahead):
        begin(index)
    for tick in range(total + 3 * lag):
        begin(tick + ahead)
        for stage in range(4):
            index = tick - stage * lag
            if 0 <= index < total:
                receive(index, stage)
                if stage == 0:
                    kept[index].wait()
                if stage < 3:
                    send(index, stage + 1)
    for item in sent:
        item.wait_send()


def gather(dims, shards, unit, lag=3, ahead=6):
    pieces = [pieces_of(*shard.shape, min(unit, shard.shape[0])) for shard in shards]
    total = sum(len(items) for items in pieces)
    most = max(dims) - 1
    anywhere = pl.BlockSpec(memory_space=pl.ANY)
    orders = ("zbac", "zabc", "zbac", "zabc", "bzac", "azbc")
    wholes = pl.pallas_call(
        functools.partial(gather_kernel, dims, orders, lag, ahead, pieces),
        out_shape=[
            jax.ShapeDtypeStruct(dims[:2] + (2, dims[2]) + shard.shape, shard.dtype)
            for shard in shards
        ],
        in_specs=[anywhere] * len(shards),
        out_specs=[anywhere] * len(shards),
        scratch_shapes=[
            pltpu.SemaphoreType.DMA((total,)),
            pltpu.SemaphoreType.DMA((total, 4, most)),
            pltpu.SemaphoreType.DMA((total, 4, most)),
        ],
        compiler_params=pltpu.CompilerParams(collective_id=0, has_side_effects=True),
        name="gather",
    )(*shards)
    return [whole.reshape((-1, whole.shape[-1])) for whole in wholes]


def scatter_kernel(dims, lag, ahead, pieces, *refs):
    count = len(pieces)
    terms, owned = refs[:count], refs[count : 2 * count]
    main = refs[2 * count : 2 * count + 7]
    side = refs[2 * count + 7 : 2 * count + 12]
    local_sem, send_sem, recv_sem = refs[2 * count + 12 :]
    place = Place(dims)
    place.greet()
    spot = place.at
    chunks = []
    for array, items in enumerate(pieces):
        for ro, rn, co, cn in items:
            index = len(chunks)
            if array == 0:
                rooms = side
                order = "ab"
            else:
                half = (index - 1) // 2
                order = "ab" if index % 2 else "ba"
                first, second = (main[2], main[4]) if index % 2 else (main[3], main[5])
                rooms = (
                    main[0].at[index - 1],
                    main[1].at[index - 1],
                    first.at[half],
                    second.at[half],
                    main[6].at[index - 1],
                )
            chunks.append((terms[array], owned[array], pl.ds(ro, rn), pl.ds(co, cn), order, rooms))
    total = len(chunks)
    sent, kept = [], []

    def copy(index, stage, step, axis, source, target):
        return pltpu.make_async_remote_copy(
            source,
            target,
            send_sem.at[index, stage, step - 1],
            recv_sem.at[index, stage, step - 1],
            device_id=place.device(axis, step),
            device_id_type=MESH,
        )

    def send(index, stage, step, axis, source, target):
        item = copy(index, stage, step, axis, source, target)
        item.start()
        sent.append(item)

    def begin(index):
        if index < total:
            term, _, rows, columns, _, rooms = chunks[index]
            send(index, 0, 1, "c", term.at[:, :, 1 - spot["c"], :, rows, columns], rooms[1])
            item = pltpu.make_async_copy(
                term.at[:, :, spot["c"], :, rows, columns], rooms[0], local_sem.at[index]
            )
            item.start()
            kept.append(item)

    def await_all(index, stage, axis, room):
        for step in place.partners(axis):
            copy(index, stage, step, axis, room.at[step - 1], room.at[step - 1]).wait_recv()

    def pick(order, first, second):
        return (first, second) if order == "ab" else (second, first)

    def after_core(index):
        order, (own, other, came, _, _) = chunks[index][4:]
        kept[index].wait()
        copy(index, 0, 1, "c", other, other).wait_recv()
        axis, rest = order

        def add(where):
            for item in range(place.size[rest]):
                at = pick(order, where, item)
                own[at] = own[at] + other[at]

        for step in place.partners(axis):
            where = place.moved(axis, step)[axis]
            add(where)
            source = own.at[where] if order == "ab" else own.at[:, where]
            send(index, 1, step, axis, source, came.at[step - 1])
        add(spot[axis])

    def after_first(index):
        order, (own, _, came, later, _) = chunks[index][4:]
        axis, rest = order
        await_all(index, 1, axis, came)

        def add(where):
            at = pick(order, spot[axis], where)
            value = own[at].astype(jnp.float32)
            for step in place.partners(axis):
                value = value + came[step - 1, where].astype(jnp.float32)
            own[at] = value.astype(own.dtype)

        for step in place.partners(rest):
            where = place.moved(rest, step)[rest]
            add(where)
            at = pick(order, spot[axis], where)
            send(index, 2, step, rest, own.at[at], later.at[step - 1])
        add(spot[rest])

    def after_second(index):
        _, result, rows, columns, order, (own, _, _, later, last) = chunks[index]
        rest = order[1]
        await_all(index, 2, rest, later)

        def add(where):
            value = own[spot["a"], spot["b"], where].astype(jnp.float32)
            for step in place.partners(rest):
                value = value + later[step - 1, where].astype(jnp.float32)
            return value

        for step in place.partners("z"):
            where = place.moved("z", step)["z"]
            own[spot["a"], spot["b"], where] = add(where).astype(own.dtype)
            send(index, 3, step, "z", own.at[spot["a"], spot["b"], where], last.at[step - 1])
        result[rows, columns] = add(spot["z"])

    def after_last(index):
        _, result, rows, columns, _, (_, _, _, _, last) = chunks[index]
        await_all(index, 3, "z", last)
        value = result[rows, columns]
        for step in place.partners("z"):
            value = value + last[step - 1].astype(jnp.float32)
        result[rows, columns] = value

    for index in range(ahead):
        begin(index)
    for tick in range(total + 3 * lag):
        begin(tick + ahead)
        for stage, work in enumerate((after_core, after_first, after_second, after_last)):
            index = tick - stage * lag
            if 0 <= index < total:
                work(index)
    for item in sent:
        item.wait_send()


def rooms_of(dims, many, unit, wide, dtype):
    outer, inner, depth = dims
    ones, twos = (many + 1) // 2, many // 2
    tail = (unit, wide)
    return [
        pltpu.VMEM((many, outer, inner, depth) + tail, dtype),
        pltpu.VMEM((many, outer, inner, depth) + tail, dtype),
        pltpu.VMEM((ones, outer - 1, inner, depth) + tail, dtype),
        pltpu.VMEM((twos, inner - 1, outer, depth) + tail, dtype),
        pltpu.VMEM((ones, inner - 1, depth) + tail, dtype),
        pltpu.VMEM((twos, outer - 1, depth) + tail, dtype),
        pltpu.VMEM((many, depth - 1) + tail, dtype),
    ]


def scatter(dims, small, terms, unit, lag=2, ahead=4):
    outer, inner, depth = dims
    devices = 2 * outer * inner * depth
    lead = (outer, inner, 2, depth)
    arrays = [small.reshape(lead + small.shape[1:])] + [
        term.reshape(lead + (term.shape[0] // devices, term.shape[1])) for term in terms
    ]
    pieces = [pieces_of(*arrays[0].shape[4:], arrays[0].shape[4])]
    pieces += [pieces_of(*array.shape[4:], unit) for array in arrays[1:]]
    total = sum(len(items) for items in pieces)
    most = max(dims) - 1
    tail = small.shape[1:]
    side = [
        pltpu.VMEM((outer, inner, depth) + tail, jnp.float32),
        pltpu.VMEM((outer, inner, depth) + tail, jnp.float32),
        pltpu.VMEM((outer - 1, inner, depth) + tail, jnp.float32),
        pltpu.VMEM((inner - 1, depth) + tail, jnp.float32),
        pltpu.VMEM((depth - 1,) + tail, jnp.float32),
    ]
    return pl.pallas_call(
        functools.partial(scatter_kernel, dims, lag, ahead, pieces),
        out_shape=[jax.ShapeDtypeStruct(array.shape[4:], jnp.float32) for array in arrays],
        in_specs=[pl.BlockSpec(memory_space=pl.ANY)] * len(arrays),
        out_specs=[pl.BlockSpec(memory_space=pltpu.VMEM)] * len(arrays),
        scratch_shapes=rooms_of(dims, total - 1, unit, WIDE, jnp.bfloat16)
        + side
        + [
            pltpu.SemaphoreType.DMA((total,)),
            pltpu.SemaphoreType.DMA((total, 4, most)),
            pltpu.SemaphoreType.DMA((total, 4, most)),
        ],
        compiler_params=pltpu.CompilerParams(
            collective_id=1, has_side_effects=True, vmem_limit_bytes=60 << 20
        ),
        name="scatter",
    )(*arrays)


HIGH = lax.Precision.HIGHEST
norm_eps = 1e-05


def norm_affine(values, gain, shift):
    mean = jnp.mean(values, axis=-1, keepdims=True)
    centred = values - mean
    spread = jnp.mean(centred * centred, axis=-1, keepdims=True)
    return centred * lax.rsqrt(spread + norm_eps) * gain + shift


def feature(values):
    return jax.nn.elu(values) + 1.0


def gelu_exact(values):
    return jax.nn.gelu(values, approximate=False)


def allowed_weight(crop, keymask):
    places = jnp.arange(crop.shape[0])
    earlier = places[None, :] <= places[:, None]
    same = crop[:, None] == crop[None, :]
    visible = (keymask[None, :] > 0) | (places[None, :] == places[:, None])
    return (earlier & same & visible).astype(jnp.float32)


def attend_forward(carry, pieces):
    state, norm_state, prev_crop = carry
    query_feat, key_feat, values, crop, keymask = pieces
    weight = allowed_weight(crop, keymask)
    scores = (
        jnp.einsum("ihe,jhe->hij", query_feat, key_feat, preferred_element_type=jnp.float32)
        * weight[None]
    )
    value_wide = values.astype(jnp.float32)
    query_wide = query_feat.astype(jnp.float32)
    key_wide = key_feat.astype(jnp.float32)
    numer = jnp.einsum("hij,jhe->ihe", scores, value_wide, precision=HIGH)
    denom = jnp.sum(scores, axis=2).T
    follows = (crop == prev_crop).astype(jnp.float32)
    numer = numer + follows[:, None, None] * jnp.einsum(
        "ihe,hef->ihf", query_wide, state, precision=HIGH
    )
    denom = denom + follows[:, None] * jnp.einsum(
        "ihe,he->ih", query_wide, norm_state, precision=HIGH
    )
    last_crop = crop[crop.shape[0] - 1]
    carried = (prev_crop == last_crop).astype(jnp.float32)
    select = ((crop == last_crop) & (keymask > 0)).astype(jnp.float32)
    chosen = key_wide * select[:, None, None]
    new_state = carried * state + jnp.einsum("jhe,jhf->hef", chosen, value_wide, precision=HIGH)
    new_norm = carried * norm_state + jnp.sum(chosen, axis=0)
    return ((new_state, new_norm, last_crop), (numer / denom[:, :, None], denom, state, norm_state))


def attend_backward(carry, pieces):
    grad_state, grad_norm = carry
    (
        query_feat,
        key_feat,
        values,
        crop,
        keymask,
        prev_crop,
        state,
        norm_state,
        grad_numer,
        grad_denom,
    ) = pieces
    weight = allowed_weight(crop, keymask)
    scores = (
        jnp.einsum("ihe,jhe->hij", query_feat, key_feat, preferred_element_type=jnp.float32)
        * weight[None]
    )
    value_wide = values.astype(jnp.float32)
    query_wide = query_feat.astype(jnp.float32)
    key_wide = key_feat.astype(jnp.float32)
    grad_scores = (
        jnp.einsum("ihe,jhe->hij", grad_numer, value_wide, precision=HIGH)
        + grad_denom.T[:, :, None]
    ) * weight[None]
    follows = (crop == prev_crop).astype(jnp.float32)
    last_crop = crop[crop.shape[0] - 1]
    carried = (prev_crop == last_crop).astype(jnp.float32)
    select = ((crop == last_crop) & (keymask > 0)).astype(jnp.float32)
    grad_query = jnp.einsum("hij,jhe->ihe", grad_scores, key_wide, precision=HIGH)
    grad_query = grad_query + follows[:, None, None] * (
        jnp.einsum("ihf,hef->ihe", grad_numer, state, precision=HIGH)
        + grad_denom[:, :, None] * norm_state[None]
    )
    grad_key = jnp.einsum("hij,ihe->jhe", grad_scores, query_wide, precision=HIGH)
    grad_key = grad_key + select[:, None, None] * (
        jnp.einsum("jhf,hef->jhe", value_wide, grad_state, precision=HIGH) + grad_norm[None]
    )
    grad_value = jnp.einsum("hij,ihe->jhe", scores, grad_numer, precision=HIGH)
    grad_value = grad_value + select[:, None, None] * jnp.einsum(
        "jhe,hef->jhf", key_wide, grad_state, precision=HIGH
    )
    query_kept = query_wide * follows[:, None, None]
    earlier_state = carried * grad_state + jnp.einsum(
        "ihe,ihf->hef", query_kept, grad_numer, precision=HIGH
    )
    earlier_norm = carried * grad_norm + jnp.einsum(
        "ihe,ih->he", query_kept, grad_denom, precision=HIGH
    )
    return ((earlier_state, earlier_norm), (grad_query, grad_key, grad_value))


def split_blocks(array):
    blocks = array.shape[0] // BLOCK
    return array.reshape((blocks, BLOCK) + array.shape[1:])


def attend_slot(pieces):
    query_feat, key_feat, values, crop, keymask = pieces
    length, heads, head_width = query_feat.shape
    start = (
        jnp.zeros((heads, head_width, head_width), jnp.float32),
        jnp.zeros((heads, head_width), jnp.float32),
        jnp.int32(-1),
    )
    finish, (mixed, denom, states, norms) = lax.scan(
        attend_forward,
        start,
        (
            split_blocks(query_feat),
            split_blocks(key_feat),
            split_blocks(values),
            split_blocks(crop),
            split_blocks(keymask),
        ),
    )
    return (mixed.reshape(length, heads, head_width), denom.reshape(length, heads), states, norms)


def attend_slot_back(pieces):
    query_feat, key_feat, values, crop, keymask, states, norms, grad_numer, grad_denom = pieces
    length, heads, head_width = query_feat.shape
    crop_blocks = split_blocks(crop)
    prev_crops = jnp.concatenate([jnp.full((1,), -1, jnp.int32), crop_blocks[:-1, -1]])
    start = (
        jnp.zeros((heads, head_width, head_width), jnp.float32),
        jnp.zeros((heads, head_width), jnp.float32),
    )
    finish, (grad_query, grad_key, grad_value) = lax.scan(
        attend_backward,
        start,
        (
            split_blocks(query_feat),
            split_blocks(key_feat),
            split_blocks(values),
            crop_blocks,
            split_blocks(keymask),
            prev_crops,
            states,
            norms,
            split_blocks(grad_numer),
            split_blocks(grad_denom),
        ),
        reverse=True,
    )
    shape = (length, heads, head_width)
    return (grad_query.reshape(shape), grad_key.reshape(shape), grad_value.reshape(shape))


def general_body(
    tokens,
    crop_ids,
    kv_mask,
    norm1_gain,
    norm1_bias,
    w_query,
    w_key,
    w_value,
    w_out,
    norm2_gain,
    norm2_bias,
    w_up,
    up_bias,
    w_down,
    down_bias,
    cotangent,
):
    slots, length, width = tokens.shape
    heads = HEADS
    head_width = width // heads
    count = slots * length
    devices = lax.axis_size("dp") * lax.axis_size("fsdp")
    dims = (OUTER, lax.axis_size("dp") // (2 * OUTER), lax.axis_size("fsdp"))
    unit = width // devices
    packed = jnp.concatenate([norm1_gain, norm1_bias, norm2_gain, norm2_bias, down_bias, up_bias])
    packed = jnp.pad(packed, (0, 16 * 128 - packed.shape[0])).reshape(16, 128)
    vectors, full_query, full_key, full_value, full_out, full_up, full_down = gather(
        dims, [packed, w_query, w_key, w_value, w_out, w_up, w_down], unit
    )
    vectors = vectors.reshape(devices, 16 * 128)
    gain_one, bias_one, gain_two, bias_two, full_down_bias = (
        vectors[:, index * unit : (index + 1) * unit].reshape(-1) for index in range(5)
    )
    full_up_bias = vectors[:, 5 * unit : 5 * unit + up_bias.shape[0]].reshape(-1)
    inputs = tokens.reshape(count, width).astype(jnp.float32)
    normed_wide, pull_one = jax.vjp(
        norm_affine, inputs, gain_one.astype(jnp.float32), bias_one.astype(jnp.float32)
    )
    normed = normed_wide.astype(jnp.bfloat16)
    query = jnp.dot(normed, full_query, preferred_element_type=jnp.float32)
    keys = jnp.dot(normed, full_key, preferred_element_type=jnp.float32)
    values = jnp.dot(normed, full_value, preferred_element_type=jnp.float32).astype(jnp.bfloat16)
    query_wide, pull_query = jax.vjp(feature, query)
    key_wide, pull_key = jax.vjp(feature, keys)
    query_feat = query_wide.astype(jnp.bfloat16).reshape(slots, length, heads, head_width)
    key_feat = key_wide.astype(jnp.bfloat16).reshape(slots, length, heads, head_width)
    value_heads = values.reshape(slots, length, heads, head_width)
    mixed_wide, denom, states, norms = lax.map(
        attend_slot, (query_feat, key_feat, value_heads, crop_ids, kv_mask)
    )
    mixed = mixed_wide.reshape(count, width).astype(jnp.bfloat16)
    middle = inputs + jnp.dot(mixed, full_out, preferred_element_type=jnp.float32)
    normed_two_wide, pull_two = jax.vjp(
        norm_affine, middle, gain_two.astype(jnp.float32), bias_two.astype(jnp.float32)
    )
    normed_two = normed_two_wide.astype(jnp.bfloat16)
    upper = jnp.dot(normed_two, full_up, preferred_element_type=jnp.float32) + full_up_bias.astype(
        jnp.float32
    )
    hidden_wide, pull_gelu = jax.vjp(gelu_exact, upper)
    hidden = hidden_wide.astype(jnp.bfloat16)
    result = (
        middle
        + jnp.dot(hidden, full_down, preferred_element_type=jnp.float32)
        + full_down_bias.astype(jnp.float32)
    )
    output = result.astype(jnp.bfloat16).reshape(slots, length, width)
    back_up, back_down = full_up, full_down
    back_query, back_key, back_value, back_out = full_query, full_key, full_value, full_out
    grad_out = cotangent.reshape(count, width)
    grad_down_bias = jnp.sum(grad_out.astype(jnp.float32), axis=0)
    grad_w_down = jnp.dot(hidden.T, grad_out, preferred_element_type=jnp.float32).astype(jnp.bfloat16)
    grad_hidden = jnp.dot(grad_out, back_down.T, preferred_element_type=jnp.float32)
    grad_upper = pull_gelu(grad_hidden)[0].astype(jnp.bfloat16)
    grad_up_bias = jnp.sum(grad_upper.astype(jnp.float32), axis=0)
    grad_w_up = jnp.dot(normed_two.T, grad_upper, preferred_element_type=jnp.float32).astype(jnp.bfloat16)
    grad_normed_two = jnp.dot(grad_upper, back_up.T, preferred_element_type=jnp.float32)
    grad_middle_part, grad_gain_two, grad_bias_two = pull_two(grad_normed_two)
    grad_middle = grad_out.astype(jnp.float32) + grad_middle_part
    grad_attended = grad_middle.astype(jnp.bfloat16)
    grad_w_out = jnp.dot(mixed.T, grad_attended, preferred_element_type=jnp.float32).astype(jnp.bfloat16)
    grad_mixed = jnp.dot(grad_attended, back_out.T, preferred_element_type=jnp.float32).reshape(
        slots, length, heads, head_width
    )
    grad_numer = grad_mixed / denom[..., None]
    grad_denom = -jnp.sum(grad_mixed * mixed_wide, axis=-1) / denom
    grad_query_feat, grad_key_feat, grad_values = lax.map(
        attend_slot_back,
        (
            query_feat,
            key_feat,
            value_heads,
            crop_ids,
            kv_mask,
            states,
            norms,
            grad_numer,
            grad_denom,
        ),
    )
    grad_query = pull_query(grad_query_feat.reshape(count, width))[0].astype(jnp.bfloat16)
    grad_keys = pull_key(grad_key_feat.reshape(count, width))[0].astype(jnp.bfloat16)
    grad_values = grad_values.reshape(count, width).astype(jnp.bfloat16)
    grad_w_query = jnp.dot(normed.T, grad_query, preferred_element_type=jnp.float32).astype(jnp.bfloat16)
    grad_w_key = jnp.dot(normed.T, grad_keys, preferred_element_type=jnp.float32).astype(jnp.bfloat16)
    grad_w_value = jnp.dot(normed.T, grad_values, preferred_element_type=jnp.float32).astype(jnp.bfloat16)
    grad_normed = jnp.dot(grad_query, back_query.T, preferred_element_type=jnp.float32)
    grad_normed = grad_normed + jnp.dot(grad_keys, back_key.T, preferred_element_type=jnp.float32)
    grad_normed = grad_normed + jnp.dot(
        grad_values, back_value.T, preferred_element_type=jnp.float32
    )
    grad_input_part, grad_gain_one, grad_bias_one = pull_one(grad_normed)
    small = jnp.concatenate(
        [
            vector.reshape(devices, -1)
            for vector in (
                grad_gain_one,
                grad_bias_one,
                grad_gain_two,
                grad_bias_two,
                grad_down_bias,
                grad_up_bias,
            )
        ],
        axis=1,
    )
    small = jnp.pad(small, ((0, 0), (0, 8 * 128 - small.shape[1]))).reshape(devices, 8, 128)
    small, own_up, own_down, own_query, own_key, own_value, own_out = scatter(
        dims,
        small,
        [grad_w_up, grad_w_down, grad_w_query, grad_w_key, grad_w_value, grad_w_out],
        unit,
    )
    small = small.reshape(8 * 128)
    own_gain_one, own_bias_one, own_gain_two, own_bias_two, own_down_bias = (
        small[index * unit : (index + 1) * unit] for index in range(5)
    )
    own_up_bias = small[5 * unit : 5 * unit + up_bias.shape[0]]
    input_grad = (grad_middle + grad_input_part).astype(jnp.bfloat16).reshape(slots, length, width)
    return (
        output,
        input_grad,
        own_gain_one,
        own_bias_one,
        own_query,
        own_key,
        own_value,
        own_out,
        own_gain_two,
        own_bias_two,
        own_up,
        own_up_bias,
        own_down,
        own_down_bias,
    )


LENGTH = 512
WIDTH = 1024
HIDDEN = 4096
UNIT = 32
CHUNKS = 24
FEED = 8
ROOMS = 12
DRAINED = 12
LAG = 3
LATE = 3 * LAG
AHEAD = 4
PASS_AHEAD = 2
TERMS_AHEAD = 3
TERMS_START = 27
PASS_AFTER = 2
TERMS_PASS_AFTER = 2
VMEM_LIMIT = 63 << 20


def when(condition):
    if isinstance(condition, bool):
        return (lambda work: work()) if condition else (lambda work: None)
    return pl.when(condition)


def each(count, work):
    def step(index, carry):
        work(index)
        return carry

    lax.fori_loop(0, count, step, 0)


def dot(left, right):
    return jnp.dot(left, right, preferred_element_type=jnp.float32)


def dot_nt(left, right):
    return lax.dot_general(
        left, right, (((1,), (1,)), ((), ())), preferred_element_type=jnp.float32
    )


def dot_tn(left, right):
    return lax.dot_general(
        left, right, (((0,), (0,)), ((), ())), preferred_element_type=jnp.float32
    )


def by_order(place, orders, index, work):
    turn = (index + 3 * place.at["c"]) % len(orders)
    for order in dict.fromkeys(orders):
        turns = [number for number, item in enumerate(orders) if item == order]
        match = turn == turns[0]
        for number in turns[1:]:
            match = match | (turn == number)

        @pl.when(match)
        def _(order=order):
            work(order)


class Mover:
    def __init__(self, place, send_sem, recv_sem):
        self.place, self.send_sem, self.recv_sem = place, send_sem, recv_sem

    def copy(self, lead, stage, step, axis, source, target):
        at = lead + (stage, step - 1)
        return pltpu.make_async_remote_copy(
            source,
            target,
            self.send_sem.at[at],
            self.recv_sem.at[at],
            device_id=self.place.device(axis, step),
            device_id_type=MESH,
        )


class Gather(Mover):
    def region(self, chunk, done, spot):
        lead = tuple(slice(None) if axis in done else spot[axis] for axis in "abcz")
        return chunk.at[lead]

    def unless_passed(self, axis, step, work):
        z = self.place.at["z"]
        if axis == "z" and step == 3:
            pl.when(z != 0)(work)
        elif axis == "z" and step == 1:
            pl.when(z != 3)(work)
        else:
            work()

    def send(self, chunk, lead, order, stage):
        axis, done = order[stage], order[:stage]
        source = self.region(chunk, done, self.place.at)
        for step in self.place.partners(axis):
            self.unless_passed(
                axis, step, self.copy(lead, stage, step, axis, source, source).start
            )

    def passing(self, chunk, lead, order):
        stage = order.index("z")
        spot = dict(self.place.at)
        z = spot["z"]
        spot["z"] = 3 * (2 - z)
        source = self.region(chunk, order[:stage], spot)
        came = self.copy(lead, stage, 2, "z", source, source)
        onward = pltpu.make_async_remote_copy(
            source,
            source,
            self.send_sem.at[lead + (stage, 3)],
            self.recv_sem.at[lead + (stage, 2 * (z - 1))],
            device_id={"fsdp": 3 * (z - 1)},
            device_id_type=MESH,
        )
        return came, onward

    def pass_on(self, chunk, lead, order):
        z = self.place.at["z"]

        @pl.when((z == 1) | (z == 2))
        def _():
            came, onward = self.passing(chunk, lead, order)
            came.wait_recv()
            onward.start()

    def receive(self, chunk, lead, order, stage):
        axis, done = order[stage], order[:stage]
        z = self.place.at["z"]
        for step in self.place.partners(axis):
            spot = self.place.moved(axis, self.place.size[axis] - step)
            target = self.region(chunk, done, spot)
            item = self.copy(lead, stage, step, axis, target, target)
            if axis == "z" and step == 2:
                pl.when((z == 0) | (z == 3))(item.wait_recv)
            else:
                item.wait_recv()

    def drain(self, chunk, lead, order):
        z = self.place.at["z"]
        for stage in range(4):
            axis, done = order[stage], order[:stage]
            source = self.region(chunk, done, self.place.at)
            for step in self.place.partners(axis):
                self.unless_passed(
                    axis, step, self.copy(lead, stage, step, axis, source, source).wait_send
                )
            if axis == "z":

                @pl.when((z == 1) | (z == 2))
                def _():
                    self.passing(chunk, lead, order)[1].wait_send()


class Weights(Gather):
    orders = ("zbac", "azbc", "bzac", "zabc", "bzac", "azbc")

    def __init__(self, place, buffer, send_sem, recv_sem):
        super().__init__(place, send_sem, recv_sem)
        self.buffer, self.total = buffer, buffer.shape[0]

    def by_order(self, index, work):
        by_order(self.place, self.orders, index, work)

    def begin(self, index):
        @when(index < self.total)
        def _():
            self.by_order(
                index, lambda order: self.send(self.buffer.at[index], (index,), order, 0)
            )

    def pass_on_at(self, index, stage):
        @when((index >= 0) & (index < self.total))
        def _():
            def work(order):
                if order.index("z") == stage:
                    self.pass_on(self.buffer.at[index], (index,), order)

            self.by_order(index, work)

    def tick(self, now):
        self.begin(now + AHEAD)
        past = now - DRAINED

        @when((past >= 0) & (past < self.total))
        def _():
            self.finish_one(past)

        self.pass_on_at(now + PASS_AHEAD, 0)
        self.pass_on_at(now - PASS_AFTER, 1)
        for stage in range(4):
            index = now - stage * LAG
            live = (index >= 0) & (index < self.total)

            @when(live)
            def _(index=index, stage=stage):
                def work(order):
                    chunk = self.buffer.at[index]
                    self.receive(chunk, (index,), order, stage)
                    if stage < 3:
                        self.send(chunk, (index,), order, stage + 1)

                self.by_order(index, work)

    def finish_one(self, index):
        self.by_order(index, lambda order: self.drain(self.buffer.at[index], (index,), order))

    def finish(self, first, end):
        each(end - first, lambda step: self.finish_one(first + step))


def moments(values):
    mean = jnp.mean(values, axis=-1, keepdims=True)
    centred = values - mean
    spread = jnp.mean(centred * centred, axis=-1, keepdims=True)
    scale = lax.rsqrt(spread + norm_eps)
    return centred * scale, scale


def gelu_pair(upper):
    bell = jnp.exp(-0.5 * upper * upper) * 0.3989422804014327
    below = 0.5 * (1.0 + lax.erf(upper * 0.7071067811865476))
    return upper * below, below + upper * bell


def matrix(buffer, index):
    return buffer[index].reshape(WIDTH, WIDE)


def column_of(row):
    tall = jnp.transpose(jnp.broadcast_to(row.astype(jnp.float32), (8, row.shape[1])))
    return tall[:, 0:1]


def read_vectors(gathered, devices):
    flat = gathered[...].reshape(devices * 8, 128).astype(jnp.bfloat16)

    def line(number):
        shape = (devices, devices * 8)
        wanted = lax.broadcasted_iota(jnp.int32, shape, 0) * 8 + number
        chosen = lax.broadcasted_iota(jnp.int32, shape, 1) == wanted
        return dot(chosen.astype(jnp.bfloat16), flat).astype(jnp.bfloat16)

    def spread(lines, start, wide):
        total = wide * devices
        lane = lax.broadcasted_iota(jnp.int32, (128, total), 1)
        wanted = lax.broadcasted_iota(jnp.int32, (128, total), 0) == start + lane % wide
        found = dot(lines, wanted.astype(jnp.bfloat16))
        owner = lax.broadcasted_iota(jnp.int32, (devices, total), 1) // wide
        mine = owner == lax.broadcasted_iota(jnp.int32, (devices, total), 0)
        return jnp.sum(jnp.where(mine, found, 0.0), axis=0, keepdims=True)

    first, second = line(0), line(1)
    rows = [spread(first, index * UNIT, UNIT) for index in range(4)]
    rows.append(spread(line(2), 0, UNIT))
    return rows, [spread(second, index * UNIT, UNIT) for index in range(4)]


def write_vectors(rows, devices):
    result = None
    for index, row in enumerate(rows):
        owner = lax.broadcasted_iota(jnp.int32, (devices, WIDTH), 1) // UNIT
        mine = owner == lax.broadcasted_iota(jnp.int32, (devices, WIDTH), 0)
        spread = jnp.where(mine, row, 0.0)
        lane = lax.broadcasted_iota(jnp.int32, (WIDTH, 128), 0)
        wanted = lax.broadcasted_iota(jnp.int32, (WIDTH, 128), 1) == index * UNIT + lane % UNIT
        found = jnp.dot(
            spread,
            wanted.astype(jnp.float32),
            preferred_element_type=jnp.float32,
            precision=HIGH,
        )
        result = found if result is None else result + found
    return result


def head_lanes(which, shape):
    lane = lax.broadcasted_iota(jnp.int32, shape, 1)
    return lane < 64 if which == 0 else lane >= 64


def allowed(crop_row, mask_row):
    shape = (LENGTH, LENGTH)
    row = lax.broadcasted_iota(jnp.int32, shape, 0)
    column = lax.broadcasted_iota(jnp.int32, shape, 1)
    same = column_of(crop_row) == crop_row.astype(jnp.float32)
    seen = (mask_row > 0) | (row == column)
    return jnp.where(same & (column <= row) & seen, 1.0, 0.0).astype(jnp.bfloat16)


def allowed_back(crop_row, mask_row):
    shape = (LENGTH, LENGTH)
    row = lax.broadcasted_iota(jnp.int32, shape, 0)
    column = lax.broadcasted_iota(jnp.int32, shape, 1)
    same = column_of(crop_row) == crop_row.astype(jnp.float32)
    seen = (column_of(mask_row) > 0) | (row == column)
    return jnp.where(same & (row <= column) & seen, 1.0, 0.0).astype(jnp.bfloat16)


def transpose_into(source, target):
    def work(index):
        at = pl.ds(pl.multiple_of(index * 128, 128), 128)
        target[at, :] = jnp.transpose(source[:, at])

    each(source.shape[1] // 128, work)


def by_rows(work):
    each(LENGTH // 64, lambda index: work(pl.ds(pl.multiple_of(index * 64, 64), 64)))


def forward_heads(pair, qkv, mask, mixed, inverse, attended):
    chunk = pair // 4
    lanes = pl.ds(pl.multiple_of((pair % 4) * 128, 128), 128)
    columns = pl.ds(pl.multiple_of(pair * 128, 128), 128)
    for part in (0, 1):
        keys = 256 * (part + 1)
        rows = slice(part * 256, part * 256 + 256)
        query = qkv[chunk, rows, lanes]
        key = qkv[2 + chunk, 0:keys, lanes]
        value = qkv[4 + chunk, 0:keys, lanes]
        zero, one = jnp.zeros_like(key), jnp.ones_like(key)
        total = None
        for which in (0, 1):
            mine = head_lanes(which, key.shape)
            scores = dot_nt(query, jnp.where(mine, key, zero)).astype(jnp.bfloat16)
            scores = scores * mask[rows, 0:keys]
            right = jnp.concatenate(
                [jnp.where(mine, value, zero), jnp.where(mine, one, zero)], axis=1
            )
            term = dot(scores, right)
            total = term if total is None else total + term
        inverted = 1.0 / total[:, 128:]
        result = total[:, :128] * inverted
        mixed[rows, columns] = result
        inverse[rows, columns] = inverted
        attended[rows, columns] = result.astype(jnp.bfloat16)


def hidden_order(flip):
    shape = (4 * 128, 4 * 128)
    rows, columns = (lax.broadcasted_iota(jnp.int32, shape, axis) for axis in (0, 1))
    if flip:
        rows, columns = columns, rows
    wanted = (rows // UNIT) % 4 * 128 + rows // 128 * UNIT + rows % UNIT
    return columns == wanted


def feed_block(block, refs):
    normed, normed_t, grad_out, weights, up_bias, result, grad_normed, staged, grad_bias = refs
    group, half = block // 2, block % 2
    first = FEED + 4 * group
    up = matrix(weights, first + 2 + half)
    upper = dot(normed[...], up) + up_bias[pl.ds(block, 1), :]
    hidden, slope = gelu_pair(upper)
    hidden = hidden.astype(jnp.bfloat16)
    grad_hidden = None
    for side in (0, 1):
        columns = slice(side * WIDE, side * WIDE + WIDE)
        down = weights[first + side, half].reshape(WIDE, WIDE)
        result[:, columns] += dot(hidden, down)
        term = dot_nt(grad_out[:, columns], down)
        grad_hidden = term if grad_hidden is None else grad_hidden + term
    grad_upper = (grad_hidden * slope).astype(jnp.bfloat16)
    grad_bias[pl.ds(block, 1), :] = jnp.sum(
        grad_upper.astype(jnp.float32), axis=0, keepdims=True
    )
    grad_normed[...] += dot_nt(grad_upper, up)
    value = dot(normed_t[...], grad_upper).astype(jnp.bfloat16)
    staged[0] = value.reshape(staged.shape[1:])
    for side in (0, 1):
        columns = slice(side * WIDE, side * WIDE + WIDE)
        value = dot_tn(hidden, grad_out[:, columns]).astype(jnp.bfloat16)
        staged[1, side] = value.reshape(staged.shape[2:])


class Sums(Mover):
    def start(self, lead, stage, step, axis, source, target):
        self.copy(lead, stage, step, axis, source, target).start()

    def region(self, order, stage, where):
        at = {axis: self.place.at[axis] for axis in order[:stage]}
        at[order[stage]] = where
        return tuple(at.get(axis, slice(None)) for axis in "abz")

    def blocks(self, order, stage, where):
        rest = [axis for axis in "abz" if axis in order[stage + 1 :]]
        base = self.region(order, stage, where)
        sizes = [self.place.size[axis] for axis in rest]
        for inner in itertools.product(*(range(size) for size in sizes)):
            place = dict(zip(rest, inner))
            yield (
                tuple(place.get(axis, item) for axis, item in zip("abz", base)),
                inner,
            )

    def room(self, order, stage, rooms, step):
        if stage == 0:
            return rooms[0]
        if stage == 1:
            size = self.place.size[order[2]]
            return rooms[1].at[pl.ds((step - 1) * size, size)]
        return rooms[2].at[step - 1]

    def send_stage(self, lead, order, stage, total, rooms, add):
        axis = order[stage]
        z = self.place.at["z"]
        for step in self.place.partners(axis):
            where = self.place.moved(axis, step)[axis]
            for at, _ in self.blocks(order, stage, where):
                add(at)
            source = total.at[self.region(order, stage, where)]
            room = self.room(order, stage, rooms, step)
            item = self.copy(lead, stage + 1, step, axis, source, room)
            if axis != "z":
                item.start()
            elif step == 2:
                pl.when((z == 0) | (z == 3))(item.start)
            else:
                far = 3 if step == 1 else 0
                pl.when(z != far)(item.start)

                @pl.when(z == far)
                def _(step=step, source=source, far=far):
                    pltpu.make_async_remote_copy(
                        source,
                        self.room(order, stage, rooms, 4),
                        self.send_sem.at[lead + (stage + 1, step - 1)],
                        self.recv_sem.at[lead + (stage + 1, 3)],
                        device_id={"fsdp": 2 if far == 3 else 1},
                        device_id_type=MESH,
                    ).start()

        for at, _ in self.blocks(order, stage, self.place.at[axis]):
            add(at)

    def pass_on(self, lead, order, total, rooms):
        z = self.place.at["z"]
        stage = order.index("z")

        @pl.when((z == 1) | (z == 2))
        def _():
            came = self.room(order, stage, rooms, 4)
            self.copy(lead, stage + 1, 4, "z", came, came).wait_recv()
            where = 3 * (2 - z)
            for at, inner in self.blocks(order, stage, where):
                total[at] = total[at] + (came[inner] if inner else came[...])
            source = total.at[self.region(order, stage, where)]
            self.start(lead, stage + 1, 2, "z", source, self.room(order, stage, rooms, 2))

    def await_stage(self, lead, order, stage, rooms):
        axis = order[stage]
        for step in self.place.partners(axis):
            room = self.room(order, stage, rooms, step)
            item = self.copy(lead, stage + 1, step, axis, room, room)
            if axis == "z" and step != 2:
                pl.when(self.place.at["z"] != (0 if step == 1 else 3))(item.wait_recv)
            else:
                item.wait_recv()

    def after_core(self, lead, order, own, total, rooms):
        def add(at):
            total[at] = own[at] + total[at]

        self.send_stage(lead, order, 0, total, rooms, add)

    def came_in(self, order, stage, total, rooms, at):
        rest = [axis for axis in "abz" if axis in order[stage + 1 :]]
        inner = tuple(item for axis, item in zip("abz", at) if axis in rest)
        steps = self.place.partners(order[stage])
        wide = total.dtype if len(steps) == 1 and stage < 2 else jnp.float32
        value = total[at].astype(wide)
        for step in steps:
            room = self.room(order, stage, rooms, step)
            term = (room[inner] if inner else room[...]).astype(wide)
            if order[stage] == "z" and step != 2:
                near = self.place.at["z"] != (0 if step == 1 else 3)
                term = jnp.where(near, term, jnp.zeros_like(term))
            value = value + term
        return value

    def after_stage(self, lead, order, stage, total, rooms):
        self.await_stage(lead, order, stage - 1, rooms)

        def add(at):
            total[at] = self.came_in(order, stage - 1, total, rooms, at).astype(total.dtype)

        self.send_stage(lead, order, stage, total, rooms, add)

    def after_last(self, lead, order, total, rooms):
        self.await_stage(lead, order, 2, rooms)
        at = tuple(self.place.at[axis] for axis in "abz")
        return self.came_in(order, 2, total, rooms, at)

    def drain(self, lead, order, total, rooms):
        self.copy(lead, 0, 1, "c", total, total).wait_send()
        for stage in range(3):
            axis = order[stage]
            for step in self.place.partners(axis):
                room = self.room(order, stage, rooms, step)
                self.copy(lead, stage + 1, step, axis, room, room).wait_send()


class Gradients(Sums):
    orders = ("baz", "azb", "bza", "abz", "bza", "azb")

    def __init__(self, place, terms, sums, rooms, results, ring, ring_sem, send_sem, recv_sem):
        super().__init__(place, send_sem, recv_sem)
        self.terms, self.sums, self.rooms, self.results = terms, sums, rooms, results
        self.ring, self.ring_sem = ring, ring_sem
        self.total = results.shape[0]

    def sum_at(self, index):
        return self.sums.at[index // 2, :, :, index % 2]

    def by_order(self, index, work):
        rooms = [room.at[index % ROOMS] for room in self.rooms]
        total = self.sum_at(index)
        by_order(self.place, self.orders, index, lambda order: work(order, total, rooms))

    def begin(self, index):
        @when(index < self.total)
        def _():
            side = self.place.at["c"]
            slot = index % (TERMS_AHEAD + 1)
            source = self.terms.at[index]
            self.start((index,), 0, 1, "c", source.at[:, :, 1 - side], self.sum_at(index))
            pltpu.make_async_copy(
                source.at[:, :, side], self.ring.at[slot], self.ring_sem.at[slot]
            ).start()

    def tick(self, now):
        self.begin(now + TERMS_AHEAD)

        def live(index):
            return (index >= 0) & (index < self.total)

        @when(live(now - DRAINED))
        def _():
            self.finish_one(now - DRAINED)

        @when(live(now))
        def _():
            slot = now % (TERMS_AHEAD + 1)
            own = self.ring.at[slot]
            pltpu.make_async_copy(own, own, self.ring_sem.at[slot]).wait()
            total = self.sum_at(now)
            self.copy((now,), 0, 1, "c", total, total).wait_recv()
            self.by_order(
                now,
                lambda order, total, rooms: self.after_core((now,), order, own, total, rooms),
            )

        for stage in (1, 2):
            index = now - stage * LAG

            @when(live(index))
            def _(index=index, stage=stage):
                self.by_order(
                    index,
                    lambda order, total, rooms: self.after_stage(
                        (index,), order, stage, total, rooms
                    ),
                )

        for stage in (1, 2):
            index = now - stage * LAG - TERMS_PASS_AFTER

            @when(live(index))
            def _(index=index, stage=stage):
                def work(order, total, rooms):
                    if order.index("z") == stage:
                        self.pass_on((index,), order, total, rooms)

                self.by_order(index, work)

        index = now - 3 * LAG

        @when(live(index))
        def _():
            def work(order, total, rooms):
                self.results[index] = self.after_last((index,), order, total, rooms)

            self.by_order(index, work)

    def finish_one(self, index):
        self.by_order(
            index, lambda order, total, rooms: self.drain((index,), order, total, rooms)
        )

    def finish(self, first):
        each(self.total - first, lambda step: self.finish_one(first + step))


def backward_heads(pair, qkv, mask, mask_t, mixed, inverse, grad_mixed):
    chunk = pair // 4
    lanes = pl.ds(pl.multiple_of((pair % 4) * 128, 128), 128)
    columns = pl.ds(pl.multiple_of(pair * 128, 128), 128)
    query = qkv[chunk, :, lanes]
    key = qkv[2 + chunk, :, lanes]
    value = qkv[4 + chunk, :, lanes]
    grad_numer = (grad_mixed[:, columns] * inverse[:, columns]).astype(jnp.bfloat16)
    part = grad_numer.astype(jnp.float32) * mixed[:, columns]
    high = part.astype(jnp.bfloat16)
    low = pltpu.roll(part - high.astype(jnp.float32), 64, 1).astype(jnp.bfloat16)
    zero, minus = jnp.zeros_like(query), jnp.full_like(query, -1.0)
    heads = []
    for which in (0, 1):
        mine = head_lanes(which, query.shape)
        heads.append(
            (
                jnp.concatenate([grad_numer, jnp.where(mine, high, low)], axis=1),
                jnp.concatenate([jnp.where(mine, value, zero), minus], axis=1),
                jnp.where(mine, query, zero),
                jnp.where(mine, key, zero),
                jnp.where(mine, grad_numer, zero),
            )
        )
    for part in (0, 1):
        keys = 256 * (part + 1)
        rows = slice(part * 256, part * 256 + 256)
        total = None
        for left, right, _, own_key, _ in heads:
            grad_scores = dot_nt(left[rows], right[:keys]).astype(jnp.bfloat16)
            term = dot(grad_scores * mask[rows, 0:keys], own_key[:keys])
            total = term if total is None else total + term
        slope = jnp.minimum(query[rows].astype(jnp.float32), 1.0)
        qkv[chunk, rows, lanes] = (total * slope).astype(jnp.bfloat16)
    for part in (0, 1):
        start = part * 256
        rows = slice(start, start + 256)
        grad_key = grad_value = None
        for left, right, own_query, own_key, own_grad in heads:
            seen = mask_t[rows, start:LENGTH]
            scores = dot_nt(own_key[rows], query[start:]).astype(jnp.bfloat16) * seen
            grad_scores = dot_nt(right[rows], left[start:]).astype(jnp.bfloat16) * seen
            term = dot(scores, own_grad[start:])
            grad_value = term if grad_value is None else grad_value + term
            term = dot(grad_scores, own_query[start:])
            grad_key = term if grad_key is None else grad_key + term
        slope = jnp.minimum(key[rows].astype(jnp.float32), 1.0)
        qkv[2 + chunk, rows, lanes] = (grad_key * slope).astype(jnp.bfloat16)
        qkv[4 + chunk, rows, lanes] = grad_value.astype(jnp.bfloat16)


def layer_kernel(dims, *refs):
    crops, kept, gain_one, bias_one, gain_two, bias_two, bias_down, bias_up = refs[:8]
    tokens_in, grad_out_in = refs[8:10]
    shards = refs[10:16]
    output, input_grad, mixed_kept, inverse_kept, normed_t_kept, attention_kept, terms = refs[16:23]
    owned_out, owned_up_out, owned_small = refs[23:26]
    (
        owned,
        owned_up,
        pixels,
        grad_out,
        weights,
        up_shard,
        vectors,
        rows,
        up_bias,
        mask,
        mask_t,
        qkv,
        normed,
        turned_one,
        turned_two,
        middle,
        wide_one,
        wide_two,
        wide_three,
        staged,
        grad_up_bias,
        sums,
        small,
        ring,
        rooms_one,
        rooms_two,
        rooms_three,
        side_total,
        side_one,
        side_two,
        side_three,
        send_sem,
        recv_sem,
        vector_send_sem,
        vector_recv_sem,
        load_sem,
        store_sem,
        stage_sem,
        ring_sem,
        terms_send_sem,
        terms_recv_sem,
        side_send_sem,
        side_recv_sem,
        sibling_sem,
    ) = refs[26:]
    outer, inner, depth = dims
    devices = 2 * outer * inner * depth
    place = Place(dims)
    spot = (place.at["a"], place.at["b"], place.at["c"], place.at["z"])
    copies = {}

    def move(name, source, target):
        item = pltpu.make_async_copy(source, target, load_sem.at[len(copies)])
        item.start()
        copies[name] = item

    for index in range(FEED):
        source = shards[index // 2].at[:, pl.ds((index % 2) * WIDE, WIDE)]
        move(index, source, weights.at[(index,) + spot])
    move("tokens", tokens_in, pixels)
    move("up", shards[4], up_shard)
    for group in range(4):
        for half in (0, 1):
            source = shards[5].at[pl.ds(group * UNIT, UNIT), pl.ds(half * WIDE, WIDE)]
            index = FEED + 4 * group + half
            move(index, source, weights.at[(index,) + spot])
    move("grad_out", grad_out_in, grad_out)

    vector_gather = Gather(place, vector_send_sem, vector_recv_sem)
    vector_order = "zbac"
    lines = [
        jnp.concatenate([item[...] for item in (gain_one, bias_one, gain_two, bias_two)], axis=1),
        bias_up[...],
        jnp.concatenate([bias_down[...], jnp.zeros((1, 128 - UNIT), jnp.bfloat16)], axis=1),
    ]
    vectors[spot] = jnp.concatenate(
        [line.astype(jnp.float32) for line in lines] + [jnp.zeros((5, 128), jnp.float32)], axis=0
    )
    place.greet()
    vector_gather.send(vectors, (), vector_order, 0)
    gather_all = Weights(place, weights, send_sem, recv_sem)
    for index in range(AHEAD):
        copies[index].wait()
        gather_all.begin(index)
    for index in range(PASS_AHEAD):
        gather_all.pass_on_at(index, 0)
    for name, item in copies.items():
        if name not in range(AHEAD) and name not in ("up", "tokens", "grad_out"):
            item.wait()
    vector_gather.pass_on(vectors, (), vector_order)
    vector_gather.receive(vectors, (), vector_order, 0)
    vector_gather.send(vectors, (), vector_order, 1)
    gather_all.tick(0)
    copies["up"].wait()
    stacked = jnp.concatenate(
        [up_shard[:, index * WIDE : (index + 1) * WIDE] for index in range(8)], axis=0
    )
    stacked = dot(stacked, hidden_order(False).astype(jnp.bfloat16)).astype(jnp.bfloat16)
    for part in range(8):
        for group in range(4):
            at = (FEED + 4 * group + 2 + part // 4,) + spot
            lanes = slice((part % 4) * 128, (part % 4) * 128 + 128)
            weights[at + (slice(None), lanes)] = stacked[
                part * UNIT : (part + 1) * UNIT, group * 128 : (group + 1) * 128
            ]
    vector_gather.receive(vectors, (), vector_order, 1)
    vector_gather.send(vectors, (), vector_order, 2)
    gather_all.tick(1)
    mask[...] = allowed(crops[...], kept[...])
    vector_gather.receive(vectors, (), vector_order, 2)
    vector_gather.send(vectors, (), vector_order, 3)
    gather_all.tick(2)
    copies["tokens"].wait()
    copies["grad_out"].wait()
    sums[...] = jnp.zeros(sums.shape, jnp.float32)
    vector_gather.receive(vectors, (), vector_order, 3)
    width_rows, up_rows = read_vectors(vectors, devices)
    for index, row in enumerate(width_rows):
        rows[index : index + 1, :] = row
    for group, row in enumerate(up_rows):
        for half in (0, 1):
            up_bias[2 * group + half : 2 * group + half + 1, :] = row[
                :, half * WIDE : half * WIDE + WIDE
            ]
    gather_all.tick(3)

    def first_norm(at):
        value = pixels[at, :].astype(jnp.float32)
        unit, _ = moments(value)
        normed[at, :] = (unit * rows[0:1, :] + rows[1:2, :]).astype(jnp.bfloat16)
        middle[at, :] = value

    by_rows(first_norm)
    gather_all.tick(4)
    stores = {}

    def store(name, source, target):
        item = pltpu.make_async_copy(source, target, store_sem.at[len(stores)])
        item.start()
        stores[name] = item

    transpose_into(normed, turned_one)
    store("normed", turned_one, normed_t_kept)
    each(LATE - 5, lambda index: gather_all.tick(5 + index))

    def project(index):
        gather_all.tick(LATE + index)
        value = dot(normed[...], matrix(weights, index))
        mapped = jnp.where(value > 0, value + 1.0, jnp.exp(jnp.minimum(value, 0.0)))
        qkv[index] = jnp.where(index < 4, mapped, value).astype(jnp.bfloat16)

    each(6, project)
    attended, mixed, inverse = pixels, wide_one, wide_two

    def heads(pair):
        @pl.when(pair % 2 == 0)
        def _():
            gather_all.tick(LATE + 6 + pair // 2)

        forward_heads(pair, qkv, mask, mixed, inverse, attended)

    each(8, heads)
    store("mixed", mixed, mixed_kept)
    store("inverse", inverse, inverse_kept)
    store("attention", weights.at[pl.ds(0, FEED)], attention_kept)
    mask_t[...] = allowed_back(crops[...], kept[...])
    for half in (0, 1):
        columns = slice(half * WIDE, half * WIDE + WIDE)
        middle[:, columns] += dot(attended[...], matrix(weights, 6 + half))
    stores["normed"].wait()
    transpose_into(attended, turned_one)
    result, grad_normed, normed_two = wide_one, wide_two, normed
    stores["mixed"].wait()
    stores["inverse"].wait()

    def second_norm(at):
        value = middle[at, :]
        unit, _ = moments(value)
        normed_two[at, :] = (unit * rows[2:3, :] + rows[3:4, :]).astype(jnp.bfloat16)
        result[at, :] = value + rows[4:5, :]
        grad_normed[at, :] = jnp.zeros((64, WIDTH), jnp.float32)

    by_rows(second_norm)
    transpose_into(normed_two, turned_two)

    adder = Gradients(
        place,
        terms,
        weights,
        (rooms_one, rooms_two, rooms_three),
        owned,
        ring,
        ring_sem,
        terms_send_sem,
        terms_recv_sem,
    )

    def leave(block):
        first, half = 4 * (block // 2), block % 2
        return (
            pltpu.make_async_copy(staged.at[0], terms.at[first + 2 + half], stage_sem.at[0]),
            pltpu.make_async_copy(
                staged.at[1], terms.at[pl.ds(first, 2), half], stage_sem.at[1]
            ),
        )

    def last_tick(block):
        return LATE + 10 + 4 * (block // 2) + block % 2

    def feed(block):
        begin = last_tick(block - 1) + 1

        def both(step, carry):
            @pl.when(step >= LATE + 10)
            def _():
                gather_all.tick(step)

            @pl.when((step == begin) & (block > 0))
            def _():
                for item in leave(block - 1):
                    item.wait()

            @pl.when(step == TERMS_START)
            def _():
                pl.semaphore_wait(sibling_sem, 1)
                for index in range(TERMS_AHEAD):
                    adder.begin(index)

            @pl.when(step >= TERMS_START)
            def _():
                adder.tick(step - TERMS_START)

            return carry

        lax.fori_loop(begin, last_tick(block) + 1, both, 0)
        feed_block(
            block,
            (
                normed_two,
                turned_two,
                grad_out,
                weights,
                up_bias,
                result,
                grad_normed,
                staged,
                grad_up_bias,
            ),
        )
        for item in leave(block):
            item.start()

        @pl.when(block == 2)
        def _():
            stores["attention"].wait()
            pl.semaphore_signal(
                sibling_sem, 1, device_id=place.device("c", 1), device_id_type=MESH
            )

    each(8, feed)
    done = last_tick(7) + 1 - TERMS_START
    adder.tick(done)
    for item in leave(7):
        item.wait()
    gather_all.finish(LATE + 24 - DRAINED, CHUNKS)
    loads = {}

    def load(name, source, target):
        item = pltpu.make_async_copy(source, target, store_sem.at[4 + len(loads)])
        item.start()
        loads[name] = item

    load("out", attention_kept.at[pl.ds(6, 2)], weights.at[pl.ds(ROOMS + 6, 2)])
    load("normed", normed_t_kept, turned_two)
    load("rest", attention_kept.at[pl.ds(0, 6)], weights.at[pl.ds(ROOMS, 6)])
    grad_attended, shown, grad_middle = pixels, normed, middle

    def close_branch(at):
        unit, scale = moments(middle[at, :])
        grad = grad_out[at, :].astype(jnp.float32)
        value = grad_normed[at, :]
        shown[at, :] = result[at, :].astype(jnp.bfloat16)
        sums[0:1, :] += jnp.sum(value * unit, axis=0, keepdims=True)
        sums[1:2, :] += jnp.sum(value, axis=0, keepdims=True)
        sums[2:3, :] += jnp.sum(grad, axis=0, keepdims=True)
        scaled = value * rows[2:3, :]
        summed = grad + scale * (
            scaled
            - jnp.mean(scaled, axis=-1, keepdims=True)
            - unit * jnp.mean(scaled * unit, axis=-1, keepdims=True)
        )
        grad_middle[at, :] = summed
        grad_attended[at, :] = summed.astype(jnp.bfloat16)

    by_rows(close_branch)
    load("mixed", mixed_kept, mixed)
    load("inverse", inverse_kept, inverse)
    load("output", shown, output)
    adder.tick(done + 1)
    loads["out"].wait()
    grad_mixed = wide_three
    grad_mixed[...] = dot_nt(grad_attended[:, 0:WIDE], matrix(weights, ROOMS + 6)) + dot_nt(
        grad_attended[:, WIDE:WIDTH], matrix(weights, ROOMS + 7)
    )
    adder.tick(done + 2)

    def stage_out(slot, index):
        return pltpu.make_async_copy(staged.at[slot], terms.at[index], stage_sem.at[slot])

    for half in (0, 1):
        columns = slice(half * WIDE, half * WIDE + WIDE)
        value = dot(turned_one[...], grad_attended[:, columns]).astype(jnp.bfloat16)
        staged[half] = value.reshape(staged.shape[1:])
        stage_out(half, 16 + half).start()
    load("tokens", tokens_in, pixels)
    adder.tick(done + 3)
    for name in ("mixed", "inverse", "normed", "rest"):
        loads[name].wait()
    for half in (0, 1):
        stage_out(half, 16 + half).wait()
    spread = 14 - (done + 4)

    def back_heads(pair):
        @pl.when((pair + 1) * spread // 8 > pair * spread // 8)
        def _():
            adder.tick(done + 4 + pair * spread // 8)

        backward_heads(pair, qkv, mask, mask_t, mixed, inverse, grad_mixed)

    each(8, back_heads)
    grad_first = grad_mixed
    grad_first[...] = jnp.zeros(grad_first.shape, jnp.float32)

    def back_project(index):
        value = dot(turned_two[...], qkv[index]).astype(jnp.bfloat16)
        staged[index % 2] = value.reshape(staged.shape[1:])
        stage_out(index % 2, 18 + index).start()
        grad_first[...] += dot_nt(qkv[index], matrix(weights, ROOMS + index))

        @pl.when(index > 0)
        def _():
            stage_out((index - 1) % 2, 17 + index).wait()

        adder.tick(14 + index)

    each(6, back_project)
    stage_out(1, 23).wait()
    adder.tick(20)
    loads["tokens"].wait()
    loads["output"].wait()

    def close(at):
        unit, scale = moments(pixels[at, :].astype(jnp.float32))
        value = grad_first[at, :]
        sums[3:4, :] += jnp.sum(value * unit, axis=0, keepdims=True)
        sums[4:5, :] += jnp.sum(value, axis=0, keepdims=True)
        scaled = value * rows[0:1, :]
        shown[at, :] = (
            grad_middle[at, :]
            + scale
            * (
                scaled
                - jnp.mean(scaled, axis=-1, keepdims=True)
                - unit * jnp.mean(scaled * unit, axis=-1, keepdims=True)
            )
        ).astype(jnp.bfloat16)

    by_rows(close)
    load("input_grad", shown, input_grad)
    adder.tick(21)
    groups = [
        jnp.concatenate(
            [grad_up_bias[2 * group + half : 2 * group + half + 1, :] for half in (0, 1)], axis=1
        )
        for group in range(4)
    ]
    lines = [
        write_vectors([sums[index : index + 1, :] for index in (3, 4, 0, 1)], devices),
        write_vectors(groups, devices),
        write_vectors([sums[2:3, :]], devices),
    ]
    for device in range(devices):
        at = (
            device // (2 * inner * depth),
            (device // (2 * depth)) % inner,
            (device // depth) % 2,
            device % depth,
        )
        for row, line in enumerate(lines):
            small[at + (slice(row, row + 1),)] = line[device : device + 1, :]
        small[at + (slice(3, 8),)] = jnp.zeros((5, 128), jnp.float32)
    side = Sums(place, side_send_sem, side_recv_sem)
    rooms = (side_one, side_two, side_three)
    core = place.at["c"]
    side.start((), 0, 1, "c", small.at[:, :, 1 - core], side_total)

    def last_ticks(step):
        adder.tick(22 + step)

        @pl.when(step == 0)
        def _():
            side.copy((), 0, 1, "c", side_total, side_total).wait_recv()
            side.after_core((), "abz", small.at[:, :, core], side_total, rooms)

        for stage in (1, 2):

            @pl.when(step == stage)
            def _(stage=stage):
                side.after_stage((), "abz", stage, side_total, rooms)

        @pl.when(step == 3)
        def _():
            side.pass_on((), "abz", side_total, rooms)

        @pl.when(step == 4)
        def _():
            owned_small[...] = side.after_last((), "abz", side_total, rooms)

        @pl.when(step == 5)
        def _():
            back = hidden_order(True).astype(jnp.float32)
            for part in range(8):
                lanes = slice((part % 4) * 128, (part % 4) * 128 + 128)
                value = jnp.concatenate(
                    [owned[4 * group + 2 + part // 4, :, lanes] for group in range(4)], axis=1
                )
                owned_up[:, part * WIDE : (part + 1) * WIDE] = jnp.dot(
                    value, back, preferred_element_type=jnp.float32, precision=HIGH
                )

    each(CHUNKS + LATE - 23, last_ticks)
    load("up", owned_up, owned_up_out)
    load("feed", owned.at[pl.ds(0, 16)], owned_out.at[pl.ds(0, 16)])
    adder.tick(CHUNKS + LATE - 1)
    load("attention", owned.at[pl.ds(16, 8)], owned_out.at[pl.ds(16, 8)])
    vector_gather.drain(vectors, (), vector_order)
    side.drain((), "abz", side_total, rooms)
    adder.finish(CHUNKS + LATE - DRAINED)
    for name in ("input_grad", "up", "feed", "attention"):
        loads[name].wait()


def layer(dims, tokens, cotangent, crops, kept, small, shards):
    outer, inner, depth = dims
    most = max(dims)
    lead = (outer, inner, 2, depth)
    chip = (outer, inner, depth)
    tile, small_tile = (UNIT, WIDE), (8, 128)
    whole, turned = (LENGTH, WIDTH), (WIDTH, LENGTH)
    f32, bf16 = jnp.float32, jnp.bfloat16
    shape = jax.ShapeDtypeStruct
    room, dma = pltpu.VMEM, pltpu.SemaphoreType.DMA
    vmem, anywhere = pl.BlockSpec(memory_space=pltpu.VMEM), pl.BlockSpec(memory_space=pl.ANY)
    return pl.pallas_call(
        functools.partial(layer_kernel, dims),
        out_shape=[
            shape(whole, bf16),
            shape(whole, bf16),
            shape(whole, f32),
            shape(whole, f32),
            shape(turned, bf16),
            shape((FEED,) + lead + tile, bf16),
            shape((CHUNKS,) + lead + tile, bf16),
            shape((CHUNKS,) + tile, f32),
            shape((UNIT, HIDDEN), f32),
            shape(small_tile, f32),
        ],
        in_specs=[vmem] * 8 + [anywhere] * 8,
        out_specs=[anywhere] * 9 + [vmem],
        scratch_shapes=[
            room((CHUNKS,) + tile, f32),
            room((UNIT, HIDDEN), f32),
            room(whole, bf16),
            room(whole, bf16),
            room((CHUNKS,) + lead + tile, bf16),
            room((UNIT, HIDDEN), bf16),
            room(lead + small_tile, f32),
            room((8, WIDTH), f32),
            room((8, WIDE), f32),
            room((LENGTH, LENGTH), bf16),
            room((LENGTH, LENGTH), bf16),
            room((6, LENGTH, WIDE), bf16),
            room(whole, bf16),
            room(turned, bf16),
            room(turned, bf16),
            room(whole, f32),
            room(whole, f32),
            room(whole, f32),
            room(whole, f32),
            room((2,) + lead + tile, bf16),
            room((8, WIDE), f32),
            room((8, WIDTH), f32),
            room(lead + small_tile, f32),
            room((TERMS_AHEAD + 1,) + chip + tile, bf16),
            room((ROOMS, 2, 4) + tile, bf16),
            room((ROOMS, 8) + tile, bf16),
            room((ROOMS, 4) + tile, bf16),
            room(chip + small_tile, f32),
            room((2, 4) + small_tile, f32),
            room((8,) + small_tile, f32),
            room((4,) + small_tile, f32),
            dma((CHUNKS, 4, most)),
            dma((CHUNKS, 4, most)),
            dma((4, most)),
            dma((4, most)),
            dma((19,)),
            dma((15,)),
            dma((2,)),
            dma((TERMS_AHEAD + 1,)),
            dma((CHUNKS, 4, most)),
            dma((CHUNKS, 4, most)),
            dma((4, most)),
            dma((4, most)),
            pltpu.SemaphoreType.REGULAR,
        ],
        compiler_params=pltpu.CompilerParams(
            collective_id=0, has_side_effects=True, vmem_limit_bytes=VMEM_LIMIT
        ),
        name="layer",
    )(crops, kept, *small, tokens, cotangent, *shards)


def place_kernel(*refs):
    result, input_grad, owned, owned_up, small = refs[:5]
    outs, vectors, bias_up = refs[5:13], refs[13:18], refs[18]
    buffers, in_sem, out_sem = refs[19:27], refs[27], refs[28]
    _, _, query, key, value, out, _, down = buffers
    parts = [[(result, buffers[0].at[0])], [(input_grad, buffers[1].at[0])]]
    for number in (1, 2, 3, 0):
        target = (out, query, key, value)[number]
        parts.append(
            [
                (owned.at[16 + 2 * number + half], target.at[:, pl.ds(half * WIDE, WIDE)])
                for half in (0, 1)
            ]
        )
    parts.append([(owned_up, buffers[6])])
    parts.append(
        [
            (
                owned.at[4 * group + half],
                down.at[pl.ds(group * UNIT, UNIT), pl.ds(half * WIDE, WIDE)],
            )
            for group in range(4)
            for half in (0, 1)
        ]
    )
    loads, count = [], 0
    for items in parts:
        group = []
        for source, target in items:
            group.append(pltpu.make_async_copy(source, target, in_sem.at[count]))
            group[-1].start()
            count += 1
        loads.append(group)
    for index in range(4):
        vectors[index][...] = small[0, index * UNIT : (index + 1) * UNIT]
    vectors[4][...] = small[2, 0:UNIT]
    bias_up[...] = small[1, :]
    stores = []
    for index, group in enumerate(loads):
        for item in group:
            item.wait()
        stores.append(pltpu.make_async_copy(buffers[index], outs[index], out_sem.at[index]))
        stores[-1].start()
    for item in stores:
        item.wait()


def place_results(result, input_grad, owned, owned_up, small):
    f32, bf16 = jnp.float32, jnp.bfloat16
    shape = jax.ShapeDtypeStruct
    vmem, anywhere = pl.BlockSpec(memory_space=pltpu.VMEM), pl.BlockSpec(memory_space=pl.ANY)
    large = (
        [shape((1, LENGTH, WIDTH), bf16)] * 2
        + [shape((UNIT, WIDTH), f32)] * 4
        + [shape((UNIT, HIDDEN), f32), shape((4 * UNIT, WIDTH), f32)]
    )
    return pl.pallas_call(
        place_kernel,
        out_shape=large + [shape((UNIT,), f32)] * 5 + [shape((4 * UNIT,), f32)],
        in_specs=[anywhere] * 4 + [vmem],
        out_specs=[anywhere] * 8 + [vmem] * 6,
        scratch_shapes=[pltpu.VMEM(item.shape, item.dtype) for item in large]
        + [pltpu.SemaphoreType.DMA((19,)), pltpu.SemaphoreType.DMA((8,))],
        name="results",
    )(result, input_grad, owned, owned_up, small)


def body(
    tokens,
    crop_ids,
    kv_mask,
    norm1_gain,
    norm1_bias,
    w_query,
    w_key,
    w_value,
    w_out,
    norm2_gain,
    norm2_bias,
    w_up,
    up_bias,
    w_down,
    down_bias,
    cotangent,
):
    inner = lax.axis_size("dp") // (2 * OUTER)
    dims = (OUTER, inner, lax.axis_size("fsdp"))
    fits = (
        tokens.shape == (1, LENGTH, WIDTH)
        and w_up.shape == (UNIT, HIDDEN)
        and w_down.shape == (HIDDEN // WIDTH * UNIT, WIDTH)
        and dims == (2, 2, 4)
    )
    if not fits:
        return general_body(
            tokens,
            crop_ids,
            kv_mask,
            norm1_gain,
            norm1_bias,
            w_query,
            w_key,
            w_value,
            w_out,
            norm2_gain,
            norm2_bias,
            w_up,
            up_bias,
            w_down,
            down_bias,
            cotangent,
        )
    small = [
        vector.reshape(1, -1)
        for vector in (norm1_gain, norm1_bias, norm2_gain, norm2_bias, down_bias, up_bias)
    ]
    pixels, grads = tokens.reshape(LENGTH, WIDTH), cotangent.reshape(LENGTH, WIDTH)
    shards = (w_query, w_key, w_value, w_out, w_up, w_down)
    result, input_grad, *_, owned, owned_up, owned_small = layer(
        dims, pixels, grads, crop_ids, kv_mask, small, shards
    )
    (
        output,
        grad_tokens,
        grad_query,
        grad_key,
        grad_value,
        grad_out,
        grad_up,
        grad_down,
        grad_gain_one,
        grad_bias_one,
        grad_gain_two,
        grad_bias_two,
        grad_bias_down,
        grad_bias_up,
    ) = place_results(result, input_grad, owned, owned_up, owned_small)
    return (
        output,
        grad_tokens,
        grad_gain_one,
        grad_bias_one,
        grad_query,
        grad_key,
        grad_value,
        grad_out,
        grad_gain_two,
        grad_bias_two,
        grad_up,
        grad_bias_up,
        grad_down,
        grad_bias_down,
    )


def solution(mesh):
    return jax.shard_map(
        body,
        mesh=mesh,
        in_specs=(
            P(("dp", "fsdp"), None, None),
            P(("dp", "fsdp"), None),
            P(("dp", "fsdp"), None),
            P(("dp", "fsdp")),
            P(("dp", "fsdp")),
            P(("dp", "fsdp"), None),
            P(("dp", "fsdp"), None),
            P(("dp", "fsdp"), None),
            P(("dp", "fsdp"), None),
            P(("dp", "fsdp")),
            P(("dp", "fsdp")),
            P(("dp", "fsdp"), None),
            P(("dp", "fsdp")),
            P(("dp", "fsdp"), None),
            P(("dp", "fsdp")),
            P(("dp", "fsdp"), None, None),
        ),
        out_specs=(
            P(("dp", "fsdp"), None, None),
            P(("dp", "fsdp"), None, None),
            P(("dp", "fsdp")),
            P(("dp", "fsdp")),
            P(("dp", "fsdp"), None),
            P(("dp", "fsdp"), None),
            P(("dp", "fsdp"), None),
            P(("dp", "fsdp"), None),
            P(("dp", "fsdp")),
            P(("dp", "fsdp")),
            P(("dp", "fsdp"), None),
            P(("dp", "fsdp")),
            P(("dp", "fsdp"), None),
            P(("dp", "fsdp")),
        ),
        check_vma=False,
    )
```
